32 devices in a mesh: dp: 16 (over z, y, core), seq: 2 (over x).
Axes of the slice: x: 2, y: 2, z: 4, core: 2. Of those that a mesh axis runs over, the one named last changes fastest.
Arguments:
- latents: bfloat16 [16, 1024, 1152], P('dp', 'seq'), may hold values from -6 to 6
- out_grad: bfloat16 [16, 1024, 1152], P('dp', 'seq'), may hold values from -6 to 6
- time_table: bfloat16 [1000, 1152], replicated, may hold values from -6 to 6
- class_table: bfloat16 [1000, 1152], replicated, may hold values from -6 to 6
- buckets: int32 [16], replicated, may hold values from 0 to 999
- labels: int32 [16], replicated, may hold values from 0 to 999
- row_start: int32 [16, 2], P('dp', 'seq'), may hold values from 0 to 63
- ada_weight: bfloat16 [1, 1152, 6912], P(None, None, 'dp'), may hold values from -0.1875 to 0.1875
- qkv_weight: bfloat16 [1, 1152, 3456], P(None, 'seq', 'dp'), may hold values from -0.1875 to 0.1875
- proj_weight: bfloat16 [1, 1152, 1152], P(None, 'seq', 'dp'), may hold values from -4 to 4
- gate_weight: bfloat16 [1, 1152, 3072], P(None, 'seq', 'dp'), may hold values from -0.1875 to 0.1875
- up_weight: bfloat16 [1, 1152, 3072], P(None, 'seq', 'dp'), may hold values from -0.1875 to 0.1875
- down_weight: bfloat16 [1, 3072, 1152], P(None, 'seq', 'dp'), may hold values from -0.21875 to 0.21875
- query_gain: float32 [1, 72], replicated, may hold values from 0.1 to 1.9
- key_gain: float32 [1, 72], replicated, may hold values from 0.1 to 1.9
Outputs:
- result: bfloat16 [16, 1024, 1152], P('dp', 'seq')
- latent_grad: float32 [16, 1024, 1152], P('dp', 'seq')
- time_grad: float32 [1000, 1152], replicated
- class_grad: float32 [1000, 1152], replicated
- ada_grad: float32 [1, 1152, 6912], P(None, None, 'dp')
- qkv_grad: float32 [1, 1152, 3456], P(None, 'seq', 'dp')
- proj_grad: float32 [1, 1152, 1152], P(None, 'seq', 'dp')
- gate_grad: float32 [1, 1152, 3072], P(None, 'seq', 'dp')
- up_grad: float32 [1, 1152, 3072], P(None, 'seq', 'dp')
- down_grad: float32 [1, 3072, 1152], P(None, 'seq', 'dp')
- query_grad: float32 [1, 72], replicated
- key_grad: float32 [1, 72], replicated
The draws below stay inside these ranges and needn't reach their ends.
All inputs are finite; a program needn't handle non-finite values.
Results may differ from the reference program's by a relative error of at most 0.025.
Values may be sent and summed in bfloat16 or wider, within the bound.
No kernel may reach another device: no remote copies, remote signals or barrier semaphores. Data moves between devices by JAX's collectives and lax.ppermute only.
A program may use at most 256 MiB of HBM per device.

```python
import jax
import jax.numpy as jnp
from jax import lax

D = 1152
HEADS = 16
FF = 3072
CLASSES = 1000
BUCKETS = 1000
SIDE = 32
LAYERS = 1
HEAD_DIM = 72
SEQ = 1024
ITEMS = 16
N_SEQ = 2


def plant(array, key, least, high):
    place = [jax.random.randint(jax.random.fold_in(key, axis), (), 0, length) for axis, length in enumerate(array.shape)]
    main_axis = array.shape.index(max(array.shape))
    neighbour = place[:main_axis] + [(place[main_axis] + 1) % array.shape[main_axis]] + place[main_axis + 1:]
    return array.at[tuple(place)].set(least).at[tuple(neighbour)].set(high)


def block_scale(rng, extent, pieces, smallest, top_value):
    loudness, own = 1.0, jax.random.fold_in(rng, 6)
    for dim, parts in pieces:
        heights = jnp.exp(jax.random.uniform(jax.random.fold_in(own, dim), (parts,), jnp.float32, smallest / len(pieces), top_value / len(pieces)))
        loudness = loudness * jnp.repeat(heights, extent[dim] // parts).reshape([-1 if axis == dim else 1 for axis in range(len(extent))])
    return loudness


def normal_values(stream_key, dims, width, bound, cuts=(), kind=jnp.bfloat16):
    loudness = block_scale(stream_key, dims, cuts, -0.22, 0.18) if cuts else 1.0
    entries = jax.random.normal(stream_key, dims, jnp.float32) * width * loudness
    return jnp.minimum(jnp.maximum(entries, -bound), bound).astype(kind)


def setup_inputs(seed: int = 0) -> dict:
    arg_keys = jax.random.split(jax.random.key(seed), 16)
    return {
        "latents": normal_values(arg_keys[0], (ITEMS, SEQ, D), 1.0, 6.0, ((0, 16), (1, 2))),
        "out_grad": normal_values(arg_keys[1], (ITEMS, SEQ, D), 1.0, 6.0, ((0, 16), (1, 2))),
        "time_table": normal_values(arg_keys[2], (BUCKETS, D), 1.0, 6.0),
        "class_table": normal_values(arg_keys[3], (CLASSES, D), 1.0, 6.0),
        "buckets": plant(jax.random.randint(arg_keys[4], (ITEMS,), 0, BUCKETS), jax.random.fold_in(arg_keys[4], 1), 0, BUCKETS - 1).astype(jnp.int32),
        "labels": plant(jax.random.randint(arg_keys[5], (ITEMS,), 0, CLASSES), jax.random.fold_in(arg_keys[5], 1), 0, CLASSES - 1).astype(jnp.int32),
        "row_start": plant(jax.random.randint(arg_keys[6], (ITEMS, N_SEQ), 0, 2 * SIDE), jax.random.fold_in(arg_keys[6], 1), 0, (2 * SIDE) - 1).astype(jnp.int32),
        "ada_weight": normal_values(arg_keys[7], (LAYERS, D, 6 * D), D ** -0.5, 0.1875, ((2, 16),)),
        "qkv_weight": normal_values(arg_keys[8], (LAYERS, D, 3 * D), D ** -0.5, 0.1875, ((1, 2), (2, 16))),
        "proj_weight": normal_values(arg_keys[9], (LAYERS, D, D), 2 ** -0.5, 4.0, ((1, 2), (2, 16))),
        "gate_weight": normal_values(arg_keys[10], (LAYERS, D, FF), D ** -0.5, 0.1875, ((1, 2), (2, 16))),
        "up_weight": normal_values(arg_keys[11], (LAYERS, D, FF), D ** -0.5, 0.1875, ((1, 2), (2, 16))),
        "down_weight": normal_values(arg_keys[12], (LAYERS, FF, D), (FF // 4) ** -0.5, 0.21875, ((1, 2), (2, 16))),
        "query_gain": jnp.clip(1.0 + 0.18 * jax.random.normal(arg_keys[13], (LAYERS, HEAD_DIM), jnp.float32), 0.1, 1.9),
        "key_gain": jnp.clip(1.0 + 0.18 * jax.random.normal(arg_keys[14], (LAYERS, HEAD_DIM), jnp.float32), 0.1, 1.9),
    }


EPS = 1e-06
THETA = 10000.0
HIGHEST = lax.Precision.HIGHEST

@jax.custom_vjp
def low(v):
    return lax.optimization_barrier(v.astype(jnp.bfloat16)).astype(jnp.float32)

@jax.custom_vjp
def low_back(v):
    return v

def low_keep(v):
    return (low(v), None)

def low_pass(kept, grad):
    return (grad,)

def back_keep(v):
    return (v, None)

def back_low(kept, grad):
    return (low(grad),)
low.defvjp(low_keep, low_pass)
low_back.defvjp(back_keep, back_low)

def norm_factor(values):
    return lax.rsqrt(lax.optimization_barrier(jnp.mean(values * values, axis=-1, keepdims=True)) + EPS)

def modulate(values, shift_by, scale_by):
    return values * norm_factor(values) * (1.0 + scale_by) + shift_by

def rope_tables(row_pos, col_pos, head_dim):
    quarter = head_dim // 4
    frequency = THETA ** (-jnp.arange(quarter, dtype=jnp.float32) / quarter)
    angles = jnp.concatenate([row_pos[..., None] * frequency, col_pos[..., None] * frequency], axis=-1)
    cos_part = jnp.cos(angles)
    sin_part = jnp.sin(angles)
    return (jnp.concatenate([cos_part, cos_part], axis=-1), jnp.concatenate([sin_part, sin_part], axis=-1))

def rotate(values, cos_part, sin_part):
    half_dim = values.shape[-1] // 2
    turned = jnp.concatenate([-values[..., half_dim:], values[..., :half_dim]], axis=-1)
    return values * cos_part + turned * sin_part

def query_key(query_pre, key_pre, gain_query, gain_key, cos_part, sin_part):
    query_out = rotate(query_pre * norm_factor(query_pre) * gain_query, cos_part, sin_part)
    key_out = rotate(key_pre * norm_factor(key_pre) * gain_key, cos_part, sin_part)
    return (query_out, key_out)

def swiglu(gate_pre, up_pre):
    return jax.nn.silu(gate_pre) * up_pre

def layer_forward(residual, item_mod, qkv_mat, proj_mat, gate_mat, up_mat, down_mat, gain_query, gain_key, cos_part, sin_part):
    seq_len, model_width = residual.shape
    head_dim = gain_query.shape[0]
    head_count = model_width // head_dim
    inv_root = head_dim ** (-0.5)
    shift_attn, scale_attn, gate_attn, shift_mlp, scale_mlp, gate_mlp = jnp.split(item_mod, 6)
    normed = low(modulate(residual, shift_attn, scale_attn))
    projected = low_back(jnp.dot(normed, qkv_mat, precision=HIGHEST))
    query_pre = projected[:, :model_width].reshape(seq_len, head_count, head_dim)
    key_pre = projected[:, model_width:2 * model_width].reshape(seq_len, head_count, head_dim)
    queries, key_rows = query_key(query_pre, key_pre, gain_query, gain_key, cos_part, sin_part)
    queries = low(queries)
    key_rows = low(key_rows)
    value_rows = low(projected[:, 2 * model_width:]).reshape(seq_len, head_count, head_dim)
    scores = low_back(jnp.einsum('bhe,nhe->hbn', queries, key_rows, precision=HIGHEST) * inv_root)
    attn_probs = low(jax.nn.softmax(scores, axis=-1))
    attended = jnp.einsum('hbn,nhe->bhe', attn_probs, value_rows, precision=HIGHEST).reshape(seq_len, model_width)
    attended = low(low_back(attended))
    branch = low_back(jnp.dot(attended, proj_mat, precision=HIGHEST))
    middle = residual + gate_attn * branch
    normed_mid = low(modulate(middle, shift_mlp, scale_mlp))
    gate_pre = low_back(jnp.dot(normed_mid, gate_mat, precision=HIGHEST))
    up_pre = low_back(jnp.dot(normed_mid, up_mat, precision=HIGHEST))
    hidden = low(swiglu(gate_pre, up_pre))
    mlp_out = low_back(jnp.dot(hidden, down_mat, precision=HIGHEST))
    return middle + gate_mlp * mlp_out

def reference(latents, out_grad, time_table, class_table, buckets, labels, row_start, ada_weight, qkv_weight, proj_weight, gate_weight, up_weight, down_weight, query_gain, key_gain):
    head_dim = D // HEADS
    band_rows = SIDE * SIDE // N_SEQ
    tokens = jnp.arange(SIDE * SIDE, dtype=jnp.int32)
    band_index = tokens // band_rows
    within = tokens % band_rows
    row_pos = (row_start[:, band_index] + (within // SIDE)[None, :]).astype(jnp.float32)
    col_pos = jnp.broadcast_to((within % SIDE).astype(jnp.float32)[None, :], row_pos.shape)
    cos_all, sin_all = rope_tables(row_pos, col_pos, head_dim)

    def forward(latent_in, time_in, class_in, ada_in, qkv_in, proj_in, gate_in, up_in, down_in, qgain_in, kgain_in):
        cond = time_in[buckets] + class_in[labels]
        cond_act = low(jax.nn.silu(cond))
        modulation = low_back(jnp.einsum('id,ldm->ilm', cond_act, ada_in, precision=HIGHEST))

        def one_item(operands):
            residual, item_mod, item_cos, item_sin = operands
            for layer_no in range(ada_in.shape[0]):
                residual = layer_forward(residual, item_mod[layer_no], qkv_in[layer_no], proj_in[layer_no], gate_in[layer_no], up_in[layer_no], down_in[layer_no], qgain_in[layer_no], kgain_in[layer_no], item_cos[:, None, :], item_sin[:, None, :])
            return residual
        return lax.map(jax.checkpoint(one_item), (latent_in, modulation, cos_all, sin_all))
    outputs, pullback = jax.vjp(forward, latents.astype(jnp.float32), time_table.astype(jnp.float32), class_table.astype(jnp.float32), ada_weight.astype(jnp.float32), qkv_weight.astype(jnp.float32), proj_weight.astype(jnp.float32), gate_weight.astype(jnp.float32), up_weight.astype(jnp.float32), down_weight.astype(jnp.float32), query_gain, key_gain)
    grads = pullback(out_grad.astype(jnp.float32))
    return (outputs.astype(jnp.bfloat16), grads[0], grads[1], grads[2], grads[3], grads[4], grads[5], grads[6], grads[7], grads[8], grads[9], grads[10])
```

```python
import jax
import jax.numpy as jnp
from jax import lax
from jax.experimental import pallas as pl
from jax.experimental.layout import Layout, with_layout_constraint
from jax.experimental.pallas import tpu as pltpu
from jax.sharding import PartitionSpec as P

HEADS = 16
CLASSES = 1000
BUCKETS = 1000
SIDE = 32


EPS = 1e-06
THETA = 10000.0
HIGHEST = lax.Precision.HIGHEST


def norm_factor(values):
    return lax.rsqrt(jnp.mean(values * values, axis=-1, keepdims=True) + EPS)


def modulate(values, shift_by, scale_by):
    return values * norm_factor(values) * (1.0 + scale_by) + shift_by


def rope_tables(row_pos, col_pos, head_dim):
    quarter = head_dim // 4
    frequency = THETA ** (-jnp.arange(quarter, dtype=jnp.float32) / quarter)
    angles = jnp.concatenate(
        [row_pos[..., None] * frequency, col_pos[..., None] * frequency], axis=-1
    )
    cos_part = jnp.cos(angles)
    sin_part = jnp.sin(angles)
    return (
        jnp.concatenate([cos_part, cos_part], axis=-1),
        jnp.concatenate([sin_part, sin_part], axis=-1),
    )


def rotate(values, cos_part, sin_part):
    half_dim = values.shape[-1] // 2
    turned = jnp.concatenate([-values[..., half_dim:], values[..., :half_dim]], axis=-1)
    return values * cos_part + turned * sin_part


def query_key(query_pre, key_pre, gain_query, gain_key, cos_part, sin_part):
    query_out = rotate(query_pre * norm_factor(query_pre) * gain_query, cos_part, sin_part)
    key_out = rotate(key_pre * norm_factor(key_pre) * gain_key, cos_part, sin_part)
    return (query_out, key_out)


def swiglu(gate_pre, up_pre):
    return jax.nn.silu(gate_pre) * up_pre


def gather_layer(layer_no, qkv_weight, proj_weight, gate_weight, up_weight, down_weight):
    row_parts = (
        lax.all_gather(qkv_weight[layer_no], "seq", axis=0, tiled=True),
        lax.all_gather(proj_weight[layer_no], "seq", axis=0, tiled=True),
        lax.all_gather(gate_weight[layer_no], "seq", axis=0, tiled=True),
        lax.all_gather(up_weight[layer_no], "seq", axis=0, tiled=True),
        lax.all_gather(down_weight[layer_no], "seq", axis=0, tiled=True),
    )
    qkv_rows, proj_rows, gate_rows, up_rows, down_rows = row_parts
    return (
        lax.all_gather(qkv_rows, "dp", axis=1, tiled=True),
        lax.all_gather(proj_rows, "dp", axis=1, tiled=True),
        lax.all_gather(gate_rows, "dp", axis=1, tiled=True),
        lax.all_gather(up_rows, "dp", axis=1, tiled=True),
        lax.all_gather(down_rows, "dp", axis=1, tiled=True),
    )


def attend(queries, key_rows, value_rows, inv_root):
    items_dev, band_rows, head_count, head_dim = queries.shape
    top_score = jnp.full((items_dev, head_count, band_rows), -jnp.inf, jnp.float32)
    row_mass = jnp.zeros((items_dev, head_count, band_rows), jnp.float32)
    weighted = jnp.zeros((items_dev, band_rows, head_count, head_dim), jnp.float32)
    key_seg = lax.all_gather(key_rows, "seq", axis=1, tiled=True)
    value_seg = lax.all_gather(value_rows, "seq", axis=1, tiled=True)
    seg_rows = key_seg.shape[1]
    key_heads = key_seg.reshape(items_dev, seg_rows, head_count, head_dim)
    value_heads = value_seg.reshape(items_dev, seg_rows, head_count, head_dim)
    scores = (
        jnp.einsum("ibhe,inhe->ihbn", queries, key_heads, preferred_element_type=jnp.float32)
        * inv_root
    )
    new_top = jnp.max(scores, axis=-1)
    shrink = jnp.exp(top_score - new_top)
    weights = jnp.exp(scores - new_top[..., None])
    new_mass = row_mass * shrink + jnp.sum(weights, axis=-1)
    update = jnp.einsum(
        "ihbn,inhe->ibhe",
        weights.astype(jnp.bfloat16),
        value_heads,
        preferred_element_type=jnp.float32,
    )
    new_weighted = weighted * jnp.transpose(shrink, (0, 2, 1))[..., None] + update
    log_mass = new_top + jnp.log(new_mass)
    attended = new_weighted / jnp.transpose(new_mass, (0, 2, 1))[..., None]
    return (attended, log_mass)


def attend_back(queries, keys_all, values_all, attended_grad, log_mass, delta, inv_root):
    items_dev, band_rows, head_count, head_dim = queries.shape
    seq_len = keys_all.shape[1]
    key_heads = keys_all.reshape(items_dev, seq_len, head_count, head_dim)
    value_heads = values_all.reshape(items_dev, seq_len, head_count, head_dim)

    def one_item(operands):
        query_item, key_item, value_item, grad_item, mass_item, delta_item = operands
        scores = (
            jnp.einsum("bhe,nhe->hbn", query_item, key_item, preferred_element_type=jnp.float32)
            * inv_root
        )
        probs_full = jnp.exp(scores - mass_item[..., None])
        prob_grad = jnp.einsum(
            "bhe,nhe->hbn", grad_item, value_item, preferred_element_type=jnp.float32
        )
        score_grad = (probs_full * (prob_grad - delta_item[..., None])).astype(jnp.bfloat16)
        query_out_grad = (
            jnp.einsum("hbn,nhe->bhe", score_grad, key_item, preferred_element_type=jnp.float32)
            * inv_root
        )
        key_out_grad = (
            jnp.einsum("hbn,bhe->nhe", score_grad, query_item, preferred_element_type=jnp.float32)
            * inv_root
        )
        value_grad = jnp.einsum(
            "hbn,bhe->nhe",
            probs_full.astype(jnp.bfloat16),
            grad_item,
            preferred_element_type=jnp.float32,
        )
        return (query_out_grad, key_out_grad, value_grad)

    return lax.map(one_item, (queries, key_heads, value_heads, attended_grad, log_mass, delta))


def forward_layer(residual, modulation, weights, gain_query, gain_key, cos_part, sin_part):
    qkv_full, proj_full, gate_full, up_full, down_full = weights
    items_dev, band_rows, model_width = residual.shape
    head_count = HEADS
    head_dim = model_width // head_count
    inv_root = head_dim ** (-0.5)
    shift_attn, scale_attn, gate_attn, shift_mlp, scale_mlp, gate_mlp = jnp.split(
        modulation[:, None, :], 6, axis=-1
    )
    normed = modulate(residual, shift_attn, scale_attn).astype(jnp.bfloat16)
    projected = jnp.einsum("ibd,de->ibe", normed, qkv_full, preferred_element_type=jnp.float32)
    query_pre = projected[..., :model_width].reshape(items_dev, band_rows, head_count, head_dim)
    key_pre = projected[..., model_width : 2 * model_width].reshape(
        items_dev, band_rows, head_count, head_dim
    )
    queries, key_rows = query_key(query_pre, key_pre, gain_query, gain_key, cos_part, sin_part)
    queries = queries.astype(jnp.bfloat16)
    key_rows = key_rows.astype(jnp.bfloat16).reshape(items_dev, band_rows, model_width)
    value_rows = projected[..., 2 * model_width :].astype(jnp.bfloat16)
    attended, log_mass = attend(queries, key_rows, value_rows, inv_root)
    attended_low = attended.reshape(items_dev, band_rows, model_width).astype(jnp.bfloat16)
    branch = jnp.einsum("ibd,de->ibe", attended_low, proj_full, preferred_element_type=jnp.float32)
    middle = residual + gate_attn * branch
    normed_mid = modulate(middle, shift_mlp, scale_mlp).astype(jnp.bfloat16)
    gate_pre = jnp.einsum("ibd,df->ibf", normed_mid, gate_full, preferred_element_type=jnp.float32)
    up_pre = jnp.einsum("ibd,df->ibf", normed_mid, up_full, preferred_element_type=jnp.float32)
    hidden = swiglu(gate_pre, up_pre).astype(jnp.bfloat16)
    mlp_out = jnp.einsum("ibf,fd->ibd", hidden, down_full, preferred_element_type=jnp.float32)
    output = middle + gate_mlp * mlp_out
    stored = (
        residual,
        normed,
        query_pre,
        key_pre,
        queries,
        key_rows,
        value_rows,
        attended,
        attended_low,
        log_mass,
        branch,
        middle,
        normed_mid,
        gate_pre,
        up_pre,
        hidden,
        mlp_out,
    )
    return (output, stored)


def weight_terms(
    normed,
    attended_low,
    normed_mid,
    hidden,
    projected_grad,
    branch_grad,
    gate_pre_grad,
    up_pre_grad,
    mlp_grad,
):
    qkv_term = jnp.einsum("ibd,ibe->de", normed, projected_grad, preferred_element_type=jnp.float32)
    proj_term = jnp.einsum(
        "ibd,ibe->de", attended_low, branch_grad, preferred_element_type=jnp.float32
    )
    gate_term = jnp.einsum(
        "ibd,ibf->df", normed_mid, gate_pre_grad, preferred_element_type=jnp.float32
    )
    up_term = jnp.einsum("ibd,ibf->df", normed_mid, up_pre_grad, preferred_element_type=jnp.float32)
    down_term = jnp.einsum("ibf,ibd->fd", hidden, mlp_grad, preferred_element_type=jnp.float32)
    col_parts = (
        lax.psum_scatter(
            qkv_term.astype(jnp.bfloat16), "dp", scatter_dimension=1, tiled=True
        ).astype(jnp.float32),
        lax.psum_scatter(
            proj_term.astype(jnp.bfloat16), "dp", scatter_dimension=1, tiled=True
        ).astype(jnp.float32),
        lax.psum_scatter(
            gate_term.astype(jnp.bfloat16), "dp", scatter_dimension=1, tiled=True
        ).astype(jnp.float32),
        lax.psum_scatter(
            up_term.astype(jnp.bfloat16), "dp", scatter_dimension=1, tiled=True
        ).astype(jnp.float32),
        lax.psum_scatter(
            down_term.astype(jnp.bfloat16), "dp", scatter_dimension=1, tiled=True
        ).astype(jnp.float32),
    )
    qkv_cols, proj_cols, gate_cols, up_cols, down_cols = col_parts
    return (
        lax.psum_scatter(
            qkv_cols.astype(jnp.bfloat16), "seq", scatter_dimension=0, tiled=True
        ).astype(jnp.float32),
        lax.psum_scatter(
            proj_cols.astype(jnp.bfloat16), "seq", scatter_dimension=0, tiled=True
        ).astype(jnp.float32),
        lax.psum_scatter(
            gate_cols.astype(jnp.bfloat16), "seq", scatter_dimension=0, tiled=True
        ).astype(jnp.float32),
        lax.psum_scatter(
            up_cols.astype(jnp.bfloat16), "seq", scatter_dimension=0, tiled=True
        ).astype(jnp.float32),
        lax.psum_scatter(
            down_cols.astype(jnp.bfloat16), "seq", scatter_dimension=0, tiled=True
        ).astype(jnp.float32),
    )


def backward_layer(
    stored, resid_grad, modulation, weights, gain_query, gain_key, cos_part, sin_part
):
    qkv_full, proj_full, gate_full, up_full, down_full = weights
    (
        residual,
        normed,
        query_pre,
        key_pre,
        queries,
        key_rows,
        value_rows,
        attended,
        attended_low,
        log_mass,
        branch,
        middle,
        normed_mid,
        gate_pre,
        up_pre,
        hidden,
        mlp_out,
    ) = stored
    items_dev, band_rows, head_count, head_dim = queries.shape
    model_width = residual.shape[-1]
    inv_root = head_dim ** (-0.5)
    shift_attn, scale_attn, gate_attn, shift_mlp, scale_mlp, gate_mlp = jnp.split(
        modulation[:, None, :], 6, axis=-1
    )
    mlp_grad = (gate_mlp * resid_grad).astype(jnp.bfloat16)
    gate_mlp_grad = jnp.sum(resid_grad * mlp_out, axis=1, keepdims=True)
    hidden_grad = jnp.einsum("ibd,fd->ibf", mlp_grad, down_full, preferred_element_type=jnp.float32)
    unused_out, swiglu_back = jax.vjp(swiglu, gate_pre, up_pre)
    gate_pre_grad, up_pre_grad = swiglu_back(hidden_grad)
    gate_pre_grad = gate_pre_grad.astype(jnp.bfloat16)
    up_pre_grad = up_pre_grad.astype(jnp.bfloat16)
    normed_mid_grad = jnp.einsum(
        "ibf,df->ibd", gate_pre_grad, gate_full, preferred_element_type=jnp.float32
    )
    normed_mid_grad = normed_mid_grad + jnp.einsum(
        "ibf,df->ibd", up_pre_grad, up_full, preferred_element_type=jnp.float32
    )
    unused_mid, mid_back = jax.vjp(modulate, middle, shift_mlp, scale_mlp)
    mid_norm_grad, shift_mlp_grad, scale_mlp_grad = mid_back(normed_mid_grad)
    mid_grad = resid_grad + mid_norm_grad
    branch_grad = (gate_attn * mid_grad).astype(jnp.bfloat16)
    gate_attn_grad = jnp.sum(mid_grad * branch, axis=1, keepdims=True)
    attended_grad = jnp.einsum(
        "ibe,de->ibd", branch_grad, proj_full, preferred_element_type=jnp.float32
    ).astype(jnp.bfloat16)
    attended_grad = attended_grad.reshape(items_dev, band_rows, head_count, head_dim)
    delta = jnp.transpose(jnp.sum(attended_grad.astype(jnp.float32) * attended, axis=-1), (0, 2, 1))
    keys_all, values_all = (
        lax.all_gather(key_rows, "seq", axis=1, tiled=True),
        lax.all_gather(value_rows, "seq", axis=1, tiled=True),
    )
    query_out_grad, key_out_grad, value_grad = attend_back(
        queries, keys_all, values_all, attended_grad, log_mass, delta, inv_root
    )
    seq_len = keys_all.shape[1]
    key_band_grad, value_band_grad = (
        lax.psum_scatter(
            key_out_grad.reshape(items_dev, seq_len, model_width).astype(jnp.bfloat16),
            "seq",
            scatter_dimension=1,
            tiled=True,
        ).astype(jnp.float32),
        lax.psum_scatter(
            value_grad.reshape(items_dev, seq_len, model_width).astype(jnp.bfloat16),
            "seq",
            scatter_dimension=1,
            tiled=True,
        ).astype(jnp.float32),
    )

    def rotate_pair(query_in, key_in, gain_q, gain_k):
        return query_key(query_in, key_in, gain_q, gain_k, cos_part, sin_part)

    unused_pair, pair_back = jax.vjp(rotate_pair, query_pre, key_pre, gain_query, gain_key)
    query_pre_grad, key_pre_grad, query_gain_term, key_gain_term = pair_back(
        (query_out_grad, key_band_grad.reshape(items_dev, band_rows, head_count, head_dim))
    )
    projected_grad = jnp.concatenate(
        [
            query_pre_grad.reshape(items_dev, band_rows, model_width),
            key_pre_grad.reshape(items_dev, band_rows, model_width),
            value_band_grad,
        ],
        axis=-1,
    ).astype(jnp.bfloat16)
    normed_grad = jnp.einsum(
        "ibe,de->ibd", projected_grad, qkv_full, preferred_element_type=jnp.float32
    )
    unused_in, input_back = jax.vjp(modulate, residual, shift_attn, scale_attn)
    input_norm_grad, shift_attn_grad, scale_attn_grad = input_back(normed_grad)
    input_grad = mid_grad + input_norm_grad
    mod_grad = jnp.concatenate(
        [
            shift_attn_grad,
            scale_attn_grad,
            gate_attn_grad,
            shift_mlp_grad,
            scale_mlp_grad,
            gate_mlp_grad,
        ],
        axis=-1,
    )[:, 0, :]
    own_grads = weight_terms(
        normed,
        attended_low,
        normed_mid,
        hidden,
        projected_grad,
        branch_grad,
        gate_pre_grad,
        up_pre_grad,
        mlp_grad,
    )
    return (input_grad, mod_grad, own_grads, query_gain_term, key_gain_term)


def shards(
    latents,
    out_grad,
    time_table,
    class_table,
    buckets,
    labels,
    row_start,
    ada_weight,
    qkv_weight,
    proj_weight,
    gate_weight,
    up_weight,
    down_weight,
    query_gain,
    key_gain,
):
    items_dev, band_rows, model_width = latents.shape
    layer_count = qkv_weight.shape[0]
    head_dim = model_width // HEADS
    offsets = jnp.arange(band_rows, dtype=jnp.int32)
    row_pos = (row_start + (offsets // SIDE)[None, :]).astype(jnp.float32)
    col_pos = (offsets % SIDE).astype(jnp.float32)[None, :]
    cos_part, sin_part = rope_tables(row_pos, col_pos, head_dim)
    cos_part = cos_part[:, :, None, :]
    sin_part = sin_part[:, :, None, :]
    bucket_hot = (buckets[:, None] == jnp.arange(BUCKETS, dtype=jnp.int32)[None, :]).astype(
        jnp.bfloat16
    )
    class_hot = (labels[:, None] == jnp.arange(CLASSES, dtype=jnp.int32)[None, :]).astype(
        jnp.bfloat16
    )
    cond = jnp.dot(bucket_hot, time_table, preferred_element_type=jnp.float32) + jnp.dot(
        class_hot, class_table, preferred_element_type=jnp.float32
    )
    cond_act = jax.nn.silu(cond).astype(jnp.bfloat16)
    mod_cols = jnp.einsum("id,ldm->lim", cond_act, ada_weight, preferred_element_type=jnp.float32)
    modulation = lax.all_to_all(mod_cols, "dp", split_axis=1, concat_axis=2, tiled=True)
    residual = latents.astype(jnp.float32)
    gathered_all = []
    layer_no = 0
    weights = gather_layer(layer_no, qkv_weight, proj_weight, gate_weight, up_weight, down_weight)
    gathered_all.append(weights)
    residual, stored = forward_layer(
        residual,
        modulation[layer_no],
        weights,
        query_gain[layer_no],
        key_gain[layer_no],
        cos_part,
        sin_part,
    )
    stored_all = [stored]
    result = residual.astype(jnp.bfloat16)
    resid_grad = out_grad.astype(jnp.float32)
    mod_grads = [None] * layer_count
    grad_shards = [None] * layer_count
    query_terms = [None] * layer_count
    key_terms = [None] * layer_count
    for layer_no in reversed(range(layer_count)):
        weights = gather_layer(
            layer_no, qkv_weight, proj_weight, gate_weight, up_weight, down_weight
        )
        resid_grad, mod_grad, own_grads, query_term, key_term = backward_layer(
            stored_all[layer_no],
            resid_grad,
            modulation[layer_no],
            weights,
            query_gain[layer_no],
            key_gain[layer_no],
            cos_part,
            sin_part,
        )
        mod_grads[layer_no] = mod_grad
        grad_shards[layer_no] = own_grads
        query_terms[layer_no] = query_term
        key_terms[layer_no] = key_term
    band_mod, band_query, band_key = lax.psum(
        (jnp.stack(mod_grads), jnp.stack(query_terms), jnp.stack(key_terms)), "seq"
    )
    mod_cols_grad = lax.all_to_all(
        band_mod.astype(jnp.bfloat16), "dp", split_axis=2, concat_axis=1, tiled=True
    )
    ada_grad = jnp.einsum(
        "id,lim->ldm", cond_act, mod_cols_grad, preferred_element_type=jnp.float32
    )
    cond_act_part = jnp.einsum(
        "lim,ldm->id", mod_cols_grad, ada_weight, preferred_element_type=jnp.float32
    )
    cond_act_grad, query_grad, key_grad = (
        lax.psum(cond_act_part.astype(jnp.bfloat16), "dp").astype(jnp.float32),
        lax.psum(band_query.astype(jnp.bfloat16), "dp").astype(jnp.float32),
        lax.psum(band_key.astype(jnp.bfloat16), "dp").astype(jnp.float32),
    )
    unused_cond, silu_back = jax.vjp(jax.nn.silu, cond)
    cond_grad = silu_back(cond_act_grad)[0]
    time_grad = jnp.einsum(
        "ib,id->bd", bucket_hot.astype(jnp.float32), cond_grad, precision=HIGHEST
    )
    class_grad = jnp.einsum(
        "ib,id->bd", class_hot.astype(jnp.float32), cond_grad, precision=HIGHEST
    )
    qkv_grad = jnp.stack([grad_shards[0][0]])
    proj_grad = jnp.stack([grad_shards[0][1]])
    gate_grad = jnp.stack([grad_shards[0][2]])
    up_grad = jnp.stack([grad_shards[0][3]])
    down_grad = jnp.stack([grad_shards[0][4]])
    return (
        result,
        resid_grad,
        time_grad,
        class_grad,
        ada_grad,
        qkv_grad,
        proj_grad,
        gate_grad,
        up_grad,
        down_grad,
        query_grad,
        key_grad,
    )


BF16 = jnp.bfloat16
F32 = jnp.float32
LOG2E = 1.4426950408889634
LN2 = 0.6931471805599453
DP_AXES = ("z", "y", "c")


def together(*arrays):
    return lax.optimization_barrier(arrays)


def swap(values, axis):
    return lax.ppermute(values, axis, [(0, 1), (1, 0)])


def in_order(own, other, axis):
    first = lax.axis_index(axis) == 0
    return jnp.stack([jnp.where(first, own, other), jnp.where(first, other, own)])


def spread(values, axis):
    return in_order(values, swap(values, axis), axis)


def by_rows(values):
    return with_layout_constraint(values, Layout(major_to_minor=tuple(range(values.ndim))))


def gather_z(values):
    n_z = lax.axis_size("z")
    return lax.all_gather(values, "z", axis=0, tiled=True).reshape(n_z, *values.shape)


def add_low(*terms):
    total = terms[0].astype(F32)
    for term in terms[1:]:
        total = total + term.astype(F32)
    return total.astype(BF16)


def dot_f32(left, right, contract):
    return lax.dot_general(left, right, (contract, ((), ())), preferred_element_type=F32)


def assemble(pieces, plan, out_rows):
    n_z = pieces[0][0].shape[2]
    widths = [own.shape[-1] for own, _, _ in pieces]

    def kernel(core_ref, *refs):
        ins, outs = refs[: 2 * len(pieces)], refs[2 * len(pieces) :]
        for side in range(2):
            core = core_ref[0] if side == 0 else 1 - core_ref[0]
            for out_ref, parts in zip(outs, plan):
                row = 0
                for piece, start, rows in parts:
                    block = ins[2 * piece + side]
                    x_first = pieces[piece][2]
                    low = block[0, 0, 0] if x_first else block[0, 0, 0]
                    high = block[1, 0, 0] if x_first else block[0, 1, 0]
                    joined = jnp.concatenate([low[start : start + rows], high[start : start + rows]], axis=1)
                    out_ref[0, core, row : row + rows, :] = joined
                    row += rows

    in_specs = []
    operands = []
    for own, other, x_first in pieces:
        rows, width = own.shape[3:]
        if x_first:
            spec = pl.BlockSpec((2, 1, 1, rows, width), lambda i, core: (0, i % 2, i // 2, 0, 0))
        else:
            spec = pl.BlockSpec((1, 2, 1, rows, width), lambda i, core: (i % 2, 0, i // 2, 0, 0))
        in_specs += [spec, spec]
        operands += [own, other]
    out_shape, out_specs = [], []
    for parts, rows in zip(plan, out_rows):
        width = 2 * widths[parts[0][0]]
        out_shape.append(jax.ShapeDtypeStruct((2 * n_z, 2, rows, width), BF16))
        out_specs.append(pl.BlockSpec((1, 2, rows, width), lambda i, core: (i, 0, 0, 0)))
    outs = pl.pallas_call(
        kernel,
        grid_spec=pltpu.PrefetchScalarGridSpec(
            num_scalar_prefetch=1, grid=(2 * n_z,), in_specs=in_specs, out_specs=out_specs
        ),
        out_shape=out_shape,
        compiler_params=pltpu.CompilerParams(vmem_limit_bytes=40 << 20),
        name="assemble",
    )(lax.axis_index("c").astype(jnp.int32)[None], *operands)
    return [out.reshape(-1, out.shape[-1]) for out in outs]


def qkv_heads(normed, qkv_t, cos_t, sin_t, gains_t, head_dim, band):
    seq_len, width = normed.shape
    heads_all = qkv_t.shape[0] // head_dim
    heads = heads_all // 3
    group = 3
    q_scale = head_dim**-0.5 * LOG2E

    def kernel(norm_ref, w_ref, cos_ref, sin_ref, gain_ref, out_ref, hat_ref, fac_ref, acc_ref):
        acc_ref[...] = dot_f32(w_ref[...], norm_ref[...], ((1,), (1,)))
        step = pl.program_id(0)
        for i in range(group):
            head = step * group + i
            rows = pl.ds(i * head_dim, head_dim)

            @pl.when(head < 2 * heads)
            def _():
                values = acc_ref[rows, :]
                fac = lax.rsqrt(jnp.mean(values * values, axis=0, keepdims=True) + EPS)
                hat = values * fac
                gained = hat * jnp.where(head < heads, gain_ref[:, 0:1] * q_scale, gain_ref[:, 1:2])
                turned = jnp.concatenate([gained[head_dim // 2 :], gained[: head_dim // 2]], axis=0)
                out_ref[i] = (gained * cos_ref[...] + turned * sin_ref[...]).astype(BF16)
                hat_ref[i] = hat[:, :band].astype(BF16)
                fac_ref[i] = fac[:, :band]

            @pl.when(head >= 2 * heads)
            def _():
                out_ref[i] = acc_ref[rows, :].astype(BF16)
                hat_ref[i] = jnp.zeros((head_dim, band), BF16)
                fac_ref[i] = jnp.zeros((1, band), F32)

    whole = lambda i: (0, 0)
    return pl.pallas_call(
        kernel,
        grid=(heads_all // group,),
        in_specs=[
            pl.BlockSpec((seq_len, width), whole),
            pl.BlockSpec((group * head_dim, width), lambda i: (i, 0)),
            pl.BlockSpec((head_dim, seq_len), whole),
            pl.BlockSpec((head_dim, seq_len), whole),
            pl.BlockSpec((head_dim, 2), whole),
        ],
        out_specs=[
            pl.BlockSpec((group, head_dim, seq_len), lambda i: (i, 0, 0)),
            pl.BlockSpec((group, head_dim, band), lambda i: (i, 0, 0)),
            pl.BlockSpec((group, 1, band), lambda i: (i, 0, 0)),
        ],
        out_shape=[
            jax.ShapeDtypeStruct((heads_all, head_dim, seq_len), BF16),
            jax.ShapeDtypeStruct((heads_all, head_dim, band), BF16),
            jax.ShapeDtypeStruct((heads_all, 1, band), F32),
        ],
        scratch_shapes=[pltpu.VMEM((group * head_dim, seq_len), F32)],
        compiler_params=pltpu.CompilerParams(vmem_limit_bytes=40 << 20),
        name="qkv_heads",
    )(normed, qkv_t, cos_t, sin_t, gains_t)


def attention_forward(qkv, heads, band):
    _, head_dim, seq_len = qkv.shape

    def kernel(q_ref, k_ref, v_ref, out_ref, mass_ref):
        scores = dot_f32(k_ref[0], q_ref[0], ((0,), (0,)))
        weights = jnp.exp2(scores)
        mass = jnp.sum(weights, axis=0, keepdims=True)
        mixed = dot_f32(v_ref[0], weights.astype(BF16), ((1,), (0,)))
        out_ref[0] = (mixed / mass).astype(BF16)
        mass_ref[0] = jnp.log2(mass)

    return pl.pallas_call(
        kernel,
        grid=(heads,),
        in_specs=[
            pl.BlockSpec((1, head_dim, band), lambda h: (h, 0, 0)),
            pl.BlockSpec((1, head_dim, seq_len), lambda h: (heads + h, 0, 0)),
            pl.BlockSpec((1, head_dim, seq_len), lambda h: (2 * heads + h, 0, 0)),
        ],
        out_specs=[
            pl.BlockSpec((1, head_dim, band), lambda h: (h, 0, 0)),
            pl.BlockSpec((1, 1, band), lambda h: (h, 0, 0)),
        ],
        out_shape=[
            jax.ShapeDtypeStruct((heads, head_dim, band), BF16),
            jax.ShapeDtypeStruct((heads, 1, band), F32),
        ],
        compiler_params=pltpu.CompilerParams(vmem_limit_bytes=40 << 20),
        name="attention_forward",
    )(qkv, qkv, qkv)


def attention_back_own(qkv, out_grad, log_mass, delta, heads, band):
    _, head_dim, seq_len = qkv.shape

    def kernel(q_ref, k_ref, v_ref, grad_ref, mass_ref, delta_ref, dq_ref, dk_ref, dv_ref):
        grad = grad_ref[0]
        scores = dot_f32(k_ref[0], q_ref[0], ((0,), (0,)))
        probs = jnp.exp2(scores - mass_ref[0])
        prob_grad = dot_f32(v_ref[0], grad, ((0,), (0,)))
        score_grad = (probs * (prob_grad - delta_ref[0])).astype(BF16)
        dq_ref[0] = dot_f32(k_ref[0], score_grad, ((1,), (0,)))
        dk_ref[0] = dot_f32(q_ref[0], score_grad[:band], ((1,), (1,)))
        dv_ref[0] = dot_f32(grad, probs[:band].astype(BF16), ((1,), (1,)))

    one = pl.BlockSpec((1, head_dim, band), lambda h: (h, 0, 0))
    row = pl.BlockSpec((1, 1, band), lambda h: (h, 0, 0))
    return pl.pallas_call(
        kernel,
        grid=(heads,),
        in_specs=[
            one,
            pl.BlockSpec((1, head_dim, seq_len), lambda h: (heads + h, 0, 0)),
            pl.BlockSpec((1, head_dim, seq_len), lambda h: (2 * heads + h, 0, 0)),
            one,
            row,
            row,
        ],
        out_specs=[one, one, one],
        out_shape=[jax.ShapeDtypeStruct((heads, head_dim, band), F32)] * 3,
        compiler_params=pltpu.CompilerParams(vmem_limit_bytes=40 << 20),
        name="attention_back_own",
    )(qkv, qkv, qkv, out_grad, log_mass, delta)


def attention_back_other(
    qkv, hat, fac, cos_t, sin_t, gains_t, dq, dk, dv, grad, mass, delta, heads, band
):
    _, head_dim, seq_len = qkv.shape
    inv_root = head_dim**-0.5

    def kernel(
        q_ref, k_ref, v_ref, hq_ref, hk_ref, fq_ref, fk_ref, cos_ref, sin_ref, gain_ref,
        dq_ref, dk_ref, dv_ref, grad_ref, mass_ref, delta_ref, out_ref, gq_ref, gk_ref,
    ):
        grad = grad_ref[0]
        scores = dot_f32(k_ref[0], q_ref[0], ((0,), (0,)))
        probs = jnp.exp2(scores - mass_ref[0])
        prob_grad = dot_f32(v_ref[0], grad, ((0,), (0,)))
        score_grad = (probs * (prob_grad - delta_ref[0])).astype(BF16)
        key_grad = (dk_ref[0] + dot_f32(q_ref[0], score_grad, ((1,), (1,)))) * LN2
        value_grad = dv_ref[0] + dot_f32(grad, probs.astype(BF16), ((1,), (1,)))
        query_grad = dq_ref[0] * inv_root

        def back(turned_grad, hat, fac, gain):
            spun = turned_grad * sin_ref[...]
            spun = jnp.concatenate([spun[head_dim // 2 :], spun[: head_dim // 2]], axis=0)
            gained_grad = turned_grad * cos_ref[...] + spun
            gain_grad = jnp.sum(gained_grad * hat, axis=1, keepdims=True)
            hat_grad = gained_grad * gain
            along = jnp.mean(hat_grad * hat, axis=0, keepdims=True)
            return (fac * (hat_grad - hat * along)).astype(BF16), gain_grad

        out_ref[0, 0], gq_ref[0] = back(query_grad, hq_ref[0].astype(F32), fq_ref[0], gain_ref[:, 0:1])
        out_ref[1, 0], gk_ref[0] = back(key_grad, hk_ref[0].astype(F32), fk_ref[0], gain_ref[:, 1:2])
        out_ref[2, 0] = value_grad.astype(BF16)

    one = pl.BlockSpec((1, head_dim, band), lambda h: (h, 0, 0))
    row = pl.BlockSpec((1, 1, band), lambda h: (h, 0, 0))
    key_one = pl.BlockSpec((1, head_dim, band), lambda h: (heads + h, 0, 0))
    key_row = pl.BlockSpec((1, 1, band), lambda h: (heads + h, 0, 0))
    table = pl.BlockSpec((head_dim, band), lambda h: (0, 0))
    column = pl.BlockSpec((1, head_dim, 1), lambda h: (h, 0, 0))
    return pl.pallas_call(
        kernel,
        grid=(heads,),
        in_specs=[
            pl.BlockSpec((1, head_dim, band), lambda h: (h, 0, 1)),
            key_one,
            pl.BlockSpec((1, head_dim, band), lambda h: (2 * heads + h, 0, 0)),
            one, key_one, row, key_row, table, table,
            pl.BlockSpec((head_dim, 2), lambda h: (0, 0)),
            one, one, one, one, row, row,
        ],
        out_specs=[pl.BlockSpec((3, 1, head_dim, band), lambda h: (0, h, 0, 0)), column, column],
        out_shape=[
            jax.ShapeDtypeStruct((3, heads, head_dim, band), BF16),
            jax.ShapeDtypeStruct((heads, head_dim, 1), F32),
            jax.ShapeDtypeStruct((heads, head_dim, 1), F32),
        ],
        compiler_params=pltpu.CompilerParams(vmem_limit_bytes=40 << 20),
        name="attention_back_other",
    )(qkv, qkv, qkv, hat, hat, fac, fac, cos_t, sin_t, gains_t, dq, dk, dv, grad, mass, delta)


def split_rows(left_t):
    n_z = lax.axis_size("z")
    blocks = left_t.reshape(n_z, 2, 2, -1, left_t.shape[-1])
    core, row = lax.axis_index("c"), lax.axis_index("y")

    def part(which):
        picked = lax.dynamic_index_in_dim(blocks, which, 2, keepdims=False)
        own = lax.dynamic_index_in_dim(picked, row, 1, keepdims=False)
        other = lax.dynamic_index_in_dim(picked, 1 - row, 1, keepdims=False)
        return jnp.stack([own, other])

    return part(1 - core), part(core)


def split_columns(right, half):
    own = lax.axis_index("x") == 0
    low, high = right[:, :half], right[:, half:]
    return jnp.where(own, low, high), jnp.where(own, high, low)


def term(left, right):
    return jnp.einsum("yzrt,tk->yzrk", left, right, preferred_element_type=F32)


def fast_shards(
    latents, out_grad, time_table, class_table, buckets, labels, row_start,
    ada_weight, qkv_weight, proj_weight, gate_weight, up_weight, down_weight, query_gain, key_gain,
):
    band, width = latents.shape[1:]
    head_dim = width // HEADS
    lat, out_g = latents[0], out_grad[0]
    half = width // 2
    n_z = lax.axis_size("z")

    qkv_s, proj_s = qkv_weight[0].T, proj_weight[0].T
    gate_s, up_s, down_s = gate_weight[0].T, up_weight[0].T, by_rows(down_weight[0].T)
    cut = 144
    rest = qkv_s.shape[0] - cut
    gap = -rest % 16
    proj_rows = proj_s.shape[0]
    first = by_rows(jnp.concatenate([qkv_s, jnp.zeros((gap, half), BF16), proj_s]))
    second = by_rows(jnp.concatenate([gate_s, up_s]))
    gate_rows = gate_s.shape[0]

    first_z = gather_z(first)
    down_x = in_order(down_s, swap(down_s, "x"), "x")
    start_other = swap(row_start.astype(F32), "x")
    second_z = gather_z(second)

    bucket_hot = (buckets[:, None] == jnp.arange(BUCKETS, dtype=jnp.int32)[None, :]).astype(BF16)
    class_hot = (labels[:, None] == jnp.arange(CLASSES, dtype=jnp.int32)[None, :]).astype(BF16)
    cond = jnp.dot(bucket_hot, time_table, preferred_element_type=F32) + jnp.dot(
        class_hot, class_table, preferred_element_type=F32
    )
    cond_act = jax.nn.silu(cond).astype(BF16)
    mod_cols = jnp.dot(cond_act, ada_weight[0], preferred_element_type=F32)
    modulation = lax.all_to_all(mod_cols, DP_AXES, split_axis=0, concat_axis=1, tiled=True)
    shift_attn, scale_attn, gate_attn, shift_mlp, scale_mlp, gate_mlp = jnp.split(modulation, 6, axis=-1)

    offsets = jnp.arange(band, dtype=jnp.int32)
    rows_in = (offsets // SIDE).astype(F32)
    row_pos = jnp.concatenate([row_start.astype(F32)[0, 0] + rows_in, start_other[0, 0] + rows_in])
    col_pos = jnp.tile((offsets % SIDE).astype(F32), 2)
    quarter = head_dim // 4
    frequency = THETA ** (-jnp.arange(quarter, dtype=F32) / quarter)
    angles = jnp.concatenate([frequency[:, None] * row_pos[None], frequency[:, None] * col_pos[None]])
    cos_h, sin_h = jnp.cos(angles), jnp.sin(angles)
    cos_t = jnp.concatenate([cos_h, cos_h])
    sin_t = jnp.concatenate([-sin_h, sin_h])
    gains_t = jnp.concatenate([query_gain, key_gain]).T

    down_x, lat_x = together(down_x, lat)
    lat_other = swap(lat_x, "x")
    down_y = in_order(down_x, swap(down_x, "y"), "y")

    first_z, lat_other, down_y = together(first_z, lat_other, down_y)
    down_z = gather_z(down_y.reshape(-1, down_y.shape[-1]))
    part_a, part_b = together(spread(first_z[:, :cut], "y"), spread(first_z[:, cut:], "x"))
    lat_full = jnp.concatenate([lat, lat_other]).astype(F32)
    normed_full = modulate(lat_full, shift_attn, scale_attn).astype(BF16)

    part_a, part_b = together(spread(part_a, "x"), spread(part_b, "y"))
    second_z, part_a, part_b, normed_full = together(second_z, part_a, part_b, normed_full)

    part_a_c, part_b_c = swap(part_a, "c"), swap(part_b, "c")
    gate_y = spread(second_z[:, :gate_rows], "y")
    up_x = spread(second_z[:, gate_rows:], "x")
    qkv_t, proj_t = assemble(
        [(part_a, part_a_c, True), (part_b, part_b_c, False)],
        [[(0, 0, cut), (1, 0, rest)], [(1, rest + gap, proj_rows)]],
        [cut + rest, proj_rows],
    )
    qkv, hat, fac = qkv_heads(normed_full, qkv_t, cos_t, sin_t, gains_t, head_dim, band)
    qkv, gate_y, up_x = together(qkv, gate_y, up_x)

    gate_p, up_p = spread(gate_y, "x"), spread(up_x, "y")
    attended_t, log_mass = attention_forward(qkv, HEADS, band)
    attended_t = attended_t.reshape(width, band)
    branch = dot_f32(attended_t, proj_t, ((0,), (1,)))
    residual = lat.astype(F32)
    middle = residual + gate_attn * branch
    normed_mid = modulate(middle, shift_mlp, scale_mlp).astype(BF16)
    gate_p, up_p, down_z, normed_mid = together(gate_p, up_p, down_z, normed_mid)

    down_p = down_z.reshape(n_z, 2, 2, -1, down_z.shape[-1]).transpose(1, 2, 0, 3, 4)
    gate_c, up_c, down_c = swap(gate_p, "c"), swap(up_p, "c"), swap(down_p, "c")
    (gate_t,) = assemble([(gate_p, gate_c, True)], [[(0, 0, gate_rows)]], [gate_rows])
    (up_t,) = assemble([(up_p, up_c, False)], [[(0, 0, gate_rows)]], [gate_rows])
    (down_t,) = assemble([(down_p, down_c, False)], [[(0, 0, proj_rows)]], [proj_rows])

    nt = ((1,), (1,))
    gate_pre = dot_f32(normed_mid, gate_t, nt)
    up_pre = dot_f32(normed_mid, up_t, nt)
    hidden = swiglu(gate_pre, up_pre).astype(BF16)
    mlp_out = dot_f32(hidden, down_t, nt)
    result = (middle + gate_mlp * mlp_out).astype(BF16)

    resid_grad = out_g.astype(F32)
    mlp_grad = (gate_mlp * resid_grad).astype(BF16)
    gate_mlp_grad = jnp.sum(resid_grad * mlp_out, axis=0, keepdims=True)
    hidden_grad = dot_f32(mlp_grad, down_t, ((1,), (0,)))
    _, swiglu_back = jax.vjp(swiglu, gate_pre, up_pre)
    gate_pre_grad, up_pre_grad = swiglu_back(hidden_grad)
    gate_pre_grad, up_pre_grad = gate_pre_grad.astype(BF16), up_pre_grad.astype(BF16)

    hid_own, hid_other = split_columns(hidden, hidden.shape[1] // 2)
    mid_own, mid_other = split_columns(normed_mid, half)
    down_send, down_keep = split_rows(mlp_grad.T)
    gate_send, gate_keep = split_rows(gate_pre_grad.T)
    up_send, up_keep = split_rows(up_pre_grad.T)

    down_0 = term(down_send, hid_own).astype(BF16)
    down_1 = term(down_send, hid_other).astype(BF16)
    down_0, down_1, gate_send, up_send = together(down_0, down_1, gate_send, up_send)
    down_0r, down_1r = swap(down_0, "c"), swap(down_1, "c")
    gate_0, gate_1 = term(gate_send, mid_own).astype(BF16), term(gate_send, mid_other).astype(BF16)
    up_0, up_1 = term(up_send, mid_own).astype(BF16), term(up_send, mid_other).astype(BF16)
    normed_mid_grad = dot_f32(gate_pre_grad, gate_t, ((1,), (0,)))
    normed_mid_grad = normed_mid_grad + dot_f32(up_pre_grad, up_t, ((1,), (0,)))
    down_0r, down_1r, gate_0, gate_1, up_0, up_1, normed_mid_grad = together(
        down_0r, down_1r, gate_0, gate_1, up_0, up_1, normed_mid_grad
    )

    gate_0r, gate_1r, up_0r, up_1r = swap(gate_0, "c"), swap(gate_1, "c"), swap(up_0, "c"), swap(up_1, "c")
    down_0 = (term(down_keep, hid_own) + down_0r).astype(BF16)
    down_1 = (term(down_keep, hid_other) + down_1r).astype(BF16)
    down_sum = jnp.stack([down_0, down_1]).transpose(2, 0, 1, 3, 4)
    down_sum = lax.psum_scatter(
        down_sum.reshape(-1, down_sum.shape[-1]), "z", scatter_dimension=0, tiled=True
    ).reshape(2, 2, proj_rows, -1)
    _, mid_back = jax.vjp(modulate, middle, shift_mlp, scale_mlp)
    mid_norm_grad, shift_mlp_grad, scale_mlp_grad = mid_back(normed_mid_grad)
    mid_grad = resid_grad + mid_norm_grad
    branch_grad = (gate_attn * mid_grad).astype(BF16)
    gate_attn_grad = jnp.sum(mid_grad * branch, axis=0, keepdims=True)
    attended_grad = dot_f32(proj_t, branch_grad, ((0,), (1,))).astype(BF16)
    by_head = attended_grad.reshape(HEADS, head_dim, band)
    delta = jnp.sum(
        by_head.astype(F32) * attended_t.reshape(HEADS, head_dim, band).astype(F32), axis=1, keepdims=True
    )
    gate_0r, gate_1r, up_0r, up_1r, by_head, delta = together(gate_0r, gate_1r, up_0r, up_1r, by_head, delta)

    other_grad = swap(by_head, "x")
    other_rows = swap(jnp.stack([log_mass, delta]), "x")
    dq, dk, dv = attention_back_own(qkv, by_head, log_mass, delta, HEADS, band)
    up_0s, up_1s = (term(up_keep[1:], mid_own) + up_0r[1:]).astype(BF16), (
        term(up_keep[1:], mid_other) + up_1r[1:]
    ).astype(BF16)
    up_0r2, up_1r2 = swap(up_0s, "y"), swap(up_1s, "y")
    gate_s1 = (term(gate_keep, mid_other) + gate_1r).astype(BF16)
    gate_k = (term(gate_keep, mid_own) + gate_0r).astype(BF16)
    up_0k, up_1k = (term(up_keep[:1], mid_own) + up_0r[:1]).astype(BF16), (
        term(up_keep[:1], mid_other) + up_1r[:1]
    ).astype(BF16)
    other_grad, other_rows, dq, gate_s1, gate_k, up_0k, up_1k = together(
        other_grad, other_rows, dq, gate_s1, gate_k, up_0k, up_1k
    )

    gate_r1 = swap(gate_s1, "x")
    heads_grad, gain_q, gain_k = attention_back_other(
        qkv, hat, fac, cos_t, sin_t, gains_t, dq, dk, dv,
        other_grad, other_rows[0], other_rows[1], HEADS, band,
    )
    projected_t = heads_grad.reshape(3 * width, band)
    normed = normed_full[:band]
    nor_own, nor_other = split_columns(normed, half)
    att = attended_t.T
    att_own, att_other = split_columns(att, half)
    left_send, left_keep = split_rows(projected_t)
    proj_send, proj_keep = split_rows(branch_grad.T)
    q_0, q_1 = term(left_send, nor_own).astype(BF16), term(left_send, nor_other).astype(BF16)
    p_0, p_1 = term(proj_send, att_own).astype(BF16), term(proj_send, att_other).astype(BF16)
    q_0r, q_1r, p_0r, p_1r = swap(q_0, "c"), swap(q_1, "c"), swap(p_0, "c"), swap(p_1, "c")
    normed_grad = dot_f32(projected_t, qkv_t, ((0,), (0,)))
    _, input_back = jax.vjp(modulate, residual, shift_attn, scale_attn)
    input_norm_grad, shift_attn_grad, scale_attn_grad = input_back(normed_grad)
    input_grad = mid_grad + input_norm_grad
    q_0, q_1 = (term(left_keep, nor_own) + q_0r).astype(BF16), (term(left_keep, nor_other) + q_1r).astype(BF16)
    p_0, p_1 = (term(proj_keep, att_own) + p_0r).astype(BF16), (term(proj_keep, att_other) + p_1r).astype(BF16)
    low0, low1 = jnp.concatenate([q_0, p_0], axis=2), jnp.concatenate([q_1, p_1], axis=2)
    gate_r1, up_0r2, up_1r2, low0, low1, input_grad = together(gate_r1, up_0r2, up_1r2, low0, low1, input_grad)

    gate_s2 = add_low(gate_k[1], gate_r1[1])
    up_s2 = add_low(up_1k, up_1r2)[0]
    gate_r2, up_r2 = swap(gate_s2, "y"), swap(up_s2, "x")
    mod_grad = jnp.concatenate(
        [shift_attn_grad, scale_attn_grad, gate_attn_grad, shift_mlp_grad, scale_mlp_grad, gate_mlp_grad], axis=-1
    )
    small = jnp.concatenate([mod_grad, gain_q.sum(0).T, gain_k.sum(0).T], axis=-1)
    small = small + swap(small, "x")
    band_mod, band_gain = small[:, : 6 * width], small[:, 6 * width :]
    mod_cols_grad = lax.all_to_all(band_mod.astype(BF16), DP_AXES, split_axis=1, concat_axis=0, tiled=True)
    ada_grad = dot_f32(cond_act, mod_cols_grad, ((0,), (0,)))
    cond_act_part = dot_f32(mod_cols_grad, ada_weight[0], ((1,), (1,)))
    gate_r2, up_r2, low0, low1 = together(gate_r2, up_r2, low0, low1)

    gate_sum = add_low(gate_k[0], gate_r1[0], gate_r2)
    up_sum = add_low(up_0k[0], up_0r2[0], up_r2)
    gu = jnp.concatenate([gate_sum, up_sum], axis=1)
    gu = lax.psum_scatter(gu.reshape(-1, half), "z", scatter_dimension=0, tiled=True)
    row_a = cut
    a_r1 = swap(low1[:, :, :row_a], "x")
    b_r1a, b_r1b = swap(low0[1, :, row_a:], "y"), swap(low1[1, :, row_a:], "y")
    down_r = swap(down_sum[:, 1], "y")
    down_sum = add_low(down_sum[:, 0], down_r)
    a_r1, b_r1a, b_r1b, down_sum = together(a_r1, b_r1a, b_r1b, down_sum)

    a_r2 = swap(add_low(low0[1, :, :row_a], a_r1[1]), "y")
    b_r2 = swap(add_low(low1[0, :, row_a:], b_r1b), "x")
    down_r2 = swap(down_sum[1], "x")
    a_r2, b_r2, down_r2 = together(a_r2, b_r2, down_r2)

    a_sum = add_low(low0[0, :, :row_a], a_r1[0], a_r2)
    b_sum = add_low(low0[0, :, row_a:], b_r1a, b_r2)
    last = jnp.concatenate([a_sum, b_sum], axis=1)
    last = lax.psum_scatter(last.reshape(-1, half), "z", scatter_dimension=0, tiled=True)
    cond_act_grad, gains_grad = (
        lax.psum(cond_act_part.astype(BF16), DP_AXES).astype(F32),
        lax.psum(band_gain.astype(BF16), DP_AXES).astype(F32),
    )
    _, silu_back = jax.vjp(jax.nn.silu, cond)
    cond_grad = silu_back(cond_act_grad)[0]
    time_grad = jnp.einsum("ib,id->bd", bucket_hot.astype(F32), cond_grad, precision=HIGHEST)
    class_grad = jnp.einsum("ib,id->bd", class_hot.astype(F32), cond_grad, precision=HIGHEST)

    qkv_rows = cut + rest
    down_out = down_sum[0].astype(F32) + down_r2.astype(F32)

    def out(values):
        return values.T.astype(F32)[None]

    return (
        result[None],
        input_grad[None],
        time_grad,
        class_grad,
        ada_grad[None],
        out(last[:qkv_rows]),
        out(last[qkv_rows:]),
        out(gu[:gate_rows]),
        out(gu[gate_rows:]),
        out(down_out),
        gains_grad[:, :head_dim],
        gains_grad[:, head_dim:],
    )


def fast_solution(mesh):
    dp = mesh.shape["dp"]
    fine = jax.sharding.Mesh(mesh.devices.reshape(dp // 4, 2, 2, 2), ("z", "y", "c", "x"))
    items, last = P(DP_AXES, "x", None), P(None, "x", DP_AXES)
    in_specs = (items, items, P(), P(), P(), P(), P(DP_AXES, "x"), P(None, None, DP_AXES)) + (last,) * 5 + (P(), P())
    out_specs = (items, items, P(), P(), P(None, None, DP_AXES)) + (last,) * 5 + (P(), P())
    return jax.shard_map(fast_shards, mesh=fine, in_specs=in_specs, out_specs=out_specs, check_vma=False)


def solution(mesh):
    if mesh.shape["dp"] == 16 and mesh.shape["seq"] == 2:
        return fast_solution(mesh)
    in_specs = (
        P("dp", "seq", None),
        P("dp", "seq", None),
        P(),
        P(),
        P(),
        P(),
        P("dp", "seq"),
        P(None, None, "dp"),
        P(None, "seq", "dp"),
        P(None, "seq", "dp"),
        P(None, "seq", "dp"),
        P(None, "seq", "dp"),
        P(None, "seq", "dp"),
        P(),
        P(),
    )
    out_specs = (
        P("dp", "seq", None),
        P("dp", "seq", None),
        P(),
        P(),
        P(None, None, "dp"),
        P(None, "seq", "dp"),
        P(None, "seq", "dp"),
        P(None, "seq", "dp"),
        P(None, "seq", "dp"),
        P(None, "seq", "dp"),
        P(),
        P(),
    )
    return jax.shard_map(shards, mesh=mesh, in_specs=in_specs, out_specs=out_specs, check_vma=False)
```

```python
import jax
import jax.numpy as jnp
from jax import lax
from jax.experimental import pallas as pl
from jax.experimental.layout import Layout, with_layout_constraint
from jax.experimental.pallas import tpu as pltpu
from jax.sharding import PartitionSpec as P

HEADS = 16
CLASSES = 1000
BUCKETS = 1000
SIDE = 32


EPS = 1e-06
THETA = 10000.0
HIGHEST = lax.Precision.HIGHEST


def norm_factor(values):
    return lax.rsqrt(jnp.mean(values * values, axis=-1, keepdims=True) + EPS)


def modulate(values, shift_by, scale_by):
    return values * norm_factor(values) * (1.0 + scale_by) + shift_by


def rope_tables(row_pos, col_pos, head_dim):
    quarter = head_dim // 4
    frequency = THETA ** (-jnp.arange(quarter, dtype=jnp.float32) / quarter)
    angles = jnp.concatenate(
        [row_pos[..., None] * frequency, col_pos[..., None] * frequency], axis=-1
    )
    cos_part = jnp.cos(angles)
    sin_part = jnp.sin(angles)
    return (
        jnp.concatenate([cos_part, cos_part], axis=-1),
        jnp.concatenate([sin_part, sin_part], axis=-1),
    )


def rotate(values, cos_part, sin_part):
    half_dim = values.shape[-1] // 2
    turned = jnp.concatenate([-values[..., half_dim:], values[..., :half_dim]], axis=-1)
    return values * cos_part + turned * sin_part


def query_key(query_pre, key_pre, gain_query, gain_key, cos_part, sin_part):
    query_out = rotate(query_pre * norm_factor(query_pre) * gain_query, cos_part, sin_part)
    key_out = rotate(key_pre * norm_factor(key_pre) * gain_key, cos_part, sin_part)
    return (query_out, key_out)


def swiglu(gate_pre, up_pre):
    return jax.nn.silu(gate_pre) * up_pre


def gather_layer(layer_no, qkv_weight, proj_weight, gate_weight, up_weight, down_weight):
    row_parts = (
        lax.all_gather(qkv_weight[layer_no], "seq", axis=0, tiled=True),
        lax.all_gather(proj_weight[layer_no], "seq", axis=0, tiled=True),
        lax.all_gather(gate_weight[layer_no], "seq", axis=0, tiled=True),
        lax.all_gather(up_weight[layer_no], "seq", axis=0, tiled=True),
        lax.all_gather(down_weight[layer_no], "seq", axis=0, tiled=True),
    )
    qkv_rows, proj_rows, gate_rows, up_rows, down_rows = row_parts
    return (
        lax.all_gather(qkv_rows, "dp", axis=1, tiled=True),
        lax.all_gather(proj_rows, "dp", axis=1, tiled=True),
        lax.all_gather(gate_rows, "dp", axis=1, tiled=True),
        lax.all_gather(up_rows, "dp", axis=1, tiled=True),
        lax.all_gather(down_rows, "dp", axis=1, tiled=True),
    )


def attend(queries, key_rows, value_rows, inv_root):
    items_dev, band_rows, head_count, head_dim = queries.shape
    top_score = jnp.full((items_dev, head_count, band_rows), -jnp.inf, jnp.float32)
    row_mass = jnp.zeros((items_dev, head_count, band_rows), jnp.float32)
    weighted = jnp.zeros((items_dev, band_rows, head_count, head_dim), jnp.float32)
    key_seg = lax.all_gather(key_rows, "seq", axis=1, tiled=True)
    value_seg = lax.all_gather(value_rows, "seq", axis=1, tiled=True)
    seg_rows = key_seg.shape[1]
    key_heads = key_seg.reshape(items_dev, seg_rows, head_count, head_dim)
    value_heads = value_seg.reshape(items_dev, seg_rows, head_count, head_dim)
    scores = (
        jnp.einsum("ibhe,inhe->ihbn", queries, key_heads, preferred_element_type=jnp.float32)
        * inv_root
    )
    new_top = jnp.max(scores, axis=-1)
    shrink = jnp.exp(top_score - new_top)
    weights = jnp.exp(scores - new_top[..., None])
    new_mass = row_mass * shrink + jnp.sum(weights, axis=-1)
    update = jnp.einsum(
        "ihbn,inhe->ibhe",
        weights.astype(jnp.bfloat16),
        value_heads,
        preferred_element_type=jnp.float32,
    )
    new_weighted = weighted * jnp.transpose(shrink, (0, 2, 1))[..., None] + update
    log_mass = new_top + jnp.log(new_mass)
    attended = new_weighted / jnp.transpose(new_mass, (0, 2, 1))[..., None]
    return (attended, log_mass)


def attend_back(queries, keys_all, values_all, attended_grad, log_mass, delta, inv_root):
    items_dev, band_rows, head_count, head_dim = queries.shape
    seq_len = keys_all.shape[1]
    key_heads = keys_all.reshape(items_dev, seq_len, head_count, head_dim)
    value_heads = values_all.reshape(items_dev, seq_len, head_count, head_dim)

    def one_item(operands):
        query_item, key_item, value_item, grad_item, mass_item, delta_item = operands
        scores = (
            jnp.einsum("bhe,nhe->hbn", query_item, key_item, preferred_element_type=jnp.float32)
            * inv_root
        )
        probs_full = jnp.exp(scores - mass_item[..., None])
        prob_grad = jnp.einsum(
            "bhe,nhe->hbn", grad_item, value_item, preferred_element_type=jnp.float32
        )
        score_grad = (probs_full * (prob_grad - delta_item[..., None])).astype(jnp.bfloat16)
        query_out_grad = (
            jnp.einsum("hbn,nhe->bhe", score_grad, key_item, preferred_element_type=jnp.float32)
            * inv_root
        )
        key_out_grad = (
            jnp.einsum("hbn,bhe->nhe", score_grad, query_item, preferred_element_type=jnp.float32)
            * inv_root
        )
        value_grad = jnp.einsum(
            "hbn,bhe->nhe",
            probs_full.astype(jnp.bfloat16),
            grad_item,
            preferred_element_type=jnp.float32,
        )
        return (query_out_grad, key_out_grad, value_grad)

    return lax.map(one_item, (queries, key_heads, value_heads, attended_grad, log_mass, delta))


def forward_layer(residual, modulation, weights, gain_query, gain_key, cos_part, sin_part):
    qkv_full, proj_full, gate_full, up_full, down_full = weights
    items_dev, band_rows, model_width = residual.shape
    head_count = HEADS
    head_dim = model_width // head_count
    inv_root = head_dim ** (-0.5)
    shift_attn, scale_attn, gate_attn, shift_mlp, scale_mlp, gate_mlp = jnp.split(
        modulation[:, None, :], 6, axis=-1
    )
    normed = modulate(residual, shift_attn, scale_attn).astype(jnp.bfloat16)
    projected = jnp.einsum("ibd,de->ibe", normed, qkv_full, preferred_element_type=jnp.float32)
    query_pre = projected[..., :model_width].reshape(items_dev, band_rows, head_count, head_dim)
    key_pre = projected[..., model_width : 2 * model_width].reshape(
        items_dev, band_rows, head_count, head_dim
    )
    queries, key_rows = query_key(query_pre, key_pre, gain_query, gain_key, cos_part, sin_part)
    queries = queries.astype(jnp.bfloat16)
    key_rows = key_rows.astype(jnp.bfloat16).reshape(items_dev, band_rows, model_width)
    value_rows = projected[..., 2 * model_width :].astype(jnp.bfloat16)
    attended, log_mass = attend(queries, key_rows, value_rows, inv_root)
    attended_low = attended.reshape(items_dev, band_rows, model_width).astype(jnp.bfloat16)
    branch = jnp.einsum("ibd,de->ibe", attended_low, proj_full, preferred_element_type=jnp.float32)
    middle = residual + gate_attn * branch
    normed_mid = modulate(middle, shift_mlp, scale_mlp).astype(jnp.bfloat16)
    gate_pre = jnp.einsum("ibd,df->ibf", normed_mid, gate_full, preferred_element_type=jnp.float32)
    up_pre = jnp.einsum("ibd,df->ibf", normed_mid, up_full, preferred_element_type=jnp.float32)
    hidden = swiglu(gate_pre, up_pre).astype(jnp.bfloat16)
    mlp_out = jnp.einsum("ibf,fd->ibd", hidden, down_full, preferred_element_type=jnp.float32)
    output = middle + gate_mlp * mlp_out
    stored = (
        residual,
        normed,
        query_pre,
        key_pre,
        queries,
        key_rows,
        value_rows,
        attended,
        attended_low,
        log_mass,
        branch,
        middle,
        normed_mid,
        gate_pre,
        up_pre,
        hidden,
        mlp_out,
    )
    return (output, stored)


def weight_terms(
    normed,
    attended_low,
    normed_mid,
    hidden,
    projected_grad,
    branch_grad,
    gate_pre_grad,
    up_pre_grad,
    mlp_grad,
):
    qkv_term = jnp.einsum("ibd,ibe->de", normed, projected_grad, preferred_element_type=jnp.float32)
    proj_term = jnp.einsum(
        "ibd,ibe->de", attended_low, branch_grad, preferred_element_type=jnp.float32
    )
    gate_term = jnp.einsum(
        "ibd,ibf->df", normed_mid, gate_pre_grad, preferred_element_type=jnp.float32
    )
    up_term = jnp.einsum("ibd,ibf->df", normed_mid, up_pre_grad, preferred_element_type=jnp.float32)
    down_term = jnp.einsum("ibf,ibd->fd", hidden, mlp_grad, preferred_element_type=jnp.float32)
    col_parts = (
        lax.psum_scatter(
            qkv_term.astype(jnp.bfloat16), "dp", scatter_dimension=1, tiled=True
        ).astype(jnp.float32),
        lax.psum_scatter(
            proj_term.astype(jnp.bfloat16), "dp", scatter_dimension=1, tiled=True
        ).astype(jnp.float32),
        lax.psum_scatter(
            gate_term.astype(jnp.bfloat16), "dp", scatter_dimension=1, tiled=True
        ).astype(jnp.float32),
        lax.psum_scatter(
            up_term.astype(jnp.bfloat16), "dp", scatter_dimension=1, tiled=True
        ).astype(jnp.float32),
        lax.psum_scatter(
            down_term.astype(jnp.bfloat16), "dp", scatter_dimension=1, tiled=True
        ).astype(jnp.float32),
    )
    qkv_cols, proj_cols, gate_cols, up_cols, down_cols = col_parts
    return (
        lax.psum_scatter(
            qkv_cols.astype(jnp.bfloat16), "seq", scatter_dimension=0, tiled=True
        ).astype(jnp.float32),
        lax.psum_scatter(
            proj_cols.astype(jnp.bfloat16), "seq", scatter_dimension=0, tiled=True
        ).astype(jnp.float32),
        lax.psum_scatter(
            gate_cols.astype(jnp.bfloat16), "seq", scatter_dimension=0, tiled=True
        ).astype(jnp.float32),
        lax.psum_scatter(
            up_cols.astype(jnp.bfloat16), "seq", scatter_dimension=0, tiled=True
        ).astype(jnp.float32),
        lax.psum_scatter(
            down_cols.astype(jnp.bfloat16), "seq", scatter_dimension=0, tiled=True
        ).astype(jnp.float32),
    )


def backward_layer(
    stored, resid_grad, modulation, weights, gain_query, gain_key, cos_part, sin_part
):
    qkv_full, proj_full, gate_full, up_full, down_full = weights
    (
        residual,
        normed,
        query_pre,
        key_pre,
        queries,
        key_rows,
        value_rows,
        attended,
        attended_low,
        log_mass,
        branch,
        middle,
        normed_mid,
        gate_pre,
        up_pre,
        hidden,
        mlp_out,
    ) = stored
    items_dev, band_rows, head_count, head_dim = queries.shape
    model_width = residual.shape[-1]
    inv_root = head_dim ** (-0.5)
    shift_attn, scale_attn, gate_attn, shift_mlp, scale_mlp, gate_mlp = jnp.split(
        modulation[:, None, :], 6, axis=-1
    )
    mlp_grad = (gate_mlp * resid_grad).astype(jnp.bfloat16)
    gate_mlp_grad = jnp.sum(resid_grad * mlp_out, axis=1, keepdims=True)
    hidden_grad = jnp.einsum("ibd,fd->ibf", mlp_grad, down_full, preferred_element_type=jnp.float32)
    unused_out, swiglu_back = jax.vjp(swiglu, gate_pre, up_pre)
    gate_pre_grad, up_pre_grad = swiglu_back(hidden_grad)
    gate_pre_grad = gate_pre_grad.astype(jnp.bfloat16)
    up_pre_grad = up_pre_grad.astype(jnp.bfloat16)
    normed_mid_grad = jnp.einsum(
        "ibf,df->ibd", gate_pre_grad, gate_full, preferred_element_type=jnp.float32
    )
    normed_mid_grad = normed_mid_grad + jnp.einsum(
        "ibf,df->ibd", up_pre_grad, up_full, preferred_element_type=jnp.float32
    )
    unused_mid, mid_back = jax.vjp(modulate, middle, shift_mlp, scale_mlp)
    mid_norm_grad, shift_mlp_grad, scale_mlp_grad = mid_back(normed_mid_grad)
    mid_grad = resid_grad + mid_norm_grad
    branch_grad = (gate_attn * mid_grad).astype(jnp.bfloat16)
    gate_attn_grad = jnp.sum(mid_grad * branch, axis=1, keepdims=True)
    attended_grad = jnp.einsum(
        "ibe,de->ibd", branch_grad, proj_full, preferred_element_type=jnp.float32
    ).astype(jnp.bfloat16)
    attended_grad = attended_grad.reshape(items_dev, band_rows, head_count, head_dim)
    delta = jnp.transpose(jnp.sum(attended_grad.astype(jnp.float32) * attended, axis=-1), (0, 2, 1))
    keys_all, values_all = (
        lax.all_gather(key_rows, "seq", axis=1, tiled=True),
        lax.all_gather(value_rows, "seq", axis=1, tiled=True),
    )
    query_out_grad, key_out_grad, value_grad = attend_back(
        queries, keys_all, values_all, attended_grad, log_mass, delta, inv_root
    )
    seq_len = keys_all.shape[1]
    key_band_grad, value_band_grad = (
        lax.psum_scatter(
            key_out_grad.reshape(items_dev, seq_len, model_width).astype(jnp.bfloat16),
            "seq",
            scatter_dimension=1,
            tiled=True,
        ).astype(jnp.float32),
        lax.psum_scatter(
            value_grad.reshape(items_dev, seq_len, model_width).astype(jnp.bfloat16),
            "seq",
            scatter_dimension=1,
            tiled=True,
        ).astype(jnp.float32),
    )

    def rotate_pair(query_in, key_in, gain_q, gain_k):
        return query_key(query_in, key_in, gain_q, gain_k, cos_part, sin_part)

    unused_pair, pair_back = jax.vjp(rotate_pair, query_pre, key_pre, gain_query, gain_key)
    query_pre_grad, key_pre_grad, query_gain_term, key_gain_term = pair_back(
        (query_out_grad, key_band_grad.reshape(items_dev, band_rows, head_count, head_dim))
    )
    projected_grad = jnp.concatenate(
        [
            query_pre_grad.reshape(items_dev, band_rows, model_width),
            key_pre_grad.reshape(items_dev, band_rows, model_width),
            value_band_grad,
        ],
        axis=-1,
    ).astype(jnp.bfloat16)
    normed_grad = jnp.einsum(
        "ibe,de->ibd", projected_grad, qkv_full, preferred_element_type=jnp.float32
    )
    unused_in, input_back = jax.vjp(modulate, residual, shift_attn, scale_attn)
    input_norm_grad, shift_attn_grad, scale_attn_grad = input_back(normed_grad)
    input_grad = mid_grad + input_norm_grad
    mod_grad = jnp.concatenate(
        [
            shift_attn_grad,
            scale_attn_grad,
            gate_attn_grad,
            shift_mlp_grad,
            scale_mlp_grad,
            gate_mlp_grad,
        ],
        axis=-1,
    )[:, 0, :]
    own_grads = weight_terms(
        normed,
        attended_low,
        normed_mid,
        hidden,
        projected_grad,
        branch_grad,
        gate_pre_grad,
        up_pre_grad,
        mlp_grad,
    )
    return (input_grad, mod_grad, own_grads, query_gain_term, key_gain_term)


def shards(
    latents,
    out_grad,
    time_table,
    class_table,
    buckets,
    labels,
    row_start,
    ada_weight,
    qkv_weight,
    proj_weight,
    gate_weight,
    up_weight,
    down_weight,
    query_gain,
    key_gain,
):
    items_dev, band_rows, model_width = latents.shape
    layer_count = qkv_weight.shape[0]
    head_dim = model_width // HEADS
    offsets = jnp.arange(band_rows, dtype=jnp.int32)
    row_pos = (row_start + (offsets // SIDE)[None, :]).astype(jnp.float32)
    col_pos = (offsets % SIDE).astype(jnp.float32)[None, :]
    cos_part, sin_part = rope_tables(row_pos, col_pos, head_dim)
    cos_part = cos_part[:, :, None, :]
    sin_part = sin_part[:, :, None, :]
    bucket_hot = (buckets[:, None] == jnp.arange(BUCKETS, dtype=jnp.int32)[None, :]).astype(
        jnp.bfloat16
    )
    class_hot = (labels[:, None] == jnp.arange(CLASSES, dtype=jnp.int32)[None, :]).astype(
        jnp.bfloat16
    )
    cond = jnp.dot(bucket_hot, time_table, preferred_element_type=jnp.float32) + jnp.dot(
        class_hot, class_table, preferred_element_type=jnp.float32
    )
    cond_act = jax.nn.silu(cond).astype(jnp.bfloat16)
    mod_cols = jnp.einsum("id,ldm->lim", cond_act, ada_weight, preferred_element_type=jnp.float32)
    modulation = lax.all_to_all(mod_cols, "dp", split_axis=1, concat_axis=2, tiled=True)
    residual = latents.astype(jnp.float32)
    gathered_all = []
    layer_no = 0
    weights = gather_layer(layer_no, qkv_weight, proj_weight, gate_weight, up_weight, down_weight)
    gathered_all.append(weights)
    residual, stored = forward_layer(
        residual,
        modulation[layer_no],
        weights,
        query_gain[layer_no],
        key_gain[layer_no],
        cos_part,
        sin_part,
    )
    stored_all = [stored]
    result = residual.astype(jnp.bfloat16)
    resid_grad = out_grad.astype(jnp.float32)
    mod_grads = [None] * layer_count
    grad_shards = [None] * layer_count
    query_terms = [None] * layer_count
    key_terms = [None] * layer_count
    for layer_no in reversed(range(layer_count)):
        weights = gather_layer(
            layer_no, qkv_weight, proj_weight, gate_weight, up_weight, down_weight
        )
        resid_grad, mod_grad, own_grads, query_term, key_term = backward_layer(
            stored_all[layer_no],
            resid_grad,
            modulation[layer_no],
            weights,
            query_gain[layer_no],
            key_gain[layer_no],
            cos_part,
            sin_part,
        )
        mod_grads[layer_no] = mod_grad
        grad_shards[layer_no] = own_grads
        query_terms[layer_no] = query_term
        key_terms[layer_no] = key_term
    band_mod, band_query, band_key = lax.psum(
        (jnp.stack(mod_grads), jnp.stack(query_terms), jnp.stack(key_terms)), "seq"
    )
    mod_cols_grad = lax.all_to_all(
        band_mod.astype(jnp.bfloat16), "dp", split_axis=2, concat_axis=1, tiled=True
    )
    ada_grad = jnp.einsum(
        "id,lim->ldm", cond_act, mod_cols_grad, preferred_element_type=jnp.float32
    )
    cond_act_part = jnp.einsum(
        "lim,ldm->id", mod_cols_grad, ada_weight, preferred_element_type=jnp.float32
    )
    cond_act_grad, query_grad, key_grad = (
        lax.psum(cond_act_part.astype(jnp.bfloat16), "dp").astype(jnp.float32),
        lax.psum(band_query.astype(jnp.bfloat16), "dp").astype(jnp.float32),
        lax.psum(band_key.astype(jnp.bfloat16), "dp").astype(jnp.float32),
    )
    unused_cond, silu_back = jax.vjp(jax.nn.silu, cond)
    cond_grad = silu_back(cond_act_grad)[0]
    time_grad = jnp.einsum(
        "ib,id->bd", bucket_hot.astype(jnp.float32), cond_grad, precision=HIGHEST
    )
    class_grad = jnp.einsum(
        "ib,id->bd", class_hot.astype(jnp.float32), cond_grad, precision=HIGHEST
    )
    qkv_grad = jnp.stack([grad_shards[0][0]])
    proj_grad = jnp.stack([grad_shards[0][1]])
    gate_grad = jnp.stack([grad_shards[0][2]])
    up_grad = jnp.stack([grad_shards[0][3]])
    down_grad = jnp.stack([grad_shards[0][4]])
    return (
        result,
        resid_grad,
        time_grad,
        class_grad,
        ada_grad,
        qkv_grad,
        proj_grad,
        gate_grad,
        up_grad,
        down_grad,
        query_grad,
        key_grad,
    )


BF16 = jnp.bfloat16
F32 = jnp.float32
LOG2E = 1.4426950408889634
LN2 = 0.6931471805599453
DP_AXES = ("z", "y", "c")
SMALL = pl.CostEstimate(flops=1, bytes_accessed=1, transcendentals=0)


def kernel_call(kernel, **options):
    return pl.pallas_call(kernel, cost_estimate=SMALL, **options)


def together(*arrays):
    return lax.optimization_barrier(arrays)


def swap(values, axis):
    return lax.ppermute(values, axis, [(0, 1), (1, 0)])


def in_order(own, other, axis):
    first = lax.axis_index(axis) == 0
    return jnp.stack([jnp.where(first, own, other), jnp.where(first, other, own)])


def spread(values, axis):
    return in_order(values, swap(values, axis), axis)


def by_rows(values):
    return with_layout_constraint(values, Layout(major_to_minor=tuple(range(values.ndim))))


def gather_z(values):
    n_z = lax.axis_size("z")
    return lax.all_gather(values, "z", axis=0, tiled=True).reshape(n_z, *values.shape)


def add_low(*terms):
    total = terms[0].astype(F32)
    for term in terms[1:]:
        total = total + term.astype(F32)
    return total.astype(BF16)


def dot_f32(left, right, contract):
    return lax.dot_general(left, right, (contract, ((), ())), preferred_element_type=F32)


def piece_targets(pieces, at):
    for k, (array, z_first, x, y, c) in enumerate(pieces):
        for z in range(array.shape[0]):
            block = ((z_first + z) * 2 + (at[2] + y) % 2) * 2 + (at[0] + c) % 2
            yield k, z, (at[1] + x) % 2, block


def join_rows(pieces, first_row, rows):
    width = pieces[0][0].shape[-1]
    half = width // 2
    blocks = sum(piece[0].shape[0] for piece in pieces) // 2

    def kernel(at, *refs):
        out_ref, buf, sems = refs[len(pieces) :]
        copies = []
        for k, z, x, block in piece_targets(pieces, at):
            copy = pltpu.make_async_copy(
                refs[k].at[z, pl.ds(first_row, rows)], buf.at[x, block], sems.at[x, block]
            )
            copy.start()
            copies.append(copy)
        for copy in copies:
            copy.wait()
        for block in range(blocks):
            out_ref[block] = jnp.concatenate([buf[0, block][:, half:], buf[1, block][:, half:]], axis=1)

    return kernel_call(
        kernel,
        grid_spec=pltpu.PrefetchScalarGridSpec(
            num_scalar_prefetch=1,
            grid=(1,),
            in_specs=[pl.BlockSpec(memory_space=pl.ANY)] * len(pieces),
            out_specs=[pl.BlockSpec((blocks, rows, width), lambda i, at: (0, 0, 0))],
            scratch_shapes=[pltpu.VMEM((2, blocks, rows, width), BF16), pltpu.SemaphoreType.DMA((2, blocks))],
        ),
        out_shape=[jax.ShapeDtypeStruct((blocks, rows, width), BF16)],
        compiler_params=pltpu.CompilerParams(vmem_limit_bytes=24 << 20),
        name="join_rows",
    )(place(), *[piece[0] for piece in pieces])[0]


def qkv_heads(normed, pieces, cos_t, sin_t, gains_t, head_dim, band, before=()):
    seq_len, width = normed.shape
    heads = HEADS
    group = 3
    rows_all = group * head_dim
    half = width // 2
    sent = pieces[0][0].shape[1]
    q_scale = head_dim**-0.5 * LOG2E
    side = pieces[0][4]
    steps = sum(piece[0].shape[0] for piece in pieces) // 2
    n_in = len(pieces)

    def kernel(at, norm_ref, cos_ref, sin_ref, gain_ref, *refs):
        out_ref, hat_ref, fac_ref, whole_ref, acc_ref, buf, sems = refs[n_in + len(before) :]

        @pl.when(pl.program_id(0) == 0)
        def _():
            for k, z, x, block in piece_targets(pieces, at):
                local = block // 2
                pltpu.make_async_copy(refs[k].at[z], buf.at[x, local], sems.at[x, local]).start()

        local = pl.program_id(0)
        step = 2 * local + (at[0] + side) % 2
        for x in range(2):
            pltpu.make_async_copy(refs[0].at[0], buf.at[x, local], sems.at[x, local]).wait()
        low, high = buf[0, local], buf[1, local]
        whole_ref[:sent] = jnp.concatenate([low[:, :half], high[:, :half]], axis=1)
        whole_ref[sent:] = jnp.concatenate([low[: rows_all - sent, half:], high[: rows_all - sent, half:]], axis=1)
        acc_ref[...] = dot_f32(whole_ref[...], norm_ref[...], ((1,), (1,)))
        for i in range(group):
            head = step * group + i
            rows = pl.ds(i * head_dim, head_dim)

            @pl.when(head < 2 * heads)
            def _():
                values = acc_ref[rows, :]
                fac = lax.rsqrt(jnp.mean(values * values, axis=0, keepdims=True) + EPS)
                hat = values * fac
                gained = hat * jnp.where(head < heads, gain_ref[:, 0:1] * q_scale, gain_ref[:, 1:2])
                turned = jnp.concatenate([gained[head_dim // 2 :], gained[: head_dim // 2]], axis=0)
                out_ref[i] = (gained * cos_ref[...] + turned * sin_ref[...]).astype(BF16)
                hat_ref[i] = hat[:, :band].astype(BF16)
                fac_ref[i] = fac[:, :band]

            @pl.when(head >= 2 * heads)
            def _():
                out_ref[i] = acc_ref[rows, :].astype(BF16)
                hat_ref[i] = jnp.zeros((head_dim, band), BF16)
                fac_ref[i] = jnp.zeros((1, band), F32)

    whole = lambda i, at: (0, 0)
    return kernel_call(
        kernel,
        grid_spec=pltpu.PrefetchScalarGridSpec(
            num_scalar_prefetch=1,
            grid=(steps,),
            in_specs=[
                pl.BlockSpec((seq_len, width), whole),
                pl.BlockSpec((head_dim, seq_len), whole),
                pl.BlockSpec((head_dim, seq_len), whole),
                pl.BlockSpec((head_dim, 2), whole),
            ]
            + [pl.BlockSpec(memory_space=pl.ANY)] * (n_in + len(before)),
            out_specs=[
                pl.BlockSpec((group, head_dim, seq_len), lambda i, at: (2 * i + (at[0] + side) % 2, 0, 0)),
                pl.BlockSpec((group, head_dim, band), lambda i, at: (2 * i + (at[0] + side) % 2, 0, 0)),
                pl.BlockSpec((group, 1, band), lambda i, at: (2 * i + (at[0] + side) % 2, 0, 0)),
                pl.BlockSpec((rows_all, width), lambda i, at: (2 * i + (at[0] + side) % 2, 0)),
            ],
            scratch_shapes=[
                pltpu.VMEM((rows_all, seq_len), F32),
                pltpu.VMEM((2, steps, sent, width), BF16),
                pltpu.SemaphoreType.DMA((2, steps)),
            ],
        ),
        out_shape=[
            jax.ShapeDtypeStruct((3 * heads, head_dim, seq_len), BF16),
            jax.ShapeDtypeStruct((3 * heads, head_dim, band), BF16),
            jax.ShapeDtypeStruct((3 * heads, 1, band), F32),
            jax.ShapeDtypeStruct((3 * width, width), BF16),
        ],
        input_output_aliases={5 + n_in + k: k for k in range(len(before))},
        compiler_params=pltpu.CompilerParams(vmem_limit_bytes=32 << 20),
        name="qkv_heads",
    )(place(), normed, cos_t, sin_t, gains_t, *[piece[0] for piece in pieces], *before)


def attention_forward(qkv, heads, band):
    _, head_dim, seq_len = qkv.shape

    def kernel(q_ref, k_ref, v_ref, out_ref, mass_ref):
        scores = dot_f32(k_ref[0], q_ref[0], ((0,), (0,)))
        weights = jnp.exp2(scores)
        mass = jnp.sum(weights, axis=0, keepdims=True)
        mixed = dot_f32(v_ref[0], weights.astype(BF16), ((1,), (0,)))
        out_ref[0] = (mixed / mass).astype(BF16)
        mass_ref[0] = jnp.log2(mass)

    return kernel_call(
        kernel,
        grid=(heads,),
        in_specs=[
            pl.BlockSpec((1, head_dim, band), lambda h: (h, 0, 0)),
            pl.BlockSpec((1, head_dim, seq_len), lambda h: (heads + h, 0, 0)),
            pl.BlockSpec((1, head_dim, seq_len), lambda h: (2 * heads + h, 0, 0)),
        ],
        out_specs=[
            pl.BlockSpec((1, head_dim, band), lambda h: (h, 0, 0)),
            pl.BlockSpec((1, 1, band), lambda h: (h, 0, 0)),
        ],
        out_shape=[
            jax.ShapeDtypeStruct((heads, head_dim, band), BF16),
            jax.ShapeDtypeStruct((heads, 1, band), F32),
        ],
        compiler_params=pltpu.CompilerParams(vmem_limit_bytes=20 << 20),
        name="attention_forward",
    )(qkv, qkv, qkv)


def attention_back_own(qkv, out_grad, log_mass, delta, heads, band):
    _, head_dim, seq_len = qkv.shape

    def kernel(q_ref, k_ref, v_ref, grad_ref, mass_ref, delta_ref, dq_ref, dk_ref, dv_ref):
        grad = grad_ref[0]
        scores = dot_f32(k_ref[0], q_ref[0], ((0,), (0,)))
        probs = jnp.exp2(scores - mass_ref[0])
        prob_grad = dot_f32(v_ref[0], grad, ((0,), (0,)))
        score_grad = (probs * (prob_grad - delta_ref[0])).astype(BF16)
        dq_ref[0] = dot_f32(k_ref[0], score_grad, ((1,), (0,)))
        dk_ref[0] = dot_f32(q_ref[0], score_grad[:band], ((1,), (1,)))
        dv_ref[0] = dot_f32(grad, probs[:band].astype(BF16), ((1,), (1,)))

    one = pl.BlockSpec((1, head_dim, band), lambda h: (h, 0, 0))
    row = pl.BlockSpec((1, 1, band), lambda h: (h, 0, 0))
    return kernel_call(
        kernel,
        grid=(heads,),
        in_specs=[
            one,
            pl.BlockSpec((1, head_dim, seq_len), lambda h: (heads + h, 0, 0)),
            pl.BlockSpec((1, head_dim, seq_len), lambda h: (2 * heads + h, 0, 0)),
            one,
            row,
            row,
        ],
        out_specs=[one, one, one],
        out_shape=[jax.ShapeDtypeStruct((heads, head_dim, band), F32)] * 3,
        compiler_params=pltpu.CompilerParams(vmem_limit_bytes=24 << 20),
        name="attention_back_own",
    )(qkv, qkv, qkv, out_grad, log_mass, delta)


def attention_back_other(
    qkv, hat, fac, cos_t, sin_t, gains_t, dq, dk, dv, grad, mass, delta, heads, band
):
    _, head_dim, seq_len = qkv.shape
    inv_root = head_dim**-0.5

    def kernel(
        q_ref, k_ref, v_ref, hq_ref, hk_ref, fq_ref, fk_ref, cos_ref, sin_ref, gain_ref,
        dq_ref, dk_ref, dv_ref, grad_ref, mass_ref, delta_ref, out_ref, gq_ref, gk_ref,
    ):
        grad = grad_ref[0]
        scores = dot_f32(k_ref[0], q_ref[0], ((0,), (0,)))
        probs = jnp.exp2(scores - mass_ref[0])
        prob_grad = dot_f32(v_ref[0], grad, ((0,), (0,)))
        score_grad = (probs * (prob_grad - delta_ref[0])).astype(BF16)
        key_grad = (dk_ref[0] + dot_f32(q_ref[0], score_grad, ((1,), (1,)))) * LN2
        value_grad = dv_ref[0] + dot_f32(grad, probs.astype(BF16), ((1,), (1,)))
        query_grad = dq_ref[0] * inv_root

        def back(turned_grad, hat, fac, gain):
            spun = turned_grad * sin_ref[...]
            spun = jnp.concatenate([spun[head_dim // 2 :], spun[: head_dim // 2]], axis=0)
            gained_grad = turned_grad * cos_ref[...] + spun
            gain_grad = jnp.sum(gained_grad * hat, axis=1, keepdims=True)
            hat_grad = gained_grad * gain
            along = jnp.mean(hat_grad * hat, axis=0, keepdims=True)
            return (fac * (hat_grad - hat * along)).astype(BF16), gain_grad

        out_ref[0, 0], gq_ref[0] = back(query_grad, hq_ref[0].astype(F32), fq_ref[0], gain_ref[:, 0:1])
        out_ref[1, 0], gk_ref[0] = back(key_grad, hk_ref[0].astype(F32), fk_ref[0], gain_ref[:, 1:2])
        out_ref[2, 0] = value_grad.astype(BF16)

    one = pl.BlockSpec((1, head_dim, band), lambda h: (h, 0, 0))
    row = pl.BlockSpec((1, 1, band), lambda h: (h, 0, 0))
    key_one = pl.BlockSpec((1, head_dim, band), lambda h: (heads + h, 0, 0))
    key_row = pl.BlockSpec((1, 1, band), lambda h: (heads + h, 0, 0))
    table = pl.BlockSpec((head_dim, band), lambda h: (0, 0))
    column = pl.BlockSpec((1, head_dim, 1), lambda h: (h, 0, 0))
    return kernel_call(
        kernel,
        grid=(heads,),
        in_specs=[
            pl.BlockSpec((1, head_dim, band), lambda h: (h, 0, 1)),
            key_one,
            pl.BlockSpec((1, head_dim, band), lambda h: (2 * heads + h, 0, 0)),
            one, key_one, row, key_row, table, table,
            pl.BlockSpec((head_dim, 2), lambda h: (0, 0)),
            one, one, one, one, row, row,
        ],
        out_specs=[pl.BlockSpec((3, 1, head_dim, band), lambda h: (0, h, 0, 0)), column, column],
        out_shape=[
            jax.ShapeDtypeStruct((3, heads, head_dim, band), BF16),
            jax.ShapeDtypeStruct((heads, head_dim, 1), F32),
            jax.ShapeDtypeStruct((heads, head_dim, 1), F32),
        ],
        compiler_params=pltpu.CompilerParams(vmem_limit_bytes=20 << 20),
        name="attention_back_other",
    )(qkv, qkv, qkv, hat, hat, fac, fac, cos_t, sin_t, gains_t, dq, dk, dv, grad, mass, delta)


def mlp(mid, mlp_grad, pieces, down_own, down_other):
    band, width = mlp_grad.shape
    rows = pieces[0][0].shape[1]
    half = width // 2
    blocks = sum(piece[0].shape[0] for piece in pieces) // 2
    steps = 4
    per = blocks // steps
    units = per * rows
    chunk = band // 2
    n_z, _, _, down_rows, down_width = down_own.shape

    def kernel(at, mid_ref, mg_ref, *refs):
        downs = refs[len(pieces) : len(pieces) + 2]
        hid_ref, gg_ref, ug_ref, out_ref, grad_ref, buf, down_buf, sems, down_sems = refs[len(pieces) + 2 :]
        step = pl.program_id(0)

        @pl.when(step == 0)
        def _():
            for x in range(2):
                for z in range(n_z):
                    for y in range(2):
                        for c in range(2):
                            block = (z * 2 + y) * 2 + (at[0] + c) % 2
                            target = down_buf.at[x, pl.ds(pl.multiple_of(block * down_rows, 8), down_rows)]
                            pltpu.make_async_copy(downs[c].at[z, y, x], target, down_sems.at[x, block]).start()
            for k, z, x, block in piece_targets(pieces, at):
                pltpu.make_async_copy(refs[k].at[z], buf.at[x, block], sems.at[x, block]).start()
            out_ref[...] = jnp.zeros_like(out_ref)
            grad_ref[...] = jnp.zeros_like(grad_ref)

        for b in range(per):
            for x in range(2):
                block = step * per + b
                pltpu.make_async_copy(refs[0].at[0], buf.at[x, block], sems.at[x, block]).wait()
        @pl.when(step % 2 == 0)
        def _():
            for block in range(4 * n_z):
                target = down_buf.at[step // 2, pl.ds(block * down_rows, down_rows)]
                pltpu.make_async_copy(downs[0].at[0, 0, 0], target, down_sems.at[step // 2, block]).wait()

        low = buf[0, pl.ds(step * per, per)].reshape(units, width)
        high = buf[1, pl.ds(step * per, per)].reshape(units, width)
        gate = jnp.concatenate([low[:, :half], high[:, :half]], axis=1)
        up = jnp.concatenate([low[:, half:], high[:, half:]], axis=1)
        down = down_buf[step // 2, :, pl.ds(pl.multiple_of(step % 2 * units, 128), units)]
        nt, nn = ((1,), (1,)), ((1,), (0,))
        for part in range(2):
            at_rows = pl.ds(part * chunk, chunk)
            mid = mid_ref[at_rows, :]
            gate_pre = dot_f32(mid, gate, nt)
            up_pre = dot_f32(mid, up, nt)
            hidden_grad = dot_f32(mg_ref[at_rows, :], down, nn)
            sig = 1.0 / (1.0 + jnp.exp(-gate_pre))
            act = gate_pre * sig
            hidden = (act * up_pre).astype(BF16)
            gate_grad = (hidden_grad * up_pre * (sig * (1.0 + gate_pre * (1.0 - sig)))).astype(BF16)
            up_grad = (hidden_grad * act).astype(BF16)
            hid_ref[at_rows, :] = hidden
            gg_ref[:, at_rows] = gate_grad.T
            ug_ref[:, at_rows] = up_grad.T
            out_ref[at_rows, :] += dot_f32(hidden, down, nt)
            grad_ref[at_rows, :] += dot_f32(gate_grad, gate, nn) + dot_f32(up_grad, up, nn)

    whole = lambda i, at: (0, 0)
    once = pl.Buffered(1)
    return kernel_call(
        kernel,
        grid_spec=pltpu.PrefetchScalarGridSpec(
            num_scalar_prefetch=1,
            grid=(steps,),
            in_specs=[
                pl.BlockSpec((band, width), whole, pipeline_mode=once),
                pl.BlockSpec((band, width), whole, pipeline_mode=once),
            ]
            + [pl.BlockSpec(memory_space=pl.ANY)] * (len(pieces) + 2),
            out_specs=[
                pl.BlockSpec((band, units), lambda i, at: (0, i)),
                pl.BlockSpec((units, band), lambda i, at: (i, 0)),
                pl.BlockSpec((units, band), lambda i, at: (i, 0)),
                pl.BlockSpec((band, width), whole, pipeline_mode=once),
                pl.BlockSpec((band, width), whole, pipeline_mode=once),
            ],
            scratch_shapes=[
                pltpu.VMEM((2, blocks, rows, width), BF16),
                pltpu.VMEM((2, width, down_width), BF16),
                pltpu.SemaphoreType.DMA((2, blocks)),
                pltpu.SemaphoreType.DMA((2, 4 * n_z)),
            ],
        ),
        out_shape=[
            jax.ShapeDtypeStruct((band, blocks * rows), BF16),
            jax.ShapeDtypeStruct((blocks * rows, band), BF16),
            jax.ShapeDtypeStruct((blocks * rows, band), BF16),
            jax.ShapeDtypeStruct((band, width), F32),
            jax.ShapeDtypeStruct((band, width), F32),
        ],
        compiler_params=pltpu.CompilerParams(vmem_limit_bytes=56 << 20),
        name="mlp",
    )(place(), mid, mlp_grad, *[piece[0] for piece in pieces], down_own, down_other)


def after_attention(attended_t, proj_t, residual_low, modulation):
    width, band = attended_t.shape
    half = width // 2
    block = 128

    def kernel(att_ref, proj_ref, low_ref, mod_ref, branch_ref, middle_ref, normed_ref, mid_ref, att_out_ref):
        branch = dot_f32(att_ref[...], proj_ref[...], ((0,), (1,)))
        middle = low_ref[...].astype(F32) + mod_ref[2:3, :] * branch
        normed = modulate(middle, mod_ref[3:4, :], mod_ref[4:5, :]).astype(BF16)
        attended = att_ref[...].T
        branch_ref[...] = branch.astype(BF16)
        middle_ref[...] = middle
        normed_ref[...] = normed
        for x in range(2):
            mid_ref[x] = normed[:, x * half : (x + 1) * half]
            att_out_ref[x] = attended[:, x * half : (x + 1) * half]

    rows = pl.BlockSpec((block, width), lambda i: (i, 0))
    halves = pl.BlockSpec((2, block, half), lambda i: (0, i, 0))
    return kernel_call(
        kernel,
        grid=(band // block,),
        in_specs=[
            pl.BlockSpec((width, block), lambda i: (0, i)),
            pl.BlockSpec((width, width), lambda i: (0, 0)),
            rows,
            pl.BlockSpec((6, width), lambda i: (0, 0)),
        ],
        out_specs=[rows, rows, rows, halves, halves],
        out_shape=[
            jax.ShapeDtypeStruct((band, width), BF16),
            jax.ShapeDtypeStruct((band, width), F32),
            jax.ShapeDtypeStruct((band, width), BF16),
            jax.ShapeDtypeStruct((2, band, half), BF16),
            jax.ShapeDtypeStruct((2, band, half), BF16),
        ],
        compiler_params=pltpu.CompilerParams(vmem_limit_bytes=20 << 20),
        name="after_attention",
    )(attended_t, proj_t, residual_low, modulation)


def middle_back(normed_mid_grad, middle, out_grad, branch, mlp_out, proj_t, attended_t, modulation):
    band, width = middle.shape
    half = width // 2
    head_dim = width // HEADS
    block = 128

    def kernel(
        normed_grad_ref, mid_ref, out_ref, branch_ref, mlp_ref, proj_ref, att_ref, mod_ref,
        grad_ref, bg_ref, att_grad_ref, delta_ref, result_ref, sums_ref,
    ):
        @pl.when(pl.program_id(0) == 0)
        def _():
            sums_ref[...] = jnp.zeros_like(sums_ref)

        normed_grad = normed_grad_ref[...]
        middle, grad, mlp_out = mid_ref[...], out_ref[...].astype(F32), mlp_ref[...]
        fac = norm_factor(middle)
        hat = middle * fac
        hat_grad = normed_grad * (1.0 + mod_ref[4:5, :])
        along = jnp.mean(hat_grad * hat, axis=-1, keepdims=True)
        mid_grad = grad + fac * (hat_grad - hat * along)
        branch_grad = (mod_ref[2:3, :] * mid_grad).astype(BF16)
        attended_grad = dot_f32(branch_grad, proj_ref[...], ((1,), (0,))).astype(BF16).T
        grad_ref[...] = mid_grad
        bg_ref[...] = branch_grad.T
        att_grad_ref[...] = attended_grad
        both = attended_grad.astype(F32) * att_ref[...].astype(F32)
        delta_ref[...] = jnp.sum(both.reshape(HEADS, head_dim, block), axis=1, keepdims=True)
        result_ref[...] = (middle + mod_ref[5:6, :] * mlp_out).astype(BF16)
        sums_ref[0:1, :] += jnp.sum(normed_grad, axis=0, keepdims=True)
        sums_ref[1:2, :] += jnp.sum(normed_grad * hat, axis=0, keepdims=True)
        sums_ref[2:3, :] += jnp.sum(mid_grad * branch_ref[...].astype(F32), axis=0, keepdims=True)
        sums_ref[3:4, :] += jnp.sum(grad * mlp_out, axis=0, keepdims=True)

    rows = pl.BlockSpec((block, width), lambda i: (i, 0))
    columns = pl.BlockSpec((width, block), lambda i: (0, i))
    return kernel_call(
        kernel,
        grid=(band // block,),
        in_specs=[
            rows, rows, rows, rows, rows,
            pl.BlockSpec((width, width), lambda i: (0, 0)),
            columns,
            pl.BlockSpec((6, width), lambda i: (0, 0)),
        ],
        out_specs=[
            rows, columns, columns,
            pl.BlockSpec((HEADS, 1, block), lambda i: (0, 0, i)),
            rows,
            pl.BlockSpec((8, width), lambda i: (0, 0)),
        ],
        out_shape=[
            jax.ShapeDtypeStruct((band, width), F32),
            jax.ShapeDtypeStruct((width, band), BF16),
            jax.ShapeDtypeStruct((width, band), BF16),
            jax.ShapeDtypeStruct((HEADS, 1, band), F32),
            jax.ShapeDtypeStruct((band, width), BF16),
            jax.ShapeDtypeStruct((8, width), F32),
        ],
        compiler_params=pltpu.CompilerParams(vmem_limit_bytes=24 << 20),
        name="middle_back",
    )(normed_mid_grad, middle, out_grad, branch, mlp_out, proj_t, attended_t, modulation)


def input_back(projected_t, qkv_t, latents, mid_grad, modulation):
    inner, band = projected_t.shape
    width = qkv_t.shape[1]
    block = 128

    def kernel(left_ref, weight_ref, low_ref, grad_ref, mod_ref, out_ref, sums_ref):
        @pl.when(pl.program_id(0) == 0)
        def _():
            sums_ref[...] = jnp.zeros_like(sums_ref)

        normed_grad = dot_f32(left_ref[...], weight_ref[...], ((0,), (0,)))
        residual = low_ref[...].astype(F32)
        fac = norm_factor(residual)
        hat = residual * fac
        hat_grad = normed_grad * (1.0 + mod_ref[1:2, :])
        along = jnp.mean(hat_grad * hat, axis=-1, keepdims=True)
        out_ref[...] = grad_ref[...] + fac * (hat_grad - hat * along)
        sums_ref[0:1, :] += jnp.sum(normed_grad, axis=0, keepdims=True)
        sums_ref[1:2, :] += jnp.sum(normed_grad * hat, axis=0, keepdims=True)

    rows = pl.BlockSpec((block, width), lambda i: (i, 0))
    return kernel_call(
        kernel,
        grid=(band // block,),
        in_specs=[
            pl.BlockSpec((inner, block), lambda i: (0, i)),
            pl.BlockSpec((inner, width), lambda i: (0, 0), pipeline_mode=pl.Buffered(1)),
            rows,
            rows,
            pl.BlockSpec((6, width), lambda i: (0, 0)),
        ],
        out_specs=[rows, pl.BlockSpec((8, width), lambda i: (0, 0))],
        out_shape=[jax.ShapeDtypeStruct((band, width), F32), jax.ShapeDtypeStruct((8, width), F32)],
        compiler_params=pltpu.CompilerParams(vmem_limit_bytes=24 << 20),
        name="input_back",
    )(projected_t, qkv_t, latents, mid_grad, modulation)


def place():
    return jnp.stack([lax.axis_index(axis) for axis in ("c", "x", "y")]).astype(jnp.int32)


def terms(lefts, right, rows, side, received=None, z_first=0, n_z=4, y=(0, 1), order=(0, 1), stacked=True, split=0):
    patches = right.shape[0] if right.ndim == 2 else right.shape[1]
    wide = right.ndim == 2
    each = right.shape[-1] // 2 if wide else right.shape[-1]
    width = each * len(lefts)
    count = split or len(y) * n_z
    n = len(lefts)

    def left_map(i, at):
        if split:
            return (i, 0)
        z = z_first + i % n_z
        return ((z * 2 + (y[0] + i // n_z + at[2]) % 2) * 2 + (at[0] + side) % 2, 0)

    def right_spec(h):
        if wide:
            return pl.BlockSpec((patches, each), lambda i, at: (0, (at[1] + h) % 2))
        return pl.BlockSpec((1, patches, each), lambda i, at: ((at[1] + h) % 2, 0, 0))

    def kernel(at, *refs):
        rights, outs = refs[n : n + 2], refs[n + 2 :]
        if received is not None:
            got, outs = refs[n + 2 : n + 4], refs[n + 4 :]
        for k in range(2):
            half = rights[k][...] if wide else rights[k][0]
            values = [dot_f32(refs[m][...], half, ((1,), (0,))) for m in range(n)]
            value = values[0] if n == 1 else jnp.concatenate(values, axis=1)
            if received is not None:
                value = value + got[k][0, 0].astype(F32)
            if not stacked:
                outs[k][0] = value.astype(BF16)
            elif split:
                outs[0][0, k] = value.astype(BF16)
            else:
                outs[0][k, 0] = value.astype(BF16)

    received_specs = []
    if received is not None:
        skip = 0 if split else y[0] * n_z
        received_specs = [
            pl.BlockSpec((1, 1, rows, width), lambda i, at, k=k: (i, k, 0, 0) if split else (k, i + skip, 0, 0))
            for k in range(2)
        ]
    if stacked and split:
        out_shape = [jax.ShapeDtypeStruct((count, 2, rows, width), BF16)]
        out_specs = [pl.BlockSpec((1, 2, rows, width), lambda i, at: (i, 0, 0, 0))]
    elif stacked:
        out_shape = [jax.ShapeDtypeStruct((2, count, rows, width), BF16)]
        out_specs = [pl.BlockSpec((2, 1, rows, width), lambda i, at: (0, i, 0, 0))]
    else:
        out_shape = [jax.ShapeDtypeStruct((count, rows, width), BF16)] * 2
        out_specs = [pl.BlockSpec((1, rows, width), lambda i, at: (i, 0, 0))] * 2
    outs = kernel_call(
        kernel,
        grid_spec=pltpu.PrefetchScalarGridSpec(
            num_scalar_prefetch=1,
            grid=(count,),
            in_specs=[pl.BlockSpec((rows, patches), left_map)] * n
            + [right_spec(h) for h in order]
            + received_specs,
            out_specs=out_specs,
        ),
        out_shape=out_shape,
        compiler_params=pltpu.CompilerParams(vmem_limit_bytes=14 << 20),
        name="terms",
    )(place(), *lefts, right, right, *([received] * 2 if received is not None else []))
    return outs[0] if stacked else outs


def last_terms(left, right, rows, cut, received):
    patches, width = left.shape[-1], right.shape[-1]
    n_z = 4
    late = rows - cut

    def row_of(i):
        return 1 - i // n_z

    def kernel(at, left_ref, own_ref, other_ref, r0_ref, r1_ref, keep_ref, send_ref, up_send_ref, up_keep_ref):
        values = [
            (dot_f32(left_ref[...], ref[0], ((1,), (0,))) + got[0, 0].astype(F32)).astype(BF16)
            for ref, got in ((own_ref, r0_ref), (other_ref, r1_ref))
        ]
        keep_ref[0] = values[0][:cut]
        send_ref[0] = values[1][:cut]

        @pl.when(pl.program_id(0) < n_z)
        def _():
            for k in range(2):
                up_send_ref[1 - k, 0] = values[k][cut:]

        @pl.when(pl.program_id(0) >= n_z)
        def _():
            for k in range(2):
                up_keep_ref[1 - k, 0] = values[k][cut:]

    def got(h):
        return pl.BlockSpec((1, 1, rows, width), lambda i, at: (h, row_of(i) * n_z + i % n_z, 0, 0))

    early_spec = pl.BlockSpec((1, cut, width), lambda i, at: (row_of(i) * n_z + i % n_z, 0, 0))
    return kernel_call(
        kernel,
        grid_spec=pltpu.PrefetchScalarGridSpec(
            num_scalar_prefetch=1,
            grid=(2 * n_z,),
            in_specs=[
                pl.BlockSpec(
                    (rows, patches), lambda i, at: ((i % n_z * 2 + (row_of(i) + at[2]) % 2) * 2 + at[0], 0)
                ),
                pl.BlockSpec((1, patches, width), lambda i, at: (at[1], 0, 0)),
                pl.BlockSpec((1, patches, width), lambda i, at: ((at[1] + 1) % 2, 0, 0)),
                got(0),
                got(1),
            ],
            out_specs=[
                early_spec,
                early_spec,
                pl.BlockSpec((2, 1, late, width), lambda i, at: (0, jnp.minimum(i, n_z - 1), 0, 0)),
                pl.BlockSpec((2, 1, late, width), lambda i, at: (0, jnp.maximum(i - n_z, 0), 0, 0)),
            ],
        ),
        out_shape=[jax.ShapeDtypeStruct((2 * n_z, cut, width), BF16)] * 2
        + [jax.ShapeDtypeStruct((2, n_z, late, width), BF16)] * 2,
        compiler_params=pltpu.CompilerParams(vmem_limit_bytes=20 << 20),
        name="last_terms",
    )(place(), left, right, right, received, received)


def split_rows(left_t, z_first):
    n_z, patches = lax.axis_size("z"), left_t.shape[-1]
    blocks = left_t.reshape(n_z, 2, 2, -1, patches)
    core, row = lax.axis_index("c"), lax.axis_index("y")

    def part(which):
        picked = lax.dynamic_index_in_dim(blocks, which, 2, keepdims=False)
        own = lax.dynamic_index_in_dim(picked, row, 1, keepdims=False)
        other = lax.dynamic_index_in_dim(picked, 1 - row, 1, keepdims=False)
        return jnp.stack([own, other], axis=1 if z_first else 0).reshape(-1, patches)

    return part(1 - core), part(core)


def sum_along_z(values):
    n_z, hop = lax.axis_size("z"), 1
    while hop < n_z:
        values = values + lax.ppermute(values, "z", [(i, i ^ hop) for i in range(n_z)])
        hop *= 2
    return values


def fast_shards(
    latents, out_grad, time_table, class_table, buckets, labels, row_start,
    ada_weight, qkv_weight, proj_weight, gate_weight, up_weight, down_weight, query_gain, key_gain,
):
    band, width = latents.shape[1:]
    head_dim = width // HEADS
    lat, out_g = latents[0], out_grad[0]
    half = width // 2
    n_z = lax.axis_size("z")

    qkv_s, proj_s = qkv_weight[0].T, proj_weight[0].T
    gate_s, up_s, down_s = gate_weight[0].T, up_weight[0].T, by_rows(down_weight[0].T)
    qkv_rows, proj_rows, gate_rows = qkv_s.shape[0], proj_s.shape[0], gate_s.shape[0]
    cut = (qkv_rows + proj_rows) // 2
    first = by_rows(jnp.concatenate([qkv_s[:cut], jnp.concatenate([qkv_s[cut:], proj_s])], axis=1))
    second = by_rows(jnp.concatenate([gate_s, up_s], axis=1))

    first_z = gather_z(first)
    second_z = gather_z(second)
    start_other = swap(row_start.astype(F32), "x")
    (down_r,) = together(swap(down_s, "x"))
    down_x = in_order(down_s, down_r, "x")
    down_x, lat_x = together(down_x, lat)
    lat_other = swap(lat_x, "x")
    down_r = swap(down_x, "y")

    bucket_hot = (buckets[:, None] == jnp.arange(BUCKETS, dtype=jnp.int32)[None, :]).astype(BF16)
    class_hot = (labels[:, None] == jnp.arange(CLASSES, dtype=jnp.int32)[None, :]).astype(BF16)
    cond = jnp.dot(bucket_hot, time_table, preferred_element_type=F32) + jnp.dot(
        class_hot, class_table, preferred_element_type=F32
    )
    cond_act = jax.nn.silu(cond).astype(BF16)
    mod_cols = jnp.dot(cond_act, ada_weight[0], preferred_element_type=F32)

    offsets = jnp.arange(band, dtype=jnp.int32)
    rows_in = (offsets // SIDE).astype(F32)
    row_pos = jnp.concatenate([row_start.astype(F32)[0, 0] + rows_in, start_other[0, 0] + rows_in])
    col_pos = jnp.tile((offsets % SIDE).astype(F32), 2)
    quarter = head_dim // 4
    frequency = THETA ** (-jnp.arange(quarter, dtype=F32) / quarter)
    angles = jnp.concatenate([frequency[:, None] * row_pos[None], frequency[:, None] * col_pos[None]])
    cos_h, sin_h = jnp.cos(angles), jnp.sin(angles)
    cos_t = jnp.concatenate([cos_h, cos_h])
    sin_t = jnp.concatenate([-sin_h, sin_h])
    gains_t = jnp.concatenate([query_gain, key_gain]).T
    first_z, lat_other, down_r, mod_cols, cos_t, sin_t = together(first_z, lat_other, down_r, mod_cols, cos_t, sin_t)

    a, b = by_rows(first_z[:2]), by_rows(first_z[2:])
    a_y, b_x, a_c, b_c = swap(a, "y"), swap(b, "x"), swap(a, "c"), swap(b, "c")
    down_z = gather_z(in_order(down_x, down_r, "y").reshape(-1, down_x.shape[-1]))
    modulation = lax.all_to_all(mod_cols, DP_AXES, split_axis=0, concat_axis=1, tiled=True)
    a_y, b_x, a_c, b_c, modulation = together(a_y, b_x, a_c, b_c, modulation)

    a_x, b_y, a_yc, b_xc = swap(a, "x"), swap(b, "y"), swap(a_y, "c"), swap(b_x, "c")
    mods = modulation.reshape(6, width)
    shift_attn, scale_attn, gate_attn, shift_mlp, scale_mlp, gate_mlp = jnp.split(modulation, 6, axis=-1)
    lat_full = jnp.concatenate([lat, lat_other]).astype(F32)
    normed_full = modulate(lat_full, shift_attn, scale_attn).astype(BF16)
    a_x, b_y, a_yc, b_xc, normed_full = together(a_x, b_y, a_yc, b_xc, normed_full)

    a_yx, b_xy, a_xc, b_yc = swap(a_y, "x"), swap(b_x, "y"), swap(a_x, "c"), swap(b_y, "c")
    mlp_grad = (gate_mlp * out_g.astype(F32)).astype(BF16)
    down_send, down_keep = split_rows(mlp_grad.T, True)
    normed = normed_full[:band]
    normed_2 = jnp.stack([normed[:, :half], normed[:, half:]])
    second_z, a_yx, b_xy, a_xc, b_yc, mlp_grad, down_send, down_keep, normed_2 = together(
        second_z, a_yx, b_xy, a_xc, b_yc, mlp_grad, down_send, down_keep, normed_2
    )

    a_yxc, b_xyc = swap(a_yx, "c"), swap(b_xy, "c")
    e, f = by_rows(second_z[:2]), by_rows(second_z[2:])
    e_y, f_x = swap(e, "y"), swap(f, "x")
    pieces_own = [
        (a, 0, 0, 0, 0), (a_y, 0, 0, 1, 0), (a_x, 0, 1, 0, 0), (a_yx, 0, 1, 1, 0),
        (b, 2, 0, 0, 0), (b_x, 2, 1, 0, 0), (b_y, 2, 0, 1, 0), (b_xy, 2, 1, 1, 0),
    ]
    tables = (cos_t, sin_t, gains_t, head_dim, band)
    parts = qkv_heads(normed_full, pieces_own, *tables)
    *parts, e_y, f_x, a_yxc, b_xyc = together(*parts, e_y, f_x, a_yxc, b_xyc)

    e_x, f_y, e_c, f_c, e_yc = swap(e, "x"), swap(f, "y"), swap(e, "c"), swap(f, "c"), swap(e_y, "c")
    pieces_other = [
        (a_c, 0, 0, 0, 1), (a_yc, 0, 0, 1, 1), (a_xc, 0, 1, 0, 1), (a_yxc, 0, 1, 1, 1),
        (b_c, 2, 0, 0, 1), (b_xc, 2, 1, 0, 1), (b_yc, 2, 0, 1, 1), (b_xyc, 2, 1, 1, 1),
    ]
    qkv, hat, fac, qkv_t = qkv_heads(normed_full, pieces_other, *tables, before=parts)
    e_x, f_y, e_c, f_c, e_yc, qkv = together(e_x, f_y, e_c, f_c, e_yc, qkv)

    e_yx, f_xy = swap(e_y, "x"), swap(f_x, "y")
    f_xc, e_xc, f_yc = swap(f_x, "c"), swap(e_x, "c"), swap(f_y, "c")
    attended_t, log_mass = attention_forward(qkv, HEADS, band)
    proj_t = join_rows(pieces_own + pieces_other, qkv_rows - cut, proj_rows).reshape(width, width)
    e_yx, f_xy, f_xc, e_xc, f_yc, attended_t, proj_t, down_z = together(
        e_yx, f_xy, f_xc, e_xc, f_yc, attended_t, proj_t, down_z
    )

    down_own = down_z.reshape(n_z, 2, 2, -1, down_z.shape[-1])
    down_other, e_yxc, f_xyc = swap(down_own, "c"), swap(e_yx, "c"), swap(f_xy, "c")
    attended_t = attended_t.reshape(width, band)
    branch, middle, normed_mid, mid_2, att_2 = after_attention(attended_t, proj_t, lat, mods)
    pieces = [
        (e, 0, 0, 0, 0), (e_y, 0, 0, 1, 0), (e_x, 0, 1, 0, 0), (e_yx, 0, 1, 1, 0),
        (e_c, 0, 0, 0, 1), (e_yc, 0, 0, 1, 1), (e_xc, 0, 1, 0, 1), (e_yxc, 0, 1, 1, 1),
        (f, 2, 0, 0, 0), (f_x, 2, 1, 0, 0), (f_y, 2, 0, 1, 0), (f_xy, 2, 1, 1, 0),
        (f_c, 2, 0, 0, 1), (f_xc, 2, 1, 0, 1), (f_yc, 2, 0, 1, 1), (f_xyc, 2, 1, 1, 1),
    ]
    hidden, gate_grad_t, up_grad_t, mlp_out, normed_mid_grad = mlp(
        normed_mid, mlp_grad, pieces, down_own, down_other
    )

    gates = (gate_grad_t, up_grad_t)
    a_g = terms(gates, mid_2, gate_rows, 1, n_z=2)
    a_g, hidden, *gates, mlp_out, normed_mid_grad = together(a_g, hidden, *gates, mlp_out, normed_mid_grad)

    a_gr = swap(a_g, "c")
    mid_grad, branch_grad_t, attended_grad, delta, result, sums = middle_back(
        normed_mid_grad, middle, out_g, branch, mlp_out, proj_t, attended_t, mods
    )
    b_g = terms(gates, mid_2, gate_rows, 1, z_first=2, n_z=2, order=(1, 0))
    by_head = attended_grad.reshape(HEADS, head_dim, band)
    a_gr, b_g, by_head, delta, branch_grad_t = together(a_gr, b_g, by_head, delta, branch_grad_t)

    b_gr = swap(b_g, "c")
    other_first = swap(by_head[:6], "x")
    a_k, a_s = terms(gates, mid_2, gate_rows, 0, received=a_gr, n_z=2, stacked=False)
    proj_send, proj_keep = split_rows(branch_grad_t, False)
    down_g = terms((down_send,), hidden, 2 * proj_rows, 1, split=n_z)
    b_gr, other_first, a_k, a_s, down_g, proj_send, proj_keep = together(
        b_gr, other_first, a_k, a_s, down_g, proj_send, proj_keep
    )

    down_gr = swap(down_g, "c")
    a_r1 = [swap(a_s[2:3], "x")]
    b_s = terms(gates, mid_2, gate_rows, 0, received=b_gr, z_first=2, n_z=2, y=(1,), order=(1, 0))
    b_k = terms(gates, mid_2, gate_rows, 0, received=b_gr, z_first=2, n_z=2, y=(0,), order=(1, 0))
    proj_g = terms((proj_send,), att_2, n_z * proj_rows, 1, split=2)
    down_gr, a_r1[0], b_s, b_k, proj_g = together(down_gr, a_r1[0], b_s, b_k, proj_g)

    proj_gr = swap(proj_g, "c")
    a_r1.append(swap(a_s[3:4], "x"))
    b_s = b_s.reshape(4, gate_rows, width)
    b_r1 = [swap(b_s[:1], "y")]
    down_sum = terms((down_keep,), hidden, 2 * proj_rows, 0, received=down_gr, split=n_z)
    proj_gr, a_r1[1], b_r1[0], down_sum = together(proj_gr, a_r1[1], b_r1[0], down_sum)

    down_sum = lax.psum_scatter(
        down_sum.reshape(-1, down_sum.shape[-1]), "z", scatter_dimension=0, tiled=True
    ).reshape(2, 2, proj_rows, -1)
    other_last = swap(by_head[6:], "x")
    other_rows = swap(jnp.stack([log_mass, delta]), "x")
    b_r1.append(swap(b_s[1:3], "y"))
    proj_sum = terms((proj_keep,), att_2, n_z * proj_rows, 0, received=proj_gr, split=2)
    dq, dk, dv = attention_back_own(qkv, by_head, log_mass, delta, HEADS, band)
    other_last, other_rows, b_r1[1], proj_sum, dq = together(other_last, other_rows, b_r1[1], proj_sum, dq)

    a_r1.append(swap(a_s[:2], "x"))
    b_r1.append(swap(b_s[3:], "y"))
    a_s2 = add_low(a_k[2:], jnp.concatenate(a_r1[:2]))
    a_r2 = [swap(a_s2[:1], "y")]
    other_grad = jnp.concatenate([other_first, other_last])
    heads_grad, gain_q, gain_k = attention_back_other(
        qkv, hat, fac, cos_t, sin_t, gains_t, dq, dk, dv,
        other_grad, other_rows[0], other_rows[1], HEADS, band,
    )
    projected_t = heads_grad.reshape(3 * width, band)
    a_r1[2], b_r1[2], a_r2[0], projected_t = together(a_r1[2], b_r1[2], a_r2[0], projected_t)

    b_r1 = jnp.concatenate(b_r1).reshape(2, 2, gate_rows, width)
    b_s2 = add_low(b_k[0], b_r1[0])
    b_r2 = [swap(b_s2[:1], "x")]
    a_r2.append(swap(a_s2[1:], "y"))
    q_g = terms((projected_t,), normed_2, qkv_rows, 1)
    b_r2[0], a_r2[1], q_g = together(b_r2[0], a_r2[1], q_g)

    q_gr = swap(q_g, "c")
    b_r2.append(swap(b_s2[1:], "x"))
    proj_r1 = swap(proj_sum[1], "y")
    input_grad, in_sums = input_back(projected_t, qkv_t, lat, mid_grad, mods)
    mod_grad = jnp.concatenate([in_sums[0:1], in_sums[1:2], sums[2:3], sums[0:1], sums[1:2], sums[3:4]], axis=-1)
    small = jnp.concatenate([mod_grad, gain_q.sum(0).T, gain_k.sum(0).T], axis=-1)
    q_gr, b_r2[1], proj_r1, small = together(q_gr, b_r2[1], proj_r1, small)

    small_r = swap(small, "x")
    row_a = 80
    qa_keep, qa_send, qb_send, qb_keep = last_terms(projected_t, normed_2, qkv_rows, row_a, q_gr)
    down_r = swap(down_sum[:, 1], "y")
    proj_k = proj_sum[0].reshape(2, n_z, proj_rows, half)
    proj_r1 = proj_r1.reshape(2, n_z, proj_rows, half)
    proj_r2 = swap(add_low(proj_k[1], proj_r1[1]), "x")
    qa_keep, qa_send, qb_send, qb_keep, down_r, small_r, proj_r2 = together(
        qa_keep, qa_send, qb_send, qb_keep, down_r, small_r, proj_r2
    )

    gu = jnp.concatenate(
        [add_low(a_k[:2], a_r1[2], jnp.concatenate(a_r2)), add_low(b_k[1], b_r1[1], jnp.concatenate(b_r2))]
    )
    gu = lax.psum_scatter(gu.reshape(-1, width), "z", scatter_dimension=0, tiled=True)
    qa_r1, qb_r1 = swap(qa_send, "x"), swap(qb_send, "y")
    small = small + small_r
    band_mod, band_gain = small[:, : 6 * width], small[:, 6 * width :]
    mod_cols_grad = lax.all_to_all(band_mod.astype(BF16), DP_AXES, split_axis=1, concat_axis=0, tiled=True)
    cond_act_part = dot_f32(mod_cols_grad, ada_weight[0], ((1,), (1,)))
    tail = jnp.zeros((8, width), F32).at[0, : 2 * head_dim].set(band_gain[0])
    summed = jnp.concatenate([cond_act_part, tail])
    summed = summed + swap(summed, "c")
    qa_r1, qb_r1, summed = together(qa_r1, qb_r1, summed)

    qa_keep, qa_r1 = qa_keep.reshape(2, n_z, row_a, half), qa_r1.reshape(2, n_z, row_a, half)
    qa_r2 = swap(add_low(qa_keep[1], qa_r1[1]), "y")
    qb_r2 = swap(add_low(qb_keep[0], qb_r1[0]), "x")
    down_sum = add_low(down_sum[:, 0], down_r)
    down_r2 = swap(down_sum[1], "x")
    summed = sum_along_z(summed)
    qa_r2, qb_r2, summed = together(qa_r2, qb_r2, summed)

    last = jnp.concatenate(
        [
            add_low(qa_keep[0], qa_r1[0], qa_r2),
            add_low(qb_keep[1], qb_r1[1], qb_r2),
            add_low(proj_k[0], proj_r1[0], proj_r2),
        ],
        axis=1,
    )
    last = lax.psum_scatter(last.reshape(-1, half), "z", scatter_dimension=0, tiled=True)
    summed = summed + swap(summed, "y")
    ada_grad = dot_f32(cond_act, mod_cols_grad, ((0,), (0,)))
    items = cond.shape[0]
    _, silu_back = jax.vjp(jax.nn.silu, cond)
    cond_grad = silu_back(summed[:items])[0]
    time_grad = jnp.einsum("ib,id->bd", bucket_hot.astype(F32), cond_grad, precision=HIGHEST)
    class_grad = jnp.einsum("ib,id->bd", class_hot.astype(F32), cond_grad, precision=HIGHEST)
    down_out = down_sum[0].astype(F32) + down_r2.astype(F32)

    def out(values):
        return values.T.astype(F32)[None]

    return (
        result[None],
        input_grad[None],
        time_grad,
        class_grad,
        ada_grad[None],
        out(last[:qkv_rows]),
        out(last[qkv_rows:]),
        out(gu[:, :half]),
        out(gu[:, half:]),
        out(down_out),
        summed[items : items + 1, :head_dim],
        summed[items : items + 1, head_dim : 2 * head_dim],
    )


def fast_solution(mesh):
    dp = mesh.shape["dp"]
    fine = jax.sharding.Mesh(mesh.devices.reshape(dp // 4, 2, 2, 2), ("z", "y", "c", "x"))
    items, last = P(DP_AXES, "x", None), P(None, "x", DP_AXES)
    in_specs = (items, items, P(), P(), P(), P(), P(DP_AXES, "x"), P(None, None, DP_AXES)) + (last,) * 5 + (P(), P())
    out_specs = (items, items, P(), P(), P(None, None, DP_AXES)) + (last,) * 5 + (P(), P())
    return jax.shard_map(fast_shards, mesh=fine, in_specs=in_specs, out_specs=out_specs, check_vma=False)


def solution(mesh):
    if mesh.shape["dp"] == 16 and mesh.shape["seq"] == 2:
        return fast_solution(mesh)
    in_specs = (
        P("dp", "seq", None),
        P("dp", "seq", None),
        P(),
        P(),
        P(),
        P(),
        P("dp", "seq"),
        P(None, None, "dp"),
        P(None, "seq", "dp"),
        P(None, "seq", "dp"),
        P(None, "seq", "dp"),
        P(None, "seq", "dp"),
        P(None, "seq", "dp"),
        P(),
        P(),
    )
    out_specs = (
        P("dp", "seq", None),
        P("dp", "seq", None),
        P(),
        P(),
        P(None, None, "dp"),
        P(None, "seq", "dp"),
        P(None, "seq", "dp"),
        P(None, "seq", "dp"),
        P(None, "seq", "dp"),
        P(None, "seq", "dp"),
        P(),
        P(),
    )
    return jax.shard_map(shards, mesh=mesh, in_specs=in_specs, out_specs=out_specs, check_vma=False)
```

```python
import jax
import jax.numpy as jnp
from jax import lax
from jax.experimental import pallas as pl
from jax.experimental.layout import Layout, with_layout_constraint
from jax.experimental.pallas import tpu as pltpu
from jax.sharding import PartitionSpec as P

HEADS = 16
CLASSES = 1000
BUCKETS = 1000
SIDE = 32


EPS = 1e-06
THETA = 10000.0
HIGHEST = lax.Precision.HIGHEST


def norm_factor(values):
    return lax.rsqrt(jnp.mean(values * values, axis=-1, keepdims=True) + EPS)


def modulate(values, shift_by, scale_by):
    return values * norm_factor(values) * (1.0 + scale_by) + shift_by


def rope_tables(row_pos, col_pos, head_dim):
    quarter = head_dim // 4
    frequency = THETA ** (-jnp.arange(quarter, dtype=jnp.float32) / quarter)
    angles = jnp.concatenate(
        [row_pos[..., None] * frequency, col_pos[..., None] * frequency], axis=-1
    )
    cos_part = jnp.cos(angles)
    sin_part = jnp.sin(angles)
    return (
        jnp.concatenate([cos_part, cos_part], axis=-1),
        jnp.concatenate([sin_part, sin_part], axis=-1),
    )


def rotate(values, cos_part, sin_part):
    half_dim = values.shape[-1] // 2
    turned = jnp.concatenate([-values[..., half_dim:], values[..., :half_dim]], axis=-1)
    return values * cos_part + turned * sin_part


def query_key(query_pre, key_pre, gain_query, gain_key, cos_part, sin_part):
    query_out = rotate(query_pre * norm_factor(query_pre) * gain_query, cos_part, sin_part)
    key_out = rotate(key_pre * norm_factor(key_pre) * gain_key, cos_part, sin_part)
    return (query_out, key_out)


def swiglu(gate_pre, up_pre):
    return jax.nn.silu(gate_pre) * up_pre


def gather_layer(layer_no, qkv_weight, proj_weight, gate_weight, up_weight, down_weight):
    row_parts = (
        lax.all_gather(qkv_weight[layer_no], "seq", axis=0, tiled=True),
        lax.all_gather(proj_weight[layer_no], "seq", axis=0, tiled=True),
        lax.all_gather(gate_weight[layer_no], "seq", axis=0, tiled=True),
        lax.all_gather(up_weight[layer_no], "seq", axis=0, tiled=True),
        lax.all_gather(down_weight[layer_no], "seq", axis=0, tiled=True),
    )
    qkv_rows, proj_rows, gate_rows, up_rows, down_rows = row_parts
    return (
        lax.all_gather(qkv_rows, "dp", axis=1, tiled=True),
        lax.all_gather(proj_rows, "dp", axis=1, tiled=True),
        lax.all_gather(gate_rows, "dp", axis=1, tiled=True),
        lax.all_gather(up_rows, "dp", axis=1, tiled=True),
        lax.all_gather(down_rows, "dp", axis=1, tiled=True),
    )


def attend(queries, key_rows, value_rows, inv_root):
    items_dev, band_rows, head_count, head_dim = queries.shape
    top_score = jnp.full((items_dev, head_count, band_rows), -jnp.inf, jnp.float32)
    row_mass = jnp.zeros((items_dev, head_count, band_rows), jnp.float32)
    weighted = jnp.zeros((items_dev, band_rows, head_count, head_dim), jnp.float32)
    key_seg = lax.all_gather(key_rows, "seq", axis=1, tiled=True)
    value_seg = lax.all_gather(value_rows, "seq", axis=1, tiled=True)
    seg_rows = key_seg.shape[1]
    key_heads = key_seg.reshape(items_dev, seg_rows, head_count, head_dim)
    value_heads = value_seg.reshape(items_dev, seg_rows, head_count, head_dim)
    scores = (
        jnp.einsum("ibhe,inhe->ihbn", queries, key_heads, preferred_element_type=jnp.float32)
        * inv_root
    )
    new_top = jnp.max(scores, axis=-1)
    shrink = jnp.exp(top_score - new_top)
    weights = jnp.exp(scores - new_top[..., None])
    new_mass = row_mass * shrink + jnp.sum(weights, axis=-1)
    update = jnp.einsum(
        "ihbn,inhe->ibhe",
        weights.astype(jnp.bfloat16),
        value_heads,
        preferred_element_type=jnp.float32,
    )
    new_weighted = weighted * jnp.transpose(shrink, (0, 2, 1))[..., None] + update
    log_mass = new_top + jnp.log(new_mass)
    attended = new_weighted / jnp.transpose(new_mass, (0, 2, 1))[..., None]
    return (attended, log_mass)


def attend_back(queries, keys_all, values_all, attended_grad, log_mass, delta, inv_root):
    items_dev, band_rows, head_count, head_dim = queries.shape
    seq_len = keys_all.shape[1]
    key_heads = keys_all.reshape(items_dev, seq_len, head_count, head_dim)
    value_heads = values_all.reshape(items_dev, seq_len, head_count, head_dim)

    def one_item(operands):
        query_item, key_item, value_item, grad_item, mass_item, delta_item = operands
        scores = (
            jnp.einsum("bhe,nhe->hbn", query_item, key_item, preferred_element_type=jnp.float32)
            * inv_root
        )
        probs_full = jnp.exp(scores - mass_item[..., None])
        prob_grad = jnp.einsum(
            "bhe,nhe->hbn", grad_item, value_item, preferred_element_type=jnp.float32
        )
        score_grad = (probs_full * (prob_grad - delta_item[..., None])).astype(jnp.bfloat16)
        query_out_grad = (
            jnp.einsum("hbn,nhe->bhe", score_grad, key_item, preferred_element_type=jnp.float32)
            * inv_root
        )
        key_out_grad = (
            jnp.einsum("hbn,bhe->nhe", score_grad, query_item, preferred_element_type=jnp.float32)
            * inv_root
        )
        value_grad = jnp.einsum(
            "hbn,bhe->nhe",
            probs_full.astype(jnp.bfloat16),
            grad_item,
            preferred_element_type=jnp.float32,
        )
        return (query_out_grad, key_out_grad, value_grad)

    return lax.map(one_item, (queries, key_heads, value_heads, attended_grad, log_mass, delta))


def forward_layer(residual, modulation, weights, gain_query, gain_key, cos_part, sin_part):
    qkv_full, proj_full, gate_full, up_full, down_full = weights
    items_dev, band_rows, model_width = residual.shape
    head_count = HEADS
    head_dim = model_width // head_count
    inv_root = head_dim ** (-0.5)
    shift_attn, scale_attn, gate_attn, shift_mlp, scale_mlp, gate_mlp = jnp.split(
        modulation[:, None, :], 6, axis=-1
    )
    normed = modulate(residual, shift_attn, scale_attn).astype(jnp.bfloat16)
    projected = jnp.einsum("ibd,de->ibe", normed, qkv_full, preferred_element_type=jnp.float32)
    query_pre = projected[..., :model_width].reshape(items_dev, band_rows, head_count, head_dim)
    key_pre = projected[..., model_width : 2 * model_width].reshape(
        items_dev, band_rows, head_count, head_dim
    )
    queries, key_rows = query_key(query_pre, key_pre, gain_query, gain_key, cos_part, sin_part)
    queries = queries.astype(jnp.bfloat16)
    key_rows = key_rows.astype(jnp.bfloat16).reshape(items_dev, band_rows, model_width)
    value_rows = projected[..., 2 * model_width :].astype(jnp.bfloat16)
    attended, log_mass = attend(queries, key_rows, value_rows, inv_root)
    attended_low = attended.reshape(items_dev, band_rows, model_width).astype(jnp.bfloat16)
    branch = jnp.einsum("ibd,de->ibe", attended_low, proj_full, preferred_element_type=jnp.float32)
    middle = residual + gate_attn * branch
    normed_mid = modulate(middle, shift_mlp, scale_mlp).astype(jnp.bfloat16)
    gate_pre = jnp.einsum("ibd,df->ibf", normed_mid, gate_full, preferred_element_type=jnp.float32)
    up_pre = jnp.einsum("ibd,df->ibf", normed_mid, up_full, preferred_element_type=jnp.float32)
    hidden = swiglu(gate_pre, up_pre).astype(jnp.bfloat16)
    mlp_out = jnp.einsum("ibf,fd->ibd", hidden, down_full, preferred_element_type=jnp.float32)
    output = middle + gate_mlp * mlp_out
    stored = (
        residual,
        normed,
        query_pre,
        key_pre,
        queries,
        key_rows,
        value_rows,
        attended,
        attended_low,
        log_mass,
        branch,
        middle,
        normed_mid,
        gate_pre,
        up_pre,
        hidden,
        mlp_out,
    )
    return (output, stored)


def weight_terms(
    normed,
    attended_low,
    normed_mid,
    hidden,
    projected_grad,
    branch_grad,
    gate_pre_grad,
    up_pre_grad,
    mlp_grad,
):
    qkv_term = jnp.einsum("ibd,ibe->de", normed, projected_grad, preferred_element_type=jnp.float32)
    proj_term = jnp.einsum(
        "ibd,ibe->de", attended_low, branch_grad, preferred_element_type=jnp.float32
    )
    gate_term = jnp.einsum(
        "ibd,ibf->df", normed_mid, gate_pre_grad, preferred_element_type=jnp.float32
    )
    up_term = jnp.einsum("ibd,ibf->df", normed_mid, up_pre_grad, preferred_element_type=jnp.float32)
    down_term = jnp.einsum("ibf,ibd->fd", hidden, mlp_grad, preferred_element_type=jnp.float32)
    col_parts = (
        lax.psum_scatter(
            qkv_term.astype(jnp.bfloat16), "dp", scatter_dimension=1, tiled=True
        ).astype(jnp.float32),
        lax.psum_scatter(
            proj_term.astype(jnp.bfloat16), "dp", scatter_dimension=1, tiled=True
        ).astype(jnp.float32),
        lax.psum_scatter(
            gate_term.astype(jnp.bfloat16), "dp", scatter_dimension=1, tiled=True
        ).astype(jnp.float32),
        lax.psum_scatter(
            up_term.astype(jnp.bfloat16), "dp", scatter_dimension=1, tiled=True
        ).astype(jnp.float32),
        lax.psum_scatter(
            down_term.astype(jnp.bfloat16), "dp", scatter_dimension=1, tiled=True
        ).astype(jnp.float32),
    )
    qkv_cols, proj_cols, gate_cols, up_cols, down_cols = col_parts
    return (
        lax.psum_scatter(
            qkv_cols.astype(jnp.bfloat16), "seq", scatter_dimension=0, tiled=True
        ).astype(jnp.float32),
        lax.psum_scatter(
            proj_cols.astype(jnp.bfloat16), "seq", scatter_dimension=0, tiled=True
        ).astype(jnp.float32),
        lax.psum_scatter(
            gate_cols.astype(jnp.bfloat16), "seq", scatter_dimension=0, tiled=True
        ).astype(jnp.float32),
        lax.psum_scatter(
            up_cols.astype(jnp.bfloat16), "seq", scatter_dimension=0, tiled=True
        ).astype(jnp.float32),
        lax.psum_scatter(
            down_cols.astype(jnp.bfloat16), "seq", scatter_dimension=0, tiled=True
        ).astype(jnp.float32),
    )


def backward_layer(
    stored, resid_grad, modulation, weights, gain_query, gain_key, cos_part, sin_part
):
    qkv_full, proj_full, gate_full, up_full, down_full = weights
    (
        residual,
        normed,
        query_pre,
        key_pre,
        queries,
        key_rows,
        value_rows,
        attended,
        attended_low,
        log_mass,
        branch,
        middle,
        normed_mid,
        gate_pre,
        up_pre,
        hidden,
        mlp_out,
    ) = stored
    items_dev, band_rows, head_count, head_dim = queries.shape
    model_width = residual.shape[-1]
    inv_root = head_dim ** (-0.5)
    shift_attn, scale_attn, gate_attn, shift_mlp, scale_mlp, gate_mlp = jnp.split(
        modulation[:, None, :], 6, axis=-1
    )
    mlp_grad = (gate_mlp * resid_grad).astype(jnp.bfloat16)
    gate_mlp_grad = jnp.sum(resid_grad * mlp_out, axis=1, keepdims=True)
    hidden_grad = jnp.einsum("ibd,fd->ibf", mlp_grad, down_full, preferred_element_type=jnp.float32)
    unused_out, swiglu_back = jax.vjp(swiglu, gate_pre, up_pre)
    gate_pre_grad, up_pre_grad = swiglu_back(hidden_grad)
    gate_pre_grad = gate_pre_grad.astype(jnp.bfloat16)
    up_pre_grad = up_pre_grad.astype(jnp.bfloat16)
    normed_mid_grad = jnp.einsum(
        "ibf,df->ibd", gate_pre_grad, gate_full, preferred_element_type=jnp.float32
    )
    normed_mid_grad = normed_mid_grad + jnp.einsum(
        "ibf,df->ibd", up_pre_grad, up_full, preferred_element_type=jnp.float32
    )
    unused_mid, mid_back = jax.vjp(modulate, middle, shift_mlp, scale_mlp)
    mid_norm_grad, shift_mlp_grad, scale_mlp_grad = mid_back(normed_mid_grad)
    mid_grad = resid_grad + mid_norm_grad
    branch_grad = (gate_attn * mid_grad).astype(jnp.bfloat16)
    gate_attn_grad = jnp.sum(mid_grad * branch, axis=1, keepdims=True)
    attended_grad = jnp.einsum(
        "ibe,de->ibd", branch_grad, proj_full, preferred_element_type=jnp.float32
    ).astype(jnp.bfloat16)
    attended_grad = attended_grad.reshape(items_dev, band_rows, head_count, head_dim)
    delta = jnp.transpose(jnp.sum(attended_grad.astype(jnp.float32) * attended, axis=-1), (0, 2, 1))
    keys_all, values_all = (
        lax.all_gather(key_rows, "seq", axis=1, tiled=True),
        lax.all_gather(value_rows, "seq", axis=1, tiled=True),
    )
    query_out_grad, key_out_grad, value_grad = attend_back(
        queries, keys_all, values_all, attended_grad, log_mass, delta, inv_root
    )
    seq_len = keys_all.shape[1]
    key_band_grad, value_band_grad = (
        lax.psum_scatter(
            key_out_grad.reshape(items_dev, seq_len, model_width).astype(jnp.bfloat16),
            "seq",
            scatter_dimension=1,
            tiled=True,
        ).astype(jnp.float32),
        lax.psum_scatter(
            value_grad.reshape(items_dev, seq_len, model_width).astype(jnp.bfloat16),
            "seq",
            scatter_dimension=1,
            tiled=True,
        ).astype(jnp.float32),
    )

    def rotate_pair(query_in, key_in, gain_q, gain_k):
        return query_key(query_in, key_in, gain_q, gain_k, cos_part, sin_part)

    unused_pair, pair_back = jax.vjp(rotate_pair, query_pre, key_pre, gain_query, gain_key)
    query_pre_grad, key_pre_grad, query_gain_term, key_gain_term = pair_back(
        (query_out_grad, key_band_grad.reshape(items_dev, band_rows, head_count, head_dim))
    )
    projected_grad = jnp.concatenate(
        [
            query_pre_grad.reshape(items_dev, band_rows, model_width),
            key_pre_grad.reshape(items_dev, band_rows, model_width),
            value_band_grad,
        ],
        axis=-1,
    ).astype(jnp.bfloat16)
    normed_grad = jnp.einsum(
        "ibe,de->ibd", projected_grad, qkv_full, preferred_element_type=jnp.float32
    )
    unused_in, input_back = jax.vjp(modulate, residual, shift_attn, scale_attn)
    input_norm_grad, shift_attn_grad, scale_attn_grad = input_back(normed_grad)
    input_grad = mid_grad + input_norm_grad
    mod_grad = jnp.concatenate(
        [
            shift_attn_grad,
            scale_attn_grad,
            gate_attn_grad,
            shift_mlp_grad,
            scale_mlp_grad,
            gate_mlp_grad,
        ],
        axis=-1,
    )[:, 0, :]
    own_grads = weight_terms(
        normed,
        attended_low,
        normed_mid,
        hidden,
        projected_grad,
        branch_grad,
        gate_pre_grad,
        up_pre_grad,
        mlp_grad,
    )
    return (input_grad, mod_grad, own_grads, query_gain_term, key_gain_term)


def shards(
    latents,
    out_grad,
    time_table,
    class_table,
    buckets,
    labels,
    row_start,
    ada_weight,
    qkv_weight,
    proj_weight,
    gate_weight,
    up_weight,
    down_weight,
    query_gain,
    key_gain,
):
    items_dev, band_rows, model_width = latents.shape
    layer_count = qkv_weight.shape[0]
    head_dim = model_width // HEADS
    offsets = jnp.arange(band_rows, dtype=jnp.int32)
    row_pos = (row_start + (offsets // SIDE)[None, :]).astype(jnp.float32)
    col_pos = (offsets % SIDE).astype(jnp.float32)[None, :]
    cos_part, sin_part = rope_tables(row_pos, col_pos, head_dim)
    cos_part = cos_part[:, :, None, :]
    sin_part = sin_part[:, :, None, :]
    bucket_hot = (buckets[:, None] == jnp.arange(BUCKETS, dtype=jnp.int32)[None, :]).astype(
        jnp.bfloat16
    )
    class_hot = (labels[:, None] == jnp.arange(CLASSES, dtype=jnp.int32)[None, :]).astype(
        jnp.bfloat16
    )
    cond = jnp.dot(bucket_hot, time_table, preferred_element_type=jnp.float32) + jnp.dot(
        class_hot, class_table, preferred_element_type=jnp.float32
    )
    cond_act = jax.nn.silu(cond).astype(jnp.bfloat16)
    mod_cols = jnp.einsum("id,ldm->lim", cond_act, ada_weight, preferred_element_type=jnp.float32)
    modulation = lax.all_to_all(mod_cols, "dp", split_axis=1, concat_axis=2, tiled=True)
    residual = latents.astype(jnp.float32)
    gathered_all = []
    layer_no = 0
    weights = gather_layer(layer_no, qkv_weight, proj_weight, gate_weight, up_weight, down_weight)
    gathered_all.append(weights)
    residual, stored = forward_layer(
        residual,
        modulation[layer_no],
        weights,
        query_gain[layer_no],
        key_gain[layer_no],
        cos_part,
        sin_part,
    )
    stored_all = [stored]
    result = residual.astype(jnp.bfloat16)
    resid_grad = out_grad.astype(jnp.float32)
    mod_grads = [None] * layer_count
    grad_shards = [None] * layer_count
    query_terms = [None] * layer_count
    key_terms = [None] * layer_count
    for layer_no in reversed(range(layer_count)):
        weights = gather_layer(
            layer_no, qkv_weight, proj_weight, gate_weight, up_weight, down_weight
        )
        resid_grad, mod_grad, own_grads, query_term, key_term = backward_layer(
            stored_all[layer_no],
            resid_grad,
            modulation[layer_no],
            weights,
            query_gain[layer_no],
            key_gain[layer_no],
            cos_part,
            sin_part,
        )
        mod_grads[layer_no] = mod_grad
        grad_shards[layer_no] = own_grads
        query_terms[layer_no] = query_term
        key_terms[layer_no] = key_term
    band_mod, band_query, band_key = lax.psum(
        (jnp.stack(mod_grads), jnp.stack(query_terms), jnp.stack(key_terms)), "seq"
    )
    mod_cols_grad = lax.all_to_all(
        band_mod.astype(jnp.bfloat16), "dp", split_axis=2, concat_axis=1, tiled=True
    )
    ada_grad = jnp.einsum(
        "id,lim->ldm", cond_act, mod_cols_grad, preferred_element_type=jnp.float32
    )
    cond_act_part = jnp.einsum(
        "lim,ldm->id", mod_cols_grad, ada_weight, preferred_element_type=jnp.float32
    )
    cond_act_grad, query_grad, key_grad = (
        lax.psum(cond_act_part.astype(jnp.bfloat16), "dp").astype(jnp.float32),
        lax.psum(band_query.astype(jnp.bfloat16), "dp").astype(jnp.float32),
        lax.psum(band_key.astype(jnp.bfloat16), "dp").astype(jnp.float32),
    )
    unused_cond, silu_back = jax.vjp(jax.nn.silu, cond)
    cond_grad = silu_back(cond_act_grad)[0]
    time_grad = jnp.einsum(
        "ib,id->bd", bucket_hot.astype(jnp.float32), cond_grad, precision=HIGHEST
    )
    class_grad = jnp.einsum(
        "ib,id->bd", class_hot.astype(jnp.float32), cond_grad, precision=HIGHEST
    )
    qkv_grad = jnp.stack([grad_shards[0][0]])
    proj_grad = jnp.stack([grad_shards[0][1]])
    gate_grad = jnp.stack([grad_shards[0][2]])
    up_grad = jnp.stack([grad_shards[0][3]])
    down_grad = jnp.stack([grad_shards[0][4]])
    return (
        result,
        resid_grad,
        time_grad,
        class_grad,
        ada_grad,
        qkv_grad,
        proj_grad,
        gate_grad,
        up_grad,
        down_grad,
        query_grad,
        key_grad,
    )


BF16 = jnp.bfloat16
F32 = jnp.float32
LOG2E = 1.4426950408889634
LN2 = 0.6931471805599453
DP_AXES = ("z", "y", "c")
SMALL = pl.CostEstimate(flops=1, bytes_accessed=1, transcendentals=0)


def kernel_call(kernel, **options):
    return pl.pallas_call(kernel, cost_estimate=SMALL, **options)


def together(*arrays):
    return lax.optimization_barrier(arrays)


def swap(values, axis):
    return lax.ppermute(values, axis, [(0, 1), (1, 0)])


def in_order(own, other, axis):
    first = lax.axis_index(axis) == 0
    return jnp.stack([jnp.where(first, own, other), jnp.where(first, other, own)])


def spread(values, axis):
    return in_order(values, swap(values, axis), axis)


def by_rows(values):
    return with_layout_constraint(values, Layout(major_to_minor=tuple(range(values.ndim))))


def gather_z(values):
    n_z = lax.axis_size("z")
    return lax.all_gather(values, "z", axis=0, tiled=True).reshape(n_z, *values.shape)


def add_low(*terms):
    total = terms[0].astype(F32)
    for term in terms[1:]:
        total = total + term.astype(F32)
    return total.astype(BF16)


def dot_f32(left, right, contract):
    return lax.dot_general(left, right, (contract, ((), ())), preferred_element_type=F32)


def piece_targets(pieces, at):
    for k, (array, z_first, x, y, c) in enumerate(pieces):
        for z in range(array.shape[0]):
            block = ((z_first + z) * 2 + (at[2] + y) % 2) * 2 + (at[0] + c) % 2
            yield k, z, (at[1] + x) % 2, block


def join_rows(pieces, first_row, rows):
    width = pieces[0][0].shape[-1]
    half = width // 2
    blocks = sum(piece[0].shape[0] for piece in pieces) // 2

    def kernel(at, *refs):
        out_ref, buf, sems = refs[len(pieces) :]
        copies = []
        for k, z, x, block in piece_targets(pieces, at):
            copy = pltpu.make_async_copy(
                refs[k].at[z, pl.ds(first_row, rows)], buf.at[x, block], sems.at[x, block]
            )
            copy.start()
            copies.append(copy)
        for copy in copies:
            copy.wait()
        for block in range(blocks):
            out_ref[block] = jnp.concatenate([buf[0, block][:, half:], buf[1, block][:, half:]], axis=1)

    return kernel_call(
        kernel,
        grid_spec=pltpu.PrefetchScalarGridSpec(
            num_scalar_prefetch=1,
            grid=(1,),
            in_specs=[pl.BlockSpec(memory_space=pl.ANY)] * len(pieces),
            out_specs=[pl.BlockSpec((blocks, rows, width), lambda i, at: (0, 0, 0))],
            scratch_shapes=[pltpu.VMEM((2, blocks, rows, width), BF16), pltpu.SemaphoreType.DMA((2, blocks))],
        ),
        out_shape=[jax.ShapeDtypeStruct((blocks, rows, width), BF16)],
        compiler_params=pltpu.CompilerParams(vmem_limit_bytes=24 << 20),
        name="join_rows",
    )(place(), *[piece[0] for piece in pieces])[0]


def qkv_heads(normed, pieces, cos_t, sin_t, gains_t, head_dim, band, before=()):
    seq_len, width = normed.shape
    heads = HEADS
    group = 3
    rows_all = group * head_dim
    half = width // 2
    sent = pieces[0][0].shape[1]
    q_scale = head_dim**-0.5 * LOG2E
    side = pieces[0][4]
    steps = sum(piece[0].shape[0] for piece in pieces) // 2
    n_in = len(pieces)

    def kernel(at, norm_ref, cos_ref, sin_ref, gain_ref, *refs):
        out_ref, hat_ref, fac_ref, whole_ref, acc_ref, buf, sems = refs[n_in + len(before) :]

        @pl.when(pl.program_id(0) == 0)
        def _():
            for k, z, x, block in piece_targets(pieces, at):
                local = block // 2
                pltpu.make_async_copy(refs[k].at[z], buf.at[x, local], sems.at[x, local]).start()

        local = pl.program_id(0)
        step = 2 * local + (at[0] + side) % 2
        for x in range(2):
            pltpu.make_async_copy(refs[0].at[0], buf.at[x, local], sems.at[x, local]).wait()
        low, high = buf[0, local], buf[1, local]
        whole_ref[:sent] = jnp.concatenate([low[:, :half], high[:, :half]], axis=1)
        whole_ref[sent:] = jnp.concatenate([low[: rows_all - sent, half:], high[: rows_all - sent, half:]], axis=1)
        acc_ref[...] = dot_f32(whole_ref[...], norm_ref[...], ((1,), (1,)))
        for i in range(group):
            head = step * group + i
            rows = pl.ds(i * head_dim, head_dim)

            @pl.when(head < 2 * heads)
            def _():
                values = acc_ref[rows, :]
                fac = lax.rsqrt(jnp.mean(values * values, axis=0, keepdims=True) + EPS)
                hat = values * fac
                gained = hat * jnp.where(head < heads, gain_ref[:, 0:1] * q_scale, gain_ref[:, 1:2])
                turned = jnp.concatenate([gained[head_dim // 2 :], gained[: head_dim // 2]], axis=0)
                out_ref[i] = (gained * cos_ref[...] + turned * sin_ref[...]).astype(BF16)
                hat_ref[i] = hat[:, :band].astype(BF16)
                fac_ref[i] = fac[:, :band]

            @pl.when(head >= 2 * heads)
            def _():
                out_ref[i] = acc_ref[rows, :].astype(BF16)
                hat_ref[i] = jnp.zeros((head_dim, band), BF16)
                fac_ref[i] = jnp.zeros((1, band), F32)

    whole = lambda i, at: (0, 0)
    return kernel_call(
        kernel,
        grid_spec=pltpu.PrefetchScalarGridSpec(
            num_scalar_prefetch=1,
            grid=(steps,),
            in_specs=[
                pl.BlockSpec((seq_len, width), whole),
                pl.BlockSpec((head_dim, seq_len), whole),
                pl.BlockSpec((head_dim, seq_len), whole),
                pl.BlockSpec((head_dim, 2), whole),
            ]
            + [pl.BlockSpec(memory_space=pl.ANY)] * (n_in + len(before)),
            out_specs=[
                pl.BlockSpec((group, head_dim, seq_len), lambda i, at: (2 * i + (at[0] + side) % 2, 0, 0)),
                pl.BlockSpec((group, head_dim, band), lambda i, at: (2 * i + (at[0] + side) % 2, 0, 0)),
                pl.BlockSpec((group, 1, band), lambda i, at: (2 * i + (at[0] + side) % 2, 0, 0)),
                pl.BlockSpec((rows_all, width), lambda i, at: (2 * i + (at[0] + side) % 2, 0)),
            ],
            scratch_shapes=[
                pltpu.VMEM((rows_all, seq_len), F32),
                pltpu.VMEM((2, steps, sent, width), BF16),
                pltpu.SemaphoreType.DMA((2, steps)),
            ],
        ),
        out_shape=[
            jax.ShapeDtypeStruct((3 * heads, head_dim, seq_len), BF16),
            pltpu.HBM((3 * heads, head_dim, band), BF16),
            pltpu.HBM((3 * heads, 1, band), F32),
            pltpu.HBM((3 * width, width), BF16),
        ],
        input_output_aliases={5 + n_in + k: k for k in range(len(before))},
        compiler_params=pltpu.CompilerParams(vmem_limit_bytes=32 << 20),
        name="qkv_heads",
    )(place(), normed, cos_t, sin_t, gains_t, *[piece[0] for piece in pieces], *before)


def attention_forward(qkv, heads, band):
    _, head_dim, seq_len = qkv.shape

    def kernel(q_ref, k_ref, v_ref, out_ref, mass_ref):
        scores = dot_f32(k_ref[0], q_ref[0], ((0,), (0,)))
        weights = jnp.exp2(scores)
        mass = jnp.sum(weights, axis=0, keepdims=True)
        mixed = dot_f32(v_ref[0], weights.astype(BF16), ((1,), (0,)))
        out_ref[0] = (mixed / mass).astype(BF16)
        mass_ref[0] = jnp.log2(mass)

    return kernel_call(
        kernel,
        grid=(heads,),
        in_specs=[
            pl.BlockSpec((1, head_dim, band), lambda h: (h, 0, 0)),
            pl.BlockSpec((1, head_dim, seq_len), lambda h: (heads + h, 0, 0)),
            pl.BlockSpec((1, head_dim, seq_len), lambda h: (2 * heads + h, 0, 0)),
        ],
        out_specs=[
            pl.BlockSpec((1, head_dim, band), lambda h: (h, 0, 0)),
            pl.BlockSpec((1, 1, band), lambda h: (h, 0, 0)),
        ],
        out_shape=[
            jax.ShapeDtypeStruct((heads, head_dim, band), BF16),
            jax.ShapeDtypeStruct((heads, 1, band), F32),
        ],
        compiler_params=pltpu.CompilerParams(vmem_limit_bytes=14 << 20),
        name="attention_forward",
    )(qkv, qkv, qkv)


def attention_back_own(qkv, out_grad, log_mass, delta, heads, band):
    _, head_dim, seq_len = qkv.shape

    def kernel(q_ref, k_ref, v_ref, grad_ref, mass_ref, delta_ref, dq_ref, dk_ref, dv_ref):
        grad = grad_ref[0]
        scores = dot_f32(k_ref[0], q_ref[0], ((0,), (0,)))
        probs = jnp.exp2(scores - mass_ref[0])
        prob_grad = dot_f32(v_ref[0], grad, ((0,), (0,)))
        score_grad = (probs * (prob_grad - delta_ref[0])).astype(BF16)
        dq_ref[0] = dot_f32(k_ref[0], score_grad, ((1,), (0,)))
        dk_ref[0] = dot_f32(q_ref[0], score_grad[:band], ((1,), (1,)))
        dv_ref[0] = dot_f32(grad, probs[:band].astype(BF16), ((1,), (1,)))

    one = pl.BlockSpec((1, head_dim, band), lambda h: (h, 0, 0))
    row = pl.BlockSpec((1, 1, band), lambda h: (h, 0, 0))
    return kernel_call(
        kernel,
        grid=(heads,),
        in_specs=[
            one,
            pl.BlockSpec((1, head_dim, seq_len), lambda h: (heads + h, 0, 0)),
            pl.BlockSpec((1, head_dim, seq_len), lambda h: (2 * heads + h, 0, 0)),
            one,
            row,
            row,
        ],
        out_specs=[one, one, one],
        out_shape=[pltpu.HBM((heads, head_dim, band), F32)] * 3,
        compiler_params=pltpu.CompilerParams(vmem_limit_bytes=16 << 20),
        name="attention_back_own",
    )(qkv, qkv, qkv, out_grad, log_mass, delta)


def attention_back_other(
    qkv, hat, fac, cos_t, sin_t, gains_t, dq, dk, dv, grads, mass, delta, heads, band
):
    _, head_dim, seq_len = qkv.shape
    inv_root = head_dim**-0.5
    early = grads[0].shape[0]

    def kernel(
        q_ref, k_ref, v_ref, hq_ref, hk_ref, fq_ref, fk_ref, cos_ref, sin_ref, gain_ref,
        dq_ref, dk_ref, dv_ref, low_ref, high_ref, mass_ref, delta_ref, out_ref, gq_ref, gk_ref,
    ):
        grad = jnp.where(pl.program_id(0) < early, low_ref[0], high_ref[0])
        scores = dot_f32(k_ref[0], q_ref[0], ((0,), (0,)))
        probs = jnp.exp2(scores - mass_ref[0])
        prob_grad = dot_f32(v_ref[0], grad, ((0,), (0,)))
        score_grad = (probs * (prob_grad - delta_ref[0])).astype(BF16)
        key_grad = (dk_ref[0] + dot_f32(q_ref[0], score_grad, ((1,), (1,)))) * LN2
        value_grad = dv_ref[0] + dot_f32(grad, probs.astype(BF16), ((1,), (1,)))
        query_grad = dq_ref[0] * inv_root

        def back(turned_grad, hat, fac, gain):
            spun = turned_grad * sin_ref[...]
            spun = jnp.concatenate([spun[head_dim // 2 :], spun[: head_dim // 2]], axis=0)
            gained_grad = turned_grad * cos_ref[...] + spun
            gain_grad = jnp.sum(gained_grad * hat, axis=1, keepdims=True)
            hat_grad = gained_grad * gain
            along = jnp.mean(hat_grad * hat, axis=0, keepdims=True)
            return (fac * (hat_grad - hat * along)).astype(BF16), gain_grad

        out_ref[0, 0], gq_ref[0] = back(query_grad, hq_ref[0].astype(F32), fq_ref[0], gain_ref[:, 0:1])
        out_ref[1, 0], gk_ref[0] = back(key_grad, hk_ref[0].astype(F32), fk_ref[0], gain_ref[:, 1:2])
        out_ref[2, 0] = value_grad.astype(BF16)

    one = pl.BlockSpec((1, head_dim, band), lambda h: (h, 0, 0))
    row = pl.BlockSpec((1, 1, band), lambda h: (h, 0, 0))
    key_one = pl.BlockSpec((1, head_dim, band), lambda h: (heads + h, 0, 0))
    key_row = pl.BlockSpec((1, 1, band), lambda h: (heads + h, 0, 0))
    table = pl.BlockSpec((head_dim, band), lambda h: (0, 0))
    column = pl.BlockSpec((1, head_dim, 1), lambda h: (h, 0, 0))
    return kernel_call(
        kernel,
        grid=(heads,),
        in_specs=[
            pl.BlockSpec((1, head_dim, band), lambda h: (h, 0, 1)),
            key_one,
            pl.BlockSpec((1, head_dim, band), lambda h: (2 * heads + h, 0, 0)),
            one, key_one, row, key_row, table, table,
            pl.BlockSpec((head_dim, 2), lambda h: (0, 0)),
            one, one, one,
            pl.BlockSpec((1, head_dim, band), lambda h: (jnp.minimum(h, early - 1), 0, 0)),
            pl.BlockSpec((1, head_dim, band), lambda h: (jnp.maximum(h - early, 0), 0, 0)),
            row, row,
        ],
        out_specs=[pl.BlockSpec((3, 1, head_dim, band), lambda h: (0, h, 0, 0)), column, column],
        out_shape=[
            jax.ShapeDtypeStruct((3, heads, head_dim, band), BF16),
            jax.ShapeDtypeStruct((heads, head_dim, 1), F32),
            jax.ShapeDtypeStruct((heads, head_dim, 1), F32),
        ],
        compiler_params=pltpu.CompilerParams(vmem_limit_bytes=14 << 20),
        name="attention_back_other",
    )(*[pltpu.with_memory_space_constraint(qkv, pltpu.HBM)] * 3, hat, hat, fac, fac, cos_t, sin_t, gains_t,
      *[pltpu.with_memory_space_constraint(v, pltpu.HBM) for v in (dq, dk, dv)], *grads, mass, delta)


def mlp(mid, mlp_grad, pieces, down_own, down_other):
    band, width = mlp_grad.shape
    rows = pieces[0][0].shape[1]
    half = width // 2
    blocks = sum(piece[0].shape[0] for piece in pieces) // 2
    steps = 4
    per = blocks // steps
    units = per * rows
    chunk = band // 2
    n_z, _, _, down_rows, down_width = down_own.shape

    def kernel(at, mid_ref, mg_ref, *refs):
        downs = refs[len(pieces) : len(pieces) + 2]
        hid_ref, gg_ref, ug_ref, out_ref, grad_ref, buf, down_buf, sems, down_sems = refs[len(pieces) + 2 :]
        step = pl.program_id(0)

        @pl.when(step == 0)
        def _():
            for x in range(2):
                for z in range(n_z):
                    for y in range(2):
                        for c in range(2):
                            block = (z * 2 + y) * 2 + (at[0] + c) % 2
                            target = down_buf.at[x, pl.ds(pl.multiple_of(block * down_rows, 8), down_rows)]
                            pltpu.make_async_copy(downs[c].at[z, y, x], target, down_sems.at[x, block]).start()
            for k, z, x, block in piece_targets(pieces, at):
                pltpu.make_async_copy(refs[k].at[z], buf.at[x, block], sems.at[x, block]).start()
            out_ref[...] = jnp.zeros_like(out_ref)
            grad_ref[...] = jnp.zeros_like(grad_ref)

        for b in range(per):
            for x in range(2):
                block = step * per + b
                pltpu.make_async_copy(refs[0].at[0], buf.at[x, block], sems.at[x, block]).wait()
        @pl.when(step % 2 == 0)
        def _():
            for block in range(4 * n_z):
                target = down_buf.at[step // 2, pl.ds(block * down_rows, down_rows)]
                pltpu.make_async_copy(downs[0].at[0, 0, 0], target, down_sems.at[step // 2, block]).wait()

        low = buf[0, pl.ds(step * per, per)].reshape(units, width)
        high = buf[1, pl.ds(step * per, per)].reshape(units, width)
        gate = jnp.concatenate([low[:, :half], high[:, :half]], axis=1)
        up = jnp.concatenate([low[:, half:], high[:, half:]], axis=1)
        down = down_buf[step // 2, :, pl.ds(pl.multiple_of(step % 2 * units, 128), units)]
        nt, nn = ((1,), (1,)), ((1,), (0,))
        for part in range(2):
            at_rows = pl.ds(part * chunk, chunk)
            mid = mid_ref[at_rows, :]
            gate_pre = dot_f32(mid, gate, nt)
            up_pre = dot_f32(mid, up, nt)
            hidden_grad = dot_f32(mg_ref[at_rows, :], down, nn)
            sig = 1.0 / (1.0 + jnp.exp(-gate_pre))
            act = gate_pre * sig
            hidden = (act * up_pre).astype(BF16)
            gate_grad = (hidden_grad * up_pre * (sig * (1.0 + gate_pre * (1.0 - sig)))).astype(BF16)
            up_grad = (hidden_grad * act).astype(BF16)
            hid_ref[at_rows, :] = hidden
            gg_ref[:, at_rows] = gate_grad.T
            ug_ref[:, at_rows] = up_grad.T
            out_ref[at_rows, :] += dot_f32(hidden, down, nt)
            grad_ref[at_rows, :] += dot_f32(gate_grad, gate, nn) + dot_f32(up_grad, up, nn)

    whole = lambda i, at: (0, 0)
    once = pl.Buffered(1)
    return kernel_call(
        kernel,
        grid_spec=pltpu.PrefetchScalarGridSpec(
            num_scalar_prefetch=1,
            grid=(steps,),
            in_specs=[
                pl.BlockSpec((band, width), whole, pipeline_mode=once),
                pl.BlockSpec((band, width), whole, pipeline_mode=once),
            ]
            + [pl.BlockSpec(memory_space=pl.ANY)] * (len(pieces) + 2),
            out_specs=[
                pl.BlockSpec((band, units), lambda i, at: (0, i)),
                pl.BlockSpec((units, band), lambda i, at: (i, 0)),
                pl.BlockSpec((units, band), lambda i, at: (i, 0)),
                pl.BlockSpec((band, width), whole, pipeline_mode=once),
                pl.BlockSpec((band, width), whole, pipeline_mode=once),
            ],
            scratch_shapes=[
                pltpu.VMEM((2, blocks, rows, width), BF16),
                pltpu.VMEM((2, width, down_width), BF16),
                pltpu.SemaphoreType.DMA((2, blocks)),
                pltpu.SemaphoreType.DMA((2, 4 * n_z)),
            ],
        ),
        out_shape=[
            jax.ShapeDtypeStruct((band, blocks * rows), BF16),
            jax.ShapeDtypeStruct((blocks * rows, band), BF16),
            jax.ShapeDtypeStruct((blocks * rows, band), BF16),
            jax.ShapeDtypeStruct((band, width), F32),
            jax.ShapeDtypeStruct((band, width), F32),
        ],
        compiler_params=pltpu.CompilerParams(vmem_limit_bytes=56 << 20),
        name="mlp",
    )(place(), mid, mlp_grad, *[piece[0] for piece in pieces], down_own, down_other)


def after_attention(attended_t, proj_t, residual_low, modulation):
    width, band = attended_t.shape
    half = width // 2
    block = 128

    def kernel(att_ref, proj_ref, low_ref, mod_ref, branch_ref, middle_ref, normed_ref, mid_ref, att_out_ref):
        branch = dot_f32(att_ref[...], proj_ref[...], ((0,), (1,)))
        middle = low_ref[...].astype(F32) + mod_ref[2:3, :] * branch
        normed = modulate(middle, mod_ref[3:4, :], mod_ref[4:5, :]).astype(BF16)
        attended = att_ref[...].T
        branch_ref[...] = branch.astype(BF16)
        middle_ref[...] = middle
        normed_ref[...] = normed
        for x in range(2):
            mid_ref[x] = normed[:, x * half : (x + 1) * half]
            att_out_ref[x] = attended[:, x * half : (x + 1) * half]

    rows = pl.BlockSpec((block, width), lambda i: (i, 0))
    halves = pl.BlockSpec((2, block, half), lambda i: (0, i, 0))
    return kernel_call(
        kernel,
        grid=(band // block,),
        in_specs=[
            pl.BlockSpec((width, block), lambda i: (0, i)),
            pl.BlockSpec((width, width), lambda i: (0, 0)),
            rows,
            pl.BlockSpec((6, width), lambda i: (0, 0)),
        ],
        out_specs=[rows, rows, rows, halves, halves],
        out_shape=[
            jax.ShapeDtypeStruct((band, width), BF16),
            jax.ShapeDtypeStruct((band, width), F32),
            jax.ShapeDtypeStruct((band, width), BF16),
            jax.ShapeDtypeStruct((2, band, half), BF16),
            jax.ShapeDtypeStruct((2, band, half), BF16),
        ],
        compiler_params=pltpu.CompilerParams(vmem_limit_bytes=20 << 20),
        name="after_attention",
    )(attended_t, proj_t, residual_low, modulation)


def middle_back(normed_mid_grad, middle, out_grad, branch, mlp_out, proj_t, attended_t, modulation):
    band, width = middle.shape
    half = width // 2
    head_dim = width // HEADS
    block = 128

    def kernel(
        normed_grad_ref, mid_ref, out_ref, branch_ref, mlp_ref, proj_ref, att_ref, mod_ref,
        grad_ref, bg_ref, att_grad_ref, delta_ref, result_ref, sums_ref,
    ):
        @pl.when(pl.program_id(0) == 0)
        def _():
            sums_ref[...] = jnp.zeros_like(sums_ref)

        normed_grad = normed_grad_ref[...]
        middle, grad, mlp_out = mid_ref[...], out_ref[...].astype(F32), mlp_ref[...]
        fac = norm_factor(middle)
        hat = middle * fac
        hat_grad = normed_grad * (1.0 + mod_ref[4:5, :])
        along = jnp.mean(hat_grad * hat, axis=-1, keepdims=True)
        mid_grad = grad + fac * (hat_grad - hat * along)
        branch_grad = (mod_ref[2:3, :] * mid_grad).astype(BF16)
        attended_grad = dot_f32(branch_grad, proj_ref[...], ((1,), (0,))).astype(BF16).T
        grad_ref[...] = mid_grad
        bg_ref[...] = branch_grad.T
        att_grad_ref[...] = attended_grad
        both = attended_grad.astype(F32) * att_ref[...].astype(F32)
        delta_ref[...] = jnp.sum(both.reshape(HEADS, head_dim, block), axis=1, keepdims=True)
        result_ref[...] = (middle + mod_ref[5:6, :] * mlp_out).astype(BF16)
        sums_ref[0:1, :] += jnp.sum(normed_grad, axis=0, keepdims=True)
        sums_ref[1:2, :] += jnp.sum(normed_grad * hat, axis=0, keepdims=True)
        sums_ref[2:3, :] += jnp.sum(mid_grad * branch_ref[...].astype(F32), axis=0, keepdims=True)
        sums_ref[3:4, :] += jnp.sum(grad * mlp_out, axis=0, keepdims=True)

    rows = pl.BlockSpec((block, width), lambda i: (i, 0))
    columns = pl.BlockSpec((width, block), lambda i: (0, i))
    return kernel_call(
        kernel,
        grid=(band // block,),
        in_specs=[
            rows, rows, rows, rows, rows,
            pl.BlockSpec((width, width), lambda i: (0, 0)),
            columns,
            pl.BlockSpec((6, width), lambda i: (0, 0)),
        ],
        out_specs=[
            rows, columns, columns,
            pl.BlockSpec((HEADS, 1, block), lambda i: (0, 0, i)),
            rows,
            pl.BlockSpec((8, width), lambda i: (0, 0)),
        ],
        out_shape=[
            jax.ShapeDtypeStruct((band, width), F32),
            jax.ShapeDtypeStruct((width, band), BF16),
            jax.ShapeDtypeStruct((width, band), BF16),
            jax.ShapeDtypeStruct((HEADS, 1, band), F32),
            jax.ShapeDtypeStruct((band, width), BF16),
            jax.ShapeDtypeStruct((8, width), F32),
        ],
        compiler_params=pltpu.CompilerParams(vmem_limit_bytes=20 << 20),
        name="middle_back",
    )(normed_mid_grad, middle, out_grad, branch, mlp_out, proj_t, attended_t, modulation)


def input_back(projected_t, qkv_t, latents, mid_grad, modulation):
    inner, band = projected_t.shape
    width = qkv_t.shape[1]
    block = 128

    def kernel(left_ref, weight_ref, low_ref, grad_ref, mod_ref, out_ref, sums_ref):
        @pl.when(pl.program_id(0) == 0)
        def _():
            sums_ref[...] = jnp.zeros_like(sums_ref)

        normed_grad = dot_f32(left_ref[...], weight_ref[...], ((0,), (0,)))
        residual = low_ref[...].astype(F32)
        fac = norm_factor(residual)
        hat = residual * fac
        hat_grad = normed_grad * (1.0 + mod_ref[1:2, :])
        along = jnp.mean(hat_grad * hat, axis=-1, keepdims=True)
        out_ref[...] = grad_ref[...] + fac * (hat_grad - hat * along)
        sums_ref[0:1, :] += jnp.sum(normed_grad, axis=0, keepdims=True)
        sums_ref[1:2, :] += jnp.sum(normed_grad * hat, axis=0, keepdims=True)

    rows = pl.BlockSpec((block, width), lambda i: (i, 0))
    return kernel_call(
        kernel,
        grid=(band // block,),
        in_specs=[
            pl.BlockSpec((inner, block), lambda i: (0, i)),
            pl.BlockSpec((inner, width), lambda i: (0, 0), pipeline_mode=pl.Buffered(1)),
            rows,
            rows,
            pl.BlockSpec((6, width), lambda i: (0, 0)),
        ],
        out_specs=[rows, pl.BlockSpec((8, width), lambda i: (0, 0))],
        out_shape=[jax.ShapeDtypeStruct((band, width), F32), jax.ShapeDtypeStruct((8, width), F32)],
        compiler_params=pltpu.CompilerParams(vmem_limit_bytes=24 << 20),
        name="input_back",
    )(projected_t, qkv_t, latents, mid_grad, modulation)


def place():
    return jnp.stack([lax.axis_index(axis) for axis in ("c", "x", "y")]).astype(jnp.int32)


def terms(lefts, right, rows, side, received=None, z_first=0, n_z=4, y=(0, 1), order=(0, 1), stacked=True, split=0):
    patches = right.shape[0] if right.ndim == 2 else right.shape[1]
    wide = right.ndim == 2
    each = right.shape[-1] // 2 if wide else right.shape[-1]
    width = each * len(lefts)
    count = split or len(y) * n_z
    n = len(lefts)

    def left_map(i, at):
        if split:
            return (i, 0)
        z = z_first + i % n_z
        return ((z * 2 + (y[0] + i // n_z + at[2]) % 2) * 2 + (at[0] + side) % 2, 0)

    def right_spec(h):
        if wide:
            return pl.BlockSpec((patches, each), lambda i, at: (0, (at[1] + h) % 2))
        return pl.BlockSpec((1, patches, each), lambda i, at: ((at[1] + h) % 2, 0, 0))

    def kernel(at, *refs):
        rights, outs = refs[n : n + 2], refs[n + 2 :]
        if received is not None:
            got, outs = refs[n + 2 : n + 4], refs[n + 4 :]
        for k in range(2):
            half = rights[k][...] if wide else rights[k][0]
            values = [dot_f32(refs[m][...], half, ((1,), (0,))) for m in range(n)]
            value = values[0] if n == 1 else jnp.concatenate(values, axis=1)
            if received is not None:
                value = value + got[k][0, 0].astype(F32)
            if not stacked:
                outs[k][0] = value.astype(BF16)
            elif split:
                outs[0][0, k] = value.astype(BF16)
            else:
                outs[0][k, 0] = value.astype(BF16)

    received_specs = []
    if received is not None:
        skip = 0 if split else y[0] * n_z
        received_specs = [
            pl.BlockSpec((1, 1, rows, width), lambda i, at, k=k: (i, k, 0, 0) if split else (k, i + skip, 0, 0))
            for k in range(2)
        ]
    if stacked and split:
        out_shape = [jax.ShapeDtypeStruct((count, 2, rows, width), BF16)]
        out_specs = [pl.BlockSpec((1, 2, rows, width), lambda i, at: (i, 0, 0, 0))]
    elif stacked:
        out_shape = [jax.ShapeDtypeStruct((2, count, rows, width), BF16)]
        out_specs = [pl.BlockSpec((2, 1, rows, width), lambda i, at: (0, i, 0, 0))]
    else:
        out_shape = [jax.ShapeDtypeStruct((count, rows, width), BF16)] * 2
        out_specs = [pl.BlockSpec((1, rows, width), lambda i, at: (i, 0, 0))] * 2
    outs = kernel_call(
        kernel,
        grid_spec=pltpu.PrefetchScalarGridSpec(
            num_scalar_prefetch=1,
            grid=(count,),
            in_specs=[pl.BlockSpec((rows, patches), left_map)] * n
            + [right_spec(h) for h in order]
            + received_specs,
            out_specs=out_specs,
        ),
        out_shape=out_shape,
        compiler_params=pltpu.CompilerParams(vmem_limit_bytes=12 << 20),
        name="terms",
    )(place(), *lefts, right, right, *([received] * 2 if received is not None else []))
    return outs[0] if stacked else outs


def last_terms(left, right, rows, cut, received):
    patches, width = left.shape[-1], right.shape[-1]
    n_z = 4
    late = rows - cut

    def row_of(i):
        return 1 - i // n_z

    def kernel(at, left_ref, own_ref, other_ref, r0_ref, r1_ref, keep_ref, send_ref, up_send_ref, up_keep_ref):
        values = [
            (dot_f32(left_ref[...], ref[0], ((1,), (0,))) + got[0, 0].astype(F32)).astype(BF16)
            for ref, got in ((own_ref, r0_ref), (other_ref, r1_ref))
        ]
        keep_ref[0] = values[0][:cut]
        send_ref[0] = values[1][:cut]

        @pl.when(pl.program_id(0) < n_z)
        def _():
            for k in range(2):
                up_send_ref[1 - k, 0] = values[k][cut:]

        @pl.when(pl.program_id(0) >= n_z)
        def _():
            for k in range(2):
                up_keep_ref[1 - k, 0] = values[k][cut:]

    def got(h):
        return pl.BlockSpec((1, 1, rows, width), lambda i, at: (h, row_of(i) * n_z + i % n_z, 0, 0))

    early_spec = pl.BlockSpec((1, cut, width), lambda i, at: (row_of(i) * n_z + i % n_z, 0, 0))
    return kernel_call(
        kernel,
        grid_spec=pltpu.PrefetchScalarGridSpec(
            num_scalar_prefetch=1,
            grid=(2 * n_z,),
            in_specs=[
                pl.BlockSpec(
                    (rows, patches), lambda i, at: ((i % n_z * 2 + (row_of(i) + at[2]) % 2) * 2 + at[0], 0)
                ),
                pl.BlockSpec((1, patches, width), lambda i, at: (at[1], 0, 0)),
                pl.BlockSpec((1, patches, width), lambda i, at: ((at[1] + 1) % 2, 0, 0)),
                got(0),
                got(1),
            ],
            out_specs=[
                early_spec,
                early_spec,
                pl.BlockSpec((2, 1, late, width), lambda i, at: (0, jnp.minimum(i, n_z - 1), 0, 0)),
                pl.BlockSpec((2, 1, late, width), lambda i, at: (0, jnp.maximum(i - n_z, 0), 0, 0)),
            ],
        ),
        out_shape=[jax.ShapeDtypeStruct((2 * n_z, cut, width), BF16)] * 2
        + [jax.ShapeDtypeStruct((2, n_z, late, width), BF16)] * 2,
        compiler_params=pltpu.CompilerParams(vmem_limit_bytes=12 << 20),
        name="last_terms",
    )(place(), left, right, right, received, received)


def split_rows(left_t, z_first):
    n_z, patches = lax.axis_size("z"), left_t.shape[-1]
    blocks = left_t.reshape(n_z, 2, 2, -1, patches)
    core, row = lax.axis_index("c"), lax.axis_index("y")

    def part(which):
        picked = lax.dynamic_index_in_dim(blocks, which, 2, keepdims=False)
        own = lax.dynamic_index_in_dim(picked, row, 1, keepdims=False)
        other = lax.dynamic_index_in_dim(picked, 1 - row, 1, keepdims=False)
        return jnp.stack([own, other], axis=1 if z_first else 0).reshape(-1, patches)

    return part(1 - core), part(core)


def summed_with(values, axis, hop):
    low = values.astype(BF16)
    pairs = [(i, i ^ hop) for i in range(lax.axis_size(axis))]
    return low.astype(F32) + lax.ppermute(low, axis, pairs).astype(F32)


def spread_rows(hots, values):
    items, width = values.shape
    count = hots[0].shape[1]
    block = 384

    def kernel(values_ref, *refs):
        rest, parts = values_ref[...], []
        for _ in range(3):
            high = rest.astype(BF16)
            parts.append(high)
            rest = rest - high.astype(F32)
        for hot_ref, out_ref in zip(refs[: len(hots)], refs[len(hots) :]):
            hot = hot_ref[...]
            out_ref[...] = sum(dot_f32(hot, part, ((0,), (0,))) for part in parts)

    return kernel_call(
        kernel,
        grid=(width // block,),
        in_specs=[pl.BlockSpec((items, block), lambda i: (0, i))]
        + [pl.BlockSpec((items, count), lambda i: (0, 0))] * len(hots),
        out_specs=[pl.BlockSpec((count, block), lambda i: (0, i))] * len(hots),
        out_shape=[jax.ShapeDtypeStruct((count, width), F32)] * len(hots),
        compiler_params=pltpu.CompilerParams(vmem_limit_bytes=16 << 20),
        name="spread_rows",
    )(values, *hots)


def fast_shards(
    latents, out_grad, time_table, class_table, buckets, labels, row_start,
    ada_weight, qkv_weight, proj_weight, gate_weight, up_weight, down_weight, query_gain, key_gain,
):
    band, width = latents.shape[1:]
    head_dim = width // HEADS
    lat, out_g = latents[0], out_grad[0]
    half = width // 2
    n_z = lax.axis_size("z")

    qkv_s, proj_s = qkv_weight[0].T, proj_weight[0].T
    gate_s, up_s, down_s = gate_weight[0].T, up_weight[0].T, by_rows(down_weight[0].T)
    qkv_rows, proj_rows, gate_rows = qkv_s.shape[0], proj_s.shape[0], gate_s.shape[0]
    cut = (qkv_rows + proj_rows) // 2
    first = by_rows(jnp.concatenate([qkv_s[:cut], jnp.concatenate([qkv_s[cut:], proj_s])], axis=1))
    second = by_rows(jnp.concatenate([gate_s, up_s], axis=1))

    first_z = gather_z(first)
    second_z = gather_z(second)
    start_other = swap(row_start.astype(F32), "x")
    (down_r,) = together(swap(down_s, "x"))
    down_x = in_order(down_s, down_r, "x")
    down_x, lat_x = together(down_x, lat)
    lat_other = swap(lat_x, "x")
    down_r = swap(down_x, "y")

    bucket_hot = (buckets[:, None] == jnp.arange(BUCKETS, dtype=jnp.int32)[None, :]).astype(BF16)
    class_hot = (labels[:, None] == jnp.arange(CLASSES, dtype=jnp.int32)[None, :]).astype(BF16)
    cond = jnp.dot(bucket_hot, time_table, preferred_element_type=F32) + jnp.dot(
        class_hot, class_table, preferred_element_type=F32
    )
    cond_act = jax.nn.silu(cond).astype(BF16)
    mod_cols = jnp.dot(cond_act, ada_weight[0], preferred_element_type=F32)

    offsets = jnp.arange(band, dtype=jnp.int32)
    rows_in = (offsets // SIDE).astype(F32)
    row_pos = jnp.concatenate([row_start.astype(F32)[0, 0] + rows_in, start_other[0, 0] + rows_in])
    col_pos = jnp.tile((offsets % SIDE).astype(F32), 2)
    quarter = head_dim // 4
    frequency = THETA ** (-jnp.arange(quarter, dtype=F32) / quarter)
    angles = jnp.concatenate([frequency[:, None] * row_pos[None], frequency[:, None] * col_pos[None]])
    cos_h, sin_h = jnp.cos(angles), jnp.sin(angles)
    cos_t = jnp.concatenate([cos_h, cos_h])
    sin_t = jnp.concatenate([-sin_h, sin_h])
    gains_t = jnp.concatenate([query_gain, key_gain]).T
    first_z, lat_other, down_r, mod_cols, cos_t, sin_t = together(first_z, lat_other, down_r, mod_cols, cos_t, sin_t)

    a, b = by_rows(first_z[:2]), by_rows(first_z[2:])
    a_y, b_x, a_c, b_c = swap(a, "y"), swap(b, "x"), swap(a, "c"), swap(b, "c")
    down_z = gather_z(in_order(down_x, down_r, "y").reshape(-1, down_x.shape[-1]))
    modulation = lax.all_to_all(mod_cols, DP_AXES, split_axis=0, concat_axis=1, tiled=True)
    a_y, b_x, a_c, b_c, modulation = together(a_y, b_x, a_c, b_c, modulation)

    a_x, b_y, a_yc, b_xc = swap(a, "x"), swap(b, "y"), swap(a_y, "c"), swap(b_x, "c")
    mods = modulation.reshape(6, width)
    shift_attn, scale_attn, gate_attn, shift_mlp, scale_mlp, gate_mlp = jnp.split(modulation, 6, axis=-1)
    lat_full = jnp.concatenate([lat, lat_other]).astype(F32)
    normed_full = modulate(lat_full, shift_attn, scale_attn).astype(BF16)
    a_x, b_y, a_yc, b_xc, normed_full = together(a_x, b_y, a_yc, b_xc, normed_full)

    a_yx, b_xy, a_xc, b_yc = swap(a_y, "x"), swap(b_x, "y"), swap(a_x, "c"), swap(b_y, "c")
    mlp_grad = (gate_mlp * out_g.astype(F32)).astype(BF16)
    down_send, down_keep = split_rows(mlp_grad.T, True)
    normed = normed_full[:band]
    normed_2 = jnp.stack([normed[:, :half], normed[:, half:]])
    second_z, a_yx, b_xy, a_xc, b_yc, mlp_grad, down_send, down_keep, normed_2 = together(
        second_z, a_yx, b_xy, a_xc, b_yc, mlp_grad, down_send, down_keep, normed_2
    )

    a_yxc, b_xyc = swap(a_yx, "c"), swap(b_xy, "c")
    e, f = by_rows(second_z[:2]), by_rows(second_z[2:])
    e_y, f_x = swap(e, "y"), swap(f, "x")
    pieces_own = [
        (a, 0, 0, 0, 0), (a_y, 0, 0, 1, 0), (a_x, 0, 1, 0, 0), (a_yx, 0, 1, 1, 0),
        (b, 2, 0, 0, 0), (b_x, 2, 1, 0, 0), (b_y, 2, 0, 1, 0), (b_xy, 2, 1, 1, 0),
    ]
    tables = (cos_t, sin_t, gains_t, head_dim, band)
    parts = qkv_heads(normed_full, pieces_own, *tables)
    *parts, e_y, f_x, a_yxc, b_xyc = together(*parts, e_y, f_x, a_yxc, b_xyc)

    e_x, f_y, e_c, f_c, e_yc = swap(e, "x"), swap(f, "y"), swap(e, "c"), swap(f, "c"), swap(e_y, "c")
    pieces_other = [
        (a_c, 0, 0, 0, 1), (a_yc, 0, 0, 1, 1), (a_xc, 0, 1, 0, 1), (a_yxc, 0, 1, 1, 1),
        (b_c, 2, 0, 0, 1), (b_xc, 2, 1, 0, 1), (b_yc, 2, 0, 1, 1), (b_xyc, 2, 1, 1, 1),
    ]
    qkv, hat, fac, qkv_t = qkv_heads(normed_full, pieces_other, *tables, before=parts)
    e_x, f_y, e_c, f_c, e_yc, qkv = together(e_x, f_y, e_c, f_c, e_yc, qkv)

    e_yx, f_xy = swap(e_y, "x"), swap(f_x, "y")
    f_xc, e_xc, f_yc = swap(f_x, "c"), swap(e_x, "c"), swap(f_y, "c")
    attended_t, log_mass = attention_forward(qkv, HEADS, band)
    proj_t = join_rows(pieces_own + pieces_other, qkv_rows - cut, proj_rows).reshape(width, width)
    e_yx, f_xy, f_xc, e_xc, f_yc, attended_t, proj_t, down_z = together(
        e_yx, f_xy, f_xc, e_xc, f_yc, attended_t, proj_t, down_z
    )

    down_own = down_z.reshape(n_z, 2, 2, -1, down_z.shape[-1])
    down_other, e_yxc, f_xyc = swap(down_own, "c"), swap(e_yx, "c"), swap(f_xy, "c")
    attended_t = attended_t.reshape(width, band)
    branch, middle, normed_mid, mid_2, att_2 = after_attention(attended_t, proj_t, lat, mods)
    pieces = [
        (e, 0, 0, 0, 0), (e_y, 0, 0, 1, 0), (e_x, 0, 1, 0, 0), (e_yx, 0, 1, 1, 0),
        (e_c, 0, 0, 0, 1), (e_yc, 0, 0, 1, 1), (e_xc, 0, 1, 0, 1), (e_yxc, 0, 1, 1, 1),
        (f, 2, 0, 0, 0), (f_x, 2, 1, 0, 0), (f_y, 2, 0, 1, 0), (f_xy, 2, 1, 1, 0),
        (f_c, 2, 0, 0, 1), (f_xc, 2, 1, 0, 1), (f_yc, 2, 0, 1, 1), (f_xyc, 2, 1, 1, 1),
    ]
    hidden, gate_grad_t, up_grad_t, mlp_out, normed_mid_grad = mlp(
        normed_mid, mlp_grad, pieces, down_own, down_other
    )

    gates = (gate_grad_t, up_grad_t)
    a_g = terms(gates, mid_2, gate_rows, 1, n_z=2)
    a_g, hidden, *gates, mlp_out, normed_mid_grad = together(a_g, hidden, *gates, mlp_out, normed_mid_grad)

    a_gr = swap(a_g, "c")
    mid_grad, branch_grad_t, attended_grad, delta, result, sums = middle_back(
        normed_mid_grad, middle, out_g, branch, mlp_out, proj_t, attended_t, mods
    )
    b_g = terms(gates, mid_2, gate_rows, 1, z_first=2, n_z=2, order=(1, 0))
    by_head = attended_grad.reshape(HEADS, head_dim, band)
    a_gr, b_g, by_head, delta, branch_grad_t = together(a_gr, b_g, by_head, delta, branch_grad_t)

    b_gr = swap(b_g, "c")
    other_first = swap(by_head[:6], "x")
    a_k, a_s = terms(gates, mid_2, gate_rows, 0, received=a_gr, n_z=2, stacked=False)
    proj_send, proj_keep = split_rows(branch_grad_t, False)
    down_g = terms((down_send,), hidden, 2 * proj_rows, 1, split=n_z)
    b_gr, other_first, a_k, a_s, down_g, proj_send, proj_keep = together(
        b_gr, other_first, a_k, a_s, down_g, proj_send, proj_keep
    )

    down_gr = swap(down_g, "c")
    a_r1 = [swap(a_s[2:3], "x")]
    b_s = terms(gates, mid_2, gate_rows, 0, received=b_gr, z_first=2, n_z=2, y=(1,), order=(1, 0))
    b_k = terms(gates, mid_2, gate_rows, 0, received=b_gr, z_first=2, n_z=2, y=(0,), order=(1, 0))
    proj_g = terms((proj_send,), att_2, n_z * proj_rows, 1, order=(1, 0), split=2)
    down_gr, a_r1[0], b_s, b_k, proj_g = together(down_gr, a_r1[0], b_s, b_k, proj_g)

    proj_gr = swap(proj_g, "c")
    a_r1.append(swap(a_s[3:4], "x"))
    b_s = b_s.reshape(4, gate_rows, width)
    b_r1 = [swap(b_s[:1], "y")]
    down_sum = terms((down_keep,), hidden, 2 * proj_rows, 0, received=down_gr, split=n_z)
    proj_gr, a_r1[1], b_r1[0], down_sum = together(proj_gr, a_r1[1], b_r1[0], down_sum)

    down_sum = lax.psum_scatter(
        down_sum.reshape(-1, down_sum.shape[-1]), "z", scatter_dimension=0, tiled=True
    ).reshape(2, 2, proj_rows, -1)
    other_last = swap(by_head[6:], "x")
    other_rows = swap(jnp.stack([log_mass, delta]), "x")
    b_r1.append(swap(b_s[1:3], "y"))
    dq, dk, dv = attention_back_own(qkv, by_head, log_mass, delta, HEADS, band)
    b_r1[1], other_last, other_rows, dq = together(b_r1[1], other_last, other_rows, dq)

    a_r1.append(swap(a_s[:2], "x"))
    b_r1.append(swap(b_s[3:], "y"))
    a_s2 = add_low(a_k[2:], jnp.concatenate(a_r1[:2]))
    a_r2 = [swap(a_s2[:1], "y")]
    heads_grad, gain_q, gain_k = attention_back_other(
        qkv, hat, fac, cos_t, sin_t, gains_t, dq, dk, dv,
        (other_first, other_last), other_rows[0], other_rows[1], HEADS, band,
    )
    projected_t = heads_grad.reshape(3 * width, band)
    a_r1[2], b_r1[2], a_r2[0], projected_t = together(a_r1[2], b_r1[2], a_r2[0], projected_t)

    b_r1 = jnp.concatenate(b_r1).reshape(2, 2, gate_rows, width)
    b_s2 = add_low(b_k[0], b_r1[0])
    b_r2 = [swap(b_s2[:1], "x")]
    a_r2.append(swap(a_s2[1:], "y"))
    q_g = terms((projected_t,), normed_2, qkv_rows, 1)
    b_r2[0], a_r2[1], q_g, proj_gr = together(b_r2[0], a_r2[1], q_g, proj_gr)

    q_gr = swap(q_g, "c")
    b_r2.append(swap(b_s2[1:], "x"))
    proj_sum = terms((proj_keep,), att_2, n_z * proj_rows, 0, received=proj_gr, order=(1, 0), split=2)
    proj_r1 = [swap(proj_sum[1, 0], "y")]
    q_gr, b_r2[1], proj_r1[0], proj_sum = together(q_gr, b_r2[1], proj_r1[0], proj_sum)

    row_a = 112
    qa_keep, qa_send, qb_send, qb_keep = last_terms(projected_t, normed_2, qkv_rows, row_a, q_gr)
    proj_r1.append(swap(proj_sum[1, 1], "y"))
    proj_r2 = swap(add_low(proj_sum[0, 0], proj_r1[0]), "x")
    gu = jnp.concatenate(
        [add_low(a_k[:2], a_r1[2], jnp.concatenate(a_r2)), add_low(b_k[1], b_r1[1], jnp.concatenate(b_r2))]
    )
    qa_keep, qa_send, qb_send, qb_keep, proj_r1[1], proj_r2, projected_t, gu, gain_q, gain_k = together(
        qa_keep, qa_send, qb_send, qb_keep, proj_r1[1], proj_r2, projected_t, gu, gain_q, gain_k
    )

    gu = lax.psum_scatter(gu.reshape(-1, width), "z", scatter_dimension=0, tiled=True)
    qa_r1, qb_r1 = swap(qa_send, "x"), swap(qb_send, "y")
    input_grad, in_sums = input_back(projected_t, qkv_t, lat, mid_grad, mods)
    mod_grad = jnp.concatenate([in_sums[0:1], in_sums[1:2], sums[2:3], sums[0:1], sums[1:2], sums[3:4]], axis=-1)
    small = jnp.concatenate([mod_grad, gain_q.sum(0).T, gain_k.sum(0).T], axis=-1)
    small_r = swap(small, "x")
    qa_r1, qb_r1, down_sum, small_r = together(qa_r1, qb_r1, down_sum, small_r)

    qa_keep, qa_r1 = qa_keep.reshape(2, n_z, row_a, half), qa_r1.reshape(2, n_z, row_a, half)
    qa_s2, qb_s2 = together(add_low(qa_keep[1], qa_r1[1]), add_low(qb_keep[0], qb_r1[0]))
    qa_r2, qb_r2 = swap(qa_s2, "y"), swap(qb_s2, "x")
    qa_r2, qb_r2, down_sum, small_r = together(qa_r2, qb_r2, down_sum, small_r)

    down_r = swap(down_sum[:, 1], "y")
    down_sum = add_low(down_sum[:, 0], down_r)
    down_r2 = swap(down_sum[1], "x")
    last = jnp.concatenate(
        [
            add_low(qa_keep[0], qa_r1[0], qa_r2),
            add_low(qb_keep[1], qb_r1[1], qb_r2),
            add_low(proj_sum[0, 1], proj_r1[1], proj_r2).reshape(n_z, proj_rows, half),
        ],
        axis=1,
    )
    last, small_r, gu = together(last, small_r, gu)
    last = lax.psum_scatter(last.reshape(-1, half), "z", scatter_dimension=0, tiled=True)
    small = small + small_r
    band_mod, band_gain = small[:, : 6 * width], small[:, 6 * width :]
    mod_cols_grad = lax.all_to_all(band_mod.astype(BF16), DP_AXES, split_axis=1, concat_axis=0, tiled=True)
    cond_act_part = dot_f32(mod_cols_grad, ada_weight[0], ((1,), (1,)))
    tail = jnp.zeros((8, width), F32).at[0, : 2 * head_dim].set(band_gain[0])
    summed = jnp.concatenate([cond_act_part, tail])
    for axis, size in (("c", 2), ("y", 2), ("z", n_z)):
        hop = 1
        while hop < size:
            summed = summed_with(summed, axis, hop)
            hop *= 2
    ada_grad = dot_f32(cond_act, mod_cols_grad, ((0,), (0,)))
    items = cond.shape[0]
    _, silu_back = jax.vjp(jax.nn.silu, cond)
    cond_grad = silu_back(summed[:items])[0]
    time_grad, class_grad = spread_rows((bucket_hot, class_hot), cond_grad)
    down_out = down_sum[0].astype(F32) + down_r2.astype(F32)

    def out(values):
        return values.T.astype(F32)[None]

    return (
        result[None],
        input_grad[None],
        time_grad,
        class_grad,
        ada_grad[None],
        out(last[:qkv_rows]),
        out(last[qkv_rows:]),
        out(gu[:, :half]),
        out(gu[:, half:]),
        out(down_out),
        summed[items : items + 1, :head_dim],
        summed[items : items + 1, head_dim : 2 * head_dim],
    )


def fast_solution(mesh):
    dp = mesh.shape["dp"]
    fine = jax.sharding.Mesh(mesh.devices.reshape(dp // 4, 2, 2, 2), ("z", "y", "c", "x"))
    items, last = P(DP_AXES, "x", None), P(None, "x", DP_AXES)
    in_specs = (items, items, P(), P(), P(), P(), P(DP_AXES, "x"), P(None, None, DP_AXES)) + (last,) * 5 + (P(), P())
    out_specs = (items, items, P(), P(), P(None, None, DP_AXES)) + (last,) * 5 + (P(), P())
    return jax.shard_map(fast_shards, mesh=fine, in_specs=in_specs, out_specs=out_specs, check_vma=False)


def solution(mesh):
    if mesh.shape["dp"] == 16 and mesh.shape["seq"] == 2:
        return fast_solution(mesh)
    in_specs = (
        P("dp", "seq", None),
        P("dp", "seq", None),
        P(),
        P(),
        P(),
        P(),
        P("dp", "seq"),
        P(None, None, "dp"),
        P(None, "seq", "dp"),
        P(None, "seq", "dp"),
        P(None, "seq", "dp"),
        P(None, "seq", "dp"),
        P(None, "seq", "dp"),
        P(),
        P(),
    )
    out_specs = (
        P("dp", "seq", None),
        P("dp", "seq", None),
        P(),
        P(),
        P(None, None, "dp"),
        P(None, "seq", "dp"),
        P(None, "seq", "dp"),
        P(None, "seq", "dp"),
        P(None, "seq", "dp"),
        P(None, "seq", "dp"),
        P(),
        P(),
    )
    return jax.shard_map(shards, mesh=mesh, in_specs=in_specs, out_specs=out_specs, check_vma=False)
```

```python
import jax
import jax.numpy as jnp
from jax import lax
from jax.experimental import pallas as pl
from jax.experimental.layout import Layout, with_layout_constraint
from jax.experimental.pallas import tpu as pltpu
from jax.sharding import PartitionSpec as P

HEADS = 16
CLASSES = 1000
BUCKETS = 1000
SIDE = 32


EPS = 1e-06
THETA = 10000.0
HIGHEST = lax.Precision.HIGHEST


def norm_factor(values):
    return lax.rsqrt(jnp.mean(values * values, axis=-1, keepdims=True) + EPS)


def modulate(values, shift_by, scale_by):
    return values * norm_factor(values) * (1.0 + scale_by) + shift_by


def rope_tables(row_pos, col_pos, head_dim):
    quarter = head_dim // 4
    frequency = THETA ** (-jnp.arange(quarter, dtype=jnp.float32) / quarter)
    angles = jnp.concatenate(
        [row_pos[..., None] * frequency, col_pos[..., None] * frequency], axis=-1
    )
    cos_part = jnp.cos(angles)
    sin_part = jnp.sin(angles)
    return (
        jnp.concatenate([cos_part, cos_part], axis=-1),
        jnp.concatenate([sin_part, sin_part], axis=-1),
    )


def rotate(values, cos_part, sin_part):
    half_dim = values.shape[-1] // 2
    turned = jnp.concatenate([-values[..., half_dim:], values[..., :half_dim]], axis=-1)
    return values * cos_part + turned * sin_part


def query_key(query_pre, key_pre, gain_query, gain_key, cos_part, sin_part):
    query_out = rotate(query_pre * norm_factor(query_pre) * gain_query, cos_part, sin_part)
    key_out = rotate(key_pre * norm_factor(key_pre) * gain_key, cos_part, sin_part)
    return (query_out, key_out)


def swiglu(gate_pre, up_pre):
    return jax.nn.silu(gate_pre) * up_pre


def gather_layer(layer_no, qkv_weight, proj_weight, gate_weight, up_weight, down_weight):
    row_parts = (
        lax.all_gather(qkv_weight[layer_no], "seq", axis=0, tiled=True),
        lax.all_gather(proj_weight[layer_no], "seq", axis=0, tiled=True),
        lax.all_gather(gate_weight[layer_no], "seq", axis=0, tiled=True),
        lax.all_gather(up_weight[layer_no], "seq", axis=0, tiled=True),
        lax.all_gather(down_weight[layer_no], "seq", axis=0, tiled=True),
    )
    qkv_rows, proj_rows, gate_rows, up_rows, down_rows = row_parts
    return (
        lax.all_gather(qkv_rows, "dp", axis=1, tiled=True),
        lax.all_gather(proj_rows, "dp", axis=1, tiled=True),
        lax.all_gather(gate_rows, "dp", axis=1, tiled=True),
        lax.all_gather(up_rows, "dp", axis=1, tiled=True),
        lax.all_gather(down_rows, "dp", axis=1, tiled=True),
    )


def attend(queries, key_rows, value_rows, inv_root):
    items_dev, band_rows, head_count, head_dim = queries.shape
    top_score = jnp.full((items_dev, head_count, band_rows), -jnp.inf, jnp.float32)
    row_mass = jnp.zeros((items_dev, head_count, band_rows), jnp.float32)
    weighted = jnp.zeros((items_dev, band_rows, head_count, head_dim), jnp.float32)
    key_seg = lax.all_gather(key_rows, "seq", axis=1, tiled=True)
    value_seg = lax.all_gather(value_rows, "seq", axis=1, tiled=True)
    seg_rows = key_seg.shape[1]
    key_heads = key_seg.reshape(items_dev, seg_rows, head_count, head_dim)
    value_heads = value_seg.reshape(items_dev, seg_rows, head_count, head_dim)
    scores = (
        jnp.einsum("ibhe,inhe->ihbn", queries, key_heads, preferred_element_type=jnp.float32)
        * inv_root
    )
    new_top = jnp.max(scores, axis=-1)
    shrink = jnp.exp(top_score - new_top)
    weights = jnp.exp(scores - new_top[..., None])
    new_mass = row_mass * shrink + jnp.sum(weights, axis=-1)
    update = jnp.einsum(
        "ihbn,inhe->ibhe",
        weights.astype(jnp.bfloat16),
        value_heads,
        preferred_element_type=jnp.float32,
    )
    new_weighted = weighted * jnp.transpose(shrink, (0, 2, 1))[..., None] + update
    log_mass = new_top + jnp.log(new_mass)
    attended = new_weighted / jnp.transpose(new_mass, (0, 2, 1))[..., None]
    return (attended, log_mass)


def attend_back(queries, keys_all, values_all, attended_grad, log_mass, delta, inv_root):
    items_dev, band_rows, head_count, head_dim = queries.shape
    seq_len = keys_all.shape[1]
    key_heads = keys_all.reshape(items_dev, seq_len, head_count, head_dim)
    value_heads = values_all.reshape(items_dev, seq_len, head_count, head_dim)

    def one_item(operands):
        query_item, key_item, value_item, grad_item, mass_item, delta_item = operands
        scores = (
            jnp.einsum("bhe,nhe->hbn", query_item, key_item, preferred_element_type=jnp.float32)
            * inv_root
        )
        probs_full = jnp.exp(scores - mass_item[..., None])
        prob_grad = jnp.einsum(
            "bhe,nhe->hbn", grad_item, value_item, preferred_element_type=jnp.float32
        )
        score_grad = (probs_full * (prob_grad - delta_item[..., None])).astype(jnp.bfloat16)
        query_out_grad = (
            jnp.einsum("hbn,nhe->bhe", score_grad, key_item, preferred_element_type=jnp.float32)
            * inv_root
        )
        key_out_grad = (
            jnp.einsum("hbn,bhe->nhe", score_grad, query_item, preferred_element_type=jnp.float32)
            * inv_root
        )
        value_grad = jnp.einsum(
            "hbn,bhe->nhe",
            probs_full.astype(jnp.bfloat16),
            grad_item,
            preferred_element_type=jnp.float32,
        )
        return (query_out_grad, key_out_grad, value_grad)

    return lax.map(one_item, (queries, key_heads, value_heads, attended_grad, log_mass, delta))


def forward_layer(residual, modulation, weights, gain_query, gain_key, cos_part, sin_part):
    qkv_full, proj_full, gate_full, up_full, down_full = weights
    items_dev, band_rows, model_width = residual.shape
    head_count = HEADS
    head_dim = model_width // head_count
    inv_root = head_dim ** (-0.5)
    shift_attn, scale_attn, gate_attn, shift_mlp, scale_mlp, gate_mlp = jnp.split(
        modulation[:, None, :], 6, axis=-1
    )
    normed = modulate(residual, shift_attn, scale_attn).astype(jnp.bfloat16)
    projected = jnp.einsum("ibd,de->ibe", normed, qkv_full, preferred_element_type=jnp.float32)
    query_pre = projected[..., :model_width].reshape(items_dev, band_rows, head_count, head_dim)
    key_pre = projected[..., model_width : 2 * model_width].reshape(
        items_dev, band_rows, head_count, head_dim
    )
    queries, key_rows = query_key(query_pre, key_pre, gain_query, gain_key, cos_part, sin_part)
    queries = queries.astype(jnp.bfloat16)
    key_rows = key_rows.astype(jnp.bfloat16).reshape(items_dev, band_rows, model_width)
    value_rows = projected[..., 2 * model_width :].astype(jnp.bfloat16)
    attended, log_mass = attend(queries, key_rows, value_rows, inv_root)
    attended_low = attended.reshape(items_dev, band_rows, model_width).astype(jnp.bfloat16)
    branch = jnp.einsum("ibd,de->ibe", attended_low, proj_full, preferred_element_type=jnp.float32)
    middle = residual + gate_attn * branch
    normed_mid = modulate(middle, shift_mlp, scale_mlp).astype(jnp.bfloat16)
    gate_pre = jnp.einsum("ibd,df->ibf", normed_mid, gate_full, preferred_element_type=jnp.float32)
    up_pre = jnp.einsum("ibd,df->ibf", normed_mid, up_full, preferred_element_type=jnp.float32)
    hidden = swiglu(gate_pre, up_pre).astype(jnp.bfloat16)
    mlp_out = jnp.einsum("ibf,fd->ibd", hidden, down_full, preferred_element_type=jnp.float32)
    output = middle + gate_mlp * mlp_out
    stored = (
        residual,
        normed,
        query_pre,
        key_pre,
        queries,
        key_rows,
        value_rows,
        attended,
        attended_low,
        log_mass,
        branch,
        middle,
        normed_mid,
        gate_pre,
        up_pre,
        hidden,
        mlp_out,
    )
    return (output, stored)


def weight_terms(
    normed,
    attended_low,
    normed_mid,
    hidden,
    projected_grad,
    branch_grad,
    gate_pre_grad,
    up_pre_grad,
    mlp_grad,
):
    qkv_term = jnp.einsum("ibd,ibe->de", normed, projected_grad, preferred_element_type=jnp.float32)
    proj_term = jnp.einsum(
        "ibd,ibe->de", attended_low, branch_grad, preferred_element_type=jnp.float32
    )
    gate_term = jnp.einsum(
        "ibd,ibf->df", normed_mid, gate_pre_grad, preferred_element_type=jnp.float32
    )
    up_term = jnp.einsum("ibd,ibf->df", normed_mid, up_pre_grad, preferred_element_type=jnp.float32)
    down_term = jnp.einsum("ibf,ibd->fd", hidden, mlp_grad, preferred_element_type=jnp.float32)
    col_parts = (
        lax.psum_scatter(
            qkv_term.astype(jnp.bfloat16), "dp", scatter_dimension=1, tiled=True
        ).astype(jnp.float32),
        lax.psum_scatter(
            proj_term.astype(jnp.bfloat16), "dp", scatter_dimension=1, tiled=True
        ).astype(jnp.float32),
        lax.psum_scatter(
            gate_term.astype(jnp.bfloat16), "dp", scatter_dimension=1, tiled=True
        ).astype(jnp.float32),
        lax.psum_scatter(
            up_term.astype(jnp.bfloat16), "dp", scatter_dimension=1, tiled=True
        ).astype(jnp.float32),
        lax.psum_scatter(
            down_term.astype(jnp.bfloat16), "dp", scatter_dimension=1, tiled=True
        ).astype(jnp.float32),
    )
    qkv_cols, proj_cols, gate_cols, up_cols, down_cols = col_parts
    return (
        lax.psum_scatter(
            qkv_cols.astype(jnp.bfloat16), "seq", scatter_dimension=0, tiled=True
        ).astype(jnp.float32),
        lax.psum_scatter(
            proj_cols.astype(jnp.bfloat16), "seq", scatter_dimension=0, tiled=True
        ).astype(jnp.float32),
        lax.psum_scatter(
            gate_cols.astype(jnp.bfloat16), "seq", scatter_dimension=0, tiled=True
        ).astype(jnp.float32),
        lax.psum_scatter(
            up_cols.astype(jnp.bfloat16), "seq", scatter_dimension=0, tiled=True
        ).astype(jnp.float32),
        lax.psum_scatter(
            down_cols.astype(jnp.bfloat16), "seq", scatter_dimension=0, tiled=True
        ).astype(jnp.float32),
    )


def backward_layer(
    stored, resid_grad, modulation, weights, gain_query, gain_key, cos_part, sin_part
):
    qkv_full, proj_full, gate_full, up_full, down_full = weights
    (
        residual,
        normed,
        query_pre,
        key_pre,
        queries,
        key_rows,
        value_rows,
        attended,
        attended_low,
        log_mass,
        branch,
        middle,
        normed_mid,
        gate_pre,
        up_pre,
        hidden,
        mlp_out,
    ) = stored
    items_dev, band_rows, head_count, head_dim = queries.shape
    model_width = residual.shape[-1]
    inv_root = head_dim ** (-0.5)
    shift_attn, scale_attn, gate_attn, shift_mlp, scale_mlp, gate_mlp = jnp.split(
        modulation[:, None, :], 6, axis=-1
    )
    mlp_grad = (gate_mlp * resid_grad).astype(jnp.bfloat16)
    gate_mlp_grad = jnp.sum(resid_grad * mlp_out, axis=1, keepdims=True)
    hidden_grad = jnp.einsum("ibd,fd->ibf", mlp_grad, down_full, preferred_element_type=jnp.float32)
    unused_out, swiglu_back = jax.vjp(swiglu, gate_pre, up_pre)
    gate_pre_grad, up_pre_grad = swiglu_back(hidden_grad)
    gate_pre_grad = gate_pre_grad.astype(jnp.bfloat16)
    up_pre_grad = up_pre_grad.astype(jnp.bfloat16)
    normed_mid_grad = jnp.einsum(
        "ibf,df->ibd", gate_pre_grad, gate_full, preferred_element_type=jnp.float32
    )
    normed_mid_grad = normed_mid_grad + jnp.einsum(
        "ibf,df->ibd", up_pre_grad, up_full, preferred_element_type=jnp.float32
    )
    unused_mid, mid_back = jax.vjp(modulate, middle, shift_mlp, scale_mlp)
    mid_norm_grad, shift_mlp_grad, scale_mlp_grad = mid_back(normed_mid_grad)
    mid_grad = resid_grad + mid_norm_grad
    branch_grad = (gate_attn * mid_grad).astype(jnp.bfloat16)
    gate_attn_grad = jnp.sum(mid_grad * branch, axis=1, keepdims=True)
    attended_grad = jnp.einsum(
        "ibe,de->ibd", branch_grad, proj_full, preferred_element_type=jnp.float32
    ).astype(jnp.bfloat16)
    attended_grad = attended_grad.reshape(items_dev, band_rows, head_count, head_dim)
    delta = jnp.transpose(jnp.sum(attended_grad.astype(jnp.float32) * attended, axis=-1), (0, 2, 1))
    keys_all, values_all = (
        lax.all_gather(key_rows, "seq", axis=1, tiled=True),
        lax.all_gather(value_rows, "seq", axis=1, tiled=True),
    )
    query_out_grad, key_out_grad, value_grad = attend_back(
        queries, keys_all, values_all, attended_grad, log_mass, delta, inv_root
    )
    seq_len = keys_all.shape[1]
    key_band_grad, value_band_grad = (
        lax.psum_scatter(
            key_out_grad.reshape(items_dev, seq_len, model_width).astype(jnp.bfloat16),
            "seq",
            scatter_dimension=1,
            tiled=True,
        ).astype(jnp.float32),
        lax.psum_scatter(
            value_grad.reshape(items_dev, seq_len, model_width).astype(jnp.bfloat16),
            "seq",
            scatter_dimension=1,
            tiled=True,
        ).astype(jnp.float32),
    )

    def rotate_pair(query_in, key_in, gain_q, gain_k):
        return query_key(query_in, key_in, gain_q, gain_k, cos_part, sin_part)

    unused_pair, pair_back = jax.vjp(rotate_pair, query_pre, key_pre, gain_query, gain_key)
    query_pre_grad, key_pre_grad, query_gain_term, key_gain_term = pair_back(
        (query_out_grad, key_band_grad.reshape(items_dev, band_rows, head_count, head_dim))
    )
    projected_grad = jnp.concatenate(
        [
            query_pre_grad.reshape(items_dev, band_rows, model_width),
            key_pre_grad.reshape(items_dev, band_rows, model_width),
            value_band_grad,
        ],
        axis=-1,
    ).astype(jnp.bfloat16)
    normed_grad = jnp.einsum(
        "ibe,de->ibd", projected_grad, qkv_full, preferred_element_type=jnp.float32
    )
    unused_in, input_back = jax.vjp(modulate, residual, shift_attn, scale_attn)
    input_norm_grad, shift_attn_grad, scale_attn_grad = input_back(normed_grad)
    input_grad = mid_grad + input_norm_grad
    mod_grad = jnp.concatenate(
        [
            shift_attn_grad,
            scale_attn_grad,
            gate_attn_grad,
            shift_mlp_grad,
            scale_mlp_grad,
            gate_mlp_grad,
        ],
        axis=-1,
    )[:, 0, :]
    own_grads = weight_terms(
        normed,
        attended_low,
        normed_mid,
        hidden,
        projected_grad,
        branch_grad,
        gate_pre_grad,
        up_pre_grad,
        mlp_grad,
    )
    return (input_grad, mod_grad, own_grads, query_gain_term, key_gain_term)


def shards(
    latents,
    out_grad,
    time_table,
    class_table,
    buckets,
    labels,
    row_start,
    ada_weight,
    qkv_weight,
    proj_weight,
    gate_weight,
    up_weight,
    down_weight,
    query_gain,
    key_gain,
):
    items_dev, band_rows, model_width = latents.shape
    layer_count = qkv_weight.shape[0]
    head_dim = model_width // HEADS
    offsets = jnp.arange(band_rows, dtype=jnp.int32)
    row_pos = (row_start + (offsets // SIDE)[None, :]).astype(jnp.float32)
    col_pos = (offsets % SIDE).astype(jnp.float32)[None, :]
    cos_part, sin_part = rope_tables(row_pos, col_pos, head_dim)
    cos_part = cos_part[:, :, None, :]
    sin_part = sin_part[:, :, None, :]
    bucket_hot = (buckets[:, None] == jnp.arange(BUCKETS, dtype=jnp.int32)[None, :]).astype(
        jnp.bfloat16
    )
    class_hot = (labels[:, None] == jnp.arange(CLASSES, dtype=jnp.int32)[None, :]).astype(
        jnp.bfloat16
    )
    cond = jnp.dot(bucket_hot, time_table, preferred_element_type=jnp.float32) + jnp.dot(
        class_hot, class_table, preferred_element_type=jnp.float32
    )
    cond_act = jax.nn.silu(cond).astype(jnp.bfloat16)
    mod_cols = jnp.einsum("id,ldm->lim", cond_act, ada_weight, preferred_element_type=jnp.float32)
    modulation = lax.all_to_all(mod_cols, "dp", split_axis=1, concat_axis=2, tiled=True)
    residual = latents.astype(jnp.float32)
    gathered_all = []
    layer_no = 0
    weights = gather_layer(layer_no, qkv_weight, proj_weight, gate_weight, up_weight, down_weight)
    gathered_all.append(weights)
    residual, stored = forward_layer(
        residual,
        modulation[layer_no],
        weights,
        query_gain[layer_no],
        key_gain[layer_no],
        cos_part,
        sin_part,
    )
    stored_all = [stored]
    result = residual.astype(jnp.bfloat16)
    resid_grad = out_grad.astype(jnp.float32)
    mod_grads = [None] * layer_count
    grad_shards = [None] * layer_count
    query_terms = [None] * layer_count
    key_terms = [None] * layer_count
    for layer_no in reversed(range(layer_count)):
        weights = gather_layer(
            layer_no, qkv_weight, proj_weight, gate_weight, up_weight, down_weight
        )
        resid_grad, mod_grad, own_grads, query_term, key_term = backward_layer(
            stored_all[layer_no],
            resid_grad,
            modulation[layer_no],
            weights,
            query_gain[layer_no],
            key_gain[layer_no],
            cos_part,
            sin_part,
        )
        mod_grads[layer_no] = mod_grad
        grad_shards[layer_no] = own_grads
        query_terms[layer_no] = query_term
        key_terms[layer_no] = key_term
    band_mod, band_query, band_key = lax.psum(
        (jnp.stack(mod_grads), jnp.stack(query_terms), jnp.stack(key_terms)), "seq"
    )
    mod_cols_grad = lax.all_to_all(
        band_mod.astype(jnp.bfloat16), "dp", split_axis=2, concat_axis=1, tiled=True
    )
    ada_grad = jnp.einsum(
        "id,lim->ldm", cond_act, mod_cols_grad, preferred_element_type=jnp.float32
    )
    cond_act_part = jnp.einsum(
        "lim,ldm->id", mod_cols_grad, ada_weight, preferred_element_type=jnp.float32
    )
    cond_act_grad, query_grad, key_grad = (
        lax.psum(cond_act_part.astype(jnp.bfloat16), "dp").astype(jnp.float32),
        lax.psum(band_query.astype(jnp.bfloat16), "dp").astype(jnp.float32),
        lax.psum(band_key.astype(jnp.bfloat16), "dp").astype(jnp.float32),
    )
    unused_cond, silu_back = jax.vjp(jax.nn.silu, cond)
    cond_grad = silu_back(cond_act_grad)[0]
    time_grad = jnp.einsum(
        "ib,id->bd", bucket_hot.astype(jnp.float32), cond_grad, precision=HIGHEST
    )
    class_grad = jnp.einsum(
        "ib,id->bd", class_hot.astype(jnp.float32), cond_grad, precision=HIGHEST
    )
    qkv_grad = jnp.stack([grad_shards[0][0]])
    proj_grad = jnp.stack([grad_shards[0][1]])
    gate_grad = jnp.stack([grad_shards[0][2]])
    up_grad = jnp.stack([grad_shards[0][3]])
    down_grad = jnp.stack([grad_shards[0][4]])
    return (
        result,
        resid_grad,
        time_grad,
        class_grad,
        ada_grad,
        qkv_grad,
        proj_grad,
        gate_grad,
        up_grad,
        down_grad,
        query_grad,
        key_grad,
    )


BF16 = jnp.bfloat16
F32 = jnp.float32
LOG2E = 1.4426950408889634
LN2 = 0.6931471805599453
DP_AXES = ("z", "y", "c")
SMALL = pl.CostEstimate(flops=1, bytes_accessed=1, transcendentals=0)


def kernel_call(kernel, **options):
    return pl.pallas_call(kernel, cost_estimate=SMALL, **options)


def together(*arrays):
    return lax.optimization_barrier(arrays)


def swap(values, axis):
    return lax.ppermute(values, axis, [(0, 1), (1, 0)])


def in_order(own, other, axis):
    first = lax.axis_index(axis) == 0
    return jnp.stack([jnp.where(first, own, other), jnp.where(first, other, own)])


def spread(values, axis):
    return in_order(values, swap(values, axis), axis)


def by_rows(values):
    return with_layout_constraint(values, Layout(major_to_minor=tuple(range(values.ndim))))


def gather_z(values):
    n_z = lax.axis_size("z")
    return lax.all_gather(values, "z", axis=0, tiled=True).reshape(n_z, *values.shape)


def add_low(*terms):
    total = terms[0].astype(F32)
    for term in terms[1:]:
        total = total + term.astype(F32)
    return total.astype(BF16)


def dot_f32(left, right, contract):
    return lax.dot_general(left, right, (contract, ((), ())), preferred_element_type=F32)


def piece_targets(pieces, at):
    for k, (array, z_first, x, y, c) in enumerate(pieces):
        for z in range(array.shape[0]):
            block = ((z_first + z) * 2 + (at[2] + y) % 2) * 2 + (at[0] + c) % 2
            yield k, z, (at[1] + x) % 2, block


def join_rows(pieces, first_row, rows):
    width = pieces[0][0].shape[-1]
    half = width // 2
    blocks = sum(piece[0].shape[0] for piece in pieces) // 2

    def kernel(at, *refs):
        out_ref, buf, sems = refs[len(pieces) :]
        copies = []
        for k, z, x, block in piece_targets(pieces, at):
            copy = pltpu.make_async_copy(
                refs[k].at[z, pl.ds(first_row, rows)], buf.at[x, block], sems.at[x, block]
            )
            copy.start()
            copies.append(copy)
        for copy in copies:
            copy.wait()
        for block in range(blocks):
            out_ref[block] = jnp.concatenate([buf[0, block][:, half:], buf[1, block][:, half:]], axis=1)

    return kernel_call(
        kernel,
        grid_spec=pltpu.PrefetchScalarGridSpec(
            num_scalar_prefetch=1,
            grid=(1,),
            in_specs=[pl.BlockSpec(memory_space=pl.ANY)] * len(pieces),
            out_specs=[pl.BlockSpec((blocks, rows, width), lambda i, at: (0, 0, 0))],
            scratch_shapes=[pltpu.VMEM((2, blocks, rows, width), BF16), pltpu.SemaphoreType.DMA((2, blocks))],
        ),
        out_shape=[jax.ShapeDtypeStruct((blocks, rows, width), BF16)],
        compiler_params=pltpu.CompilerParams(vmem_limit_bytes=24 << 20),
        name="join_rows",
    )(place(), *[piece[0] for piece in pieces])[0]


def qkv_heads(normed, pieces, cos_t, sin_t, gains_t, head_dim, band, before=()):
    seq_len, width = normed.shape
    heads = HEADS
    group = 3
    rows_all = group * head_dim
    half = width // 2
    sent = pieces[0][0].shape[1]
    q_scale = head_dim**-0.5 * LOG2E
    side = pieces[0][4]
    steps = sum(piece[0].shape[0] for piece in pieces) // 2
    n_in = len(pieces)

    def kernel(at, norm_ref, cos_ref, sin_ref, gain_ref, *refs):
        out_ref, hat_ref, fac_ref, whole_ref, acc_ref, buf, sems = refs[n_in + len(before) :]

        @pl.when(pl.program_id(0) == 0)
        def _():
            for k, z, x, block in piece_targets(pieces, at):
                local = block // 2
                pltpu.make_async_copy(refs[k].at[z], buf.at[x, local], sems.at[x, local]).start()

        local = pl.program_id(0)
        step = 2 * local + (at[0] + side) % 2
        for x in range(2):
            pltpu.make_async_copy(refs[0].at[0], buf.at[x, local], sems.at[x, local]).wait()
        low, high = buf[0, local], buf[1, local]
        whole_ref[:sent] = jnp.concatenate([low[:, :half], high[:, :half]], axis=1)
        whole_ref[sent:] = jnp.concatenate([low[: rows_all - sent, half:], high[: rows_all - sent, half:]], axis=1)
        acc_ref[...] = dot_f32(whole_ref[...], norm_ref[...], ((1,), (1,)))
        for i in range(group):
            head = step * group + i
            rows = pl.ds(i * head_dim, head_dim)

            @pl.when(head < 2 * heads)
            def _():
                values = acc_ref[rows, :]
                fac = lax.rsqrt(jnp.mean(values * values, axis=0, keepdims=True) + EPS)
                hat = values * fac
                gained = hat * jnp.where(head < heads, gain_ref[:, 0:1] * q_scale, gain_ref[:, 1:2])
                turned = jnp.concatenate([gained[head_dim // 2 :], gained[: head_dim // 2]], axis=0)
                out_ref[i] = (gained * cos_ref[...] + turned * sin_ref[...]).astype(BF16)
                hat_ref[i] = hat[:, :band].astype(BF16)
                fac_ref[i] = fac[:, :band]

            @pl.when(head >= 2 * heads)
            def _():
                out_ref[i] = acc_ref[rows, :].astype(BF16)
                hat_ref[i] = jnp.zeros((head_dim, band), BF16)
                fac_ref[i] = jnp.zeros((1, band), F32)

    whole = lambda i, at: (0, 0)
    return kernel_call(
        kernel,
        grid_spec=pltpu.PrefetchScalarGridSpec(
            num_scalar_prefetch=1,
            grid=(steps,),
            in_specs=[
                pl.BlockSpec((seq_len, width), whole),
                pl.BlockSpec((head_dim, seq_len), whole),
                pl.BlockSpec((head_dim, seq_len), whole),
                pl.BlockSpec((head_dim, 2), whole),
            ]
            + [pl.BlockSpec(memory_space=pl.ANY)] * (n_in + len(before)),
            out_specs=[
                pl.BlockSpec((group, head_dim, seq_len), lambda i, at: (2 * i + (at[0] + side) % 2, 0, 0)),
                pl.BlockSpec((group, head_dim, band), lambda i, at: (2 * i + (at[0] + side) % 2, 0, 0)),
                pl.BlockSpec((group, 1, band), lambda i, at: (2 * i + (at[0] + side) % 2, 0, 0)),
                pl.BlockSpec((rows_all, width), lambda i, at: (2 * i + (at[0] + side) % 2, 0)),
            ],
            scratch_shapes=[
                pltpu.VMEM((rows_all, seq_len), F32),
                pltpu.VMEM((2, steps, sent, width), BF16),
                pltpu.SemaphoreType.DMA((2, steps)),
            ],
        ),
        out_shape=[
            jax.ShapeDtypeStruct((3 * heads, head_dim, seq_len), BF16),
            pltpu.HBM((3 * heads, head_dim, band), BF16),
            pltpu.HBM((3 * heads, 1, band), F32),
            pltpu.HBM((3 * width, width), BF16),
        ],
        input_output_aliases={5 + n_in + k: k for k in range(len(before))},
        compiler_params=pltpu.CompilerParams(vmem_limit_bytes=32 << 20),
        name="qkv_heads",
    )(place(), normed, cos_t, sin_t, gains_t, *[piece[0] for piece in pieces], *before)


def attention_forward(qkv, heads, band):
    _, head_dim, seq_len = qkv.shape

    def kernel(q_ref, k_ref, v_ref, out_ref, mass_ref):
        scores = dot_f32(k_ref[0], q_ref[0], ((0,), (0,)))
        weights = jnp.exp2(scores)
        mass = jnp.sum(weights, axis=0, keepdims=True)
        mixed = dot_f32(v_ref[0], weights.astype(BF16), ((1,), (0,)))
        out_ref[0] = (mixed / mass).astype(BF16)
        mass_ref[0] = jnp.log2(mass)

    return kernel_call(
        kernel,
        grid=(heads,),
        in_specs=[
            pl.BlockSpec((1, head_dim, band), lambda h: (h, 0, 0)),
            pl.BlockSpec((1, head_dim, seq_len), lambda h: (heads + h, 0, 0)),
            pl.BlockSpec((1, head_dim, seq_len), lambda h: (2 * heads + h, 0, 0)),
        ],
        out_specs=[
            pl.BlockSpec((1, head_dim, band), lambda h: (h, 0, 0)),
            pl.BlockSpec((1, 1, band), lambda h: (h, 0, 0)),
        ],
        out_shape=[
            jax.ShapeDtypeStruct((heads, head_dim, band), BF16),
            jax.ShapeDtypeStruct((heads, 1, band), F32),
        ],
        compiler_params=pltpu.CompilerParams(vmem_limit_bytes=14 << 20),
        name="attention_forward",
    )(qkv, qkv, qkv)


def attention_back_own(qkv, out_grad, log_mass, delta, heads, band):
    _, head_dim, seq_len = qkv.shape

    def kernel(q_ref, k_ref, v_ref, grad_ref, mass_ref, delta_ref, dq_ref, dk_ref, dv_ref):
        grad = grad_ref[0]
        scores = dot_f32(k_ref[0], q_ref[0], ((0,), (0,)))
        probs = jnp.exp2(scores - mass_ref[0])
        prob_grad = dot_f32(v_ref[0], grad, ((0,), (0,)))
        score_grad = (probs * (prob_grad - delta_ref[0])).astype(BF16)
        dq_ref[0] = dot_f32(k_ref[0], score_grad, ((1,), (0,)))
        dk_ref[0] = dot_f32(q_ref[0], score_grad[:band], ((1,), (1,)))
        dv_ref[0] = dot_f32(grad, probs[:band].astype(BF16), ((1,), (1,)))

    one = pl.BlockSpec((1, head_dim, band), lambda h: (h, 0, 0))
    row = pl.BlockSpec((1, 1, band), lambda h: (h, 0, 0))
    return kernel_call(
        kernel,
        grid=(heads,),
        in_specs=[
            one,
            pl.BlockSpec((1, head_dim, seq_len), lambda h: (heads + h, 0, 0)),
            pl.BlockSpec((1, head_dim, seq_len), lambda h: (2 * heads + h, 0, 0)),
            one,
            row,
            row,
        ],
        out_specs=[one, one, one],
        out_shape=[pltpu.HBM((heads, head_dim, band), F32)] * 3,
        compiler_params=pltpu.CompilerParams(vmem_limit_bytes=16 << 20),
        name="attention_back_own",
    )(qkv, qkv, qkv, out_grad, log_mass, delta)


def attention_back_other(
    qkv, hat, fac, cos_t, sin_t, gains_t, dq, dk, dv, grads, mass, delta, heads, band
):
    _, head_dim, seq_len = qkv.shape
    inv_root = head_dim**-0.5
    early = grads[0].shape[0]

    def kernel(
        q_ref, k_ref, v_ref, hq_ref, hk_ref, fq_ref, fk_ref, cos_ref, sin_ref, gain_ref,
        dq_ref, dk_ref, dv_ref, low_ref, high_ref, mass_ref, delta_ref, out_ref, gq_ref, gk_ref,
    ):
        grad = jnp.where(pl.program_id(0) < early, low_ref[0], high_ref[0])
        scores = dot_f32(k_ref[0], q_ref[0], ((0,), (0,)))
        probs = jnp.exp2(scores - mass_ref[0])
        prob_grad = dot_f32(v_ref[0], grad, ((0,), (0,)))
        score_grad = (probs * (prob_grad - delta_ref[0])).astype(BF16)
        key_grad = (dk_ref[0] + dot_f32(q_ref[0], score_grad, ((1,), (1,)))) * LN2
        value_grad = dv_ref[0] + dot_f32(grad, probs.astype(BF16), ((1,), (1,)))
        query_grad = dq_ref[0] * inv_root

        def back(turned_grad, hat, fac, gain):
            spun = turned_grad * sin_ref[...]
            spun = jnp.concatenate([spun[head_dim // 2 :], spun[: head_dim // 2]], axis=0)
            gained_grad = turned_grad * cos_ref[...] + spun
            gain_grad = jnp.sum(gained_grad * hat, axis=1, keepdims=True)
            hat_grad = gained_grad * gain
            along = jnp.mean(hat_grad * hat, axis=0, keepdims=True)
            return (fac * (hat_grad - hat * along)).astype(BF16), gain_grad

        out_ref[0, 0], gq_ref[0] = back(query_grad, hq_ref[0].astype(F32), fq_ref[0], gain_ref[:, 0:1])
        out_ref[1, 0], gk_ref[0] = back(key_grad, hk_ref[0].astype(F32), fk_ref[0], gain_ref[:, 1:2])
        out_ref[2, 0] = value_grad.astype(BF16)

    one = pl.BlockSpec((1, head_dim, band), lambda h: (h, 0, 0))
    row = pl.BlockSpec((1, 1, band), lambda h: (h, 0, 0))
    key_one = pl.BlockSpec((1, head_dim, band), lambda h: (heads + h, 0, 0))
    key_row = pl.BlockSpec((1, 1, band), lambda h: (heads + h, 0, 0))
    table = pl.BlockSpec((head_dim, band), lambda h: (0, 0))
    column = pl.BlockSpec((1, head_dim, 1), lambda h: (h, 0, 0))
    return kernel_call(
        kernel,
        grid=(heads,),
        in_specs=[
            pl.BlockSpec((1, head_dim, band), lambda h: (h, 0, 1)),
            key_one,
            pl.BlockSpec((1, head_dim, band), lambda h: (2 * heads + h, 0, 0)),
            one, key_one, row, key_row, table, table,
            pl.BlockSpec((head_dim, 2), lambda h: (0, 0)),
            one, one, one,
            pl.BlockSpec((1, head_dim, band), lambda h: (jnp.minimum(h, early - 1), 0, 0)),
            pl.BlockSpec((1, head_dim, band), lambda h: (jnp.maximum(h - early, 0), 0, 0)),
            row, row,
        ],
        out_specs=[pl.BlockSpec((3, 1, head_dim, band), lambda h: (0, h, 0, 0)), column, column],
        out_shape=[
            jax.ShapeDtypeStruct((3, heads, head_dim, band), BF16),
            jax.ShapeDtypeStruct((heads, head_dim, 1), F32),
            jax.ShapeDtypeStruct((heads, head_dim, 1), F32),
        ],
        compiler_params=pltpu.CompilerParams(vmem_limit_bytes=14 << 20),
        name="attention_back_other",
    )(*[pltpu.with_memory_space_constraint(qkv, pltpu.HBM)] * 3, hat, hat, fac, fac, cos_t, sin_t, gains_t,
      *[pltpu.with_memory_space_constraint(v, pltpu.HBM) for v in (dq, dk, dv)], *grads, mass, delta)


def mlp(mid, mlp_grad, pieces, down_own, down_other):
    band, width = mlp_grad.shape
    rows = pieces[0][0].shape[1]
    half = width // 2
    blocks = sum(piece[0].shape[0] for piece in pieces) // 2
    steps = 4
    per = blocks // steps
    units = per * rows
    chunk = band // 2
    n_z, _, _, down_rows, down_width = down_own.shape

    def kernel(at, mid_ref, mg_ref, *refs):
        downs = refs[len(pieces) : len(pieces) + 2]
        hid_ref, gg_ref, ug_ref, out_ref, grad_ref, buf, down_buf, sems, down_sems = refs[len(pieces) + 2 :]
        step = pl.program_id(0)

        @pl.when(step == 0)
        def _():
            for x in range(2):
                for z in range(n_z):
                    for y in range(2):
                        for c in range(2):
                            block = (z * 2 + y) * 2 + (at[0] + c) % 2
                            target = down_buf.at[x, pl.ds(pl.multiple_of(block * down_rows, 8), down_rows)]
                            pltpu.make_async_copy(downs[c].at[z, y, x], target, down_sems.at[x, block]).start()
            for k, z, x, block in piece_targets(pieces, at):
                pltpu.make_async_copy(refs[k].at[z], buf.at[x, block], sems.at[x, block]).start()
            out_ref[...] = jnp.zeros_like(out_ref)
            grad_ref[...] = jnp.zeros_like(grad_ref)

        for b in range(per):
            for x in range(2):
                block = step * per + b
                pltpu.make_async_copy(refs[0].at[0], buf.at[x, block], sems.at[x, block]).wait()
        @pl.when(step % 2 == 0)
        def _():
            for block in range(4 * n_z):
                target = down_buf.at[step // 2, pl.ds(block * down_rows, down_rows)]
                pltpu.make_async_copy(downs[0].at[0, 0, 0], target, down_sems.at[step // 2, block]).wait()

        low = buf[0, pl.ds(step * per, per)].reshape(units, width)
        high = buf[1, pl.ds(step * per, per)].reshape(units, width)
        gate = jnp.concatenate([low[:, :half], high[:, :half]], axis=1)
        up = jnp.concatenate([low[:, half:], high[:, half:]], axis=1)
        down = down_buf[step // 2, :, pl.ds(pl.multiple_of(step % 2 * units, 128), units)]
        nt, nn = ((1,), (1,)), ((1,), (0,))
        for part in range(2):
            at_rows = pl.ds(part * chunk, chunk)
            mid = mid_ref[at_rows, :]
            gate_pre = dot_f32(mid, gate, nt)
            up_pre = dot_f32(mid, up, nt)
            hidden_grad = dot_f32(mg_ref[at_rows, :], down, nn)
            sig = 1.0 / (1.0 + jnp.exp(-gate_pre))
            act = gate_pre * sig
            hidden = (act * up_pre).astype(BF16)
            gate_grad = (hidden_grad * up_pre * (sig * (1.0 + gate_pre * (1.0 - sig)))).astype(BF16)
            up_grad = (hidden_grad * act).astype(BF16)
            hid_ref[at_rows, :] = hidden
            gg_ref[:, at_rows] = gate_grad.T
            ug_ref[:, at_rows] = up_grad.T
            out_ref[at_rows, :] += dot_f32(hidden, down, nt)
            grad_ref[at_rows, :] += dot_f32(gate_grad, gate, nn) + dot_f32(up_grad, up, nn)

    whole = lambda i, at: (0, 0)
    once = pl.Buffered(1)
    return kernel_call(
        kernel,
        grid_spec=pltpu.PrefetchScalarGridSpec(
            num_scalar_prefetch=1,
            grid=(steps,),
            in_specs=[
                pl.BlockSpec((band, width), whole, pipeline_mode=once),
                pl.BlockSpec((band, width), whole, pipeline_mode=once),
            ]
            + [pl.BlockSpec(memory_space=pl.ANY)] * (len(pieces) + 2),
            out_specs=[
                pl.BlockSpec((band, units), lambda i, at: (0, i)),
                pl.BlockSpec((units, band), lambda i, at: (i, 0)),
                pl.BlockSpec((units, band), lambda i, at: (i, 0)),
                pl.BlockSpec((band, width), whole, pipeline_mode=once),
                pl.BlockSpec((band, width), whole, pipeline_mode=once),
            ],
            scratch_shapes=[
                pltpu.VMEM((2, blocks, rows, width), BF16),
                pltpu.VMEM((2, width, down_width), BF16),
                pltpu.SemaphoreType.DMA((2, blocks)),
                pltpu.SemaphoreType.DMA((2, 4 * n_z)),
            ],
        ),
        out_shape=[
            jax.ShapeDtypeStruct((band, blocks * rows), BF16),
            jax.ShapeDtypeStruct((blocks * rows, band), BF16),
            jax.ShapeDtypeStruct((blocks * rows, band), BF16),
            jax.ShapeDtypeStruct((band, width), F32),
            jax.ShapeDtypeStruct((band, width), F32),
        ],
        compiler_params=pltpu.CompilerParams(vmem_limit_bytes=56 << 20),
        name="mlp",
    )(place(), mid, mlp_grad, *[piece[0] for piece in pieces], down_own, down_other)


def after_attention(attended_t, proj_t, residual_low, modulation):
    width, band = attended_t.shape
    half = width // 2
    block = 128

    def kernel(att_ref, proj_ref, low_ref, mod_ref, branch_ref, middle_ref, normed_ref, mid_ref, att_out_ref):
        branch = dot_f32(att_ref[...], proj_ref[...], ((0,), (1,)))
        middle = low_ref[...].astype(F32) + mod_ref[2:3, :] * branch
        normed = modulate(middle, mod_ref[3:4, :], mod_ref[4:5, :]).astype(BF16)
        attended = att_ref[...].T
        branch_ref[...] = branch.astype(BF16)
        middle_ref[...] = middle
        normed_ref[...] = normed
        for x in range(2):
            mid_ref[x] = normed[:, x * half : (x + 1) * half]
            att_out_ref[x] = attended[:, x * half : (x + 1) * half]

    rows = pl.BlockSpec((block, width), lambda i: (i, 0))
    halves = pl.BlockSpec((2, block, half), lambda i: (0, i, 0))
    return kernel_call(
        kernel,
        grid=(band // block,),
        in_specs=[
            pl.BlockSpec((width, block), lambda i: (0, i)),
            pl.BlockSpec((width, width), lambda i: (0, 0)),
            rows,
            pl.BlockSpec((6, width), lambda i: (0, 0)),
        ],
        out_specs=[rows, rows, rows, halves, halves],
        out_shape=[
            jax.ShapeDtypeStruct((band, width), BF16),
            jax.ShapeDtypeStruct((band, width), F32),
            jax.ShapeDtypeStruct((band, width), BF16),
            jax.ShapeDtypeStruct((2, band, half), BF16),
            jax.ShapeDtypeStruct((2, band, half), BF16),
        ],
        compiler_params=pltpu.CompilerParams(vmem_limit_bytes=20 << 20),
        name="after_attention",
    )(attended_t, proj_t, residual_low, modulation)


def middle_back(normed_mid_grad, middle, out_grad, branch, mlp_out, proj_t, attended_t, modulation):
    band, width = middle.shape
    half = width // 2
    head_dim = width // HEADS
    block = 128

    def kernel(
        normed_grad_ref, mid_ref, out_ref, branch_ref, mlp_ref, proj_ref, att_ref, mod_ref,
        grad_ref, bg_ref, att_grad_ref, delta_ref, result_ref, sums_ref,
    ):
        @pl.when(pl.program_id(0) == 0)
        def _():
            sums_ref[...] = jnp.zeros_like(sums_ref)

        normed_grad = normed_grad_ref[...]
        middle, grad, mlp_out = mid_ref[...], out_ref[...].astype(F32), mlp_ref[...]
        fac = norm_factor(middle)
        hat = middle * fac
        hat_grad = normed_grad * (1.0 + mod_ref[4:5, :])
        along = jnp.mean(hat_grad * hat, axis=-1, keepdims=True)
        mid_grad = grad + fac * (hat_grad - hat * along)
        branch_grad = (mod_ref[2:3, :] * mid_grad).astype(BF16)
        attended_grad = dot_f32(branch_grad, proj_ref[...], ((1,), (0,))).astype(BF16).T
        grad_ref[...] = mid_grad
        bg_ref[...] = branch_grad.T
        att_grad_ref[...] = attended_grad
        both = attended_grad.astype(F32) * att_ref[...].astype(F32)
        delta_ref[...] = jnp.sum(both.reshape(HEADS, head_dim, block), axis=1, keepdims=True)
        result_ref[...] = (middle + mod_ref[5:6, :] * mlp_out).astype(BF16)
        sums_ref[0:1, :] += jnp.sum(normed_grad, axis=0, keepdims=True)
        sums_ref[1:2, :] += jnp.sum(normed_grad * hat, axis=0, keepdims=True)
        sums_ref[2:3, :] += jnp.sum(mid_grad * branch_ref[...].astype(F32), axis=0, keepdims=True)
        sums_ref[3:4, :] += jnp.sum(grad * mlp_out, axis=0, keepdims=True)

    rows = pl.BlockSpec((block, width), lambda i: (i, 0))
    columns = pl.BlockSpec((width, block), lambda i: (0, i))
    return kernel_call(
        kernel,
        grid=(band // block,),
        in_specs=[
            rows, rows, rows, rows, rows,
            pl.BlockSpec((width, width), lambda i: (0, 0)),
            columns,
            pl.BlockSpec((6, width), lambda i: (0, 0)),
        ],
        out_specs=[
            rows, columns, columns,
            pl.BlockSpec((HEADS, 1, block), lambda i: (0, 0, i)),
            rows,
            pl.BlockSpec((8, width), lambda i: (0, 0)),
        ],
        out_shape=[
            jax.ShapeDtypeStruct((band, width), F32),
            jax.ShapeDtypeStruct((width, band), BF16),
            jax.ShapeDtypeStruct((width, band), BF16),
            jax.ShapeDtypeStruct((HEADS, 1, band), F32),
            jax.ShapeDtypeStruct((band, width), BF16),
            jax.ShapeDtypeStruct((8, width), F32),
        ],
        compiler_params=pltpu.CompilerParams(vmem_limit_bytes=20 << 20),
        name="middle_back",
    )(normed_mid_grad, middle, out_grad, branch, mlp_out, proj_t, attended_t, modulation)


def input_back(projected_t, qkv_t, latents, mid_grad, modulation):
    inner, band = projected_t.shape
    width = qkv_t.shape[1]
    block = 128

    def kernel(left_ref, weight_ref, low_ref, grad_ref, mod_ref, out_ref, sums_ref):
        @pl.when(pl.program_id(0) == 0)
        def _():
            sums_ref[...] = jnp.zeros_like(sums_ref)

        normed_grad = dot_f32(left_ref[...], weight_ref[...], ((0,), (0,)))
        residual = low_ref[...].astype(F32)
        fac = norm_factor(residual)
        hat = residual * fac
        hat_grad = normed_grad * (1.0 + mod_ref[1:2, :])
        along = jnp.mean(hat_grad * hat, axis=-1, keepdims=True)
        out_ref[...] = grad_ref[...] + fac * (hat_grad - hat * along)
        sums_ref[0:1, :] += jnp.sum(normed_grad, axis=0, keepdims=True)
        sums_ref[1:2, :] += jnp.sum(normed_grad * hat, axis=0, keepdims=True)

    rows = pl.BlockSpec((block, width), lambda i: (i, 0))
    return kernel_call(
        kernel,
        grid=(band // block,),
        in_specs=[
            pl.BlockSpec((inner, block), lambda i: (0, i)),
            pl.BlockSpec((inner, width), lambda i: (0, 0), pipeline_mode=pl.Buffered(1)),
            rows,
            rows,
            pl.BlockSpec((6, width), lambda i: (0, 0)),
        ],
        out_specs=[rows, pl.BlockSpec((8, width), lambda i: (0, 0))],
        out_shape=[jax.ShapeDtypeStruct((band, width), F32), jax.ShapeDtypeStruct((8, width), F32)],
        compiler_params=pltpu.CompilerParams(vmem_limit_bytes=24 << 20),
        name="input_back",
    )(projected_t, qkv_t, latents, mid_grad, modulation)


def place():
    return jnp.stack([lax.axis_index(axis) for axis in ("c", "x", "y")]).astype(jnp.int32)


def terms(lefts, right, rows, side, received=None, z_first=0, n_z=4, y=(0, 1), order=(0, 1), stacked=True, split=0):
    patches = right.shape[0] if right.ndim == 2 else right.shape[1]
    wide = right.ndim == 2
    each = right.shape[-1] // 2 if wide else right.shape[-1]
    width = each * len(lefts)
    count = split or len(y) * n_z
    n = len(lefts)

    def left_map(i, at):
        if split:
            return (i, 0)
        z = z_first + i % n_z
        return ((z * 2 + (y[0] + i // n_z + at[2]) % 2) * 2 + (at[0] + side) % 2, 0)

    def right_spec(h):
        if wide:
            return pl.BlockSpec((patches, each), lambda i, at: (0, (at[1] + h) % 2))
        return pl.BlockSpec((1, patches, each), lambda i, at: ((at[1] + h) % 2, 0, 0))

    def kernel(at, *refs):
        rights, outs = refs[n : n + 2], refs[n + 2 :]
        if received is not None:
            got, outs = refs[n + 2 : n + 4], refs[n + 4 :]
        for k in range(2):
            half = rights[k][...] if wide else rights[k][0]
            values = [dot_f32(refs[m][...], half, ((1,), (0,))) for m in range(n)]
            value = values[0] if n == 1 else jnp.concatenate(values, axis=1)
            if received is not None:
                value = value + got[k][0, 0].astype(F32)
            if not stacked:
                outs[k][0] = value.astype(BF16)
            elif split:
                outs[0][0, k] = value.astype(BF16)
            else:
                outs[0][k, 0] = value.astype(BF16)

    received_specs = []
    if received is not None:
        skip = 0 if split else y[0] * n_z
        received_specs = [
            pl.BlockSpec((1, 1, rows, width), lambda i, at, k=k: (i, k, 0, 0) if split else (k, i + skip, 0, 0))
            for k in range(2)
        ]
    if stacked and split:
        out_shape = [jax.ShapeDtypeStruct((count, 2, rows, width), BF16)]
        out_specs = [pl.BlockSpec((1, 2, rows, width), lambda i, at: (i, 0, 0, 0))]
    elif stacked:
        out_shape = [jax.ShapeDtypeStruct((2, count, rows, width), BF16)]
        out_specs = [pl.BlockSpec((2, 1, rows, width), lambda i, at: (0, i, 0, 0))]
    else:
        out_shape = [jax.ShapeDtypeStruct((count, rows, width), BF16)] * 2
        out_specs = [pl.BlockSpec((1, rows, width), lambda i, at: (i, 0, 0))] * 2
    outs = kernel_call(
        kernel,
        grid_spec=pltpu.PrefetchScalarGridSpec(
            num_scalar_prefetch=1,
            grid=(count,),
            in_specs=[pl.BlockSpec((rows, patches), left_map)] * n
            + [right_spec(h) for h in order]
            + received_specs,
            out_specs=out_specs,
        ),
        out_shape=out_shape,
        compiler_params=pltpu.CompilerParams(vmem_limit_bytes=12 << 20),
        name="terms",
    )(place(), *lefts, right, right, *([received] * 2 if received is not None else []))
    return outs[0] if stacked else outs


def last_terms(left, right, rows, cut, received):
    patches, width = left.shape[-1], right.shape[-1]
    n_z = 4
    late = rows - cut

    def row_of(i):
        return 1 - i // n_z

    def kernel(at, left_ref, own_ref, other_ref, r0_ref, r1_ref, keep_ref, send_ref, up_send_ref, up_keep_ref):
        values = [
            (dot_f32(left_ref[...], ref[0], ((1,), (0,))) + got[0, 0].astype(F32)).astype(BF16)
            for ref, got in ((own_ref, r0_ref), (other_ref, r1_ref))
        ]
        keep_ref[0] = values[0][:cut]
        send_ref[0] = values[1][:cut]

        @pl.when(pl.program_id(0) < n_z)
        def _():
            for k in range(2):
                up_send_ref[1 - k, 0] = values[k][cut:]

        @pl.when(pl.program_id(0) >= n_z)
        def _():
            for k in range(2):
                up_keep_ref[1 - k, 0] = values[k][cut:]

    def got(h):
        return pl.BlockSpec((1, 1, rows, width), lambda i, at: (h, row_of(i) * n_z + i % n_z, 0, 0))

    early_spec = pl.BlockSpec((1, cut, width), lambda i, at: (row_of(i) * n_z + i % n_z, 0, 0))
    return kernel_call(
        kernel,
        grid_spec=pltpu.PrefetchScalarGridSpec(
            num_scalar_prefetch=1,
            grid=(2 * n_z,),
            in_specs=[
                pl.BlockSpec(
                    (rows, patches), lambda i, at: ((i % n_z * 2 + (row_of(i) + at[2]) % 2) * 2 + at[0], 0)
                ),
                pl.BlockSpec((1, patches, width), lambda i, at: (at[1], 0, 0)),
                pl.BlockSpec((1, patches, width), lambda i, at: ((at[1] + 1) % 2, 0, 0)),
                got(0),
                got(1),
            ],
            out_specs=[
                early_spec,
                early_spec,
                pl.BlockSpec((2, 1, late, width), lambda i, at: (0, jnp.minimum(i, n_z - 1), 0, 0)),
                pl.BlockSpec((2, 1, late, width), lambda i, at: (0, jnp.maximum(i - n_z, 0), 0, 0)),
            ],
        ),
        out_shape=[jax.ShapeDtypeStruct((2 * n_z, cut, width), BF16)] * 2
        + [jax.ShapeDtypeStruct((2, n_z, late, width), BF16)] * 2,
        compiler_params=pltpu.CompilerParams(vmem_limit_bytes=12 << 20),
        name="last_terms",
    )(place(), left, right, right, received, received)


def split_rows(left_t, z_first):
    n_z, patches = lax.axis_size("z"), left_t.shape[-1]
    blocks = left_t.reshape(n_z, 2, 2, -1, patches)
    core, row = lax.axis_index("c"), lax.axis_index("y")

    def part(which):
        picked = lax.dynamic_index_in_dim(blocks, which, 2, keepdims=False)
        own = lax.dynamic_index_in_dim(picked, row, 1, keepdims=False)
        other = lax.dynamic_index_in_dim(picked, 1 - row, 1, keepdims=False)
        return jnp.stack([own, other], axis=1 if z_first else 0).reshape(-1, patches)

    return part(1 - core), part(core)


def summed_over(values, axes, size):
    low = values.astype(BF16)
    parts = [low] + [lax.ppermute(low, axes, [(i, i ^ hop) for i in range(size)]) for hop in range(1, size)]
    parts = [part.astype(F32) for part in parts]
    while len(parts) > 1:
        parts = [left + right for left, right in zip(parts[::2], parts[1::2])]
    return parts[0]


def spread_rows(hots, values):
    items, width = values.shape
    count = hots[0].shape[1]
    block = 384

    def kernel(values_ref, *refs):
        rest, parts = values_ref[...], []
        for _ in range(3):
            high = rest.astype(BF16)
            parts.append(high)
            rest = rest - high.astype(F32)
        for hot_ref, out_ref in zip(refs[: len(hots)], refs[len(hots) :]):
            hot = hot_ref[...]
            out_ref[...] = sum(dot_f32(hot, part, ((0,), (0,))) for part in parts)

    return kernel_call(
        kernel,
        grid=(width // block,),
        in_specs=[pl.BlockSpec((items, block), lambda i: (0, i))]
        + [pl.BlockSpec((items, count), lambda i: (0, 0))] * len(hots),
        out_specs=[pl.BlockSpec((count, block), lambda i: (0, i))] * len(hots),
        out_shape=[jax.ShapeDtypeStruct((count, width), F32)] * len(hots),
        compiler_params=pltpu.CompilerParams(vmem_limit_bytes=16 << 20),
        name="spread_rows",
    )(values, *hots)


def fast_shards(
    latents, out_grad, time_table, class_table, buckets, labels, row_start,
    ada_weight, qkv_weight, proj_weight, gate_weight, up_weight, down_weight, query_gain, key_gain,
):
    band, width = latents.shape[1:]
    head_dim = width // HEADS
    lat, out_g = latents[0], out_grad[0]
    half = width // 2
    n_z = lax.axis_size("z")

    qkv_s, proj_s = qkv_weight[0].T, proj_weight[0].T
    gate_s, up_s, down_s = gate_weight[0].T, up_weight[0].T, by_rows(down_weight[0].T)
    qkv_rows, proj_rows, gate_rows = qkv_s.shape[0], proj_s.shape[0], gate_s.shape[0]
    cut = (qkv_rows + proj_rows) // 2
    first = by_rows(jnp.concatenate([qkv_s[:cut], jnp.concatenate([qkv_s[cut:], proj_s])], axis=1))
    second = by_rows(jnp.concatenate([gate_s, up_s], axis=1))

    first_z = gather_z(first)
    second_z = gather_z(second)
    start_other = swap(row_start.astype(F32), "x")
    (down_r,) = together(swap(down_s, "x"))
    down_x = in_order(down_s, down_r, "x")
    down_x, lat_x = together(down_x, lat)
    lat_other = swap(lat_x, "x")
    down_r = swap(down_x, "y")

    bucket_hot = (buckets[:, None] == jnp.arange(BUCKETS, dtype=jnp.int32)[None, :]).astype(BF16)
    class_hot = (labels[:, None] == jnp.arange(CLASSES, dtype=jnp.int32)[None, :]).astype(BF16)
    cond = jnp.dot(bucket_hot, time_table, preferred_element_type=F32) + jnp.dot(
        class_hot, class_table, preferred_element_type=F32
    )
    cond_act = jax.nn.silu(cond).astype(BF16)
    mod_cols = jnp.dot(cond_act, ada_weight[0], preferred_element_type=F32)

    offsets = jnp.arange(band, dtype=jnp.int32)
    rows_in = (offsets // SIDE).astype(F32)
    row_pos = jnp.concatenate([row_start.astype(F32)[0, 0] + rows_in, start_other[0, 0] + rows_in])
    col_pos = jnp.tile((offsets % SIDE).astype(F32), 2)
    quarter = head_dim // 4
    frequency = THETA ** (-jnp.arange(quarter, dtype=F32) / quarter)
    angles = jnp.concatenate([frequency[:, None] * row_pos[None], frequency[:, None] * col_pos[None]])
    cos_h, sin_h = jnp.cos(angles), jnp.sin(angles)
    cos_t = jnp.concatenate([cos_h, cos_h])
    sin_t = jnp.concatenate([-sin_h, sin_h])
    gains_t = jnp.concatenate([query_gain, key_gain]).T
    first_z, lat_other, down_r, mod_cols, cos_t, sin_t = together(first_z, lat_other, down_r, mod_cols, cos_t, sin_t)

    a, b = by_rows(first_z[:2]), by_rows(first_z[2:])
    a_y, b_x, a_c, b_c = swap(a, "y"), swap(b, "x"), swap(a, "c"), swap(b, "c")
    down_z = gather_z(in_order(down_x, down_r, "y").reshape(-1, down_x.shape[-1]))
    modulation = lax.all_to_all(mod_cols, DP_AXES, split_axis=0, concat_axis=1, tiled=True)
    a_y, b_x, a_c, b_c, modulation = together(a_y, b_x, a_c, b_c, modulation)

    a_x, b_y, a_yc, b_xc = swap(a, "x"), swap(b, "y"), swap(a_y, "c"), swap(b_x, "c")
    mods = modulation.reshape(6, width)
    shift_attn, scale_attn, gate_attn, shift_mlp, scale_mlp, gate_mlp = jnp.split(modulation, 6, axis=-1)
    lat_full = jnp.concatenate([lat, lat_other]).astype(F32)
    normed_full = modulate(lat_full, shift_attn, scale_attn).astype(BF16)
    a_x, b_y, a_yc, b_xc, normed_full = together(a_x, b_y, a_yc, b_xc, normed_full)

    a_yx, b_xy, a_xc, b_yc = swap(a_y, "x"), swap(b_x, "y"), swap(a_x, "c"), swap(b_y, "c")
    mlp_grad = (gate_mlp * out_g.astype(F32)).astype(BF16)
    down_send, down_keep = split_rows(mlp_grad.T, True)
    normed = normed_full[:band]
    normed_2 = jnp.stack([normed[:, :half], normed[:, half:]])
    second_z, a_yx, b_xy, a_xc, b_yc, mlp_grad, down_send, down_keep, normed_2 = together(
        second_z, a_yx, b_xy, a_xc, b_yc, mlp_grad, down_send, down_keep, normed_2
    )

    a_yxc, b_xyc = swap(a_yx, "c"), swap(b_xy, "c")
    e, f = by_rows(second_z[:2]), by_rows(second_z[2:])
    e_y, f_x = swap(e, "y"), swap(f, "x")
    pieces_own = [
        (a, 0, 0, 0, 0), (a_y, 0, 0, 1, 0), (a_x, 0, 1, 0, 0), (a_yx, 0, 1, 1, 0),
        (b, 2, 0, 0, 0), (b_x, 2, 1, 0, 0), (b_y, 2, 0, 1, 0), (b_xy, 2, 1, 1, 0),
    ]
    tables = (cos_t, sin_t, gains_t, head_dim, band)
    parts = qkv_heads(normed_full, pieces_own, *tables)
    *parts, e_y, f_x, a_yxc, b_xyc = together(*parts, e_y, f_x, a_yxc, b_xyc)

    e_x, f_y, e_c, f_c, e_yc = swap(e, "x"), swap(f, "y"), swap(e, "c"), swap(f, "c"), swap(e_y, "c")
    pieces_other = [
        (a_c, 0, 0, 0, 1), (a_yc, 0, 0, 1, 1), (a_xc, 0, 1, 0, 1), (a_yxc, 0, 1, 1, 1),
        (b_c, 2, 0, 0, 1), (b_xc, 2, 1, 0, 1), (b_yc, 2, 0, 1, 1), (b_xyc, 2, 1, 1, 1),
    ]
    qkv, hat, fac, qkv_t = qkv_heads(normed_full, pieces_other, *tables, before=parts)
    e_x, f_y, e_c, f_c, e_yc, qkv = together(e_x, f_y, e_c, f_c, e_yc, qkv)

    e_yx, f_xy = swap(e_y, "x"), swap(f_x, "y")
    f_xc, e_xc, f_yc = swap(f_x, "c"), swap(e_x, "c"), swap(f_y, "c")
    attended_t, log_mass = attention_forward(qkv, HEADS, band)
    proj_t = join_rows(pieces_own + pieces_other, qkv_rows - cut, proj_rows).reshape(width, width)
    e_yx, f_xy, f_xc, e_xc, f_yc, attended_t, proj_t, down_z = together(
        e_yx, f_xy, f_xc, e_xc, f_yc, attended_t, proj_t, down_z
    )

    down_own = down_z.reshape(n_z, 2, 2, -1, down_z.shape[-1])
    down_other, e_yxc, f_xyc = swap(down_own, "c"), swap(e_yx, "c"), swap(f_xy, "c")
    attended_t = attended_t.reshape(width, band)
    branch, middle, normed_mid, mid_2, att_2 = after_attention(attended_t, proj_t, lat, mods)
    pieces = [
        (e, 0, 0, 0, 0), (e_y, 0, 0, 1, 0), (e_x, 0, 1, 0, 0), (e_yx, 0, 1, 1, 0),
        (e_c, 0, 0, 0, 1), (e_yc, 0, 0, 1, 1), (e_xc, 0, 1, 0, 1), (e_yxc, 0, 1, 1, 1),
        (f, 2, 0, 0, 0), (f_x, 2, 1, 0, 0), (f_y, 2, 0, 1, 0), (f_xy, 2, 1, 1, 0),
        (f_c, 2, 0, 0, 1), (f_xc, 2, 1, 0, 1), (f_yc, 2, 0, 1, 1), (f_xyc, 2, 1, 1, 1),
    ]
    hidden, gate_grad_t, up_grad_t, mlp_out, normed_mid_grad = mlp(
        normed_mid, mlp_grad, pieces, down_own, down_other
    )

    gates = (gate_grad_t, up_grad_t)
    a_g = terms([pltpu.with_memory_space_constraint(v, pltpu.HBM) for v in gates], mid_2, gate_rows, 1, n_z=2)
    a_g, hidden, *gates, mlp_out, normed_mid_grad = together(a_g, hidden, *gates, mlp_out, normed_mid_grad)

    a_gr = swap(a_g, "c")
    mid_grad, branch_grad_t, attended_grad, delta, result, sums = middle_back(
        normed_mid_grad, middle, out_g, branch, mlp_out, proj_t, attended_t, mods
    )
    b_g = terms(gates, mid_2, gate_rows, 1, z_first=2, n_z=2, order=(1, 0))
    by_head = attended_grad.reshape(HEADS, head_dim, band)
    a_gr, b_g, by_head, delta, branch_grad_t = together(a_gr, b_g, by_head, delta, branch_grad_t)

    b_gr = swap(b_g, "c")
    other_first = swap(by_head[:6], "x")
    a_k, a_s = terms(gates, mid_2, gate_rows, 0, received=a_gr, n_z=2, stacked=False)
    proj_send, proj_keep = split_rows(branch_grad_t, False)
    down_g = terms((down_send,), hidden, 2 * proj_rows, 1, split=n_z)
    b_gr, other_first, a_k, a_s, down_g, proj_send, proj_keep = together(
        b_gr, other_first, a_k, a_s, down_g, proj_send, proj_keep
    )

    down_gr = swap(down_g, "c")
    a_r1 = [swap(a_s[2:3], "x")]
    b_s = terms(gates, mid_2, gate_rows, 0, received=b_gr, z_first=2, n_z=2, y=(1,), order=(1, 0))
    b_k = terms(gates, mid_2, gate_rows, 0, received=b_gr, z_first=2, n_z=2, y=(0,), order=(1, 0))
    proj_g = terms((proj_send,), att_2, n_z * proj_rows, 1, order=(1, 0), split=2)
    down_gr, a_r1[0], b_s, b_k, proj_g = together(down_gr, a_r1[0], b_s, b_k, proj_g)

    proj_gr = swap(proj_g, "c")
    a_r1.append(swap(a_s[3:4], "x"))
    b_s = b_s.reshape(4, gate_rows, width)
    b_r1 = [swap(b_s[:1], "y")]
    down_sum = terms((down_keep,), hidden, 2 * proj_rows, 0, received=down_gr, split=n_z)
    proj_gr, a_r1[1], b_r1[0], down_sum = together(proj_gr, a_r1[1], b_r1[0], down_sum)

    down_sum = lax.psum_scatter(
        down_sum.reshape(-1, down_sum.shape[-1]), "z", scatter_dimension=0, tiled=True
    ).reshape(2, 2, proj_rows, -1)
    other_last = swap(by_head[6:], "x")
    other_rows = swap(jnp.stack([log_mass, delta]), "x")
    b_r1.append(swap(b_s[1:3], "y"))
    dq, dk, dv = attention_back_own(qkv, by_head, log_mass, delta, HEADS, band)
    b_r1[1], other_last, other_rows, dq = together(b_r1[1], other_last, other_rows, dq)

    a_r1.append(swap(a_s[:2], "x"))
    b_r1.append(swap(b_s[3:], "y"))
    a_s2 = add_low(a_k[2:], jnp.concatenate(a_r1[:2]))
    a_r2 = [swap(a_s2[:1], "y")]
    heads_grad, gain_q, gain_k = attention_back_other(
        qkv, hat, fac, cos_t, sin_t, gains_t, dq, dk, dv,
        (other_first, other_last), other_rows[0], other_rows[1], HEADS, band,
    )
    projected_t = heads_grad.reshape(3 * width, band)
    a_r1[2], b_r1[2], a_r2[0], projected_t = together(a_r1[2], b_r1[2], a_r2[0], projected_t)

    b_r1 = jnp.concatenate(b_r1).reshape(2, 2, gate_rows, width)
    b_s2 = add_low(b_k[0], b_r1[0])
    b_r2 = [swap(b_s2[:1], "x")]
    a_r2.append(swap(a_s2[1:], "y"))
    q_g = terms((projected_t,), normed_2, qkv_rows, 1)
    b_r2[0], a_r2[1], q_g, proj_gr = together(b_r2[0], a_r2[1], q_g, proj_gr)

    q_gr = swap(q_g, "c")
    b_r2.append(swap(b_s2[1:], "x"))
    proj_sum = terms((proj_keep,), att_2, n_z * proj_rows, 0, received=proj_gr, order=(1, 0), split=2)
    proj_r1 = [swap(proj_sum[1, 0], "y")]
    q_gr, b_r2[1], proj_r1[0], proj_sum = together(q_gr, b_r2[1], proj_r1[0], proj_sum)

    row_a = 112
    qa_keep, qa_send, qb_send, qb_keep = last_terms(projected_t, normed_2, qkv_rows, row_a, q_gr)
    proj_r1.append(swap(proj_sum[1, 1], "y"))
    proj_r2 = swap(add_low(proj_sum[0, 0], proj_r1[0]), "x")
    gu = jnp.concatenate(
        [add_low(a_k[:2], a_r1[2], jnp.concatenate(a_r2)), add_low(b_k[1], b_r1[1], jnp.concatenate(b_r2))]
    )
    qa_keep, qa_send, qb_send, qb_keep, proj_r1[1], proj_r2, projected_t, gu, gain_q, gain_k = together(
        qa_keep, qa_send, qb_send, qb_keep, proj_r1[1], proj_r2, projected_t, gu, gain_q, gain_k
    )

    gu = lax.psum_scatter(gu.reshape(-1, width), "z", scatter_dimension=0, tiled=True)
    qa_r1, qb_r1 = swap(qa_send, "x"), swap(qb_send, "y")
    input_grad, in_sums = input_back(projected_t, qkv_t, lat, mid_grad, mods)
    mod_grad = jnp.concatenate([in_sums[0:1], in_sums[1:2], sums[2:3], sums[0:1], sums[1:2], sums[3:4]], axis=-1)
    small = jnp.concatenate([mod_grad, gain_q.sum(0).T, gain_k.sum(0).T], axis=-1)
    small_r = swap(small, "x")
    qa_r1, qb_r1, down_sum, small_r = together(qa_r1, qb_r1, down_sum, small_r)

    qa_keep, qa_r1 = qa_keep.reshape(2, n_z, row_a, half), qa_r1.reshape(2, n_z, row_a, half)
    qa_s2, qb_s2, small = together(
        add_low(qa_keep[1], qa_r1[1]), add_low(qb_keep[0], qb_r1[0]), small + small_r
    )
    qa_r2, qb_r2 = swap(qa_s2, "y"), swap(qb_s2, "x")
    band_mod, band_gain = small[:, : 6 * width], small[:, 6 * width :]
    mod_cols_grad = lax.all_to_all(band_mod.astype(BF16), DP_AXES, split_axis=1, concat_axis=0, tiled=True)
    qa_r2, qb_r2, down_sum, mod_cols_grad = together(qa_r2, qb_r2, down_sum, mod_cols_grad)

    last = jnp.concatenate(
        [
            add_low(qa_keep[0], qa_r1[0], qa_r2),
            add_low(qb_keep[1], qb_r1[1], qb_r2),
            add_low(proj_sum[0, 1], proj_r1[1], proj_r2).reshape(n_z, proj_rows, half),
        ],
        axis=1,
    )
    last, gu, mod_cols_grad = together(last, gu, mod_cols_grad)
    last = lax.psum_scatter(last.reshape(-1, half), "z", scatter_dimension=0, tiled=True)
    cond_act_part = dot_f32(mod_cols_grad, ada_weight[0], ((1,), (1,)))
    tail = jnp.zeros((8, width), F32).at[0, : 2 * head_dim].set(band_gain[0])
    summed = summed_over(jnp.concatenate([cond_act_part, tail]), ("y", "c"), 4)
    summed, down_sum = together(summed, down_sum)
    down_r = swap(down_sum[:, 1], "y")
    down_sum = add_low(down_sum[:, 0], down_r)
    down_r2 = swap(down_sum[1], "x")
    summed = summed_over(summed, "z", n_z)
    ada_grad = dot_f32(cond_act, mod_cols_grad, ((0,), (0,)))
    items = cond.shape[0]
    _, silu_back = jax.vjp(jax.nn.silu, cond)
    cond_grad = silu_back(summed[:items])[0]
    time_grad, class_grad = spread_rows((bucket_hot, class_hot), cond_grad)
    down_out = down_sum[0].astype(F32) + down_r2.astype(F32)

    def out(values):
        return values.T.astype(F32)[None]

    return (
        result[None],
        input_grad[None],
        time_grad,
        class_grad,
        ada_grad[None],
        out(last[:qkv_rows]),
        out(last[qkv_rows:]),
        out(gu[:, :half]),
        out(gu[:, half:]),
        out(down_out),
        summed[items : items + 1, :head_dim],
        summed[items : items + 1, head_dim : 2 * head_dim],
    )


def fast_solution(mesh):
    dp = mesh.shape["dp"]
    fine = jax.sharding.Mesh(mesh.devices.reshape(dp // 4, 2, 2, 2), ("z", "y", "c", "x"))
    items, last = P(DP_AXES, "x", None), P(None, "x", DP_AXES)
    in_specs = (items, items, P(), P(), P(), P(), P(DP_AXES, "x"), P(None, None, DP_AXES)) + (last,) * 5 + (P(), P())
    out_specs = (items, items, P(), P(), P(None, None, DP_AXES)) + (last,) * 5 + (P(), P())
    return jax.shard_map(fast_shards, mesh=fine, in_specs=in_specs, out_specs=out_specs, check_vma=False)


def solution(mesh):
    if mesh.shape["dp"] == 16 and mesh.shape["seq"] == 2:
        return fast_solution(mesh)
    in_specs = (
        P("dp", "seq", None),
        P("dp", "seq", None),
        P(),
        P(),
        P(),
        P(),
        P("dp", "seq"),
        P(None, None, "dp"),
        P(None, "seq", "dp"),
        P(None, "seq", "dp"),
        P(None, "seq", "dp"),
        P(None, "seq", "dp"),
        P(None, "seq", "dp"),
        P(),
        P(),
    )
    out_specs = (
        P("dp", "seq", None),
        P("dp", "seq", None),
        P(),
        P(),
        P(None, None, "dp"),
        P(None, "seq", "dp"),
        P(None, "seq", "dp"),
        P(None, "seq", "dp"),
        P(None, "seq", "dp"),
        P(None, "seq", "dp"),
        P(),
        P(),
    )
    return jax.shard_map(shards, mesh=mesh, in_specs=in_specs, out_specs=out_specs, check_vma=False)
```

```python
import jax
import jax.numpy as jnp
from jax import lax
from jax.experimental import pallas as pl
from jax.experimental.layout import Layout, with_layout_constraint
from jax.experimental.pallas import tpu as pltpu
from jax.sharding import PartitionSpec as P

HEADS = 16
CLASSES = 1000
BUCKETS = 1000
SIDE = 32


EPS = 1e-06
THETA = 10000.0
HIGHEST = lax.Precision.HIGHEST


def norm_factor(values):
    return lax.rsqrt(jnp.mean(values * values, axis=-1, keepdims=True) + EPS)


def modulate(values, shift_by, scale_by):
    return values * norm_factor(values) * (1.0 + scale_by) + shift_by


def rope_tables(row_pos, col_pos, head_dim):
    quarter = head_dim // 4
    frequency = THETA ** (-jnp.arange(quarter, dtype=jnp.float32) / quarter)
    angles = jnp.concatenate(
        [row_pos[..., None] * frequency, col_pos[..., None] * frequency], axis=-1
    )
    cos_part = jnp.cos(angles)
    sin_part = jnp.sin(angles)
    return (
        jnp.concatenate([cos_part, cos_part], axis=-1),
        jnp.concatenate([sin_part, sin_part], axis=-1),
    )


def rotate(values, cos_part, sin_part):
    half_dim = values.shape[-1] // 2
    turned = jnp.concatenate([-values[..., half_dim:], values[..., :half_dim]], axis=-1)
    return values * cos_part + turned * sin_part


def query_key(query_pre, key_pre, gain_query, gain_key, cos_part, sin_part):
    query_out = rotate(query_pre * norm_factor(query_pre) * gain_query, cos_part, sin_part)
    key_out = rotate(key_pre * norm_factor(key_pre) * gain_key, cos_part, sin_part)
    return (query_out, key_out)


def swiglu(gate_pre, up_pre):
    return jax.nn.silu(gate_pre) * up_pre


def gather_layer(layer_no, qkv_weight, proj_weight, gate_weight, up_weight, down_weight):
    row_parts = (
        lax.all_gather(qkv_weight[layer_no], "seq", axis=0, tiled=True),
        lax.all_gather(proj_weight[layer_no], "seq", axis=0, tiled=True),
        lax.all_gather(gate_weight[layer_no], "seq", axis=0, tiled=True),
        lax.all_gather(up_weight[layer_no], "seq", axis=0, tiled=True),
        lax.all_gather(down_weight[layer_no], "seq", axis=0, tiled=True),
    )
    qkv_rows, proj_rows, gate_rows, up_rows, down_rows = row_parts
    return (
        lax.all_gather(qkv_rows, "dp", axis=1, tiled=True),
        lax.all_gather(proj_rows, "dp", axis=1, tiled=True),
        lax.all_gather(gate_rows, "dp", axis=1, tiled=True),
        lax.all_gather(up_rows, "dp", axis=1, tiled=True),
        lax.all_gather(down_rows, "dp", axis=1, tiled=True),
    )


def attend(queries, key_rows, value_rows, inv_root):
    items_dev, band_rows, head_count, head_dim = queries.shape
    top_score = jnp.full((items_dev, head_count, band_rows), -jnp.inf, jnp.float32)
    row_mass = jnp.zeros((items_dev, head_count, band_rows), jnp.float32)
    weighted = jnp.zeros((items_dev, band_rows, head_count, head_dim), jnp.float32)
    key_seg = lax.all_gather(key_rows, "seq", axis=1, tiled=True)
    value_seg = lax.all_gather(value_rows, "seq", axis=1, tiled=True)
    seg_rows = key_seg.shape[1]
    key_heads = key_seg.reshape(items_dev, seg_rows, head_count, head_dim)
    value_heads = value_seg.reshape(items_dev, seg_rows, head_count, head_dim)
    scores = (
        jnp.einsum("ibhe,inhe->ihbn", queries, key_heads, preferred_element_type=jnp.float32)
        * inv_root
    )
    new_top = jnp.max(scores, axis=-1)
    shrink = jnp.exp(top_score - new_top)
    weights = jnp.exp(scores - new_top[..., None])
    new_mass = row_mass * shrink + jnp.sum(weights, axis=-1)
    update = jnp.einsum(
        "ihbn,inhe->ibhe",
        weights.astype(jnp.bfloat16),
        value_heads,
        preferred_element_type=jnp.float32,
    )
    new_weighted = weighted * jnp.transpose(shrink, (0, 2, 1))[..., None] + update
    log_mass = new_top + jnp.log(new_mass)
    attended = new_weighted / jnp.transpose(new_mass, (0, 2, 1))[..., None]
    return (attended, log_mass)


def attend_back(queries, keys_all, values_all, attended_grad, log_mass, delta, inv_root):
    items_dev, band_rows, head_count, head_dim = queries.shape
    seq_len = keys_all.shape[1]
    key_heads = keys_all.reshape(items_dev, seq_len, head_count, head_dim)
    value_heads = values_all.reshape(items_dev, seq_len, head_count, head_dim)

    def one_item(operands):
        query_item, key_item, value_item, grad_item, mass_item, delta_item = operands
        scores = (
            jnp.einsum("bhe,nhe->hbn", query_item, key_item, preferred_element_type=jnp.float32)
            * inv_root
        )
        probs_full = jnp.exp(scores - mass_item[..., None])
        prob_grad = jnp.einsum(
            "bhe,nhe->hbn", grad_item, value_item, preferred_element_type=jnp.float32
        )
        score_grad = (probs_full * (prob_grad - delta_item[..., None])).astype(jnp.bfloat16)
        query_out_grad = (
            jnp.einsum("hbn,nhe->bhe", score_grad, key_item, preferred_element_type=jnp.float32)
            * inv_root
        )
        key_out_grad = (
            jnp.einsum("hbn,bhe->nhe", score_grad, query_item, preferred_element_type=jnp.float32)
            * inv_root
        )
        value_grad = jnp.einsum(
            "hbn,bhe->nhe",
            probs_full.astype(jnp.bfloat16),
            grad_item,
            preferred_element_type=jnp.float32,
        )
        return (query_out_grad, key_out_grad, value_grad)

    return lax.map(one_item, (queries, key_heads, value_heads, attended_grad, log_mass, delta))


def forward_layer(residual, modulation, weights, gain_query, gain_key, cos_part, sin_part):
    qkv_full, proj_full, gate_full, up_full, down_full = weights
    items_dev, band_rows, model_width = residual.shape
    head_count = HEADS
    head_dim = model_width // head_count
    inv_root = head_dim ** (-0.5)
    shift_attn, scale_attn, gate_attn, shift_mlp, scale_mlp, gate_mlp = jnp.split(
        modulation[:, None, :], 6, axis=-1
    )
    normed = modulate(residual, shift_attn, scale_attn).astype(jnp.bfloat16)
    projected = jnp.einsum("ibd,de->ibe", normed, qkv_full, preferred_element_type=jnp.float32)
    query_pre = projected[..., :model_width].reshape(items_dev, band_rows, head_count, head_dim)
    key_pre = projected[..., model_width : 2 * model_width].reshape(
        items_dev, band_rows, head_count, head_dim
    )
    queries, key_rows = query_key(query_pre, key_pre, gain_query, gain_key, cos_part, sin_part)
    queries = queries.astype(jnp.bfloat16)
    key_rows = key_rows.astype(jnp.bfloat16).reshape(items_dev, band_rows, model_width)
    value_rows = projected[..., 2 * model_width :].astype(jnp.bfloat16)
    attended, log_mass = attend(queries, key_rows, value_rows, inv_root)
    attended_low = attended.reshape(items_dev, band_rows, model_width).astype(jnp.bfloat16)
    branch = jnp.einsum("ibd,de->ibe", attended_low, proj_full, preferred_element_type=jnp.float32)
    middle = residual + gate_attn * branch
    normed_mid = modulate(middle, shift_mlp, scale_mlp).astype(jnp.bfloat16)
    gate_pre = jnp.einsum("ibd,df->ibf", normed_mid, gate_full, preferred_element_type=jnp.float32)
    up_pre = jnp.einsum("ibd,df->ibf", normed_mid, up_full, preferred_element_type=jnp.float32)
    hidden = swiglu(gate_pre, up_pre).astype(jnp.bfloat16)
    mlp_out = jnp.einsum("ibf,fd->ibd", hidden, down_full, preferred_element_type=jnp.float32)
    output = middle + gate_mlp * mlp_out
    stored = (
        residual,
        normed,
        query_pre,
        key_pre,
        queries,
        key_rows,
        value_rows,
        attended,
        attended_low,
        log_mass,
        branch,
        middle,
        normed_mid,
        gate_pre,
        up_pre,
        hidden,
        mlp_out,
    )
    return (output, stored)


def weight_terms(
    normed,
    attended_low,
    normed_mid,
    hidden,
    projected_grad,
    branch_grad,
    gate_pre_grad,
    up_pre_grad,
    mlp_grad,
):
    qkv_term = jnp.einsum("ibd,ibe->de", normed, projected_grad, preferred_element_type=jnp.float32)
    proj_term = jnp.einsum(
        "ibd,ibe->de", attended_low, branch_grad, preferred_element_type=jnp.float32
    )
    gate_term = jnp.einsum(
        "ibd,ibf->df", normed_mid, gate_pre_grad, preferred_element_type=jnp.float32
    )
    up_term = jnp.einsum("ibd,ibf->df", normed_mid, up_pre_grad, preferred_element_type=jnp.float32)
    down_term = jnp.einsum("ibf,ibd->fd", hidden, mlp_grad, preferred_element_type=jnp.float32)
    col_parts = (
        lax.psum_scatter(
            qkv_term.astype(jnp.bfloat16), "dp", scatter_dimension=1, tiled=True
        ).astype(jnp.float32),
        lax.psum_scatter(
            proj_term.astype(jnp.bfloat16), "dp", scatter_dimension=1, tiled=True
        ).astype(jnp.float32),
        lax.psum_scatter(
            gate_term.astype(jnp.bfloat16), "dp", scatter_dimension=1, tiled=True
        ).astype(jnp.float32),
        lax.psum_scatter(
            up_term.astype(jnp.bfloat16), "dp", scatter_dimension=1, tiled=True
        ).astype(jnp.float32),
        lax.psum_scatter(
            down_term.astype(jnp.bfloat16), "dp", scatter_dimension=1, tiled=True
        ).astype(jnp.float32),
    )
    qkv_cols, proj_cols, gate_cols, up_cols, down_cols = col_parts
    return (
        lax.psum_scatter(
            qkv_cols.astype(jnp.bfloat16), "seq", scatter_dimension=0, tiled=True
        ).astype(jnp.float32),
        lax.psum_scatter(
            proj_cols.astype(jnp.bfloat16), "seq", scatter_dimension=0, tiled=True
        ).astype(jnp.float32),
        lax.psum_scatter(
            gate_cols.astype(jnp.bfloat16), "seq", scatter_dimension=0, tiled=True
        ).astype(jnp.float32),
        lax.psum_scatter(
            up_cols.astype(jnp.bfloat16), "seq", scatter_dimension=0, tiled=True
        ).astype(jnp.float32),
        lax.psum_scatter(
            down_cols.astype(jnp.bfloat16), "seq", scatter_dimension=0, tiled=True
        ).astype(jnp.float32),
    )


def backward_layer(
    stored, resid_grad, modulation, weights, gain_query, gain_key, cos_part, sin_part
):
    qkv_full, proj_full, gate_full, up_full, down_full = weights
    (
        residual,
        normed,
        query_pre,
        key_pre,
        queries,
        key_rows,
        value_rows,
        attended,
        attended_low,
        log_mass,
        branch,
        middle,
        normed_mid,
        gate_pre,
        up_pre,
        hidden,
        mlp_out,
    ) = stored
    items_dev, band_rows, head_count, head_dim = queries.shape
    model_width = residual.shape[-1]
    inv_root = head_dim ** (-0.5)
    shift_attn, scale_attn, gate_attn, shift_mlp, scale_mlp, gate_mlp = jnp.split(
        modulation[:, None, :], 6, axis=-1
    )
    mlp_grad = (gate_mlp * resid_grad).astype(jnp.bfloat16)
    gate_mlp_grad = jnp.sum(resid_grad * mlp_out, axis=1, keepdims=True)
    hidden_grad = jnp.einsum("ibd,fd->ibf", mlp_grad, down_full, preferred_element_type=jnp.float32)
    unused_out, swiglu_back = jax.vjp(swiglu, gate_pre, up_pre)
    gate_pre_grad, up_pre_grad = swiglu_back(hidden_grad)
    gate_pre_grad = gate_pre_grad.astype(jnp.bfloat16)
    up_pre_grad = up_pre_grad.astype(jnp.bfloat16)
    normed_mid_grad = jnp.einsum(
        "ibf,df->ibd", gate_pre_grad, gate_full, preferred_element_type=jnp.float32
    )
    normed_mid_grad = normed_mid_grad + jnp.einsum(
        "ibf,df->ibd", up_pre_grad, up_full, preferred_element_type=jnp.float32
    )
    unused_mid, mid_back = jax.vjp(modulate, middle, shift_mlp, scale_mlp)
    mid_norm_grad, shift_mlp_grad, scale_mlp_grad = mid_back(normed_mid_grad)
    mid_grad = resid_grad + mid_norm_grad
    branch_grad = (gate_attn * mid_grad).astype(jnp.bfloat16)
    gate_attn_grad = jnp.sum(mid_grad * branch, axis=1, keepdims=True)
    attended_grad = jnp.einsum(
        "ibe,de->ibd", branch_grad, proj_full, preferred_element_type=jnp.float32
    ).astype(jnp.bfloat16)
    attended_grad = attended_grad.reshape(items_dev, band_rows, head_count, head_dim)
    delta = jnp.transpose(jnp.sum(attended_grad.astype(jnp.float32) * attended, axis=-1), (0, 2, 1))
    keys_all, values_all = (
        lax.all_gather(key_rows, "seq", axis=1, tiled=True),
        lax.all_gather(value_rows, "seq", axis=1, tiled=True),
    )
    query_out_grad, key_out_grad, value_grad = attend_back(
        queries, keys_all, values_all, attended_grad, log_mass, delta, inv_root
    )
    seq_len = keys_all.shape[1]
    key_band_grad, value_band_grad = (
        lax.psum_scatter(
            key_out_grad.reshape(items_dev, seq_len, model_width).astype(jnp.bfloat16),
            "seq",
            scatter_dimension=1,
            tiled=True,
        ).astype(jnp.float32),
        lax.psum_scatter(
            value_grad.reshape(items_dev, seq_len, model_width).astype(jnp.bfloat16),
            "seq",
            scatter_dimension=1,
            tiled=True,
        ).astype(jnp.float32),
    )

    def rotate_pair(query_in, key_in, gain_q, gain_k):
        return query_key(query_in, key_in, gain_q, gain_k, cos_part, sin_part)

    unused_pair, pair_back = jax.vjp(rotate_pair, query_pre, key_pre, gain_query, gain_key)
    query_pre_grad, key_pre_grad, query_gain_term, key_gain_term = pair_back(
        (query_out_grad, key_band_grad.reshape(items_dev, band_rows, head_count, head_dim))
    )
    projected_grad = jnp.concatenate(
        [
            query_pre_grad.reshape(items_dev, band_rows, model_width),
            key_pre_grad.reshape(items_dev, band_rows, model_width),
            value_band_grad,
        ],
        axis=-1,
    ).astype(jnp.bfloat16)
    normed_grad = jnp.einsum(
        "ibe,de->ibd", projected_grad, qkv_full, preferred_element_type=jnp.float32
    )
    unused_in, input_back = jax.vjp(modulate, residual, shift_attn, scale_attn)
    input_norm_grad, shift_attn_grad, scale_attn_grad = input_back(normed_grad)
    input_grad = mid_grad + input_norm_grad
    mod_grad = jnp.concatenate(
        [
            shift_attn_grad,
            scale_attn_grad,
            gate_attn_grad,
            shift_mlp_grad,
            scale_mlp_grad,
            gate_mlp_grad,
        ],
        axis=-1,
    )[:, 0, :]
    own_grads = weight_terms(
        normed,
        attended_low,
        normed_mid,
        hidden,
        projected_grad,
        branch_grad,
        gate_pre_grad,
        up_pre_grad,
        mlp_grad,
    )
    return (input_grad, mod_grad, own_grads, query_gain_term, key_gain_term)


def shards(
    latents,
    out_grad,
    time_table,
    class_table,
    buckets,
    labels,
    row_start,
    ada_weight,
    qkv_weight,
    proj_weight,
    gate_weight,
    up_weight,
    down_weight,
    query_gain,
    key_gain,
):
    items_dev, band_rows, model_width = latents.shape
    layer_count = qkv_weight.shape[0]
    head_dim = model_width // HEADS
    offsets = jnp.arange(band_rows, dtype=jnp.int32)
    row_pos = (row_start + (offsets // SIDE)[None, :]).astype(jnp.float32)
    col_pos = (offsets % SIDE).astype(jnp.float32)[None, :]
    cos_part, sin_part = rope_tables(row_pos, col_pos, head_dim)
    cos_part = cos_part[:, :, None, :]
    sin_part = sin_part[:, :, None, :]
    bucket_hot = (buckets[:, None] == jnp.arange(BUCKETS, dtype=jnp.int32)[None, :]).astype(
        jnp.bfloat16
    )
    class_hot = (labels[:, None] == jnp.arange(CLASSES, dtype=jnp.int32)[None, :]).astype(
        jnp.bfloat16
    )
    cond = jnp.dot(bucket_hot, time_table, preferred_element_type=jnp.float32) + jnp.dot(
        class_hot, class_table, preferred_element_type=jnp.float32
    )
    cond_act = jax.nn.silu(cond).astype(jnp.bfloat16)
    mod_cols = jnp.einsum("id,ldm->lim", cond_act, ada_weight, preferred_element_type=jnp.float32)
    modulation = lax.all_to_all(mod_cols, "dp", split_axis=1, concat_axis=2, tiled=True)
    residual = latents.astype(jnp.float32)
    gathered_all = []
    layer_no = 0
    weights = gather_layer(layer_no, qkv_weight, proj_weight, gate_weight, up_weight, down_weight)
    gathered_all.append(weights)
    residual, stored = forward_layer(
        residual,
        modulation[layer_no],
        weights,
        query_gain[layer_no],
        key_gain[layer_no],
        cos_part,
        sin_part,
    )
    stored_all = [stored]
    result = residual.astype(jnp.bfloat16)
    resid_grad = out_grad.astype(jnp.float32)
    mod_grads = [None] * layer_count
    grad_shards = [None] * layer_count
    query_terms = [None] * layer_count
    key_terms = [None] * layer_count
    for layer_no in reversed(range(layer_count)):
        weights = gather_layer(
            layer_no, qkv_weight, proj_weight, gate_weight, up_weight, down_weight
        )
        resid_grad, mod_grad, own_grads, query_term, key_term = backward_layer(
            stored_all[layer_no],
            resid_grad,
            modulation[layer_no],
            weights,
            query_gain[layer_no],
            key_gain[layer_no],
            cos_part,
            sin_part,
        )
        mod_grads[layer_no] = mod_grad
        grad_shards[layer_no] = own_grads
        query_terms[layer_no] = query_term
        key_terms[layer_no] = key_term
    band_mod, band_query, band_key = lax.psum(
        (jnp.stack(mod_grads), jnp.stack(query_terms), jnp.stack(key_terms)), "seq"
    )
    mod_cols_grad = lax.all_to_all(
        band_mod.astype(jnp.bfloat16), "dp", split_axis=2, concat_axis=1, tiled=True
    )
    ada_grad = jnp.einsum(
        "id,lim->ldm", cond_act, mod_cols_grad, preferred_element_type=jnp.float32
    )
    cond_act_part = jnp.einsum(
        "lim,ldm->id", mod_cols_grad, ada_weight, preferred_element_type=jnp.float32
    )
    cond_act_grad, query_grad, key_grad = (
        lax.psum(cond_act_part.astype(jnp.bfloat16), "dp").astype(jnp.float32),
        lax.psum(band_query.astype(jnp.bfloat16), "dp").astype(jnp.float32),
        lax.psum(band_key.astype(jnp.bfloat16), "dp").astype(jnp.float32),
    )
    unused_cond, silu_back = jax.vjp(jax.nn.silu, cond)
    cond_grad = silu_back(cond_act_grad)[0]
    time_grad = jnp.einsum(
        "ib,id->bd", bucket_hot.astype(jnp.float32), cond_grad, precision=HIGHEST
    )
    class_grad = jnp.einsum(
        "ib,id->bd", class_hot.astype(jnp.float32), cond_grad, precision=HIGHEST
    )
    qkv_grad = jnp.stack([grad_shards[0][0]])
    proj_grad = jnp.stack([grad_shards[0][1]])
    gate_grad = jnp.stack([grad_shards[0][2]])
    up_grad = jnp.stack([grad_shards[0][3]])
    down_grad = jnp.stack([grad_shards[0][4]])
    return (
        result,
        resid_grad,
        time_grad,
        class_grad,
        ada_grad,
        qkv_grad,
        proj_grad,
        gate_grad,
        up_grad,
        down_grad,
        query_grad,
        key_grad,
    )


BF16 = jnp.bfloat16
F32 = jnp.float32
LOG2E = 1.4426950408889634
LN2 = 0.6931471805599453
DP_AXES = ("z", "y", "c")
SMALL = pl.CostEstimate(flops=1, bytes_accessed=1, transcendentals=0)


def kernel_call(kernel, **options):
    return pl.pallas_call(kernel, cost_estimate=SMALL, **options)


def together(*arrays):
    return lax.optimization_barrier(arrays)


def swap(values, axis):
    return lax.ppermute(values, axis, [(0, 1), (1, 0)])


def in_order(own, other, axis):
    first = lax.axis_index(axis) == 0
    return jnp.stack([jnp.where(first, own, other), jnp.where(first, other, own)])


def spread(values, axis):
    return in_order(values, swap(values, axis), axis)


def by_rows(values):
    return with_layout_constraint(values, Layout(major_to_minor=tuple(range(values.ndim))))


def gather_z(values):
    n_z = lax.axis_size("z")
    return lax.all_gather(values, "z", axis=0, tiled=True).reshape(n_z, *values.shape)


def add_low(*terms):
    total = terms[0].astype(F32)
    for term in terms[1:]:
        total = total + term.astype(F32)
    return total.astype(BF16)


def dot_f32(left, right, contract):
    return lax.dot_general(left, right, (contract, ((), ())), preferred_element_type=F32)


def piece_targets(pieces, at):
    for k, (array, z_first, x, y, c) in enumerate(pieces):
        for z in range(array.shape[0]):
            block = ((z_first + z) * 2 + (at[2] + y) % 2) * 2 + (at[0] + c) % 2
            yield k, z, (at[1] + x) % 2, block


def join_rows(pieces, first_row, rows):
    width = pieces[0][0].shape[-1]
    half = width // 2
    blocks = sum(piece[0].shape[0] for piece in pieces) // 2

    def kernel(at, *refs):
        out_ref, buf, sems = refs[len(pieces) :]
        copies = []
        for k, z, x, block in piece_targets(pieces, at):
            copy = pltpu.make_async_copy(
                refs[k].at[z, pl.ds(first_row, rows)], buf.at[x, block], sems.at[x, block]
            )
            copy.start()
            copies.append(copy)
        for copy in copies:
            copy.wait()
        for block in range(blocks):
            out_ref[block] = jnp.concatenate([buf[0, block][:, half:], buf[1, block][:, half:]], axis=1)

    return kernel_call(
        kernel,
        grid_spec=pltpu.PrefetchScalarGridSpec(
            num_scalar_prefetch=1,
            grid=(1,),
            in_specs=[pl.BlockSpec(memory_space=pl.ANY)] * len(pieces),
            out_specs=[pl.BlockSpec((blocks, rows, width), lambda i, at: (0, 0, 0))],
            scratch_shapes=[pltpu.VMEM((2, blocks, rows, width), BF16), pltpu.SemaphoreType.DMA((2, blocks))],
        ),
        out_shape=[jax.ShapeDtypeStruct((blocks, rows, width), BF16)],
        compiler_params=pltpu.CompilerParams(vmem_limit_bytes=24 << 20),
        name="join_rows",
    )(place(), *[piece[0] for piece in pieces])[0]


def qkv_heads(normed, pieces, cos_t, sin_t, gains_t, head_dim, band, before=()):
    seq_len, width = normed.shape
    heads = HEADS
    group = 3
    rows_all = group * head_dim
    half = width // 2
    sent = pieces[0][0].shape[1]
    q_scale = head_dim**-0.5 * LOG2E
    side = pieces[0][4]
    steps = sum(piece[0].shape[0] for piece in pieces) // 2
    n_in = len(pieces)

    def kernel(at, norm_ref, cos_ref, sin_ref, gain_ref, *refs):
        out_ref, hat_ref, fac_ref, whole_ref, acc_ref, buf, sems = refs[n_in + len(before) :]

        @pl.when(pl.program_id(0) == 0)
        def _():
            for k, z, x, block in piece_targets(pieces, at):
                local = block // 2
                pltpu.make_async_copy(refs[k].at[z], buf.at[x, local], sems.at[x, local]).start()

        local = pl.program_id(0)
        step = 2 * local + (at[0] + side) % 2
        for x in range(2):
            pltpu.make_async_copy(refs[0].at[0], buf.at[x, local], sems.at[x, local]).wait()
        low, high = buf[0, local], buf[1, local]
        whole_ref[:sent] = jnp.concatenate([low[:, :half], high[:, :half]], axis=1)
        whole_ref[sent:] = jnp.concatenate([low[: rows_all - sent, half:], high[: rows_all - sent, half:]], axis=1)
        acc_ref[...] = dot_f32(whole_ref[...], norm_ref[...], ((1,), (1,)))
        for i in range(group):
            head = step * group + i
            rows = pl.ds(i * head_dim, head_dim)

            @pl.when(head < 2 * heads)
            def _():
                values = acc_ref[rows, :]
                fac = lax.rsqrt(jnp.mean(values * values, axis=0, keepdims=True) + EPS)
                hat = values * fac
                gained = hat * jnp.where(head < heads, gain_ref[:, 0:1] * q_scale, gain_ref[:, 1:2])
                turned = jnp.concatenate([gained[head_dim // 2 :], gained[: head_dim // 2]], axis=0)
                out_ref[i] = (gained * cos_ref[...] + turned * sin_ref[...]).astype(BF16)
                hat_ref[i] = hat[:, :band].astype(BF16)
                fac_ref[i] = fac[:, :band]

            @pl.when(head >= 2 * heads)
            def _():
                out_ref[i] = acc_ref[rows, :].astype(BF16)
                hat_ref[i] = jnp.zeros((head_dim, band), BF16)
                fac_ref[i] = jnp.zeros((1, band), F32)

    whole = lambda i, at: (0, 0)
    return kernel_call(
        kernel,
        grid_spec=pltpu.PrefetchScalarGridSpec(
            num_scalar_prefetch=1,
            grid=(steps,),
            in_specs=[
                pl.BlockSpec((seq_len, width), whole),
                pl.BlockSpec((head_dim, seq_len), whole),
                pl.BlockSpec((head_dim, seq_len), whole),
                pl.BlockSpec((head_dim, 2), whole),
            ]
            + [pl.BlockSpec(memory_space=pl.ANY)] * (n_in + len(before)),
            out_specs=[
                pl.BlockSpec((group, head_dim, seq_len), lambda i, at: (2 * i + (at[0] + side) % 2, 0, 0)),
                pl.BlockSpec((group, head_dim, band), lambda i, at: (2 * i + (at[0] + side) % 2, 0, 0)),
                pl.BlockSpec((group, 1, band), lambda i, at: (2 * i + (at[0] + side) % 2, 0, 0)),
                pl.BlockSpec((rows_all, width), lambda i, at: (2 * i + (at[0] + side) % 2, 0)),
            ],
            scratch_shapes=[
                pltpu.VMEM((rows_all, seq_len), F32),
                pltpu.VMEM((2, steps, sent, width), BF16),
                pltpu.SemaphoreType.DMA((2, steps)),
            ],
        ),
        out_shape=[
            jax.ShapeDtypeStruct((3 * heads, head_dim, seq_len), BF16),
            pltpu.HBM((3 * heads, head_dim, band), BF16),
            pltpu.HBM((3 * heads, 1, band), F32),
            pltpu.HBM((3 * width, width), BF16),
        ],
        input_output_aliases={5 + n_in + k: k for k in range(len(before))},
        compiler_params=pltpu.CompilerParams(vmem_limit_bytes=32 << 20),
        name="qkv_heads",
    )(place(), normed, cos_t, sin_t, gains_t, *[piece[0] for piece in pieces], *before)


def attention_forward(qkv, heads, band):
    _, head_dim, seq_len = qkv.shape

    def kernel(q_ref, k_ref, v_ref, out_ref, mass_ref):
        scores = dot_f32(k_ref[0], q_ref[0], ((0,), (0,)))
        weights = jnp.exp2(scores)
        mass = jnp.sum(weights, axis=0, keepdims=True)
        mixed = dot_f32(v_ref[0], weights.astype(BF16), ((1,), (0,)))
        out_ref[0] = (mixed / mass).astype(BF16)
        mass_ref[0] = jnp.log2(mass)

    return kernel_call(
        kernel,
        grid=(heads,),
        in_specs=[
            pl.BlockSpec((1, head_dim, band), lambda h: (h, 0, 0)),
            pl.BlockSpec((1, head_dim, seq_len), lambda h: (heads + h, 0, 0)),
            pl.BlockSpec((1, head_dim, seq_len), lambda h: (2 * heads + h, 0, 0)),
        ],
        out_specs=[
            pl.BlockSpec((1, head_dim, band), lambda h: (h, 0, 0)),
            pl.BlockSpec((1, 1, band), lambda h: (h, 0, 0)),
        ],
        out_shape=[
            jax.ShapeDtypeStruct((heads, head_dim, band), BF16),
            jax.ShapeDtypeStruct((heads, 1, band), F32),
        ],
        compiler_params=pltpu.CompilerParams(vmem_limit_bytes=14 << 20),
        name="attention_forward",
    )(qkv, qkv, qkv)


def attention_back_own(qkv, out_grad, log_mass, delta, heads, band):
    _, head_dim, seq_len = qkv.shape

    def kernel(q_ref, k_ref, v_ref, grad_ref, mass_ref, delta_ref, dq_ref, dk_ref, dv_ref):
        grad = grad_ref[0]
        scores = dot_f32(k_ref[0], q_ref[0], ((0,), (0,)))
        probs = jnp.exp2(scores - mass_ref[0])
        prob_grad = dot_f32(v_ref[0], grad, ((0,), (0,)))
        score_grad = (probs * (prob_grad - delta_ref[0])).astype(BF16)
        dq_ref[0] = dot_f32(k_ref[0], score_grad, ((1,), (0,)))
        dk_ref[0] = dot_f32(q_ref[0], score_grad[:band], ((1,), (1,)))
        dv_ref[0] = dot_f32(grad, probs[:band].astype(BF16), ((1,), (1,)))

    one = pl.BlockSpec((1, head_dim, band), lambda h: (h, 0, 0))
    row = pl.BlockSpec((1, 1, band), lambda h: (h, 0, 0))
    return kernel_call(
        kernel,
        grid=(heads,),
        in_specs=[
            one,
            pl.BlockSpec((1, head_dim, seq_len), lambda h: (heads + h, 0, 0)),
            pl.BlockSpec((1, head_dim, seq_len), lambda h: (2 * heads + h, 0, 0)),
            one,
            row,
            row,
        ],
        out_specs=[one, one, one],
        out_shape=[pltpu.HBM((heads, head_dim, band), F32)] * 3,
        compiler_params=pltpu.CompilerParams(vmem_limit_bytes=16 << 20),
        name="attention_back_own",
    )(qkv, qkv, qkv, out_grad, log_mass, delta)


def attention_back_other(
    qkv, hat, fac, cos_t, sin_t, gains_t, dq, dk, dv, grads, mass, delta, heads, band
):
    _, head_dim, seq_len = qkv.shape
    inv_root = head_dim**-0.5
    early = grads[0].shape[0]

    def kernel(
        q_ref, k_ref, v_ref, hq_ref, hk_ref, fq_ref, fk_ref, cos_ref, sin_ref, gain_ref,
        dq_ref, dk_ref, dv_ref, low_ref, high_ref, mass_ref, delta_ref, out_ref, gq_ref, gk_ref,
    ):
        grad = jnp.where(pl.program_id(0) < early, low_ref[0], high_ref[0])
        scores = dot_f32(k_ref[0], q_ref[0], ((0,), (0,)))
        probs = jnp.exp2(scores - mass_ref[0])
        prob_grad = dot_f32(v_ref[0], grad, ((0,), (0,)))
        score_grad = (probs * (prob_grad - delta_ref[0])).astype(BF16)
        key_grad = (dk_ref[0] + dot_f32(q_ref[0], score_grad, ((1,), (1,)))) * LN2
        value_grad = dv_ref[0] + dot_f32(grad, probs.astype(BF16), ((1,), (1,)))
        query_grad = dq_ref[0] * inv_root

        def back(turned_grad, hat, fac, gain):
            spun = turned_grad * sin_ref[...]
            spun = jnp.concatenate([spun[head_dim // 2 :], spun[: head_dim // 2]], axis=0)
            gained_grad = turned_grad * cos_ref[...] + spun
            gain_grad = jnp.sum(gained_grad * hat, axis=1, keepdims=True)
            hat_grad = gained_grad * gain
            along = jnp.mean(hat_grad * hat, axis=0, keepdims=True)
            return (fac * (hat_grad - hat * along)).astype(BF16), gain_grad

        out_ref[0, 0], gq_ref[0] = back(query_grad, hq_ref[0].astype(F32), fq_ref[0], gain_ref[:, 0:1])
        out_ref[1, 0], gk_ref[0] = back(key_grad, hk_ref[0].astype(F32), fk_ref[0], gain_ref[:, 1:2])
        out_ref[2, 0] = value_grad.astype(BF16)

    one = pl.BlockSpec((1, head_dim, band), lambda h: (h, 0, 0))
    row = pl.BlockSpec((1, 1, band), lambda h: (h, 0, 0))
    key_one = pl.BlockSpec((1, head_dim, band), lambda h: (heads + h, 0, 0))
    key_row = pl.BlockSpec((1, 1, band), lambda h: (heads + h, 0, 0))
    table = pl.BlockSpec((head_dim, band), lambda h: (0, 0))
    column = pl.BlockSpec((1, head_dim, 1), lambda h: (h, 0, 0))
    return kernel_call(
        kernel,
        grid=(heads,),
        in_specs=[
            pl.BlockSpec((1, head_dim, band), lambda h: (h, 0, 1)),
            key_one,
            pl.BlockSpec((1, head_dim, band), lambda h: (2 * heads + h, 0, 0)),
            one, key_one, row, key_row, table, table,
            pl.BlockSpec((head_dim, 2), lambda h: (0, 0)),
            one, one, one,
            pl.BlockSpec((1, head_dim, band), lambda h: (jnp.minimum(h, early - 1), 0, 0)),
            pl.BlockSpec((1, head_dim, band), lambda h: (jnp.maximum(h - early, 0), 0, 0)),
            row, row,
        ],
        out_specs=[pl.BlockSpec((3, 1, head_dim, band), lambda h: (0, h, 0, 0)), column, column],
        out_shape=[
            jax.ShapeDtypeStruct((3, heads, head_dim, band), BF16),
            jax.ShapeDtypeStruct((heads, head_dim, 1), F32),
            jax.ShapeDtypeStruct((heads, head_dim, 1), F32),
        ],
        compiler_params=pltpu.CompilerParams(vmem_limit_bytes=14 << 20),
        name="attention_back_other",
    )(*[pltpu.with_memory_space_constraint(qkv, pltpu.HBM)] * 3, hat, hat, fac, fac, cos_t, sin_t, gains_t,
      *[pltpu.with_memory_space_constraint(v, pltpu.HBM) for v in (dq, dk, dv)], *grads, mass, delta)


def mlp(mid, mlp_grad, pieces, down_own, down_other):
    band, width = mlp_grad.shape
    rows = pieces[0][0].shape[1]
    half = width // 2
    blocks = sum(piece[0].shape[0] for piece in pieces) // 2
    steps = 4
    per = blocks // steps
    units = per * rows
    chunk = band // 2
    n_z, _, _, down_rows, down_width = down_own.shape

    def kernel(at, mid_ref, mg_ref, *refs):
        downs = refs[len(pieces) : len(pieces) + 2]
        hid_ref, gg_ref, ug_ref, out_ref, grad_ref, buf, down_buf, sems, down_sems = refs[len(pieces) + 2 :]
        step = pl.program_id(0)

        @pl.when(step == 0)
        def _():
            for x in range(2):
                for z in range(n_z):
                    for y in range(2):
                        for c in range(2):
                            block = (z * 2 + y) * 2 + (at[0] + c) % 2
                            target = down_buf.at[x, pl.ds(pl.multiple_of(block * down_rows, 8), down_rows)]
                            pltpu.make_async_copy(downs[c].at[z, y, x], target, down_sems.at[x, block]).start()
            for k, z, x, block in piece_targets(pieces, at):
                pltpu.make_async_copy(refs[k].at[z], buf.at[x, block], sems.at[x, block]).start()
            out_ref[...] = jnp.zeros_like(out_ref)
            grad_ref[...] = jnp.zeros_like(grad_ref)

        for b in range(per):
            for x in range(2):
                block = step * per + b
                pltpu.make_async_copy(refs[0].at[0], buf.at[x, block], sems.at[x, block]).wait()
        @pl.when(step % 2 == 0)
        def _():
            for block in range(4 * n_z):
                target = down_buf.at[step // 2, pl.ds(block * down_rows, down_rows)]
                pltpu.make_async_copy(downs[0].at[0, 0, 0], target, down_sems.at[step // 2, block]).wait()

        low = buf[0, pl.ds(step * per, per)].reshape(units, width)
        high = buf[1, pl.ds(step * per, per)].reshape(units, width)
        gate = jnp.concatenate([low[:, :half], high[:, :half]], axis=1)
        up = jnp.concatenate([low[:, half:], high[:, half:]], axis=1)
        down = down_buf[step // 2, :, pl.ds(pl.multiple_of(step % 2 * units, 128), units)]
        nt, nn = ((1,), (1,)), ((1,), (0,))
        for part in range(2):
            at_rows = pl.ds(part * chunk, chunk)
            mid = mid_ref[at_rows, :]
            gate_pre = dot_f32(mid, gate, nt)
            up_pre = dot_f32(mid, up, nt)
            hidden_grad = dot_f32(mg_ref[at_rows, :], down, nn)
            sig = 1.0 / (1.0 + jnp.exp(-gate_pre))
            act = gate_pre * sig
            hidden = (act * up_pre).astype(BF16)
            gate_grad = (hidden_grad * up_pre * (sig * (1.0 + gate_pre * (1.0 - sig)))).astype(BF16)
            up_grad = (hidden_grad * act).astype(BF16)
            hid_ref[at_rows, :] = hidden
            gg_ref[:, at_rows] = gate_grad.T
            ug_ref[:, at_rows] = up_grad.T
            out_ref[at_rows, :] += dot_f32(hidden, down, nt)
            grad_ref[at_rows, :] += dot_f32(gate_grad, gate, nn) + dot_f32(up_grad, up, nn)

    whole = lambda i, at: (0, 0)
    once = pl.Buffered(1)
    return kernel_call(
        kernel,
        grid_spec=pltpu.PrefetchScalarGridSpec(
            num_scalar_prefetch=1,
            grid=(steps,),
            in_specs=[
                pl.BlockSpec((band, width), whole, pipeline_mode=once),
                pl.BlockSpec((band, width), whole, pipeline_mode=once),
            ]
            + [pl.BlockSpec(memory_space=pl.ANY)] * (len(pieces) + 2),
            out_specs=[
                pl.BlockSpec((band, units), lambda i, at: (0, i)),
                pl.BlockSpec((units, band), lambda i, at: (i, 0)),
                pl.BlockSpec((units, band), lambda i, at: (i, 0)),
                pl.BlockSpec((band, width), whole, pipeline_mode=once),
                pl.BlockSpec((band, width), whole, pipeline_mode=once),
            ],
            scratch_shapes=[
                pltpu.VMEM((2, blocks, rows, width), BF16),
                pltpu.VMEM((2, width, down_width), BF16),
                pltpu.SemaphoreType.DMA((2, blocks)),
                pltpu.SemaphoreType.DMA((2, 4 * n_z)),
            ],
        ),
        out_shape=[
            jax.ShapeDtypeStruct((band, blocks * rows), BF16),
            jax.ShapeDtypeStruct((blocks * rows, band), BF16),
            jax.ShapeDtypeStruct((blocks * rows, band), BF16),
            jax.ShapeDtypeStruct((band, width), F32),
            jax.ShapeDtypeStruct((band, width), F32),
        ],
        compiler_params=pltpu.CompilerParams(vmem_limit_bytes=56 << 20),
        name="mlp",
    )(place(), mid, mlp_grad, *[piece[0] for piece in pieces], down_own, down_other)


def after_attention(attended_t, proj_t, residual_low, modulation):
    width, band = attended_t.shape
    half = width // 2
    block = 128

    def kernel(att_ref, proj_ref, low_ref, mod_ref, branch_ref, middle_ref, normed_ref, mid_ref, att_out_ref):
        branch = dot_f32(att_ref[...], proj_ref[...], ((0,), (1,)))
        middle = low_ref[...].astype(F32) + mod_ref[2:3, :] * branch
        normed = modulate(middle, mod_ref[3:4, :], mod_ref[4:5, :]).astype(BF16)
        attended = att_ref[...].T
        branch_ref[...] = branch.astype(BF16)
        middle_ref[...] = middle
        normed_ref[...] = normed
        for x in range(2):
            mid_ref[x] = normed[:, x * half : (x + 1) * half]
            att_out_ref[x] = attended[:, x * half : (x + 1) * half]

    rows = pl.BlockSpec((block, width), lambda i: (i, 0))
    halves = pl.BlockSpec((2, block, half), lambda i: (0, i, 0))
    return kernel_call(
        kernel,
        grid=(band // block,),
        in_specs=[
            pl.BlockSpec((width, block), lambda i: (0, i)),
            pl.BlockSpec((width, width), lambda i: (0, 0)),
            rows,
            pl.BlockSpec((6, width), lambda i: (0, 0)),
        ],
        out_specs=[rows, rows, rows, halves, halves],
        out_shape=[
            pltpu.HBM((band, width), BF16),
            pltpu.HBM((band, width), F32),
            jax.ShapeDtypeStruct((band, width), BF16),
            jax.ShapeDtypeStruct((2, band, half), BF16),
            jax.ShapeDtypeStruct((2, band, half), BF16),
        ],
        compiler_params=pltpu.CompilerParams(vmem_limit_bytes=20 << 20),
        name="after_attention",
    )(*[pltpu.with_memory_space_constraint(v, pltpu.HBM) for v in (attended_t, proj_t, residual_low)], modulation)


def middle_back(normed_mid_grad, middle, out_grad, branch, mlp_out, proj_t, attended_t, modulation):
    band, width = middle.shape
    half = width // 2
    head_dim = width // HEADS
    block = 128

    def kernel(
        normed_grad_ref, mid_ref, out_ref, branch_ref, mlp_ref, proj_ref, att_ref, mod_ref,
        grad_ref, bg_ref, att_grad_ref, delta_ref, result_ref, sums_ref,
    ):
        @pl.when(pl.program_id(0) == 0)
        def _():
            sums_ref[...] = jnp.zeros_like(sums_ref)

        normed_grad = normed_grad_ref[...]
        middle, grad, mlp_out = mid_ref[...], out_ref[...].astype(F32), mlp_ref[...]
        fac = norm_factor(middle)
        hat = middle * fac
        hat_grad = normed_grad * (1.0 + mod_ref[4:5, :])
        along = jnp.mean(hat_grad * hat, axis=-1, keepdims=True)
        mid_grad = grad + fac * (hat_grad - hat * along)
        branch_grad = (mod_ref[2:3, :] * mid_grad).astype(BF16)
        attended_grad = dot_f32(branch_grad, proj_ref[...], ((1,), (0,))).astype(BF16).T
        grad_ref[...] = mid_grad
        bg_ref[...] = branch_grad.T
        att_grad_ref[...] = attended_grad
        both = attended_grad.astype(F32) * att_ref[...].astype(F32)
        delta_ref[...] = jnp.sum(both.reshape(HEADS, head_dim, block), axis=1, keepdims=True)
        result_ref[...] = (middle + mod_ref[5:6, :] * mlp_out).astype(BF16)
        sums_ref[0:1, :] += jnp.sum(normed_grad, axis=0, keepdims=True)
        sums_ref[1:2, :] += jnp.sum(normed_grad * hat, axis=0, keepdims=True)
        sums_ref[2:3, :] += jnp.sum(mid_grad * branch_ref[...].astype(F32), axis=0, keepdims=True)
        sums_ref[3:4, :] += jnp.sum(grad * mlp_out, axis=0, keepdims=True)

    rows = pl.BlockSpec((block, width), lambda i: (i, 0))
    columns = pl.BlockSpec((width, block), lambda i: (0, i))
    return kernel_call(
        kernel,
        grid=(band // block,),
        in_specs=[
            rows, rows, rows, rows, rows,
            pl.BlockSpec((width, width), lambda i: (0, 0)),
            columns,
            pl.BlockSpec((6, width), lambda i: (0, 0)),
        ],
        out_specs=[
            rows, columns, columns,
            pl.BlockSpec((HEADS, 1, block), lambda i: (0, 0, i)),
            rows,
            pl.BlockSpec((8, width), lambda i: (0, 0)),
        ],
        out_shape=[
            jax.ShapeDtypeStruct((band, width), F32),
            jax.ShapeDtypeStruct((width, band), BF16),
            jax.ShapeDtypeStruct((width, band), BF16),
            jax.ShapeDtypeStruct((HEADS, 1, band), F32),
            jax.ShapeDtypeStruct((band, width), BF16),
            jax.ShapeDtypeStruct((8, width), F32),
        ],
        compiler_params=pltpu.CompilerParams(vmem_limit_bytes=20 << 20),
        name="middle_back",
    )(normed_mid_grad, middle, out_grad, branch, mlp_out, proj_t, attended_t, modulation)


def input_back(projected_t, qkv_t, latents, mid_grad, modulation):
    inner, band = projected_t.shape
    width = qkv_t.shape[1]
    block = 128

    def kernel(left_ref, weight_ref, low_ref, grad_ref, mod_ref, out_ref, sums_ref):
        @pl.when(pl.program_id(0) == 0)
        def _():
            sums_ref[...] = jnp.zeros_like(sums_ref)

        normed_grad = dot_f32(left_ref[...], weight_ref[...], ((0,), (0,)))
        residual = low_ref[...].astype(F32)
        fac = norm_factor(residual)
        hat = residual * fac
        hat_grad = normed_grad * (1.0 + mod_ref[1:2, :])
        along = jnp.mean(hat_grad * hat, axis=-1, keepdims=True)
        out_ref[...] = grad_ref[...] + fac * (hat_grad - hat * along)
        sums_ref[0:1, :] += jnp.sum(normed_grad, axis=0, keepdims=True)
        sums_ref[1:2, :] += jnp.sum(normed_grad * hat, axis=0, keepdims=True)

    rows = pl.BlockSpec((block, width), lambda i: (i, 0))
    return kernel_call(
        kernel,
        grid=(band // block,),
        in_specs=[
            pl.BlockSpec((inner, block), lambda i: (0, i)),
            pl.BlockSpec((inner, width), lambda i: (0, 0), pipeline_mode=pl.Buffered(1)),
            rows,
            rows,
            pl.BlockSpec((6, width), lambda i: (0, 0)),
        ],
        out_specs=[rows, pl.BlockSpec((8, width), lambda i: (0, 0))],
        out_shape=[jax.ShapeDtypeStruct((band, width), F32), jax.ShapeDtypeStruct((8, width), F32)],
        compiler_params=pltpu.CompilerParams(vmem_limit_bytes=24 << 20),
        name="input_back",
    )(projected_t, qkv_t, latents, mid_grad, modulation)


def place():
    return jnp.stack([lax.axis_index(axis) for axis in ("c", "x", "y")]).astype(jnp.int32)


def terms(lefts, right, rows, side, received=None, z_first=0, n_z=4, y=(0, 1), order=(0, 1), stacked=True, split=0):
    patches = right.shape[0] if right.ndim == 2 else right.shape[1]
    wide = right.ndim == 2
    each = right.shape[-1] // 2 if wide else right.shape[-1]
    width = each * len(lefts)
    count = split or len(y) * n_z
    n = len(lefts)

    def left_map(i, at):
        if split:
            return (i, 0)
        z = z_first + i % n_z
        return ((z * 2 + (y[0] + i // n_z + at[2]) % 2) * 2 + (at[0] + side) % 2, 0)

    def right_spec(h):
        if wide:
            return pl.BlockSpec((patches, each), lambda i, at: (0, (at[1] + h) % 2))
        return pl.BlockSpec((1, patches, each), lambda i, at: ((at[1] + h) % 2, 0, 0))

    def kernel(at, *refs):
        rights, outs = refs[n : n + 2], refs[n + 2 :]
        if received is not None:
            got, outs = refs[n + 2 : n + 4], refs[n + 4 :]
        for k in range(2):
            half = rights[k][...] if wide else rights[k][0]
            values = [dot_f32(refs[m][...], half, ((1,), (0,))) for m in range(n)]
            value = values[0] if n == 1 else jnp.concatenate(values, axis=1)
            if received is not None:
                value = value + got[k][0, 0].astype(F32)
            if not stacked:
                outs[k][0] = value.astype(BF16)
            elif split:
                outs[0][0, k] = value.astype(BF16)
            else:
                outs[0][k, 0] = value.astype(BF16)

    received_specs = []
    if received is not None:
        skip = 0 if split else y[0] * n_z
        received_specs = [
            pl.BlockSpec((1, 1, rows, width), lambda i, at, k=k: (i, k, 0, 0) if split else (k, i + skip, 0, 0))
            for k in range(2)
        ]
    if stacked and split:
        out_shape = [jax.ShapeDtypeStruct((count, 2, rows, width), BF16)]
        out_specs = [pl.BlockSpec((1, 2, rows, width), lambda i, at: (i, 0, 0, 0))]
    elif stacked:
        out_shape = [jax.ShapeDtypeStruct((2, count, rows, width), BF16)]
        out_specs = [pl.BlockSpec((2, 1, rows, width), lambda i, at: (0, i, 0, 0))]
    else:
        out_shape = [jax.ShapeDtypeStruct((count, rows, width), BF16)] * 2
        out_specs = [pl.BlockSpec((1, rows, width), lambda i, at: (i, 0, 0))] * 2
    outs = kernel_call(
        kernel,
        grid_spec=pltpu.PrefetchScalarGridSpec(
            num_scalar_prefetch=1,
            grid=(count,),
            in_specs=[pl.BlockSpec((rows, patches), left_map)] * n
            + [right_spec(h) for h in order]
            + received_specs,
            out_specs=out_specs,
        ),
        out_shape=out_shape,
        compiler_params=pltpu.CompilerParams(vmem_limit_bytes=12 << 20),
        name="terms",
    )(place(), *lefts, right, right, *([received] * 2 if received is not None else []))
    return outs[0] if stacked else outs


def last_terms(left, right, rows, cut, received):
    patches, width = left.shape[-1], right.shape[-1]
    n_z = 4
    late = rows - cut

    def row_of(i):
        return 1 - i // n_z

    def kernel(at, left_ref, own_ref, other_ref, r0_ref, r1_ref, keep_ref, send_ref, up_send_ref, up_keep_ref):
        values = [
            (dot_f32(left_ref[...], ref[0], ((1,), (0,))) + got[0, 0].astype(F32)).astype(BF16)
            for ref, got in ((own_ref, r0_ref), (other_ref, r1_ref))
        ]
        keep_ref[0] = values[0][:cut]
        send_ref[0] = values[1][:cut]

        @pl.when(pl.program_id(0) < n_z)
        def _():
            for k in range(2):
                up_send_ref[1 - k, 0] = values[k][cut:]

        @pl.when(pl.program_id(0) >= n_z)
        def _():
            for k in range(2):
                up_keep_ref[1 - k, 0] = values[k][cut:]

    def got(h):
        return pl.BlockSpec((1, 1, rows, width), lambda i, at: (h, row_of(i) * n_z + i % n_z, 0, 0))

    early_spec = pl.BlockSpec((1, cut, width), lambda i, at: (row_of(i) * n_z + i % n_z, 0, 0))
    return kernel_call(
        kernel,
        grid_spec=pltpu.PrefetchScalarGridSpec(
            num_scalar_prefetch=1,
            grid=(2 * n_z,),
            in_specs=[
                pl.BlockSpec(
                    (rows, patches), lambda i, at: ((i % n_z * 2 + (row_of(i) + at[2]) % 2) * 2 + at[0], 0)
                ),
                pl.BlockSpec((1, patches, width), lambda i, at: (at[1], 0, 0)),
                pl.BlockSpec((1, patches, width), lambda i, at: ((at[1] + 1) % 2, 0, 0)),
                got(0),
                got(1),
            ],
            out_specs=[
                early_spec,
                early_spec,
                pl.BlockSpec((2, 1, late, width), lambda i, at: (0, jnp.minimum(i, n_z - 1), 0, 0)),
                pl.BlockSpec((2, 1, late, width), lambda i, at: (0, jnp.maximum(i - n_z, 0), 0, 0)),
            ],
        ),
        out_shape=[jax.ShapeDtypeStruct((2 * n_z, cut, width), BF16)] * 2
        + [jax.ShapeDtypeStruct((2, n_z, late, width), BF16)] * 2,
        compiler_params=pltpu.CompilerParams(vmem_limit_bytes=12 << 20),
        name="last_terms",
    )(place(), left, right, right, received, received)


def split_rows(left_t, z_first):
    n_z, patches = lax.axis_size("z"), left_t.shape[-1]
    blocks = left_t.reshape(n_z, 2, 2, -1, patches)
    core, row = lax.axis_index("c"), lax.axis_index("y")

    def part(which):
        picked = lax.dynamic_index_in_dim(blocks, which, 2, keepdims=False)
        own = lax.dynamic_index_in_dim(picked, row, 1, keepdims=False)
        other = lax.dynamic_index_in_dim(picked, 1 - row, 1, keepdims=False)
        return jnp.stack([own, other], axis=1 if z_first else 0).reshape(-1, patches)

    return part(1 - core), part(core)


def summed_over(values, axes, size):
    low = values.astype(BF16)
    parts = [low] + [lax.ppermute(low, axes, [(i, i ^ hop) for i in range(size)]) for hop in range(1, size)]
    parts = [part.astype(F32) for part in parts]
    while len(parts) > 1:
        parts = [left + right for left, right in zip(parts[::2], parts[1::2])]
    return parts[0]


def spread_rows(hots, values):
    items, width = values.shape
    count = hots[0].shape[1]
    block = 384

    def kernel(values_ref, *refs):
        rest, parts = values_ref[...], []
        for _ in range(3):
            high = rest.astype(BF16)
            parts.append(high)
            rest = rest - high.astype(F32)
        for hot_ref, out_ref in zip(refs[: len(hots)], refs[len(hots) :]):
            hot = hot_ref[...]
            out_ref[...] = sum(dot_f32(hot, part, ((0,), (0,))) for part in parts)

    return kernel_call(
        kernel,
        grid=(width // block,),
        in_specs=[pl.BlockSpec((items, block), lambda i: (0, i))]
        + [pl.BlockSpec((items, count), lambda i: (0, 0))] * len(hots),
        out_specs=[pl.BlockSpec((count, block), lambda i: (0, i))] * len(hots),
        out_shape=[jax.ShapeDtypeStruct((count, width), F32)] * len(hots),
        compiler_params=pltpu.CompilerParams(vmem_limit_bytes=16 << 20),
        name="spread_rows",
    )(values, *hots)


def in_float32(values, rows, columns):
    sizes = [(r, c) for r in rows for c in columns]

    def kernel(in_ref, *out_refs):
        at_row = 0
        for m, r in enumerate(rows):
            at_column = 0
            for n, c in enumerate(columns):
                part = in_ref[at_row : at_row + r, at_column : at_column + c]
                out_refs[m * len(columns) + n][...] = part.astype(F32)
                at_column += c
            at_row += r

    return kernel_call(
        kernel,
        out_shape=[jax.ShapeDtypeStruct(size, F32) for size in sizes],
        compiler_params=pltpu.CompilerParams(vmem_limit_bytes=8 << 20),
        name="in_float32",
    )(values)


def outer_terms(left, right):
    def kernel(left_ref, right_ref, out_ref):
        out_ref[...] = dot_f32(left_ref[...], right_ref[...], ((0,), (0,)))

    return kernel_call(
        kernel,
        out_shape=[jax.ShapeDtypeStruct((left.shape[1], right.shape[1]), F32)],
        compiler_params=pltpu.CompilerParams(vmem_limit_bytes=8 << 20),
        name="outer_terms",
    )(left, right)[0]


def fast_shards(
    latents, out_grad, time_table, class_table, buckets, labels, row_start,
    ada_weight, qkv_weight, proj_weight, gate_weight, up_weight, down_weight, query_gain, key_gain,
):
    band, width = latents.shape[1:]
    head_dim = width // HEADS
    lat, out_g = latents[0], out_grad[0]
    half = width // 2
    n_z = lax.axis_size("z")

    qkv_s, proj_s = qkv_weight[0].T, proj_weight[0].T
    gate_s, up_s, down_s = gate_weight[0].T, up_weight[0].T, by_rows(down_weight[0].T)
    qkv_rows, proj_rows, gate_rows = qkv_s.shape[0], proj_s.shape[0], gate_s.shape[0]
    cut = (qkv_rows + proj_rows) // 2
    first = by_rows(jnp.concatenate([qkv_s[:cut], jnp.concatenate([qkv_s[cut:], proj_s])], axis=1))
    second = by_rows(jnp.concatenate([gate_s, up_s], axis=1))

    first_z = gather_z(first)
    second_z = gather_z(second)
    start_other = swap(row_start.astype(F32), "x")
    (down_r,) = together(swap(down_s, "x"))
    down_x = in_order(down_s, down_r, "x")
    down_x, lat_x = together(down_x, lat)
    lat_other = swap(lat_x, "x")
    down_r = swap(down_x, "y")

    bucket_hot = (buckets[:, None] == jnp.arange(BUCKETS, dtype=jnp.int32)[None, :]).astype(BF16)
    class_hot = (labels[:, None] == jnp.arange(CLASSES, dtype=jnp.int32)[None, :]).astype(BF16)
    cond = jnp.dot(bucket_hot, time_table, preferred_element_type=F32) + jnp.dot(
        class_hot, class_table, preferred_element_type=F32
    )
    cond_act = jax.nn.silu(cond).astype(BF16)
    mod_cols = jnp.dot(cond_act, ada_weight[0], preferred_element_type=F32)

    offsets = jnp.arange(band, dtype=jnp.int32)
    rows_in = (offsets // SIDE).astype(F32)
    row_pos = jnp.concatenate([row_start.astype(F32)[0, 0] + rows_in, start_other[0, 0] + rows_in])
    col_pos = jnp.tile((offsets % SIDE).astype(F32), 2)
    quarter = head_dim // 4
    frequency = THETA ** (-jnp.arange(quarter, dtype=F32) / quarter)
    angles = jnp.concatenate([frequency[:, None] * row_pos[None], frequency[:, None] * col_pos[None]])
    cos_h, sin_h = jnp.cos(angles), jnp.sin(angles)
    cos_t = jnp.concatenate([cos_h, cos_h])
    sin_t = jnp.concatenate([-sin_h, sin_h])
    gains_t = jnp.concatenate([query_gain, key_gain]).T
    first_z, lat_other, down_r, mod_cols, cos_t, sin_t = together(first_z, lat_other, down_r, mod_cols, cos_t, sin_t)

    a, b = by_rows(first_z[:2]), by_rows(first_z[2:])
    a_y, b_x, a_c, b_c = swap(a, "y"), swap(b, "x"), swap(a, "c"), swap(b, "c")
    down_z = gather_z(in_order(down_x, down_r, "y").reshape(-1, down_x.shape[-1]))
    modulation = lax.all_to_all(mod_cols, DP_AXES, split_axis=0, concat_axis=1, tiled=True)
    a_y, b_x, a_c, b_c, modulation = together(a_y, b_x, a_c, b_c, modulation)

    a_x, b_y, a_yc, b_xc = swap(a, "x"), swap(b, "y"), swap(a_y, "c"), swap(b_x, "c")
    mods = modulation.reshape(6, width)
    shift_attn, scale_attn, gate_attn, shift_mlp, scale_mlp, gate_mlp = jnp.split(modulation, 6, axis=-1)
    lat_full = jnp.concatenate([lat, lat_other]).astype(F32)
    normed_full = modulate(lat_full, shift_attn, scale_attn).astype(BF16)
    a_x, b_y, a_yc, b_xc, normed_full = together(a_x, b_y, a_yc, b_xc, normed_full)

    a_yx, b_xy, a_xc, b_yc = swap(a_y, "x"), swap(b_x, "y"), swap(a_x, "c"), swap(b_y, "c")
    mlp_grad = (gate_mlp * out_g.astype(F32)).astype(BF16)
    down_send, down_keep = split_rows(mlp_grad.T, True)
    normed = normed_full[:band]
    normed_2 = jnp.stack([normed[:, :half], normed[:, half:]])
    second_z, a_yx, b_xy, a_xc, b_yc, mlp_grad, down_send, down_keep, normed_2 = together(
        second_z, a_yx, b_xy, a_xc, b_yc, mlp_grad, down_send, down_keep, normed_2
    )

    a_yxc, b_xyc = swap(a_yx, "c"), swap(b_xy, "c")
    e, f = by_rows(second_z[:2]), by_rows(second_z[2:])
    e_y, f_x = swap(e, "y"), swap(f, "x")
    pieces_own = [
        (a, 0, 0, 0, 0), (a_y, 0, 0, 1, 0), (a_x, 0, 1, 0, 0), (a_yx, 0, 1, 1, 0),
        (b, 2, 0, 0, 0), (b_x, 2, 1, 0, 0), (b_y, 2, 0, 1, 0), (b_xy, 2, 1, 1, 0),
    ]
    tables = (cos_t, sin_t, gains_t, head_dim, band)
    parts = qkv_heads(normed_full, pieces_own, *tables)
    *parts, e_y, f_x, a_yxc, b_xyc = together(*parts, e_y, f_x, a_yxc, b_xyc)

    e_x, f_y, e_c, f_c, e_yc = swap(e, "x"), swap(f, "y"), swap(e, "c"), swap(f, "c"), swap(e_y, "c")
    pieces_other = [
        (a_c, 0, 0, 0, 1), (a_yc, 0, 0, 1, 1), (a_xc, 0, 1, 0, 1), (a_yxc, 0, 1, 1, 1),
        (b_c, 2, 0, 0, 1), (b_xc, 2, 1, 0, 1), (b_yc, 2, 0, 1, 1), (b_xyc, 2, 1, 1, 1),
    ]
    qkv, hat, fac, qkv_t = qkv_heads(normed_full, pieces_other, *tables, before=parts)
    e_x, f_y, e_c, f_c, e_yc, qkv = together(e_x, f_y, e_c, f_c, e_yc, qkv)

    e_yx, f_xy = swap(e_y, "x"), swap(f_x, "y")
    f_xc, e_xc, f_yc = swap(f_x, "c"), swap(e_x, "c"), swap(f_y, "c")
    attended_t, log_mass = attention_forward(qkv, HEADS, band)
    proj_t = join_rows(pieces_own + pieces_other, qkv_rows - cut, proj_rows).reshape(width, width)
    e_yx, f_xy, f_xc, e_xc, f_yc, attended_t, proj_t, down_z = together(
        e_yx, f_xy, f_xc, e_xc, f_yc, attended_t, proj_t, down_z
    )

    down_own = down_z.reshape(n_z, 2, 2, -1, down_z.shape[-1])
    down_other, e_yxc, f_xyc = swap(down_own, "c"), swap(e_yx, "c"), swap(f_xy, "c")
    attended_t = attended_t.reshape(width, band)
    branch, middle, normed_mid, mid_2, att_2 = after_attention(attended_t, proj_t, lat, mods)
    pieces = [
        (e, 0, 0, 0, 0), (e_y, 0, 0, 1, 0), (e_x, 0, 1, 0, 0), (e_yx, 0, 1, 1, 0),
        (e_c, 0, 0, 0, 1), (e_yc, 0, 0, 1, 1), (e_xc, 0, 1, 0, 1), (e_yxc, 0, 1, 1, 1),
        (f, 2, 0, 0, 0), (f_x, 2, 1, 0, 0), (f_y, 2, 0, 1, 0), (f_xy, 2, 1, 1, 0),
        (f_c, 2, 0, 0, 1), (f_xc, 2, 1, 0, 1), (f_yc, 2, 0, 1, 1), (f_xyc, 2, 1, 1, 1),
    ]
    hidden, gate_grad_t, up_grad_t, mlp_out, normed_mid_grad = mlp(
        normed_mid, mlp_grad, pieces, down_own, down_other
    )

    gates = (gate_grad_t, up_grad_t)
    a_g = terms([pltpu.with_memory_space_constraint(v, pltpu.HBM) for v in gates], mid_2, gate_rows, 1, n_z=2)
    a_g, hidden, *gates, mlp_out, normed_mid_grad = together(a_g, hidden, *gates, mlp_out, normed_mid_grad)

    a_gr = swap(a_g, "c")
    mid_grad, branch_grad_t, attended_grad, delta, result, sums = middle_back(
        normed_mid_grad, middle, out_g, branch, mlp_out, proj_t, attended_t, mods
    )
    b_g = terms(gates, mid_2, gate_rows, 1, z_first=2, n_z=2, order=(1, 0))
    by_head = attended_grad.reshape(HEADS, head_dim, band)
    a_gr, b_g, by_head, delta, branch_grad_t = together(a_gr, b_g, by_head, delta, branch_grad_t)

    b_gr = swap(b_g, "c")
    other_first = swap(by_head[:6], "x")
    a_k, a_s = terms(gates, mid_2, gate_rows, 0, received=a_gr, n_z=2, stacked=False)
    proj_send, proj_keep = split_rows(branch_grad_t, False)
    down_g = terms((down_send,), hidden, 2 * proj_rows, 1, split=n_z)
    b_gr, other_first, a_k, a_s, down_g, proj_send, proj_keep = together(
        b_gr, other_first, a_k, a_s, down_g, proj_send, proj_keep
    )

    down_gr = swap(down_g, "c")
    a_r1 = [swap(a_s[2:3], "x")]
    b_s = terms(gates, mid_2, gate_rows, 0, received=b_gr, z_first=2, n_z=2, y=(1,), order=(1, 0))
    b_k = terms(gates, mid_2, gate_rows, 0, received=b_gr, z_first=2, n_z=2, y=(0,), order=(1, 0))
    proj_g = terms((proj_send,), att_2, n_z * proj_rows, 1, order=(1, 0), split=2)
    down_gr, a_r1[0], b_s, b_k, proj_g = together(down_gr, a_r1[0], b_s, b_k, proj_g)

    proj_gr = swap(proj_g, "c")
    a_r1.append(swap(a_s[3:4], "x"))
    b_s = b_s.reshape(4, gate_rows, width)
    b_r1 = [swap(b_s[:1], "y")]
    down_sum = terms((down_keep,), hidden, 2 * proj_rows, 0, received=down_gr, split=n_z)
    proj_gr, a_r1[1], b_r1[0], down_sum = together(proj_gr, a_r1[1], b_r1[0], down_sum)

    down_sum = lax.psum_scatter(
        down_sum.reshape(-1, down_sum.shape[-1]), "z", scatter_dimension=0, tiled=True
    ).reshape(2, 2, proj_rows, -1)
    other_last = swap(by_head[6:], "x")
    other_rows = swap(jnp.stack([log_mass, delta]), "x")
    b_r1.append(swap(b_s[1:3], "y"))
    dq, dk, dv = attention_back_own(qkv, by_head, log_mass, delta, HEADS, band)
    b_r1[1], other_last, other_rows, dq = together(b_r1[1], other_last, other_rows, dq)

    a_r1.append(swap(a_s[:2], "x"))
    b_r1.append(swap(b_s[3:], "y"))
    a_s2 = add_low(a_k[2:], jnp.concatenate(a_r1[:2]))
    a_r2 = [swap(a_s2[:1], "y")]
    heads_grad, gain_q, gain_k = attention_back_other(
        qkv, hat, fac, cos_t, sin_t, gains_t, dq, dk, dv,
        (other_first, other_last), other_rows[0], other_rows[1], HEADS, band,
    )
    projected_t = heads_grad.reshape(3 * width, band)
    a_r1[2], b_r1[2], a_r2[0], projected_t = together(a_r1[2], b_r1[2], a_r2[0], projected_t)

    b_r1 = jnp.concatenate(b_r1).reshape(2, 2, gate_rows, width)
    b_s2 = add_low(b_k[0], b_r1[0])
    b_r2 = [swap(b_s2[:1], "x")]
    a_r2.append(swap(a_s2[1:], "y"))
    q_g = terms((projected_t,), normed_2, qkv_rows, 1)
    b_r2[0], a_r2[1], q_g, proj_gr = together(b_r2[0], a_r2[1], q_g, proj_gr)

    q_gr = swap(q_g, "c")
    b_r2.append(swap(b_s2[1:], "x"))
    proj_sum = terms((proj_keep,), att_2, n_z * proj_rows, 0, received=proj_gr, order=(1, 0), split=2)
    proj_r1 = [swap(proj_sum[1, 0], "y")]
    q_gr, b_r2[1], proj_r1[0], proj_sum = together(q_gr, b_r2[1], proj_r1[0], proj_sum)

    row_a = 112
    qa_keep, qa_send, qb_send, qb_keep = last_terms(projected_t, normed_2, qkv_rows, row_a, q_gr)
    proj_r1.append(swap(proj_sum[1, 1], "y"))
    proj_r2 = swap(add_low(proj_sum[0, 0], proj_r1[0]), "x")
    gu = jnp.concatenate(
        [add_low(a_k[:2], a_r1[2], jnp.concatenate(a_r2)), add_low(b_k[1], b_r1[1], jnp.concatenate(b_r2))]
    )
    qa_keep, qa_send, qb_send, qb_keep, proj_r1[1], proj_r2, projected_t, gu, gain_q, gain_k = together(
        qa_keep, qa_send, qb_send, qb_keep, proj_r1[1], proj_r2, projected_t, gu, gain_q, gain_k
    )

    gu = lax.psum_scatter(gu.reshape(-1, width), "z", scatter_dimension=0, tiled=True)
    qa_r1, qb_r1 = swap(qa_send, "x"), swap(qb_send, "y")
    input_grad, in_sums = input_back(projected_t, qkv_t, lat, mid_grad, mods)
    mod_grad = jnp.concatenate([in_sums[0:1], in_sums[1:2], sums[2:3], sums[0:1], sums[1:2], sums[3:4]], axis=-1)
    small = jnp.concatenate([mod_grad, gain_q.sum(0).T, gain_k.sum(0).T], axis=-1)
    small_r = swap(small, "x")
    qa_r1, qb_r1, down_sum, small_r = together(qa_r1, qb_r1, down_sum, small_r)

    qa_keep, qa_r1 = qa_keep.reshape(2, n_z, row_a, half), qa_r1.reshape(2, n_z, row_a, half)
    qa_s2, qb_s2, small = together(
        add_low(qa_keep[1], qa_r1[1]), add_low(qb_keep[0], qb_r1[0]), small + small_r
    )
    qa_r2, qb_r2 = swap(qa_s2, "y"), swap(qb_s2, "x")
    band_mod, band_gain = small[:, : 6 * width], small[:, 6 * width :]
    mod_cols_grad = lax.all_to_all(band_mod.astype(BF16), DP_AXES, split_axis=1, concat_axis=0, tiled=True)
    qa_r2, qb_r2, down_sum, mod_cols_grad = together(qa_r2, qb_r2, down_sum, mod_cols_grad)

    last = jnp.concatenate(
        [
            add_low(qa_keep[0], qa_r1[0], qa_r2),
            add_low(qb_keep[1], qb_r1[1], qb_r2),
            add_low(proj_sum[0, 1], proj_r1[1], proj_r2).reshape(n_z, proj_rows, half),
        ],
        axis=1,
    )
    last, gu, mod_cols_grad = together(last, gu, mod_cols_grad)
    last = lax.psum_scatter(last.reshape(-1, half), "z", scatter_dimension=0, tiled=True)
    cond_act_part = dot_f32(mod_cols_grad, ada_weight[0], ((1,), (1,)))
    tail = jnp.zeros((8, width), F32).at[0, : 2 * head_dim].set(band_gain[0])
    summed = summed_over(jnp.concatenate([cond_act_part, tail]), ("y", "c"), 4)
    summed, down_sum = together(summed, down_sum)
    down_r = swap(down_sum[:, 1], "y")
    down_sum = add_low(down_sum[:, 0], down_r)
    down_r2 = swap(down_sum[1], "x")
    summed = summed_over(summed, "z", n_z)
    ada_grad = outer_terms(mod_cols_grad, cond_act).T
    items = cond.shape[0]
    _, silu_back = jax.vjp(jax.nn.silu, cond)
    cond_grad = silu_back(summed[:items])[0]
    time_grad, class_grad = spread_rows((bucket_hot, class_hot), cond_grad)
    down_out = down_sum[0].astype(F32) + down_r2.astype(F32)

    qkv_grad, proj_grad = in_float32(last, [qkv_rows, proj_rows], [half])
    gate_grad, up_grad = in_float32(gu, [gate_rows], [half, half])

    def out(values):
        return values.T[None]

    return (
        result[None],
        input_grad[None],
        time_grad,
        class_grad,
        ada_grad[None],
        out(qkv_grad),
        out(proj_grad),
        out(gate_grad),
        out(up_grad),
        out(down_out),
        summed[items : items + 1, :head_dim],
        summed[items : items + 1, head_dim : 2 * head_dim],
    )


def fast_solution(mesh):
    dp = mesh.shape["dp"]
    fine = jax.sharding.Mesh(mesh.devices.reshape(dp // 4, 2, 2, 2), ("z", "y", "c", "x"))
    items, last = P(DP_AXES, "x", None), P(None, "x", DP_AXES)
    in_specs = (items, items, P(), P(), P(), P(), P(DP_AXES, "x"), P(None, None, DP_AXES)) + (last,) * 5 + (P(), P())
    out_specs = (items, items, P(), P(), P(None, None, DP_AXES)) + (last,) * 5 + (P(), P())
    return jax.shard_map(fast_shards, mesh=fine, in_specs=in_specs, out_specs=out_specs, check_vma=False)


def solution(mesh):
    if mesh.shape["dp"] == 16 and mesh.shape["seq"] == 2:
        return fast_solution(mesh)
    in_specs = (
        P("dp", "seq", None),
        P("dp", "seq", None),
        P(),
        P(),
        P(),
        P(),
        P("dp", "seq"),
        P(None, None, "dp"),
        P(None, "seq", "dp"),
        P(None, "seq", "dp"),
        P(None, "seq", "dp"),
        P(None, "seq", "dp"),
        P(None, "seq", "dp"),
        P(),
        P(),
    )
    out_specs = (
        P("dp", "seq", None),
        P("dp", "seq", None),
        P(),
        P(),
        P(None, None, "dp"),
        P(None, "seq", "dp"),
        P(None, "seq", "dp"),
        P(None, "seq", "dp"),
        P(None, "seq", "dp"),
        P(None, "seq", "dp"),
        P(),
        P(),
    )
    return jax.shard_map(shards, mesh=mesh, in_specs=in_specs, out_specs=out_specs, check_vma=False)
```

```python
import jax
import jax.numpy as jnp
from jax import lax
from jax.experimental import pallas as pl
from jax.experimental.layout import Layout, with_layout_constraint
from jax.experimental.pallas import tpu as pltpu
from jax.sharding import PartitionSpec as P

HEADS = 16
CLASSES = 1000
BUCKETS = 1000
SIDE = 32


EPS = 1e-06
THETA = 10000.0
HIGHEST = lax.Precision.HIGHEST


def norm_factor(values):
    return lax.rsqrt(jnp.mean(values * values, axis=-1, keepdims=True) + EPS)


def modulate(values, shift_by, scale_by):
    return values * norm_factor(values) * (1.0 + scale_by) + shift_by


def rope_tables(row_pos, col_pos, head_dim):
    quarter = head_dim // 4
    frequency = THETA ** (-jnp.arange(quarter, dtype=jnp.float32) / quarter)
    angles = jnp.concatenate(
        [row_pos[..., None] * frequency, col_pos[..., None] * frequency], axis=-1
    )
    cos_part = jnp.cos(angles)
    sin_part = jnp.sin(angles)
    return (
        jnp.concatenate([cos_part, cos_part], axis=-1),
        jnp.concatenate([sin_part, sin_part], axis=-1),
    )


def rotate(values, cos_part, sin_part):
    half_dim = values.shape[-1] // 2
    turned = jnp.concatenate([-values[..., half_dim:], values[..., :half_dim]], axis=-1)
    return values * cos_part + turned * sin_part


def query_key(query_pre, key_pre, gain_query, gain_key, cos_part, sin_part):
    query_out = rotate(query_pre * norm_factor(query_pre) * gain_query, cos_part, sin_part)
    key_out = rotate(key_pre * norm_factor(key_pre) * gain_key, cos_part, sin_part)
    return (query_out, key_out)


def swiglu(gate_pre, up_pre):
    return jax.nn.silu(gate_pre) * up_pre


def gather_layer(layer_no, qkv_weight, proj_weight, gate_weight, up_weight, down_weight):
    row_parts = (
        lax.all_gather(qkv_weight[layer_no], "seq", axis=0, tiled=True),
        lax.all_gather(proj_weight[layer_no], "seq", axis=0, tiled=True),
        lax.all_gather(gate_weight[layer_no], "seq", axis=0, tiled=True),
        lax.all_gather(up_weight[layer_no], "seq", axis=0, tiled=True),
        lax.all_gather(down_weight[layer_no], "seq", axis=0, tiled=True),
    )
    qkv_rows, proj_rows, gate_rows, up_rows, down_rows = row_parts
    return (
        lax.all_gather(qkv_rows, "dp", axis=1, tiled=True),
        lax.all_gather(proj_rows, "dp", axis=1, tiled=True),
        lax.all_gather(gate_rows, "dp", axis=1, tiled=True),
        lax.all_gather(up_rows, "dp", axis=1, tiled=True),
        lax.all_gather(down_rows, "dp", axis=1, tiled=True),
    )


def attend(queries, key_rows, value_rows, inv_root):
    items_dev, band_rows, head_count, head_dim = queries.shape
    top_score = jnp.full((items_dev, head_count, band_rows), -jnp.inf, jnp.float32)
    row_mass = jnp.zeros((items_dev, head_count, band_rows), jnp.float32)
    weighted = jnp.zeros((items_dev, band_rows, head_count, head_dim), jnp.float32)
    key_seg = lax.all_gather(key_rows, "seq", axis=1, tiled=True)
    value_seg = lax.all_gather(value_rows, "seq", axis=1, tiled=True)
    seg_rows = key_seg.shape[1]
    key_heads = key_seg.reshape(items_dev, seg_rows, head_count, head_dim)
    value_heads = value_seg.reshape(items_dev, seg_rows, head_count, head_dim)
    scores = (
        jnp.einsum("ibhe,inhe->ihbn", queries, key_heads, preferred_element_type=jnp.float32)
        * inv_root
    )
    new_top = jnp.max(scores, axis=-1)
    shrink = jnp.exp(top_score - new_top)
    weights = jnp.exp(scores - new_top[..., None])
    new_mass = row_mass * shrink + jnp.sum(weights, axis=-1)
    update = jnp.einsum(
        "ihbn,inhe->ibhe",
        weights.astype(jnp.bfloat16),
        value_heads,
        preferred_element_type=jnp.float32,
    )
    new_weighted = weighted * jnp.transpose(shrink, (0, 2, 1))[..., None] + update
    log_mass = new_top + jnp.log(new_mass)
    attended = new_weighted / jnp.transpose(new_mass, (0, 2, 1))[..., None]
    return (attended, log_mass)


def attend_back(queries, keys_all, values_all, attended_grad, log_mass, delta, inv_root):
    items_dev, band_rows, head_count, head_dim = queries.shape
    seq_len = keys_all.shape[1]
    key_heads = keys_all.reshape(items_dev, seq_len, head_count, head_dim)
    value_heads = values_all.reshape(items_dev, seq_len, head_count, head_dim)

    def one_item(operands):
        query_item, key_item, value_item, grad_item, mass_item, delta_item = operands
        scores = (
            jnp.einsum("bhe,nhe->hbn", query_item, key_item, preferred_element_type=jnp.float32)
            * inv_root
        )
        probs_full = jnp.exp(scores - mass_item[..., None])
        prob_grad = jnp.einsum(
            "bhe,nhe->hbn", grad_item, value_item, preferred_element_type=jnp.float32
        )
        score_grad = (probs_full * (prob_grad - delta_item[..., None])).astype(jnp.bfloat16)
        query_out_grad = (
            jnp.einsum("hbn,nhe->bhe", score_grad, key_item, preferred_element_type=jnp.float32)
            * inv_root
        )
        key_out_grad = (
            jnp.einsum("hbn,bhe->nhe", score_grad, query_item, preferred_element_type=jnp.float32)
            * inv_root
        )
        value_grad = jnp.einsum(
            "hbn,bhe->nhe",
            probs_full.astype(jnp.bfloat16),
            grad_item,
            preferred_element_type=jnp.float32,
        )
        return (query_out_grad, key_out_grad, value_grad)

    return lax.map(one_item, (queries, key_heads, value_heads, attended_grad, log_mass, delta))


def forward_layer(residual, modulation, weights, gain_query, gain_key, cos_part, sin_part):
    qkv_full, proj_full, gate_full, up_full, down_full = weights
    items_dev, band_rows, model_width = residual.shape
    head_count = HEADS
    head_dim = model_width // head_count
    inv_root = head_dim ** (-0.5)
    shift_attn, scale_attn, gate_attn, shift_mlp, scale_mlp, gate_mlp = jnp.split(
        modulation[:, None, :], 6, axis=-1
    )
    normed = modulate(residual, shift_attn, scale_attn).astype(jnp.bfloat16)
    projected = jnp.einsum("ibd,de->ibe", normed, qkv_full, preferred_element_type=jnp.float32)
    query_pre = projected[..., :model_width].reshape(items_dev, band_rows, head_count, head_dim)
    key_pre = projected[..., model_width : 2 * model_width].reshape(
        items_dev, band_rows, head_count, head_dim
    )
    queries, key_rows = query_key(query_pre, key_pre, gain_query, gain_key, cos_part, sin_part)
    queries = queries.astype(jnp.bfloat16)
    key_rows = key_rows.astype(jnp.bfloat16).reshape(items_dev, band_rows, model_width)
    value_rows = projected[..., 2 * model_width :].astype(jnp.bfloat16)
    attended, log_mass = attend(queries, key_rows, value_rows, inv_root)
    attended_low = attended.reshape(items_dev, band_rows, model_width).astype(jnp.bfloat16)
    branch = jnp.einsum("ibd,de->ibe", attended_low, proj_full, preferred_element_type=jnp.float32)
    middle = residual + gate_attn * branch
    normed_mid = modulate(middle, shift_mlp, scale_mlp).astype(jnp.bfloat16)
    gate_pre = jnp.einsum("ibd,df->ibf", normed_mid, gate_full, preferred_element_type=jnp.float32)
    up_pre = jnp.einsum("ibd,df->ibf", normed_mid, up_full, preferred_element_type=jnp.float32)
    hidden = swiglu(gate_pre, up_pre).astype(jnp.bfloat16)
    mlp_out = jnp.einsum("ibf,fd->ibd", hidden, down_full, preferred_element_type=jnp.float32)
    output = middle + gate_mlp * mlp_out
    stored = (
        residual,
        normed,
        query_pre,
        key_pre,
        queries,
        key_rows,
        value_rows,
        attended,
        attended_low,
        log_mass,
        branch,
        middle,
        normed_mid,
        gate_pre,
        up_pre,
        hidden,
        mlp_out,
    )
    return (output, stored)


def weight_terms(
    normed,
    attended_low,
    normed_mid,
    hidden,
    projected_grad,
    branch_grad,
    gate_pre_grad,
    up_pre_grad,
    mlp_grad,
):
    qkv_term = jnp.einsum("ibd,ibe->de", normed, projected_grad, preferred_element_type=jnp.float32)
    proj_term = jnp.einsum(
        "ibd,ibe->de", attended_low, branch_grad, preferred_element_type=jnp.float32
    )
    gate_term = jnp.einsum(
        "ibd,ibf->df", normed_mid, gate_pre_grad, preferred_element_type=jnp.float32
    )
    up_term = jnp.einsum("ibd,ibf->df", normed_mid, up_pre_grad, preferred_element_type=jnp.float32)
    down_term = jnp.einsum("ibf,ibd->fd", hidden, mlp_grad, preferred_element_type=jnp.float32)
    col_parts = (
        lax.psum_scatter(
            qkv_term.astype(jnp.bfloat16), "dp", scatter_dimension=1, tiled=True
        ).astype(jnp.float32),
        lax.psum_scatter(
            proj_term.astype(jnp.bfloat16), "dp", scatter_dimension=1, tiled=True
        ).astype(jnp.float32),
        lax.psum_scatter(
            gate_term.astype(jnp.bfloat16), "dp", scatter_dimension=1, tiled=True
        ).astype(jnp.float32),
        lax.psum_scatter(
            up_term.astype(jnp.bfloat16), "dp", scatter_dimension=1, tiled=True
        ).astype(jnp.float32),
        lax.psum_scatter(
            down_term.astype(jnp.bfloat16), "dp", scatter_dimension=1, tiled=True
        ).astype(jnp.float32),
    )
    qkv_cols, proj_cols, gate_cols, up_cols, down_cols = col_parts
    return (
        lax.psum_scatter(
            qkv_cols.astype(jnp.bfloat16), "seq", scatter_dimension=0, tiled=True
        ).astype(jnp.float32),
        lax.psum_scatter(
            proj_cols.astype(jnp.bfloat16), "seq", scatter_dimension=0, tiled=True
        ).astype(jnp.float32),
        lax.psum_scatter(
            gate_cols.astype(jnp.bfloat16), "seq", scatter_dimension=0, tiled=True
        ).astype(jnp.float32),
        lax.psum_scatter(
            up_cols.astype(jnp.bfloat16), "seq", scatter_dimension=0, tiled=True
        ).astype(jnp.float32),
        lax.psum_scatter(
            down_cols.astype(jnp.bfloat16), "seq", scatter_dimension=0, tiled=True
        ).astype(jnp.float32),
    )


def backward_layer(
    stored, resid_grad, modulation, weights, gain_query, gain_key, cos_part, sin_part
):
    qkv_full, proj_full, gate_full, up_full, down_full = weights
    (
        residual,
        normed,
        query_pre,
        key_pre,
        queries,
        key_rows,
        value_rows,
        attended,
        attended_low,
        log_mass,
        branch,
        middle,
        normed_mid,
        gate_pre,
        up_pre,
        hidden,
        mlp_out,
    ) = stored
    items_dev, band_rows, head_count, head_dim = queries.shape
    model_width = residual.shape[-1]
    inv_root = head_dim ** (-0.5)
    shift_attn, scale_attn, gate_attn, shift_mlp, scale_mlp, gate_mlp = jnp.split(
        modulation[:, None, :], 6, axis=-1
    )
    mlp_grad = (gate_mlp * resid_grad).astype(jnp.bfloat16)
    gate_mlp_grad = jnp.sum(resid_grad * mlp_out, axis=1, keepdims=True)
    hidden_grad = jnp.einsum("ibd,fd->ibf", mlp_grad, down_full, preferred_element_type=jnp.float32)
    unused_out, swiglu_back = jax.vjp(swiglu, gate_pre, up_pre)
    gate_pre_grad, up_pre_grad = swiglu_back(hidden_grad)
    gate_pre_grad = gate_pre_grad.astype(jnp.bfloat16)
    up_pre_grad = up_pre_grad.astype(jnp.bfloat16)
    normed_mid_grad = jnp.einsum(
        "ibf,df->ibd", gate_pre_grad, gate_full, preferred_element_type=jnp.float32
    )
    normed_mid_grad = normed_mid_grad + jnp.einsum(
        "ibf,df->ibd", up_pre_grad, up_full, preferred_element_type=jnp.float32
    )
    unused_mid, mid_back = jax.vjp(modulate, middle, shift_mlp, scale_mlp)
    mid_norm_grad, shift_mlp_grad, scale_mlp_grad = mid_back(normed_mid_grad)
    mid_grad = resid_grad + mid_norm_grad
    branch_grad = (gate_attn * mid_grad).astype(jnp.bfloat16)
    gate_attn_grad = jnp.sum(mid_grad * branch, axis=1, keepdims=True)
    attended_grad = jnp.einsum(
        "ibe,de->ibd", branch_grad, proj_full, preferred_element_type=jnp.float32
    ).astype(jnp.bfloat16)
    attended_grad = attended_grad.reshape(items_dev, band_rows, head_count, head_dim)
    delta = jnp.transpose(jnp.sum(attended_grad.astype(jnp.float32) * attended, axis=-1), (0, 2, 1))
    keys_all, values_all = (
        lax.all_gather(key_rows, "seq", axis=1, tiled=True),
        lax.all_gather(value_rows, "seq", axis=1, tiled=True),
    )
    query_out_grad, key_out_grad, value_grad = attend_back(
        queries, keys_all, values_all, attended_grad, log_mass, delta, inv_root
    )
    seq_len = keys_all.shape[1]
    key_band_grad, value_band_grad = (
        lax.psum_scatter(
            key_out_grad.reshape(items_dev, seq_len, model_width).astype(jnp.bfloat16),
            "seq",
            scatter_dimension=1,
            tiled=True,
        ).astype(jnp.float32),
        lax.psum_scatter(
            value_grad.reshape(items_dev, seq_len, model_width).astype(jnp.bfloat16),
            "seq",
            scatter_dimension=1,
            tiled=True,
        ).astype(jnp.float32),
    )

    def rotate_pair(query_in, key_in, gain_q, gain_k):
        return query_key(query_in, key_in, gain_q, gain_k, cos_part, sin_part)

    unused_pair, pair_back = jax.vjp(rotate_pair, query_pre, key_pre, gain_query, gain_key)
    query_pre_grad, key_pre_grad, query_gain_term, key_gain_term = pair_back(
        (query_out_grad, key_band_grad.reshape(items_dev, band_rows, head_count, head_dim))
    )
    projected_grad = jnp.concatenate(
        [
            query_pre_grad.reshape(items_dev, band_rows, model_width),
            key_pre_grad.reshape(items_dev, band_rows, model_width),
            value_band_grad,
        ],
        axis=-1,
    ).astype(jnp.bfloat16)
    normed_grad = jnp.einsum(
        "ibe,de->ibd", projected_grad, qkv_full, preferred_element_type=jnp.float32
    )
    unused_in, input_back = jax.vjp(modulate, residual, shift_attn, scale_attn)
    input_norm_grad, shift_attn_grad, scale_attn_grad = input_back(normed_grad)
    input_grad = mid_grad + input_norm_grad
    mod_grad = jnp.concatenate(
        [
            shift_attn_grad,
            scale_attn_grad,
            gate_attn_grad,
            shift_mlp_grad,
            scale_mlp_grad,
            gate_mlp_grad,
        ],
        axis=-1,
    )[:, 0, :]
    own_grads = weight_terms(
        normed,
        attended_low,
        normed_mid,
        hidden,
        projected_grad,
        branch_grad,
        gate_pre_grad,
        up_pre_grad,
        mlp_grad,
    )
    return (input_grad, mod_grad, own_grads, query_gain_term, key_gain_term)


def shards(
    latents,
    out_grad,
    time_table,
    class_table,
    buckets,
    labels,
    row_start,
    ada_weight,
    qkv_weight,
    proj_weight,
    gate_weight,
    up_weight,
    down_weight,
    query_gain,
    key_gain,
):
    items_dev, band_rows, model_width = latents.shape
    layer_count = qkv_weight.shape[0]
    head_dim = model_width // HEADS
    offsets = jnp.arange(band_rows, dtype=jnp.int32)
    row_pos = (row_start + (offsets // SIDE)[None, :]).astype(jnp.float32)
    col_pos = (offsets % SIDE).astype(jnp.float32)[None, :]
    cos_part, sin_part = rope_tables(row_pos, col_pos, head_dim)
    cos_part = cos_part[:, :, None, :]
    sin_part = sin_part[:, :, None, :]
    bucket_hot = (buckets[:, None] == jnp.arange(BUCKETS, dtype=jnp.int32)[None, :]).astype(
        jnp.bfloat16
    )
    class_hot = (labels[:, None] == jnp.arange(CLASSES, dtype=jnp.int32)[None, :]).astype(
        jnp.bfloat16
    )
    cond = jnp.dot(bucket_hot, time_table, preferred_element_type=jnp.float32) + jnp.dot(
        class_hot, class_table, preferred_element_type=jnp.float32
    )
    cond_act = jax.nn.silu(cond).astype(jnp.bfloat16)
    mod_cols = jnp.einsum("id,ldm->lim", cond_act, ada_weight, preferred_element_type=jnp.float32)
    modulation = lax.all_to_all(mod_cols, "dp", split_axis=1, concat_axis=2, tiled=True)
    residual = latents.astype(jnp.float32)
    gathered_all = []
    layer_no = 0
    weights = gather_layer(layer_no, qkv_weight, proj_weight, gate_weight, up_weight, down_weight)
    gathered_all.append(weights)
    residual, stored = forward_layer(
        residual,
        modulation[layer_no],
        weights,
        query_gain[layer_no],
        key_gain[layer_no],
        cos_part,
        sin_part,
    )
    stored_all = [stored]
    result = residual.astype(jnp.bfloat16)
    resid_grad = out_grad.astype(jnp.float32)
    mod_grads = [None] * layer_count
    grad_shards = [None] * layer_count
    query_terms = [None] * layer_count
    key_terms = [None] * layer_count
    for layer_no in reversed(range(layer_count)):
        weights = gather_layer(
            layer_no, qkv_weight, proj_weight, gate_weight, up_weight, down_weight
        )
        resid_grad, mod_grad, own_grads, query_term, key_term = backward_layer(
            stored_all[layer_no],
            resid_grad,
            modulation[layer_no],
            weights,
            query_gain[layer_no],
            key_gain[layer_no],
            cos_part,
            sin_part,
        )
        mod_grads[layer_no] = mod_grad
        grad_shards[layer_no] = own_grads
        query_terms[layer_no] = query_term
        key_terms[layer_no] = key_term
    band_mod, band_query, band_key = lax.psum(
        (jnp.stack(mod_grads), jnp.stack(query_terms), jnp.stack(key_terms)), "seq"
    )
    mod_cols_grad = lax.all_to_all(
        band_mod.astype(jnp.bfloat16), "dp", split_axis=2, concat_axis=1, tiled=True
    )
    ada_grad = jnp.einsum(
        "id,lim->ldm", cond_act, mod_cols_grad, preferred_element_type=jnp.float32
    )
    cond_act_part = jnp.einsum(
        "lim,ldm->id", mod_cols_grad, ada_weight, preferred_element_type=jnp.float32
    )
    cond_act_grad, query_grad, key_grad = (
        lax.psum(cond_act_part.astype(jnp.bfloat16), "dp").astype(jnp.float32),
        lax.psum(band_query.astype(jnp.bfloat16), "dp").astype(jnp.float32),
        lax.psum(band_key.astype(jnp.bfloat16), "dp").astype(jnp.float32),
    )
    unused_cond, silu_back = jax.vjp(jax.nn.silu, cond)
    cond_grad = silu_back(cond_act_grad)[0]
    time_grad = jnp.einsum(
        "ib,id->bd", bucket_hot.astype(jnp.float32), cond_grad, precision=HIGHEST
    )
    class_grad = jnp.einsum(
        "ib,id->bd", class_hot.astype(jnp.float32), cond_grad, precision=HIGHEST
    )
    qkv_grad = jnp.stack([grad_shards[0][0]])
    proj_grad = jnp.stack([grad_shards[0][1]])
    gate_grad = jnp.stack([grad_shards[0][2]])
    up_grad = jnp.stack([grad_shards[0][3]])
    down_grad = jnp.stack([grad_shards[0][4]])
    return (
        result,
        resid_grad,
        time_grad,
        class_grad,
        ada_grad,
        qkv_grad,
        proj_grad,
        gate_grad,
        up_grad,
        down_grad,
        query_grad,
        key_grad,
    )


BF16 = jnp.bfloat16
F32 = jnp.float32
LOG2E = 1.4426950408889634
LN2 = 0.6931471805599453
DP_AXES = ("z", "y", "c")
SMALL = pl.CostEstimate(flops=1, bytes_accessed=1, transcendentals=0)


def kernel_call(kernel, **options):
    return pl.pallas_call(kernel, cost_estimate=SMALL, **options)


def together(*arrays):
    return lax.optimization_barrier(arrays)


def swap(values, axis):
    return lax.ppermute(values, axis, [(0, 1), (1, 0)])


def in_order(own, other, axis):
    first = lax.axis_index(axis) == 0
    return jnp.stack([jnp.where(first, own, other), jnp.where(first, other, own)])


def spread(values, axis):
    return in_order(values, swap(values, axis), axis)


def by_rows(values):
    return with_layout_constraint(values, Layout(major_to_minor=tuple(range(values.ndim))))


def gather_z(values):
    n_z = lax.axis_size("z")
    return lax.all_gather(values, "z", axis=0, tiled=True).reshape(n_z, *values.shape)


def add_low(*terms):
    total = terms[0].astype(F32)
    for term in terms[1:]:
        total = total + term.astype(F32)
    return total.astype(BF16)


def dot_f32(left, right, contract):
    return lax.dot_general(left, right, (contract, ((), ())), preferred_element_type=F32)


def piece_targets(pieces, at):
    for k, (array, z_first, x, y, c) in enumerate(pieces):
        for z in range(array.shape[0]):
            block = ((z_first + z) * 2 + (at[2] + y) % 2) * 2 + (at[0] + c) % 2
            yield k, z, (at[1] + x) % 2, block


def join_rows(pieces, first_row, rows):
    width = pieces[0][0].shape[-1]
    half = width // 2
    blocks = sum(piece[0].shape[0] for piece in pieces) // 2

    def kernel(at, *refs):
        out_ref, buf, sems = refs[len(pieces) :]
        copies = []
        for k, z, x, block in piece_targets(pieces, at):
            copy = pltpu.make_async_copy(
                refs[k].at[z, pl.ds(first_row, rows)], buf.at[x, block], sems.at[x, block]
            )
            copy.start()
            copies.append(copy)
        for copy in copies:
            copy.wait()
        for block in range(blocks):
            out_ref[block] = jnp.concatenate([buf[0, block][:, half:], buf[1, block][:, half:]], axis=1)

    return kernel_call(
        kernel,
        grid_spec=pltpu.PrefetchScalarGridSpec(
            num_scalar_prefetch=1,
            grid=(1,),
            in_specs=[pl.BlockSpec(memory_space=pl.ANY)] * len(pieces),
            out_specs=[pl.BlockSpec((blocks, rows, width), lambda i, at: (0, 0, 0))],
            scratch_shapes=[pltpu.VMEM((2, blocks, rows, width), BF16), pltpu.SemaphoreType.DMA((2, blocks))],
        ),
        out_shape=[jax.ShapeDtypeStruct((blocks, rows, width), BF16)],
        compiler_params=pltpu.CompilerParams(vmem_limit_bytes=24 << 20),
        name="join_rows",
    )(place(), *[piece[0] for piece in pieces])[0]


def qkv_heads(normed, pieces, cos_t, sin_t, gains_t, head_dim, band, before=()):
    seq_len, width = normed.shape
    heads = HEADS
    group = 3
    rows_all = group * head_dim
    half = width // 2
    sent = pieces[0][0].shape[1]
    q_scale = head_dim**-0.5 * LOG2E
    side = pieces[0][4]
    steps = sum(piece[0].shape[0] for piece in pieces) // 2
    n_in = len(pieces)

    def kernel(at, norm_ref, cos_ref, sin_ref, gain_ref, *refs):
        out_ref, hat_ref, fac_ref, whole_ref, acc_ref, buf, sems = refs[n_in + len(before) :]

        @pl.when(pl.program_id(0) == 0)
        def _():
            for k, z, x, block in piece_targets(pieces, at):
                local = block // 2
                pltpu.make_async_copy(refs[k].at[z], buf.at[x, local], sems.at[x, local]).start()

        local = pl.program_id(0)
        step = 2 * local + (at[0] + side) % 2
        for x in range(2):
            pltpu.make_async_copy(refs[0].at[0], buf.at[x, local], sems.at[x, local]).wait()
        low, high = buf[0, local], buf[1, local]
        whole_ref[:sent] = jnp.concatenate([low[:, :half], high[:, :half]], axis=1)
        whole_ref[sent:] = jnp.concatenate([low[: rows_all - sent, half:], high[: rows_all - sent, half:]], axis=1)
        acc_ref[...] = dot_f32(whole_ref[...], norm_ref[...], ((1,), (1,)))
        for i in range(group):
            head = step * group + i
            rows = pl.ds(i * head_dim, head_dim)

            @pl.when(head < 2 * heads)
            def _():
                values = acc_ref[rows, :]
                fac = lax.rsqrt(jnp.mean(values * values, axis=0, keepdims=True) + EPS)
                hat = values * fac
                gained = hat * jnp.where(head < heads, gain_ref[:, 0:1] * q_scale, gain_ref[:, 1:2])
                turned = jnp.concatenate([gained[head_dim // 2 :], gained[: head_dim // 2]], axis=0)
                out_ref[i] = (gained * cos_ref[...] + turned * sin_ref[...]).astype(BF16)
                hat_ref[i] = hat[:, :band].astype(BF16)
                fac_ref[i] = fac[:, :band]

            @pl.when(head >= 2 * heads)
            def _():
                out_ref[i] = acc_ref[rows, :].astype(BF16)
                hat_ref[i] = jnp.zeros((head_dim, band), BF16)
                fac_ref[i] = jnp.zeros((1, band), F32)

    whole = lambda i, at: (0, 0)
    return kernel_call(
        kernel,
        grid_spec=pltpu.PrefetchScalarGridSpec(
            num_scalar_prefetch=1,
            grid=(steps,),
            in_specs=[
                pl.BlockSpec((seq_len, width), whole),
                pl.BlockSpec((head_dim, seq_len), whole),
                pl.BlockSpec((head_dim, seq_len), whole),
                pl.BlockSpec((head_dim, 2), whole),
            ]
            + [pl.BlockSpec(memory_space=pl.ANY)] * (n_in + len(before)),
            out_specs=[
                pl.BlockSpec((group, head_dim, seq_len), lambda i, at: (2 * i + (at[0] + side) % 2, 0, 0)),
                pl.BlockSpec((group, head_dim, band), lambda i, at: (2 * i + (at[0] + side) % 2, 0, 0)),
                pl.BlockSpec((group, 1, band), lambda i, at: (2 * i + (at[0] + side) % 2, 0, 0)),
                pl.BlockSpec((rows_all, width), lambda i, at: (2 * i + (at[0] + side) % 2, 0)),
            ],
            scratch_shapes=[
                pltpu.VMEM((rows_all, seq_len), F32),
                pltpu.VMEM((2, steps, sent, width), BF16),
                pltpu.SemaphoreType.DMA((2, steps)),
            ],
        ),
        out_shape=[
            jax.ShapeDtypeStruct((3 * heads, head_dim, seq_len), BF16),
            pltpu.HBM((3 * heads, head_dim, band), BF16),
            pltpu.HBM((3 * heads, 1, band), F32),
            pltpu.HBM((3 * width, width), BF16),
        ],
        input_output_aliases={5 + n_in + k: k for k in range(len(before))},
        compiler_params=pltpu.CompilerParams(vmem_limit_bytes=32 << 20),
        name="qkv_heads",
    )(place(), normed, cos_t, sin_t, gains_t, *[piece[0] for piece in pieces], *before)


def attention_forward(qkv, heads, band):
    _, head_dim, seq_len = qkv.shape

    def kernel(q_ref, k_ref, v_ref, out_ref, mass_ref):
        scores = dot_f32(k_ref[0], q_ref[0], ((0,), (0,)))
        weights = jnp.exp2(scores)
        mass = jnp.sum(weights, axis=0, keepdims=True)
        mixed = dot_f32(v_ref[0], weights.astype(BF16), ((1,), (0,)))
        out_ref[0] = (mixed / mass).astype(BF16)
        mass_ref[0] = jnp.log2(mass)

    return kernel_call(
        kernel,
        grid=(heads,),
        in_specs=[
            pl.BlockSpec((1, head_dim, band), lambda h: (h, 0, 0)),
            pl.BlockSpec((1, head_dim, seq_len), lambda h: (heads + h, 0, 0)),
            pl.BlockSpec((1, head_dim, seq_len), lambda h: (2 * heads + h, 0, 0)),
        ],
        out_specs=[
            pl.BlockSpec((1, head_dim, band), lambda h: (h, 0, 0)),
            pl.BlockSpec((1, 1, band), lambda h: (h, 0, 0)),
        ],
        out_shape=[
            jax.ShapeDtypeStruct((heads, head_dim, band), BF16),
            jax.ShapeDtypeStruct((heads, 1, band), F32),
        ],
        compiler_params=pltpu.CompilerParams(vmem_limit_bytes=14 << 20),
        name="attention_forward",
    )(qkv, qkv, qkv)


def attention_back_own(qkv, out_grad, log_mass, delta, heads, band):
    _, head_dim, seq_len = qkv.shape

    def kernel(q_ref, k_ref, v_ref, grad_ref, mass_ref, delta_ref, dq_ref, dk_ref, dv_ref):
        grad = grad_ref[0]
        scores = dot_f32(k_ref[0], q_ref[0], ((0,), (0,)))
        probs = jnp.exp2(scores - mass_ref[0])
        prob_grad = dot_f32(v_ref[0], grad, ((0,), (0,)))
        score_grad = (probs * (prob_grad - delta_ref[0])).astype(BF16)
        dq_ref[0] = dot_f32(k_ref[0], score_grad, ((1,), (0,)))
        dk_ref[0] = dot_f32(q_ref[0], score_grad[:band], ((1,), (1,)))
        dv_ref[0] = dot_f32(grad, probs[:band].astype(BF16), ((1,), (1,)))

    one = pl.BlockSpec((1, head_dim, band), lambda h: (h, 0, 0))
    row = pl.BlockSpec((1, 1, band), lambda h: (h, 0, 0))
    return kernel_call(
        kernel,
        grid=(heads,),
        in_specs=[
            one,
            pl.BlockSpec((1, head_dim, seq_len), lambda h: (heads + h, 0, 0)),
            pl.BlockSpec((1, head_dim, seq_len), lambda h: (2 * heads + h, 0, 0)),
            one,
            row,
            row,
        ],
        out_specs=[one, one, one],
        out_shape=[pltpu.HBM((heads, head_dim, band), F32)] * 3,
        compiler_params=pltpu.CompilerParams(vmem_limit_bytes=16 << 20),
        name="attention_back_own",
    )(qkv, qkv, qkv, out_grad, log_mass, delta)


def attention_back_other(
    qkv, hat, fac, cos_t, sin_t, gains_t, dq, dk, dv, grads, mass, delta, heads, band
):
    _, head_dim, seq_len = qkv.shape
    inv_root = head_dim**-0.5
    early = grads[0].shape[0]

    def kernel(
        q_ref, k_ref, v_ref, hq_ref, hk_ref, fq_ref, fk_ref, cos_ref, sin_ref, gain_ref,
        dq_ref, dk_ref, dv_ref, low_ref, high_ref, mass_ref, delta_ref, out_ref, gq_ref, gk_ref,
    ):
        grad = jnp.where(pl.program_id(0) < early, low_ref[0], high_ref[0])
        scores = dot_f32(k_ref[0], q_ref[0], ((0,), (0,)))
        probs = jnp.exp2(scores - mass_ref[0])
        prob_grad = dot_f32(v_ref[0], grad, ((0,), (0,)))
        score_grad = (probs * (prob_grad - delta_ref[0])).astype(BF16)
        key_grad = (dk_ref[0] + dot_f32(q_ref[0], score_grad, ((1,), (1,)))) * LN2
        value_grad = dv_ref[0] + dot_f32(grad, probs.astype(BF16), ((1,), (1,)))
        query_grad = dq_ref[0] * inv_root

        def back(turned_grad, hat, fac, gain):
            spun = turned_grad * sin_ref[...]
            spun = jnp.concatenate([spun[head_dim // 2 :], spun[: head_dim // 2]], axis=0)
            gained_grad = turned_grad * cos_ref[...] + spun
            gain_grad = jnp.sum(gained_grad * hat, axis=1, keepdims=True)
            hat_grad = gained_grad * gain
            along = jnp.mean(hat_grad * hat, axis=0, keepdims=True)
            return (fac * (hat_grad - hat * along)).astype(BF16), gain_grad

        out_ref[0, 0], gq_ref[0] = back(query_grad, hq_ref[0].astype(F32), fq_ref[0], gain_ref[:, 0:1])
        out_ref[1, 0], gk_ref[0] = back(key_grad, hk_ref[0].astype(F32), fk_ref[0], gain_ref[:, 1:2])
        out_ref[2, 0] = value_grad.astype(BF16)

    one = pl.BlockSpec((1, head_dim, band), lambda h: (h, 0, 0))
    row = pl.BlockSpec((1, 1, band), lambda h: (h, 0, 0))
    key_one = pl.BlockSpec((1, head_dim, band), lambda h: (heads + h, 0, 0))
    key_row = pl.BlockSpec((1, 1, band), lambda h: (heads + h, 0, 0))
    table = pl.BlockSpec((head_dim, band), lambda h: (0, 0))
    column = pl.BlockSpec((1, head_dim, 1), lambda h: (h, 0, 0))
    return kernel_call(
        kernel,
        grid=(heads,),
        in_specs=[
            pl.BlockSpec((1, head_dim, band), lambda h: (h, 0, 1)),
            key_one,
            pl.BlockSpec((1, head_dim, band), lambda h: (2 * heads + h, 0, 0)),
            one, key_one, row, key_row, table, table,
            pl.BlockSpec((head_dim, 2), lambda h: (0, 0)),
            one, one, one,
            pl.BlockSpec((1, head_dim, band), lambda h: (jnp.minimum(h, early - 1), 0, 0)),
            pl.BlockSpec((1, head_dim, band), lambda h: (jnp.maximum(h - early, 0), 0, 0)),
            row, row,
        ],
        out_specs=[pl.BlockSpec((3, 1, head_dim, band), lambda h: (0, h, 0, 0)), column, column],
        out_shape=[
            jax.ShapeDtypeStruct((3, heads, head_dim, band), BF16),
            jax.ShapeDtypeStruct((heads, head_dim, 1), F32),
            jax.ShapeDtypeStruct((heads, head_dim, 1), F32),
        ],
        compiler_params=pltpu.CompilerParams(vmem_limit_bytes=14 << 20),
        name="attention_back_other",
    )(*[pltpu.with_memory_space_constraint(qkv, pltpu.HBM)] * 3, hat, hat, fac, fac, cos_t, sin_t, gains_t,
      *[pltpu.with_memory_space_constraint(v, pltpu.HBM) for v in (dq, dk, dv)], *grads, mass, delta)


def mlp(mid, mlp_grad, pieces, down_own, down_other):
    band, width = mlp_grad.shape
    rows = pieces[0][0].shape[1]
    half = width // 2
    blocks = sum(piece[0].shape[0] for piece in pieces) // 2
    steps = 4
    per = blocks // steps
    units = per * rows
    chunk = band // 2
    n_z, _, _, down_rows, down_width = down_own.shape

    def kernel(at, mid_ref, mg_ref, *refs):
        downs = refs[len(pieces) : len(pieces) + 2]
        hid_ref, gg_ref, ug_ref, out_ref, grad_ref, buf, down_buf, sems, down_sems = refs[len(pieces) + 2 :]
        step = pl.program_id(0)

        @pl.when(step == 0)
        def _():
            for x in range(2):
                for z in range(n_z):
                    for y in range(2):
                        for c in range(2):
                            block = (z * 2 + y) * 2 + (at[0] + c) % 2
                            target = down_buf.at[x, pl.ds(pl.multiple_of(block * down_rows, 8), down_rows)]
                            pltpu.make_async_copy(downs[c].at[z, y, x], target, down_sems.at[x, block]).start()
            for k, z, x, block in piece_targets(pieces, at):
                pltpu.make_async_copy(refs[k].at[z], buf.at[x, block], sems.at[x, block]).start()
            out_ref[...] = jnp.zeros_like(out_ref)
            grad_ref[...] = jnp.zeros_like(grad_ref)

        for b in range(per):
            for x in range(2):
                block = step * per + b
                pltpu.make_async_copy(refs[0].at[0], buf.at[x, block], sems.at[x, block]).wait()
        @pl.when(step % 2 == 0)
        def _():
            for block in range(4 * n_z):
                target = down_buf.at[step // 2, pl.ds(block * down_rows, down_rows)]
                pltpu.make_async_copy(downs[0].at[0, 0, 0], target, down_sems.at[step // 2, block]).wait()

        low = buf[0, pl.ds(step * per, per)].reshape(units, width)
        high = buf[1, pl.ds(step * per, per)].reshape(units, width)
        gate = jnp.concatenate([low[:, :half], high[:, :half]], axis=1)
        up = jnp.concatenate([low[:, half:], high[:, half:]], axis=1)
        down = down_buf[step // 2, :, pl.ds(pl.multiple_of(step % 2 * units, 128), units)]
        nt, nn = ((1,), (1,)), ((1,), (0,))
        for part in range(2):
            at_rows = pl.ds(part * chunk, chunk)
            mid = mid_ref[at_rows, :]
            gate_pre = dot_f32(mid, gate, nt)
            up_pre = dot_f32(mid, up, nt)
            hidden_grad = dot_f32(mg_ref[at_rows, :], down, nn)
            sig = 1.0 / (1.0 + jnp.exp(-gate_pre))
            act = gate_pre * sig
            hidden = (act * up_pre).astype(BF16)
            gate_grad = (hidden_grad * up_pre * (sig * (1.0 + gate_pre * (1.0 - sig)))).astype(BF16)
            up_grad = (hidden_grad * act).astype(BF16)
            hid_ref[at_rows, :] = hidden
            gg_ref[:, at_rows] = gate_grad.T
            ug_ref[:, at_rows] = up_grad.T
            out_ref[at_rows, :] += dot_f32(hidden, down, nt)
            grad_ref[at_rows, :] += dot_f32(gate_grad, gate, nn) + dot_f32(up_grad, up, nn)

    whole = lambda i, at: (0, 0)
    once = pl.Buffered(1)
    return kernel_call(
        kernel,
        grid_spec=pltpu.PrefetchScalarGridSpec(
            num_scalar_prefetch=1,
            grid=(steps,),
            in_specs=[
                pl.BlockSpec((band, width), whole, pipeline_mode=once),
                pl.BlockSpec((band, width), whole, pipeline_mode=once),
            ]
            + [pl.BlockSpec(memory_space=pl.ANY)] * (len(pieces) + 2),
            out_specs=[
                pl.BlockSpec((band, units), lambda i, at: (0, i)),
                pl.BlockSpec((units, band), lambda i, at: (i, 0)),
                pl.BlockSpec((units, band), lambda i, at: (i, 0)),
                pl.BlockSpec((band, width), whole, pipeline_mode=once),
                pl.BlockSpec((band, width), whole, pipeline_mode=once),
            ],
            scratch_shapes=[
                pltpu.VMEM((2, blocks, rows, width), BF16),
                pltpu.VMEM((2, width, down_width), BF16),
                pltpu.SemaphoreType.DMA((2, blocks)),
                pltpu.SemaphoreType.DMA((2, 4 * n_z)),
            ],
        ),
        out_shape=[
            jax.ShapeDtypeStruct((band, blocks * rows), BF16),
            jax.ShapeDtypeStruct((blocks * rows, band), BF16),
            jax.ShapeDtypeStruct((blocks * rows, band), BF16),
            jax.ShapeDtypeStruct((band, width), F32),
            jax.ShapeDtypeStruct((band, width), F32),
        ],
        compiler_params=pltpu.CompilerParams(vmem_limit_bytes=56 << 20),
        name="mlp",
    )(place(), mid, mlp_grad, *[piece[0] for piece in pieces], down_own, down_other)


def after_attention(attended_t, proj_t, residual_low, modulation):
    width, band = attended_t.shape
    half = width // 2
    block = 128

    def kernel(att_ref, proj_ref, low_ref, mod_ref, branch_ref, middle_ref, normed_ref, mid_ref, att_out_ref):
        branch = dot_f32(att_ref[...], proj_ref[...], ((0,), (1,)))
        middle = low_ref[...].astype(F32) + mod_ref[2:3, :] * branch
        normed = modulate(middle, mod_ref[3:4, :], mod_ref[4:5, :]).astype(BF16)
        attended = att_ref[...].T
        branch_ref[...] = branch.astype(BF16)
        middle_ref[...] = middle
        normed_ref[...] = normed
        for x in range(2):
            mid_ref[x] = normed[:, x * half : (x + 1) * half]
            att_out_ref[x] = attended[:, x * half : (x + 1) * half]

    rows = pl.BlockSpec((block, width), lambda i: (i, 0))
    halves = pl.BlockSpec((2, block, half), lambda i: (0, i, 0))
    return kernel_call(
        kernel,
        grid=(band // block,),
        in_specs=[
            pl.BlockSpec((width, block), lambda i: (0, i)),
            pl.BlockSpec((width, width), lambda i: (0, 0)),
            rows,
            pl.BlockSpec((6, width), lambda i: (0, 0)),
        ],
        out_specs=[rows, rows, rows, halves, halves],
        out_shape=[
            pltpu.HBM((band, width), BF16),
            pltpu.HBM((band, width), F32),
            jax.ShapeDtypeStruct((band, width), BF16),
            jax.ShapeDtypeStruct((2, band, half), BF16),
            jax.ShapeDtypeStruct((2, band, half), BF16),
        ],
        compiler_params=pltpu.CompilerParams(vmem_limit_bytes=20 << 20),
        name="after_attention",
    )(*[pltpu.with_memory_space_constraint(v, pltpu.HBM) for v in (attended_t, proj_t, residual_low)], modulation)


def middle_back(normed_mid_grad, middle, out_grad, branch, mlp_out, proj_t, attended_t, modulation):
    band, width = middle.shape
    half = width // 2
    head_dim = width // HEADS
    block = 128

    def kernel(
        normed_grad_ref, mid_ref, out_ref, branch_ref, mlp_ref, proj_ref, att_ref, mod_ref,
        grad_ref, bg_ref, att_grad_ref, delta_ref, result_ref, sums_ref,
    ):
        @pl.when(pl.program_id(0) == 0)
        def _():
            sums_ref[...] = jnp.zeros_like(sums_ref)

        normed_grad = normed_grad_ref[...]
        middle, grad, mlp_out = mid_ref[...], out_ref[...].astype(F32), mlp_ref[...]
        fac = norm_factor(middle)
        hat = middle * fac
        hat_grad = normed_grad * (1.0 + mod_ref[4:5, :])
        along = jnp.mean(hat_grad * hat, axis=-1, keepdims=True)
        mid_grad = grad + fac * (hat_grad - hat * along)
        branch_grad = (mod_ref[2:3, :] * mid_grad).astype(BF16)
        attended_grad = dot_f32(branch_grad, proj_ref[...], ((1,), (0,))).astype(BF16).T
        grad_ref[...] = mid_grad
        bg_ref[...] = branch_grad.T
        att_grad_ref[...] = attended_grad
        both = attended_grad.astype(F32) * att_ref[...].astype(F32)
        delta_ref[...] = jnp.sum(both.reshape(HEADS, head_dim, block), axis=1, keepdims=True)
        result_ref[...] = (middle + mod_ref[5:6, :] * mlp_out).astype(BF16)
        sums_ref[0:1, :] += jnp.sum(normed_grad, axis=0, keepdims=True)
        sums_ref[1:2, :] += jnp.sum(normed_grad * hat, axis=0, keepdims=True)
        sums_ref[2:3, :] += jnp.sum(mid_grad * branch_ref[...].astype(F32), axis=0, keepdims=True)
        sums_ref[3:4, :] += jnp.sum(grad * mlp_out, axis=0, keepdims=True)

    rows = pl.BlockSpec((block, width), lambda i: (i, 0))
    columns = pl.BlockSpec((width, block), lambda i: (0, i))
    return kernel_call(
        kernel,
        grid=(band // block,),
        in_specs=[
            rows, rows, rows, rows, rows,
            pl.BlockSpec((width, width), lambda i: (0, 0)),
            columns,
            pl.BlockSpec((6, width), lambda i: (0, 0)),
        ],
        out_specs=[
            rows, columns, columns,
            pl.BlockSpec((HEADS, 1, block), lambda i: (0, 0, i)),
            rows,
            pl.BlockSpec((8, width), lambda i: (0, 0)),
        ],
        out_shape=[
            pltpu.HBM((band, width), F32),
            jax.ShapeDtypeStruct((width, band), BF16),
            jax.ShapeDtypeStruct((width, band), BF16),
            jax.ShapeDtypeStruct((HEADS, 1, band), F32),
            jax.ShapeDtypeStruct((band, width), BF16),
            jax.ShapeDtypeStruct((8, width), F32),
        ],
        compiler_params=pltpu.CompilerParams(vmem_limit_bytes=20 << 20),
        name="middle_back",
    )(normed_mid_grad, middle, out_grad, branch, mlp_out, proj_t, attended_t, modulation)


def input_back(projected_t, qkv_t, latents, mid_grad, modulation):
    inner, band = projected_t.shape
    width = qkv_t.shape[1]
    block = 128

    def kernel(left_ref, weight_ref, low_ref, grad_ref, mod_ref, out_ref, sums_ref):
        @pl.when(pl.program_id(0) == 0)
        def _():
            sums_ref[...] = jnp.zeros_like(sums_ref)

        normed_grad = dot_f32(left_ref[...], weight_ref[...], ((0,), (0,)))
        residual = low_ref[...].astype(F32)
        fac = norm_factor(residual)
        hat = residual * fac
        hat_grad = normed_grad * (1.0 + mod_ref[1:2, :])
        along = jnp.mean(hat_grad * hat, axis=-1, keepdims=True)
        out_ref[...] = grad_ref[...] + fac * (hat_grad - hat * along)
        sums_ref[0:1, :] += jnp.sum(normed_grad, axis=0, keepdims=True)
        sums_ref[1:2, :] += jnp.sum(normed_grad * hat, axis=0, keepdims=True)

    rows = pl.BlockSpec((block, width), lambda i: (i, 0))
    return kernel_call(
        kernel,
        grid=(band // block,),
        in_specs=[
            pl.BlockSpec((inner, block), lambda i: (0, i)),
            pl.BlockSpec((inner, width), lambda i: (0, 0), pipeline_mode=pl.Buffered(1)),
            rows,
            rows,
            pl.BlockSpec((6, width), lambda i: (0, 0)),
        ],
        out_specs=[rows, pl.BlockSpec((8, width), lambda i: (0, 0))],
        out_shape=[jax.ShapeDtypeStruct((band, width), F32), jax.ShapeDtypeStruct((8, width), F32)],
        compiler_params=pltpu.CompilerParams(vmem_limit_bytes=24 << 20),
        name="input_back",
    )(projected_t, *[pltpu.with_memory_space_constraint(v, pltpu.HBM) for v in (qkv_t, latents, mid_grad)], modulation)


def place():
    return jnp.stack([lax.axis_index(axis) for axis in ("c", "x", "y")]).astype(jnp.int32)


def terms(lefts, right, rows, side, received=None, z_first=0, n_z=4, y=(0, 1), order=(0, 1), stacked=True, split=0, kind=jax.ShapeDtypeStruct):
    patches = right.shape[0] if right.ndim == 2 else right.shape[1]
    wide = right.ndim == 2
    each = right.shape[-1] // 2 if wide else right.shape[-1]
    width = each * len(lefts)
    count = split or len(y) * n_z
    n = len(lefts)

    def left_map(i, at):
        if split:
            return (i, 0)
        z = z_first + i % n_z
        return ((z * 2 + (y[0] + i // n_z + at[2]) % 2) * 2 + (at[0] + side) % 2, 0)

    def right_spec(h):
        if wide:
            return pl.BlockSpec((patches, each), lambda i, at: (0, (at[1] + h) % 2))
        return pl.BlockSpec((1, patches, each), lambda i, at: ((at[1] + h) % 2, 0, 0))

    def kernel(at, *refs):
        rights, outs = refs[n : n + 2], refs[n + 2 :]
        if received is not None:
            got, outs = refs[n + 2 : n + 4], refs[n + 4 :]
        for k in range(2):
            half = rights[k][...] if wide else rights[k][0]
            values = [dot_f32(refs[m][...], half, ((1,), (0,))) for m in range(n)]
            value = values[0] if n == 1 else jnp.concatenate(values, axis=1)
            if received is not None:
                value = value + got[k][0, 0].astype(F32)
            if not stacked:
                outs[k][0] = value.astype(BF16)
            elif split:
                outs[0][0, k] = value.astype(BF16)
            else:
                outs[0][k, 0] = value.astype(BF16)

    received_specs = []
    if received is not None:
        skip = 0 if split else y[0] * n_z
        received_specs = [
            pl.BlockSpec((1, 1, rows, width), lambda i, at, k=k: (i, k, 0, 0) if split else (k, i + skip, 0, 0))
            for k in range(2)
        ]
    if stacked and split:
        out_shape = [kind((count, 2, rows, width), BF16)]
        out_specs = [pl.BlockSpec((1, 2, rows, width), lambda i, at: (i, 0, 0, 0))]
    elif stacked:
        out_shape = [kind((2, count, rows, width), BF16)]
        out_specs = [pl.BlockSpec((2, 1, rows, width), lambda i, at: (0, i, 0, 0))]
    else:
        out_shape = [jax.ShapeDtypeStruct((count, rows, width), BF16)] * 2
        out_specs = [pl.BlockSpec((1, rows, width), lambda i, at: (i, 0, 0))] * 2
    outs = kernel_call(
        kernel,
        grid_spec=pltpu.PrefetchScalarGridSpec(
            num_scalar_prefetch=1,
            grid=(count,),
            in_specs=[pl.BlockSpec((rows, patches), left_map)] * n
            + [right_spec(h) for h in order]
            + received_specs,
            out_specs=out_specs,
        ),
        out_shape=out_shape,
        compiler_params=pltpu.CompilerParams(vmem_limit_bytes=12 << 20),
        name="terms",
    )(place(), *lefts, right, right, *([received] * 2 if received is not None else []))
    return outs[0] if stacked else outs


def last_terms(left, right, rows, cut, received):
    patches, width = left.shape[-1], right.shape[-1]
    n_z = 4
    late = rows - cut

    def row_of(i):
        return 1 - i // n_z

    def kernel(at, left_ref, own_ref, other_ref, r0_ref, r1_ref, keep_ref, send_ref, up_send_ref, up_keep_ref):
        values = [
            (dot_f32(left_ref[...], ref[0], ((1,), (0,))) + got[0, 0].astype(F32)).astype(BF16)
            for ref, got in ((own_ref, r0_ref), (other_ref, r1_ref))
        ]
        keep_ref[0] = values[0][:cut]
        send_ref[0] = values[1][:cut]

        @pl.when(pl.program_id(0) < n_z)
        def _():
            for k in range(2):
                up_send_ref[1 - k, 0] = values[k][cut:]

        @pl.when(pl.program_id(0) >= n_z)
        def _():
            for k in range(2):
                up_keep_ref[1 - k, 0] = values[k][cut:]

    def got(h):
        return pl.BlockSpec((1, 1, rows, width), lambda i, at: (h, row_of(i) * n_z + i % n_z, 0, 0))

    early_spec = pl.BlockSpec((1, cut, width), lambda i, at: (row_of(i) * n_z + i % n_z, 0, 0))
    return kernel_call(
        kernel,
        grid_spec=pltpu.PrefetchScalarGridSpec(
            num_scalar_prefetch=1,
            grid=(2 * n_z,),
            in_specs=[
                pl.BlockSpec(
                    (rows, patches), lambda i, at: ((i % n_z * 2 + (row_of(i) + at[2]) % 2) * 2 + at[0], 0)
                ),
                pl.BlockSpec((1, patches, width), lambda i, at: (at[1], 0, 0)),
                pl.BlockSpec((1, patches, width), lambda i, at: ((at[1] + 1) % 2, 0, 0)),
                got(0),
                got(1),
            ],
            out_specs=[
                early_spec,
                early_spec,
                pl.BlockSpec((2, 1, late, width), lambda i, at: (0, jnp.minimum(i, n_z - 1), 0, 0)),
                pl.BlockSpec((2, 1, late, width), lambda i, at: (0, jnp.maximum(i - n_z, 0), 0, 0)),
            ],
        ),
        out_shape=[jax.ShapeDtypeStruct((2 * n_z, cut, width), BF16)] * 2
        + [jax.ShapeDtypeStruct((2, n_z, late, width), BF16)] * 2,
        compiler_params=pltpu.CompilerParams(vmem_limit_bytes=12 << 20),
        name="last_terms",
    )(place(), left, right, right, received, received)


def split_rows(left_t, z_first):
    n_z, patches = lax.axis_size("z"), left_t.shape[-1]
    blocks = left_t.reshape(n_z, 2, 2, -1, patches)
    core, row = lax.axis_index("c"), lax.axis_index("y")

    def part(which):
        picked = lax.dynamic_index_in_dim(blocks, which, 2, keepdims=False)
        own = lax.dynamic_index_in_dim(picked, row, 1, keepdims=False)
        other = lax.dynamic_index_in_dim(picked, 1 - row, 1, keepdims=False)
        return jnp.stack([own, other], axis=1 if z_first else 0).reshape(-1, patches)

    return part(1 - core), part(core)


def summed_over(values, axes, size):
    low = values.astype(BF16)
    parts = [low] + [lax.ppermute(low, axes, [(i, i ^ hop) for i in range(size)]) for hop in range(1, size)]
    parts = [part.astype(F32) for part in parts]
    while len(parts) > 1:
        parts = [left + right for left, right in zip(parts[::2], parts[1::2])]
    return parts[0]


def spread_rows(hots, values):
    items, width = values.shape
    count = hots[0].shape[1]
    block = 384

    def kernel(values_ref, *refs):
        rest, parts = values_ref[...], []
        for _ in range(3):
            high = rest.astype(BF16)
            parts.append(high)
            rest = rest - high.astype(F32)
        for hot_ref, out_ref in zip(refs[: len(hots)], refs[len(hots) :]):
            hot = hot_ref[...]
            out_ref[...] = sum(dot_f32(hot, part, ((0,), (0,))) for part in parts)

    return kernel_call(
        kernel,
        grid=(width // block,),
        in_specs=[pl.BlockSpec((items, block), lambda i: (0, i))]
        + [pl.BlockSpec((items, count), lambda i: (0, 0))] * len(hots),
        out_specs=[pl.BlockSpec((count, block), lambda i: (0, i))] * len(hots),
        out_shape=[jax.ShapeDtypeStruct((count, width), F32)] * len(hots),
        compiler_params=pltpu.CompilerParams(vmem_limit_bytes=16 << 20),
        name="spread_rows",
    )(values, *hots)


def in_float32(values, rows, columns):
    sizes = [(r, c) for r in rows for c in columns]

    def kernel(in_ref, *out_refs):
        at_row = 0
        for m, r in enumerate(rows):
            at_column = 0
            for n, c in enumerate(columns):
                part = in_ref[at_row : at_row + r, at_column : at_column + c]
                out_refs[m * len(columns) + n][...] = part.astype(F32)
                at_column += c
            at_row += r

    return kernel_call(
        kernel,
        out_shape=[jax.ShapeDtypeStruct(size, F32) for size in sizes],
        compiler_params=pltpu.CompilerParams(vmem_limit_bytes=8 << 20),
        name="in_float32",
    )(values)


def outer_terms(left, right):
    def kernel(left_ref, right_ref, out_ref):
        out_ref[...] = dot_f32(left_ref[...], right_ref[...], ((0,), (0,)))

    return kernel_call(
        kernel,
        out_shape=[jax.ShapeDtypeStruct((left.shape[1], right.shape[1]), F32)],
        compiler_params=pltpu.CompilerParams(vmem_limit_bytes=8 << 20),
        name="outer_terms",
    )(left, right)[0]


def fast_shards(
    latents, out_grad, time_table, class_table, buckets, labels, row_start,
    ada_weight, qkv_weight, proj_weight, gate_weight, up_weight, down_weight, query_gain, key_gain,
):
    band, width = latents.shape[1:]
    head_dim = width // HEADS
    lat, out_g = latents[0], out_grad[0]
    half = width // 2
    n_z = lax.axis_size("z")

    qkv_s, proj_s = qkv_weight[0].T, proj_weight[0].T
    gate_s, up_s, down_s = gate_weight[0].T, up_weight[0].T, by_rows(down_weight[0].T)
    qkv_rows, proj_rows, gate_rows = qkv_s.shape[0], proj_s.shape[0], gate_s.shape[0]
    cut = (qkv_rows + proj_rows) // 2
    first = by_rows(jnp.concatenate([qkv_s[:cut], jnp.concatenate([qkv_s[cut:], proj_s])], axis=1))
    second = by_rows(jnp.concatenate([gate_s, up_s], axis=1))

    first_z = gather_z(first)
    second_z = gather_z(second)
    start_other = swap(row_start.astype(F32), "x")
    (down_r,) = together(swap(down_s, "x"))
    down_x = in_order(down_s, down_r, "x")
    down_x, lat_x = together(down_x, lat)
    lat_other = swap(lat_x, "x")
    down_r = swap(down_x, "y")

    bucket_hot = (buckets[:, None] == jnp.arange(BUCKETS, dtype=jnp.int32)[None, :]).astype(BF16)
    class_hot = (labels[:, None] == jnp.arange(CLASSES, dtype=jnp.int32)[None, :]).astype(BF16)
    cond = jnp.dot(bucket_hot, time_table, preferred_element_type=F32) + jnp.dot(
        class_hot, class_table, preferred_element_type=F32
    )
    cond_act = jax.nn.silu(cond).astype(BF16)
    mod_cols = jnp.dot(cond_act, ada_weight[0], preferred_element_type=F32)

    offsets = jnp.arange(band, dtype=jnp.int32)
    rows_in = (offsets // SIDE).astype(F32)
    row_pos = jnp.concatenate([row_start.astype(F32)[0, 0] + rows_in, start_other[0, 0] + rows_in])
    col_pos = jnp.tile((offsets % SIDE).astype(F32), 2)
    quarter = head_dim // 4
    frequency = THETA ** (-jnp.arange(quarter, dtype=F32) / quarter)
    angles = jnp.concatenate([frequency[:, None] * row_pos[None], frequency[:, None] * col_pos[None]])
    cos_h, sin_h = jnp.cos(angles), jnp.sin(angles)
    cos_t = jnp.concatenate([cos_h, cos_h])
    sin_t = jnp.concatenate([-sin_h, sin_h])
    gains_t = jnp.concatenate([query_gain, key_gain]).T
    first_z, lat_other, down_r, mod_cols, cos_t, sin_t = together(first_z, lat_other, down_r, mod_cols, cos_t, sin_t)

    a, b = by_rows(first_z[:2]), by_rows(first_z[2:])
    a_y, b_x, a_c, b_c = swap(a, "y"), swap(b, "x"), swap(a, "c"), swap(b, "c")
    down_z = gather_z(in_order(down_x, down_r, "y").reshape(-1, down_x.shape[-1]))
    modulation = lax.all_to_all(mod_cols, DP_AXES, split_axis=0, concat_axis=1, tiled=True)
    a_y, b_x, a_c, b_c, modulation = together(a_y, b_x, a_c, b_c, modulation)

    a_x, b_y, a_yc, b_xc = swap(a, "x"), swap(b, "y"), swap(a_y, "c"), swap(b_x, "c")
    mods = modulation.reshape(6, width)
    shift_attn, scale_attn, gate_attn, shift_mlp, scale_mlp, gate_mlp = jnp.split(modulation, 6, axis=-1)
    lat_full = jnp.concatenate([lat, lat_other]).astype(F32)
    normed_full = modulate(lat_full, shift_attn, scale_attn).astype(BF16)
    a_x, b_y, a_yc, b_xc, normed_full = together(a_x, b_y, a_yc, b_xc, normed_full)

    a_yx, b_xy, a_xc, b_yc = swap(a_y, "x"), swap(b_x, "y"), swap(a_x, "c"), swap(b_y, "c")
    mlp_grad = (gate_mlp * out_g.astype(F32)).astype(BF16)
    down_send, down_keep = split_rows(mlp_grad.T, True)
    normed = normed_full[:band]
    normed_2 = jnp.stack([normed[:, :half], normed[:, half:]])
    second_z, a_yx, b_xy, a_xc, b_yc, mlp_grad, down_send, down_keep, normed_2 = together(
        second_z, a_yx, b_xy, a_xc, b_yc, mlp_grad, down_send, down_keep, normed_2
    )

    a_yxc, b_xyc = swap(a_yx, "c"), swap(b_xy, "c")
    e, f = by_rows(second_z[:2]), by_rows(second_z[2:])
    e_y, f_x = swap(e, "y"), swap(f, "x")
    pieces_own = [
        (a, 0, 0, 0, 0), (a_y, 0, 0, 1, 0), (a_x, 0, 1, 0, 0), (a_yx, 0, 1, 1, 0),
        (b, 2, 0, 0, 0), (b_x, 2, 1, 0, 0), (b_y, 2, 0, 1, 0), (b_xy, 2, 1, 1, 0),
    ]
    tables = (cos_t, sin_t, gains_t, head_dim, band)
    parts = qkv_heads(normed_full, pieces_own, *tables)
    *parts, e_y, f_x, a_yxc, b_xyc = together(*parts, e_y, f_x, a_yxc, b_xyc)

    e_x, f_y, e_c, f_c, e_yc = swap(e, "x"), swap(f, "y"), swap(e, "c"), swap(f, "c"), swap(e_y, "c")
    pieces_other = [
        (a_c, 0, 0, 0, 1), (a_yc, 0, 0, 1, 1), (a_xc, 0, 1, 0, 1), (a_yxc, 0, 1, 1, 1),
        (b_c, 2, 0, 0, 1), (b_xc, 2, 1, 0, 1), (b_yc, 2, 0, 1, 1), (b_xyc, 2, 1, 1, 1),
    ]
    qkv, hat, fac, qkv_t = qkv_heads(normed_full, pieces_other, *tables, before=parts)
    e_x, f_y, e_c, f_c, e_yc, qkv = together(e_x, f_y, e_c, f_c, e_yc, qkv)

    e_yx, f_xy = swap(e_y, "x"), swap(f_x, "y")
    f_xc, e_xc, f_yc = swap(f_x, "c"), swap(e_x, "c"), swap(f_y, "c")
    attended_t, log_mass = attention_forward(qkv, HEADS, band)
    proj_t = join_rows(pieces_own + pieces_other, qkv_rows - cut, proj_rows).reshape(width, width)
    e_yx, f_xy, f_xc, e_xc, f_yc, attended_t, proj_t, down_z = together(
        e_yx, f_xy, f_xc, e_xc, f_yc, attended_t, proj_t, down_z
    )

    down_own = down_z.reshape(n_z, 2, 2, -1, down_z.shape[-1])
    down_other, e_yxc, f_xyc = swap(down_own, "c"), swap(e_yx, "c"), swap(f_xy, "c")
    attended_t = attended_t.reshape(width, band)
    branch, middle, normed_mid, mid_2, att_2 = after_attention(attended_t, proj_t, lat, mods)
    pieces = [
        (e, 0, 0, 0, 0), (e_y, 0, 0, 1, 0), (e_x, 0, 1, 0, 0), (e_yx, 0, 1, 1, 0),
        (e_c, 0, 0, 0, 1), (e_yc, 0, 0, 1, 1), (e_xc, 0, 1, 0, 1), (e_yxc, 0, 1, 1, 1),
        (f, 2, 0, 0, 0), (f_x, 2, 1, 0, 0), (f_y, 2, 0, 1, 0), (f_xy, 2, 1, 1, 0),
        (f_c, 2, 0, 0, 1), (f_xc, 2, 1, 0, 1), (f_yc, 2, 0, 1, 1), (f_xyc, 2, 1, 1, 1),
    ]
    hidden, gate_grad_t, up_grad_t, mlp_out, normed_mid_grad = mlp(
        normed_mid, mlp_grad, pieces, down_own, down_other
    )

    gates = (gate_grad_t, up_grad_t)
    a_g = terms([pltpu.with_memory_space_constraint(v, pltpu.HBM) for v in gates], mid_2, gate_rows, 1, n_z=2)
    a_g, hidden, *gates, mlp_out, normed_mid_grad = together(a_g, hidden, *gates, mlp_out, normed_mid_grad)

    a_gr = swap(a_g, "c")
    mid_grad, branch_grad_t, attended_grad, delta, result, sums = middle_back(
        normed_mid_grad, middle, out_g, branch, mlp_out, proj_t, attended_t, mods
    )
    b_g = terms(gates, mid_2, gate_rows, 1, z_first=2, n_z=2, order=(1, 0))
    by_head = attended_grad.reshape(HEADS, head_dim, band)
    a_gr, b_g, by_head, delta, branch_grad_t = together(a_gr, b_g, by_head, delta, branch_grad_t)

    b_gr = swap(b_g, "c")
    other_first = swap(by_head[:6], "x")
    a_k, a_s = terms(gates, mid_2, gate_rows, 0, received=a_gr, n_z=2, stacked=False)
    proj_send, proj_keep = split_rows(branch_grad_t, False)
    down_g = terms((down_send,), hidden, 2 * proj_rows, 1, split=n_z)
    b_gr, other_first, a_k, a_s, down_g, proj_send, proj_keep = together(
        b_gr, other_first, a_k, a_s, down_g, proj_send, proj_keep
    )

    down_gr = swap(down_g, "c")
    a_r1 = [swap(a_s[2:3], "x")]
    b_s = terms(gates, mid_2, gate_rows, 0, received=b_gr, z_first=2, n_z=2, y=(1,), order=(1, 0))
    b_k = terms(gates, mid_2, gate_rows, 0, received=b_gr, z_first=2, n_z=2, y=(0,), order=(1, 0), kind=pltpu.HBM)
    proj_g = terms((proj_send,), att_2, n_z * proj_rows, 1, order=(1, 0), split=2)
    down_gr, a_r1[0], b_s, b_k, proj_g = together(down_gr, a_r1[0], b_s, b_k, proj_g)

    proj_gr = swap(proj_g, "c")
    a_r1.append(swap(a_s[3:4], "x"))
    b_s = b_s.reshape(4, gate_rows, width)
    b_r1 = [swap(b_s[:1], "y")]
    down_sum = terms((down_keep,), hidden, 2 * proj_rows, 0, received=down_gr, split=n_z, kind=pltpu.HBM)
    proj_gr, a_r1[1], b_r1[0], down_sum = together(proj_gr, a_r1[1], b_r1[0], down_sum)

    down_sum = lax.psum_scatter(
        down_sum.reshape(-1, down_sum.shape[-1]), "z", scatter_dimension=0, tiled=True
    ).reshape(2, 2, proj_rows, -1)
    other_last = swap(by_head[6:], "x")
    other_rows = swap(jnp.stack([log_mass, delta]), "x")
    b_r1.append(swap(b_s[1:3], "y"))
    dq, dk, dv = attention_back_own(qkv, by_head, log_mass, delta, HEADS, band)
    b_r1[1], other_last, other_rows, dq = together(b_r1[1], other_last, other_rows, dq)

    a_r1.append(swap(a_s[:2], "x"))
    b_r1.append(swap(b_s[3:], "y"))
    a_s2 = add_low(a_k[2:], jnp.concatenate(a_r1[:2]))
    a_r2 = [swap(a_s2[:1], "y")]
    heads_grad, gain_q, gain_k = attention_back_other(
        qkv, hat, fac, cos_t, sin_t, gains_t, dq, dk, dv,
        (other_first, other_last), other_rows[0], other_rows[1], HEADS, band,
    )
    projected_t = heads_grad.reshape(3 * width, band)
    a_r1[2], b_r1[2], a_r2[0], projected_t = together(a_r1[2], b_r1[2], a_r2[0], projected_t)

    b_r1 = jnp.concatenate(b_r1).reshape(2, 2, gate_rows, width)
    b_s2 = add_low(b_k[0], b_r1[0])
    b_r2 = [swap(b_s2[:1], "x")]
    a_r2.append(swap(a_s2[1:], "y"))
    q_g = terms((projected_t,), normed_2, qkv_rows, 1)
    b_r2[0], a_r2[1], q_g, proj_gr = together(b_r2[0], a_r2[1], q_g, proj_gr)

    q_gr = swap(q_g, "c")
    b_r2.append(swap(b_s2[1:], "x"))
    proj_sum = terms((proj_keep,), att_2, n_z * proj_rows, 0, received=proj_gr, order=(1, 0), split=2)
    proj_r1 = [swap(proj_sum[1, 0], "y")]
    q_gr, b_r2[1], proj_r1[0], proj_sum = together(q_gr, b_r2[1], proj_r1[0], proj_sum)

    row_a = 112
    qa_keep, qa_send, qb_send, qb_keep = last_terms(projected_t, normed_2, qkv_rows, row_a, q_gr)
    proj_r1.append(swap(proj_sum[1, 1], "y"))
    proj_r2 = swap(add_low(proj_sum[0, 0], proj_r1[0]), "x")
    gu = jnp.concatenate(
        [add_low(a_k[:2], a_r1[2], jnp.concatenate(a_r2)), add_low(b_k[1], b_r1[1], jnp.concatenate(b_r2))]
    )
    qa_keep, qa_send, qb_send, qb_keep, proj_r1[1], proj_r2, projected_t, gu, gain_q, gain_k = together(
        qa_keep, qa_send, qb_send, qb_keep, proj_r1[1], proj_r2, projected_t, gu, gain_q, gain_k
    )

    gu = lax.psum_scatter(gu.reshape(-1, width), "z", scatter_dimension=0, tiled=True)
    qa_r1, qb_r1 = swap(qa_send, "x"), swap(qb_send, "y")
    input_grad, in_sums = input_back(projected_t, qkv_t, lat, mid_grad, mods)
    mod_grad = jnp.concatenate([in_sums[0:1], in_sums[1:2], sums[2:3], sums[0:1], sums[1:2], sums[3:4]], axis=-1)
    small = jnp.concatenate([mod_grad, gain_q.sum(0).T, gain_k.sum(0).T], axis=-1)
    small_r = swap(small, "x")
    qa_r1, qb_r1, down_sum, small_r = together(qa_r1, qb_r1, down_sum, small_r)

    qa_keep, qa_r1 = qa_keep.reshape(2, n_z, row_a, half), qa_r1.reshape(2, n_z, row_a, half)
    qa_s2, qb_s2, small = together(
        add_low(qa_keep[1], qa_r1[1]), add_low(qb_keep[0], qb_r1[0]), small + small_r
    )
    qa_r2, qb_r2 = swap(qa_s2, "y"), swap(qb_s2, "x")
    band_mod, band_gain = small[:, : 6 * width], small[:, 6 * width :]
    mod_cols_grad = lax.all_to_all(band_mod.astype(BF16), DP_AXES, split_axis=1, concat_axis=0, tiled=True)
    qa_r2, qb_r2, down_sum, mod_cols_grad = together(qa_r2, qb_r2, down_sum, mod_cols_grad)

    last = jnp.concatenate(
        [
            add_low(qa_keep[0], qa_r1[0], qa_r2),
            add_low(qb_keep[1], qb_r1[1], qb_r2),
            add_low(proj_sum[0, 1], proj_r1[1], proj_r2).reshape(n_z, proj_rows, half),
        ],
        axis=1,
    )
    last, gu, mod_cols_grad = together(last, gu, mod_cols_grad)
    last = lax.psum_scatter(last.reshape(-1, half), "z", scatter_dimension=0, tiled=True)
    cond_act_part = dot_f32(mod_cols_grad, ada_weight[0], ((1,), (1,)))
    tail = jnp.zeros((8, width), F32).at[0, : 2 * head_dim].set(band_gain[0])
    summed = summed_over(jnp.concatenate([cond_act_part, tail]), ("y", "c"), 4)
    summed, down_sum = together(summed, down_sum)
    down_r = swap(down_sum[:, 1], "y")
    down_sum = add_low(down_sum[:, 0], down_r)
    down_r2 = swap(down_sum[1], "x")
    summed = summed_over(summed, "z", n_z)
    ada_grad = outer_terms(mod_cols_grad, cond_act).T
    items = cond.shape[0]
    _, silu_back = jax.vjp(jax.nn.silu, cond)
    cond_grad = silu_back(summed[:items])[0]
    time_grad, class_grad = spread_rows((bucket_hot, class_hot), cond_grad)
    down_out = down_sum[0].astype(F32) + down_r2.astype(F32)

    qkv_grad, proj_grad = in_float32(last, [qkv_rows, proj_rows], [half])
    gate_grad, up_grad = in_float32(gu, [gate_rows], [half, half])

    def out(values):
        return values.T[None]

    return (
        result[None],
        input_grad[None],
        time_grad,
        class_grad,
        ada_grad[None],
        out(qkv_grad),
        out(proj_grad),
        out(gate_grad),
        out(up_grad),
        out(down_out),
        summed[items : items + 1, :head_dim],
        summed[items : items + 1, head_dim : 2 * head_dim],
    )


def fast_solution(mesh):
    dp = mesh.shape["dp"]
    fine = jax.sharding.Mesh(mesh.devices.reshape(dp // 4, 2, 2, 2), ("z", "y", "c", "x"))
    items, last = P(DP_AXES, "x", None), P(None, "x", DP_AXES)
    in_specs = (items, items, P(), P(), P(), P(), P(DP_AXES, "x"), P(None, None, DP_AXES)) + (last,) * 5 + (P(), P())
    out_specs = (items, items, P(), P(), P(None, None, DP_AXES)) + (last,) * 5 + (P(), P())
    return jax.shard_map(fast_shards, mesh=fine, in_specs=in_specs, out_specs=out_specs, check_vma=False)


def solution(mesh):
    if mesh.shape["dp"] == 16 and mesh.shape["seq"] == 2:
        return fast_solution(mesh)
    in_specs = (
        P("dp", "seq", None),
        P("dp", "seq", None),
        P(),
        P(),
        P(),
        P(),
        P("dp", "seq"),
        P(None, None, "dp"),
        P(None, "seq", "dp"),
        P(None, "seq", "dp"),
        P(None, "seq", "dp"),
        P(None, "seq", "dp"),
        P(None, "seq", "dp"),
        P(),
        P(),
    )
    out_specs = (
        P("dp", "seq", None),
        P("dp", "seq", None),
        P(),
        P(),
        P(None, None, "dp"),
        P(None, "seq", "dp"),
        P(None, "seq", "dp"),
        P(None, "seq", "dp"),
        P(None, "seq", "dp"),
        P(None, "seq", "dp"),
        P(),
        P(),
    )
    return jax.shard_map(shards, mesh=mesh, in_specs=in_specs, out_specs=out_specs, check_vma=False)
```

```python
import jax
import jax.numpy as jnp
from jax import lax
from jax.experimental import pallas as pl
from jax.experimental.layout import Layout, with_layout_constraint
from jax.experimental.pallas import tpu as pltpu
from jax.sharding import PartitionSpec as P

HEADS = 16
CLASSES = 1000
BUCKETS = 1000
SIDE = 32


EPS = 1e-06
THETA = 10000.0
HIGHEST = lax.Precision.HIGHEST


def norm_factor(values):
    return lax.rsqrt(jnp.mean(values * values, axis=-1, keepdims=True) + EPS)


def modulate(values, shift_by, scale_by):
    return values * norm_factor(values) * (1.0 + scale_by) + shift_by


def rope_tables(row_pos, col_pos, head_dim):
    quarter = head_dim // 4
    frequency = THETA ** (-jnp.arange(quarter, dtype=jnp.float32) / quarter)
    angles = jnp.concatenate(
        [row_pos[..., None] * frequency, col_pos[..., None] * frequency], axis=-1
    )
    cos_part = jnp.cos(angles)
    sin_part = jnp.sin(angles)
    return (
        jnp.concatenate([cos_part, cos_part], axis=-1),
        jnp.concatenate([sin_part, sin_part], axis=-1),
    )


def rotate(values, cos_part, sin_part):
    half_dim = values.shape[-1] // 2
    turned = jnp.concatenate([-values[..., half_dim:], values[..., :half_dim]], axis=-1)
    return values * cos_part + turned * sin_part


def query_key(query_pre, key_pre, gain_query, gain_key, cos_part, sin_part):
    query_out = rotate(query_pre * norm_factor(query_pre) * gain_query, cos_part, sin_part)
    key_out = rotate(key_pre * norm_factor(key_pre) * gain_key, cos_part, sin_part)
    return (query_out, key_out)


def swiglu(gate_pre, up_pre):
    return jax.nn.silu(gate_pre) * up_pre


def gather_layer(layer_no, qkv_weight, proj_weight, gate_weight, up_weight, down_weight):
    row_parts = (
        lax.all_gather(qkv_weight[layer_no], "seq", axis=0, tiled=True),
        lax.all_gather(proj_weight[layer_no], "seq", axis=0, tiled=True),
        lax.all_gather(gate_weight[layer_no], "seq", axis=0, tiled=True),
        lax.all_gather(up_weight[layer_no], "seq", axis=0, tiled=True),
        lax.all_gather(down_weight[layer_no], "seq", axis=0, tiled=True),
    )
    qkv_rows, proj_rows, gate_rows, up_rows, down_rows = row_parts
    return (
        lax.all_gather(qkv_rows, "dp", axis=1, tiled=True),
        lax.all_gather(proj_rows, "dp", axis=1, tiled=True),
        lax.all_gather(gate_rows, "dp", axis=1, tiled=True),
        lax.all_gather(up_rows, "dp", axis=1, tiled=True),
        lax.all_gather(down_rows, "dp", axis=1, tiled=True),
    )


def attend(queries, key_rows, value_rows, inv_root):
    items_dev, band_rows, head_count, head_dim = queries.shape
    top_score = jnp.full((items_dev, head_count, band_rows), -jnp.inf, jnp.float32)
    row_mass = jnp.zeros((items_dev, head_count, band_rows), jnp.float32)
    weighted = jnp.zeros((items_dev, band_rows, head_count, head_dim), jnp.float32)
    key_seg = lax.all_gather(key_rows, "seq", axis=1, tiled=True)
    value_seg = lax.all_gather(value_rows, "seq", axis=1, tiled=True)
    seg_rows = key_seg.shape[1]
    key_heads = key_seg.reshape(items_dev, seg_rows, head_count, head_dim)
    value_heads = value_seg.reshape(items_dev, seg_rows, head_count, head_dim)
    scores = (
        jnp.einsum("ibhe,inhe->ihbn", queries, key_heads, preferred_element_type=jnp.float32)
        * inv_root
    )
    new_top = jnp.max(scores, axis=-1)
    shrink = jnp.exp(top_score - new_top)
    weights = jnp.exp(scores - new_top[..., None])
    new_mass = row_mass * shrink + jnp.sum(weights, axis=-1)
    update = jnp.einsum(
        "ihbn,inhe->ibhe",
        weights.astype(jnp.bfloat16),
        value_heads,
        preferred_element_type=jnp.float32,
    )
    new_weighted = weighted * jnp.transpose(shrink, (0, 2, 1))[..., None] + update
    log_mass = new_top + jnp.log(new_mass)
    attended = new_weighted / jnp.transpose(new_mass, (0, 2, 1))[..., None]
    return (attended, log_mass)


def attend_back(queries, keys_all, values_all, attended_grad, log_mass, delta, inv_root):
    items_dev, band_rows, head_count, head_dim = queries.shape
    seq_len = keys_all.shape[1]
    key_heads = keys_all.reshape(items_dev, seq_len, head_count, head_dim)
    value_heads = values_all.reshape(items_dev, seq_len, head_count, head_dim)

    def one_item(operands):
        query_item, key_item, value_item, grad_item, mass_item, delta_item = operands
        scores = (
            jnp.einsum("bhe,nhe->hbn", query_item, key_item, preferred_element_type=jnp.float32)
            * inv_root
        )
        probs_full = jnp.exp(scores - mass_item[..., None])
        prob_grad = jnp.einsum(
            "bhe,nhe->hbn", grad_item, value_item, preferred_element_type=jnp.float32
        )
        score_grad = (probs_full * (prob_grad - delta_item[..., None])).astype(jnp.bfloat16)
        query_out_grad = (
            jnp.einsum("hbn,nhe->bhe", score_grad, key_item, preferred_element_type=jnp.float32)
            * inv_root
        )
        key_out_grad = (
            jnp.einsum("hbn,bhe->nhe", score_grad, query_item, preferred_element_type=jnp.float32)
            * inv_root
        )
        value_grad = jnp.einsum(
            "hbn,bhe->nhe",
            probs_full.astype(jnp.bfloat16),
            grad_item,
            preferred_element_type=jnp.float32,
        )
        return (query_out_grad, key_out_grad, value_grad)

    return lax.map(one_item, (queries, key_heads, value_heads, attended_grad, log_mass, delta))


def forward_layer(residual, modulation, weights, gain_query, gain_key, cos_part, sin_part):
    qkv_full, proj_full, gate_full, up_full, down_full = weights
    items_dev, band_rows, model_width = residual.shape
    head_count = HEADS
    head_dim = model_width // head_count
    inv_root = head_dim ** (-0.5)
    shift_attn, scale_attn, gate_attn, shift_mlp, scale_mlp, gate_mlp = jnp.split(
        modulation[:, None, :], 6, axis=-1
    )
    normed = modulate(residual, shift_attn, scale_attn).astype(jnp.bfloat16)
    projected = jnp.einsum("ibd,de->ibe", normed, qkv_full, preferred_element_type=jnp.float32)
    query_pre = projected[..., :model_width].reshape(items_dev, band_rows, head_count, head_dim)
    key_pre = projected[..., model_width : 2 * model_width].reshape(
        items_dev, band_rows, head_count, head_dim
    )
    queries, key_rows = query_key(query_pre, key_pre, gain_query, gain_key, cos_part, sin_part)
    queries = queries.astype(jnp.bfloat16)
    key_rows = key_rows.astype(jnp.bfloat16).reshape(items_dev, band_rows, model_width)
    value_rows = projected[..., 2 * model_width :].astype(jnp.bfloat16)
    attended, log_mass = attend(queries, key_rows, value_rows, inv_root)
    attended_low = attended.reshape(items_dev, band_rows, model_width).astype(jnp.bfloat16)
    branch = jnp.einsum("ibd,de->ibe", attended_low, proj_full, preferred_element_type=jnp.float32)
    middle = residual + gate_attn * branch
    normed_mid = modulate(middle, shift_mlp, scale_mlp).astype(jnp.bfloat16)
    gate_pre = jnp.einsum("ibd,df->ibf", normed_mid, gate_full, preferred_element_type=jnp.float32)
    up_pre = jnp.einsum("ibd,df->ibf", normed_mid, up_full, preferred_element_type=jnp.float32)
    hidden = swiglu(gate_pre, up_pre).astype(jnp.bfloat16)
    mlp_out = jnp.einsum("ibf,fd->ibd", hidden, down_full, preferred_element_type=jnp.float32)
    output = middle + gate_mlp * mlp_out
    stored = (
        residual,
        normed,
        query_pre,
        key_pre,
        queries,
        key_rows,
        value_rows,
        attended,
        attended_low,
        log_mass,
        branch,
        middle,
        normed_mid,
        gate_pre,
        up_pre,
        hidden,
        mlp_out,
    )
    return (output, stored)


def weight_terms(
    normed,
    attended_low,
    normed_mid,
    hidden,
    projected_grad,
    branch_grad,
    gate_pre_grad,
    up_pre_grad,
    mlp_grad,
):
    qkv_term = jnp.einsum("ibd,ibe->de", normed, projected_grad, preferred_element_type=jnp.float32)
    proj_term = jnp.einsum(
        "ibd,ibe->de", attended_low, branch_grad, preferred_element_type=jnp.float32
    )
    gate_term = jnp.einsum(
        "ibd,ibf->df", normed_mid, gate_pre_grad, preferred_element_type=jnp.float32
    )
    up_term = jnp.einsum("ibd,ibf->df", normed_mid, up_pre_grad, preferred_element_type=jnp.float32)
    down_term = jnp.einsum("ibf,ibd->fd", hidden, mlp_grad, preferred_element_type=jnp.float32)
    col_parts = (
        lax.psum_scatter(
            qkv_term.astype(jnp.bfloat16), "dp", scatter_dimension=1, tiled=True
        ).astype(jnp.float32),
        lax.psum_scatter(
            proj_term.astype(jnp.bfloat16), "dp", scatter_dimension=1, tiled=True
        ).astype(jnp.float32),
        lax.psum_scatter(
            gate_term.astype(jnp.bfloat16), "dp", scatter_dimension=1, tiled=True
        ).astype(jnp.float32),
        lax.psum_scatter(
            up_term.astype(jnp.bfloat16), "dp", scatter_dimension=1, tiled=True
        ).astype(jnp.float32),
        lax.psum_scatter(
            down_term.astype(jnp.bfloat16), "dp", scatter_dimension=1, tiled=True
        ).astype(jnp.float32),
    )
    qkv_cols, proj_cols, gate_cols, up_cols, down_cols = col_parts
    return (
        lax.psum_scatter(
            qkv_cols.astype(jnp.bfloat16), "seq", scatter_dimension=0, tiled=True
        ).astype(jnp.float32),
        lax.psum_scatter(
            proj_cols.astype(jnp.bfloat16), "seq", scatter_dimension=0, tiled=True
        ).astype(jnp.float32),
        lax.psum_scatter(
            gate_cols.astype(jnp.bfloat16), "seq", scatter_dimension=0, tiled=True
        ).astype(jnp.float32),
        lax.psum_scatter(
            up_cols.astype(jnp.bfloat16), "seq", scatter_dimension=0, tiled=True
        ).astype(jnp.float32),
        lax.psum_scatter(
            down_cols.astype(jnp.bfloat16), "seq", scatter_dimension=0, tiled=True
        ).astype(jnp.float32),
    )


def backward_layer(
    stored, resid_grad, modulation, weights, gain_query, gain_key, cos_part, sin_part
):
    qkv_full, proj_full, gate_full, up_full, down_full = weights
    (
        residual,
        normed,
        query_pre,
        key_pre,
        queries,
        key_rows,
        value_rows,
        attended,
        attended_low,
        log_mass,
        branch,
        middle,
        normed_mid,
        gate_pre,
        up_pre,
        hidden,
        mlp_out,
    ) = stored
    items_dev, band_rows, head_count, head_dim = queries.shape
    model_width = residual.shape[-1]
    inv_root = head_dim ** (-0.5)
    shift_attn, scale_attn, gate_attn, shift_mlp, scale_mlp, gate_mlp = jnp.split(
        modulation[:, None, :], 6, axis=-1
    )
    mlp_grad = (gate_mlp * resid_grad).astype(jnp.bfloat16)
    gate_mlp_grad = jnp.sum(resid_grad * mlp_out, axis=1, keepdims=True)
    hidden_grad = jnp.einsum("ibd,fd->ibf", mlp_grad, down_full, preferred_element_type=jnp.float32)
    unused_out, swiglu_back = jax.vjp(swiglu, gate_pre, up_pre)
    gate_pre_grad, up_pre_grad = swiglu_back(hidden_grad)
    gate_pre_grad = gate_pre_grad.astype(jnp.bfloat16)
    up_pre_grad = up_pre_grad.astype(jnp.bfloat16)
    normed_mid_grad = jnp.einsum(
        "ibf,df->ibd", gate_pre_grad, gate_full, preferred_element_type=jnp.float32
    )
    normed_mid_grad = normed_mid_grad + jnp.einsum(
        "ibf,df->ibd", up_pre_grad, up_full, preferred_element_type=jnp.float32
    )
    unused_mid, mid_back = jax.vjp(modulate, middle, shift_mlp, scale_mlp)
    mid_norm_grad, shift_mlp_grad, scale_mlp_grad = mid_back(normed_mid_grad)
    mid_grad = resid_grad + mid_norm_grad
    branch_grad = (gate_attn * mid_grad).astype(jnp.bfloat16)
    gate_attn_grad = jnp.sum(mid_grad * branch, axis=1, keepdims=True)
    attended_grad = jnp.einsum(
        "ibe,de->ibd", branch_grad, proj_full, preferred_element_type=jnp.float32
    ).astype(jnp.bfloat16)
    attended_grad = attended_grad.reshape(items_dev, band_rows, head_count, head_dim)
    delta = jnp.transpose(jnp.sum(attended_grad.astype(jnp.float32) * attended, axis=-1), (0, 2, 1))
    keys_all, values_all = (
        lax.all_gather(key_rows, "seq", axis=1, tiled=True),
        lax.all_gather(value_rows, "seq", axis=1, tiled=True),
    )
    query_out_grad, key_out_grad, value_grad = attend_back(
        queries, keys_all, values_all, attended_grad, log_mass, delta, inv_root
    )
    seq_len = keys_all.shape[1]
    key_band_grad, value_band_grad = (
        lax.psum_scatter(
            key_out_grad.reshape(items_dev, seq_len, model_width).astype(jnp.bfloat16),
            "seq",
            scatter_dimension=1,
            tiled=True,
        ).astype(jnp.float32),
        lax.psum_scatter(
            value_grad.reshape(items_dev, seq_len, model_width).astype(jnp.bfloat16),
            "seq",
            scatter_dimension=1,
            tiled=True,
        ).astype(jnp.float32),
    )

    def rotate_pair(query_in, key_in, gain_q, gain_k):
        return query_key(query_in, key_in, gain_q, gain_k, cos_part, sin_part)

    unused_pair, pair_back = jax.vjp(rotate_pair, query_pre, key_pre, gain_query, gain_key)
    query_pre_grad, key_pre_grad, query_gain_term, key_gain_term = pair_back(
        (query_out_grad, key_band_grad.reshape(items_dev, band_rows, head_count, head_dim))
    )
    projected_grad = jnp.concatenate(
        [
            query_pre_grad.reshape(items_dev, band_rows, model_width),
            key_pre_grad.reshape(items_dev, band_rows, model_width),
            value_band_grad,
        ],
        axis=-1,
    ).astype(jnp.bfloat16)
    normed_grad = jnp.einsum(
        "ibe,de->ibd", projected_grad, qkv_full, preferred_element_type=jnp.float32
    )
    unused_in, input_back = jax.vjp(modulate, residual, shift_attn, scale_attn)
    input_norm_grad, shift_attn_grad, scale_attn_grad = input_back(normed_grad)
    input_grad = mid_grad + input_norm_grad
    mod_grad = jnp.concatenate(
        [
            shift_attn_grad,
            scale_attn_grad,
            gate_attn_grad,
            shift_mlp_grad,
            scale_mlp_grad,
            gate_mlp_grad,
        ],
        axis=-1,
    )[:, 0, :]
    own_grads = weight_terms(
        normed,
        attended_low,
        normed_mid,
        hidden,
        projected_grad,
        branch_grad,
        gate_pre_grad,
        up_pre_grad,
        mlp_grad,
    )
    return (input_grad, mod_grad, own_grads, query_gain_term, key_gain_term)


def shards(
    latents,
    out_grad,
    time_table,
    class_table,
    buckets,
    labels,
    row_start,
    ada_weight,
    qkv_weight,
    proj_weight,
    gate_weight,
    up_weight,
    down_weight,
    query_gain,
    key_gain,
):
    items_dev, band_rows, model_width = latents.shape
    layer_count = qkv_weight.shape[0]
    head_dim = model_width // HEADS
    offsets = jnp.arange(band_rows, dtype=jnp.int32)
    row_pos = (row_start + (offsets // SIDE)[None, :]).astype(jnp.float32)
    col_pos = (offsets % SIDE).astype(jnp.float32)[None, :]
    cos_part, sin_part = rope_tables(row_pos, col_pos, head_dim)
    cos_part = cos_part[:, :, None, :]
    sin_part = sin_part[:, :, None, :]
    bucket_hot = (buckets[:, None] == jnp.arange(BUCKETS, dtype=jnp.int32)[None, :]).astype(
        jnp.bfloat16
    )
    class_hot = (labels[:, None] == jnp.arange(CLASSES, dtype=jnp.int32)[None, :]).astype(
        jnp.bfloat16
    )
    cond = jnp.dot(bucket_hot, time_table, preferred_element_type=jnp.float32) + jnp.dot(
        class_hot, class_table, preferred_element_type=jnp.float32
    )
    cond_act = jax.nn.silu(cond).astype(jnp.bfloat16)
    mod_cols = jnp.einsum("id,ldm->lim", cond_act, ada_weight, preferred_element_type=jnp.float32)
    modulation = lax.all_to_all(mod_cols, "dp", split_axis=1, concat_axis=2, tiled=True)
    residual = latents.astype(jnp.float32)
    gathered_all = []
    layer_no = 0
    weights = gather_layer(layer_no, qkv_weight, proj_weight, gate_weight, up_weight, down_weight)
    gathered_all.append(weights)
    residual, stored = forward_layer(
        residual,
        modulation[layer_no],
        weights,
        query_gain[layer_no],
        key_gain[layer_no],
        cos_part,
        sin_part,
    )
    stored_all = [stored]
    result = residual.astype(jnp.bfloat16)
    resid_grad = out_grad.astype(jnp.float32)
    mod_grads = [None] * layer_count
    grad_shards = [None] * layer_count
    query_terms = [None] * layer_count
    key_terms = [None] * layer_count
    for layer_no in reversed(range(layer_count)):
        weights = gather_layer(
            layer_no, qkv_weight, proj_weight, gate_weight, up_weight, down_weight
        )
        resid_grad, mod_grad, own_grads, query_term, key_term = backward_layer(
            stored_all[layer_no],
            resid_grad,
            modulation[layer_no],
            weights,
            query_gain[layer_no],
            key_gain[layer_no],
            cos_part,
            sin_part,
        )
        mod_grads[layer_no] = mod_grad
        grad_shards[layer_no] = own_grads
        query_terms[layer_no] = query_term
        key_terms[layer_no] = key_term
    band_mod, band_query, band_key = lax.psum(
        (jnp.stack(mod_grads), jnp.stack(query_terms), jnp.stack(key_terms)), "seq"
    )
    mod_cols_grad = lax.all_to_all(
        band_mod.astype(jnp.bfloat16), "dp", split_axis=2, concat_axis=1, tiled=True
    )
    ada_grad = jnp.einsum(
        "id,lim->ldm", cond_act, mod_cols_grad, preferred_element_type=jnp.float32
    )
    cond_act_part = jnp.einsum(
        "lim,ldm->id", mod_cols_grad, ada_weight, preferred_element_type=jnp.float32
    )
    cond_act_grad, query_grad, key_grad = (
        lax.psum(cond_act_part.astype(jnp.bfloat16), "dp").astype(jnp.float32),
        lax.psum(band_query.astype(jnp.bfloat16), "dp").astype(jnp.float32),
        lax.psum(band_key.astype(jnp.bfloat16), "dp").astype(jnp.float32),
    )
    unused_cond, silu_back = jax.vjp(jax.nn.silu, cond)
    cond_grad = silu_back(cond_act_grad)[0]
    time_grad = jnp.einsum(
        "ib,id->bd", bucket_hot.astype(jnp.float32), cond_grad, precision=HIGHEST
    )
    class_grad = jnp.einsum(
        "ib,id->bd", class_hot.astype(jnp.float32), cond_grad, precision=HIGHEST
    )
    qkv_grad = jnp.stack([grad_shards[0][0]])
    proj_grad = jnp.stack([grad_shards[0][1]])
    gate_grad = jnp.stack([grad_shards[0][2]])
    up_grad = jnp.stack([grad_shards[0][3]])
    down_grad = jnp.stack([grad_shards[0][4]])
    return (
        result,
        resid_grad,
        time_grad,
        class_grad,
        ada_grad,
        qkv_grad,
        proj_grad,
        gate_grad,
        up_grad,
        down_grad,
        query_grad,
        key_grad,
    )


BF16 = jnp.bfloat16
F32 = jnp.float32
LOG2E = 1.4426950408889634
LN2 = 0.6931471805599453
DP_AXES = ("z", "y", "c")
SMALL = pl.CostEstimate(flops=1, bytes_accessed=1, transcendentals=0)


def kernel_call(kernel, **options):
    return pl.pallas_call(kernel, cost_estimate=SMALL, **options)


def together(*arrays):
    return lax.optimization_barrier(arrays)


def swap(values, axis):
    return lax.ppermute(values, axis, [(0, 1), (1, 0)])


def in_order(own, other, axis):
    first = lax.axis_index(axis) == 0
    return jnp.stack([jnp.where(first, own, other), jnp.where(first, other, own)])


def spread(values, axis):
    return in_order(values, swap(values, axis), axis)


def by_rows(values):
    return with_layout_constraint(values, Layout(major_to_minor=tuple(range(values.ndim))))


def gather_z(values):
    n_z = lax.axis_size("z")
    return lax.all_gather(values, "z", axis=0, tiled=True).reshape(n_z, *values.shape)


def add_low(*terms):
    total = terms[0].astype(F32)
    for term in terms[1:]:
        total = total + term.astype(F32)
    return total.astype(BF16)


def dot_f32(left, right, contract):
    return lax.dot_general(left, right, (contract, ((), ())), preferred_element_type=F32)


def piece_targets(pieces, at):
    for k, (array, z_first, x, y, c) in enumerate(pieces):
        for z in range(array.shape[0]):
            block = ((z_first + z) * 2 + (at[2] + y) % 2) * 2 + (at[0] + c) % 2
            yield k, z, (at[1] + x) % 2, block


def join_rows(pieces, first_row, rows):
    width = pieces[0][0].shape[-1]
    half = width // 2
    blocks = sum(piece[0].shape[0] for piece in pieces) // 2

    def kernel(at, *refs):
        out_ref, buf, sems = refs[len(pieces) :]
        copies = []
        for k, z, x, block in piece_targets(pieces, at):
            copy = pltpu.make_async_copy(
                refs[k].at[z, pl.ds(first_row, rows)], buf.at[x, block], sems.at[x, block]
            )
            copy.start()
            copies.append(copy)
        for copy in copies:
            copy.wait()
        for block in range(blocks):
            out_ref[block] = jnp.concatenate([buf[0, block][:, half:], buf[1, block][:, half:]], axis=1)

    return kernel_call(
        kernel,
        grid_spec=pltpu.PrefetchScalarGridSpec(
            num_scalar_prefetch=1,
            grid=(1,),
            in_specs=[pl.BlockSpec(memory_space=pl.ANY)] * len(pieces),
            out_specs=[pl.BlockSpec((blocks, rows, width), lambda i, at: (0, 0, 0))],
            scratch_shapes=[pltpu.VMEM((2, blocks, rows, width), BF16), pltpu.SemaphoreType.DMA((2, blocks))],
        ),
        out_shape=[jax.ShapeDtypeStruct((blocks, rows, width), BF16)],
        compiler_params=pltpu.CompilerParams(vmem_limit_bytes=24 << 20),
        name="join_rows",
    )(place(), *[piece[0] for piece in pieces])[0]


def qkv_heads(normed, pieces, cos_t, sin_t, gains_t, head_dim, band, before=()):
    seq_len, width = normed.shape
    heads = HEADS
    group = 3
    rows_all = group * head_dim
    half = width // 2
    sent = pieces[0][0].shape[1]
    q_scale = head_dim**-0.5 * LOG2E
    side = pieces[0][4]
    steps = sum(piece[0].shape[0] for piece in pieces) // 2
    n_in = len(pieces)

    def kernel(at, norm_ref, cos_ref, sin_ref, gain_ref, *refs):
        out_ref, hat_ref, fac_ref, whole_ref, acc_ref, buf, sems = refs[n_in + len(before) :]

        @pl.when(pl.program_id(0) == 0)
        def _():
            for k, z, x, block in piece_targets(pieces, at):
                local = block // 2
                pltpu.make_async_copy(refs[k].at[z], buf.at[x, local], sems.at[x, local]).start()

        local = pl.program_id(0)
        step = 2 * local + (at[0] + side) % 2
        for x in range(2):
            pltpu.make_async_copy(refs[0].at[0], buf.at[x, local], sems.at[x, local]).wait()
        low, high = buf[0, local], buf[1, local]
        whole_ref[:sent] = jnp.concatenate([low[:, :half], high[:, :half]], axis=1)
        whole_ref[sent:] = jnp.concatenate([low[: rows_all - sent, half:], high[: rows_all - sent, half:]], axis=1)
        acc_ref[...] = dot_f32(whole_ref[...], norm_ref[...], ((1,), (1,)))
        for i in range(group):
            head = step * group + i
            rows = pl.ds(i * head_dim, head_dim)

            @pl.when(head < 2 * heads)
            def _():
                values = acc_ref[rows, :]
                fac = lax.rsqrt(jnp.mean(values * values, axis=0, keepdims=True) + EPS)
                hat = values * fac
                gained = hat * jnp.where(head < heads, gain_ref[:, 0:1] * q_scale, gain_ref[:, 1:2])
                turned = jnp.concatenate([gained[head_dim // 2 :], gained[: head_dim // 2]], axis=0)
                out_ref[i] = (gained * cos_ref[...] + turned * sin_ref[...]).astype(BF16)
                hat_ref[i] = hat[:, :band].astype(BF16)
                fac_ref[i] = fac[:, :band]

            @pl.when(head >= 2 * heads)
            def _():
                out_ref[i] = acc_ref[rows, :].astype(BF16)
                hat_ref[i] = jnp.zeros((head_dim, band), BF16)
                fac_ref[i] = jnp.zeros((1, band), F32)

    whole = lambda i, at: (0, 0)
    return kernel_call(
        kernel,
        grid_spec=pltpu.PrefetchScalarGridSpec(
            num_scalar_prefetch=1,
            grid=(steps,),
            in_specs=[
                pl.BlockSpec((seq_len, width), whole),
                pl.BlockSpec((head_dim, seq_len), whole),
                pl.BlockSpec((head_dim, seq_len), whole),
                pl.BlockSpec((head_dim, 2), whole),
            ]
            + [pl.BlockSpec(memory_space=pl.ANY)] * (n_in + len(before)),
            out_specs=[
                pl.BlockSpec((group, head_dim, seq_len), lambda i, at: (2 * i + (at[0] + side) % 2, 0, 0)),
                pl.BlockSpec((group, head_dim, band), lambda i, at: (2 * i + (at[0] + side) % 2, 0, 0)),
                pl.BlockSpec((group, 1, band), lambda i, at: (2 * i + (at[0] + side) % 2, 0, 0)),
                pl.BlockSpec((rows_all, width), lambda i, at: (2 * i + (at[0] + side) % 2, 0)),
            ],
            scratch_shapes=[
                pltpu.VMEM((rows_all, seq_len), F32),
                pltpu.VMEM((2, steps, sent, width), BF16),
                pltpu.SemaphoreType.DMA((2, steps)),
            ],
        ),
        out_shape=[
            jax.ShapeDtypeStruct((3 * heads, head_dim, seq_len), BF16),
            pltpu.HBM((3 * heads, head_dim, band), BF16),
            pltpu.HBM((3 * heads, 1, band), F32),
            pltpu.HBM((3 * width, width), BF16),
        ],
        input_output_aliases={5 + n_in + k: k for k in range(len(before))},
        compiler_params=pltpu.CompilerParams(vmem_limit_bytes=32 << 20),
        name="qkv_heads",
    )(place(), normed, cos_t, sin_t, gains_t, *[piece[0] for piece in pieces], *before)


def attention_forward(qkv, heads, band):
    _, head_dim, seq_len = qkv.shape

    def kernel(q_ref, k_ref, v_ref, out_ref, mass_ref):
        scores = dot_f32(k_ref[0], q_ref[0], ((0,), (0,)))
        weights = jnp.exp2(scores)
        mass = jnp.sum(weights, axis=0, keepdims=True)
        mixed = dot_f32(v_ref[0], weights.astype(BF16), ((1,), (0,)))
        out_ref[0] = (mixed / mass).astype(BF16)
        mass_ref[0] = jnp.log2(mass)

    return kernel_call(
        kernel,
        grid=(heads,),
        in_specs=[
            pl.BlockSpec((1, head_dim, band), lambda h: (h, 0, 0)),
            pl.BlockSpec((1, head_dim, seq_len), lambda h: (heads + h, 0, 0)),
            pl.BlockSpec((1, head_dim, seq_len), lambda h: (2 * heads + h, 0, 0)),
        ],
        out_specs=[
            pl.BlockSpec((1, head_dim, band), lambda h: (h, 0, 0)),
            pl.BlockSpec((1, 1, band), lambda h: (h, 0, 0)),
        ],
        out_shape=[
            jax.ShapeDtypeStruct((heads, head_dim, band), BF16),
            jax.ShapeDtypeStruct((heads, 1, band), F32),
        ],
        compiler_params=pltpu.CompilerParams(vmem_limit_bytes=14 << 20),
        name="attention_forward",
    )(qkv, qkv, qkv)


def attention_back_own(qkv, out_grad, log_mass, delta, heads, band):
    _, head_dim, seq_len = qkv.shape

    def kernel(q_ref, k_ref, v_ref, grad_ref, mass_ref, delta_ref, dq_ref, dk_ref, dv_ref):
        grad = grad_ref[0]
        scores = dot_f32(k_ref[0], q_ref[0], ((0,), (0,)))
        probs = jnp.exp2(scores - mass_ref[0])
        prob_grad = dot_f32(v_ref[0], grad, ((0,), (0,)))
        score_grad = (probs * (prob_grad - delta_ref[0])).astype(BF16)
        dq_ref[0] = dot_f32(k_ref[0], score_grad, ((1,), (0,)))
        dk_ref[0] = dot_f32(q_ref[0], score_grad[:band], ((1,), (1,)))
        dv_ref[0] = dot_f32(grad, probs[:band].astype(BF16), ((1,), (1,)))

    one = pl.BlockSpec((1, head_dim, band), lambda h: (h, 0, 0))
    row = pl.BlockSpec((1, 1, band), lambda h: (h, 0, 0))
    return kernel_call(
        kernel,
        grid=(heads,),
        in_specs=[
            one,
            pl.BlockSpec((1, head_dim, seq_len), lambda h: (heads + h, 0, 0)),
            pl.BlockSpec((1, head_dim, seq_len), lambda h: (2 * heads + h, 0, 0)),
            one,
            row,
            row,
        ],
        out_specs=[one, one, one],
        out_shape=[pltpu.HBM((heads, head_dim, band), F32)] * 3,
        compiler_params=pltpu.CompilerParams(vmem_limit_bytes=16 << 20),
        name="attention_back_own",
    )(qkv, qkv, qkv, out_grad, log_mass, delta)


def attention_back_other(
    qkv, hat, fac, cos_t, sin_t, gains_t, dq, dk, dv, grads, mass, delta, heads, band
):
    _, head_dim, seq_len = qkv.shape
    inv_root = head_dim**-0.5
    early = grads[0].shape[0]

    def kernel(
        q_ref, k_ref, v_ref, hq_ref, hk_ref, fq_ref, fk_ref, cos_ref, sin_ref, gain_ref,
        dq_ref, dk_ref, dv_ref, low_ref, high_ref, mass_ref, delta_ref, out_ref, gq_ref, gk_ref,
    ):
        grad = jnp.where(pl.program_id(0) < early, low_ref[0], high_ref[0])
        scores = dot_f32(k_ref[0], q_ref[0], ((0,), (0,)))
        probs = jnp.exp2(scores - mass_ref[0])
        prob_grad = dot_f32(v_ref[0], grad, ((0,), (0,)))
        score_grad = (probs * (prob_grad - delta_ref[0])).astype(BF16)
        key_grad = (dk_ref[0] + dot_f32(q_ref[0], score_grad, ((1,), (1,)))) * LN2
        value_grad = dv_ref[0] + dot_f32(grad, probs.astype(BF16), ((1,), (1,)))
        query_grad = dq_ref[0] * inv_root

        def back(turned_grad, hat, fac, gain):
            spun = turned_grad * sin_ref[...]
            spun = jnp.concatenate([spun[head_dim // 2 :], spun[: head_dim // 2]], axis=0)
            gained_grad = turned_grad * cos_ref[...] + spun
            gain_grad = jnp.sum(gained_grad * hat, axis=1, keepdims=True)
            hat_grad = gained_grad * gain
            along = jnp.mean(hat_grad * hat, axis=0, keepdims=True)
            return (fac * (hat_grad - hat * along)).astype(BF16), gain_grad

        out_ref[0, 0], gq_ref[0] = back(query_grad, hq_ref[0].astype(F32), fq_ref[0], gain_ref[:, 0:1])
        out_ref[1, 0], gk_ref[0] = back(key_grad, hk_ref[0].astype(F32), fk_ref[0], gain_ref[:, 1:2])
        out_ref[2, 0] = value_grad.astype(BF16)

    one = pl.BlockSpec((1, head_dim, band), lambda h: (h, 0, 0))
    row = pl.BlockSpec((1, 1, band), lambda h: (h, 0, 0))
    key_one = pl.BlockSpec((1, head_dim, band), lambda h: (heads + h, 0, 0))
    key_row = pl.BlockSpec((1, 1, band), lambda h: (heads + h, 0, 0))
    table = pl.BlockSpec((head_dim, band), lambda h: (0, 0))
    column = pl.BlockSpec((1, head_dim, 1), lambda h: (h, 0, 0))
    return kernel_call(
        kernel,
        grid=(heads,),
        in_specs=[
            pl.BlockSpec((1, head_dim, band), lambda h: (h, 0, 1)),
            key_one,
            pl.BlockSpec((1, head_dim, band), lambda h: (2 * heads + h, 0, 0)),
            one, key_one, row, key_row, table, table,
            pl.BlockSpec((head_dim, 2), lambda h: (0, 0)),
            one, one, one,
            pl.BlockSpec((1, head_dim, band), lambda h: (jnp.minimum(h, early - 1), 0, 0)),
            pl.BlockSpec((1, head_dim, band), lambda h: (jnp.maximum(h - early, 0), 0, 0)),
            row, row,
        ],
        out_specs=[pl.BlockSpec((3, 1, head_dim, band), lambda h: (0, h, 0, 0)), column, column],
        out_shape=[
            jax.ShapeDtypeStruct((3, heads, head_dim, band), BF16),
            jax.ShapeDtypeStruct((heads, head_dim, 1), F32),
            jax.ShapeDtypeStruct((heads, head_dim, 1), F32),
        ],
        compiler_params=pltpu.CompilerParams(vmem_limit_bytes=14 << 20),
        name="attention_back_other",
    )(*[pltpu.with_memory_space_constraint(qkv, pltpu.HBM)] * 3, hat, hat, fac, fac, cos_t, sin_t, gains_t,
      *[pltpu.with_memory_space_constraint(v, pltpu.HBM) for v in (dq, dk, dv)], *grads, mass, delta)


def mlp(mid, mlp_grad, pieces, down_own, down_other):
    band, width = mlp_grad.shape
    rows = pieces[0][0].shape[1]
    half = width // 2
    blocks = sum(piece[0].shape[0] for piece in pieces) // 2
    steps = 4
    per = blocks // steps
    units = per * rows
    chunk = band // 2
    n_z, _, _, down_rows, down_width = down_own.shape

    def kernel(at, mid_ref, mg_ref, *refs):
        downs = refs[len(pieces) : len(pieces) + 2]
        hid_ref, gg_ref, ug_ref, out_ref, grad_ref, buf, down_buf, sems, down_sems = refs[len(pieces) + 2 :]
        step = pl.program_id(0)

        @pl.when(step == 0)
        def _():
            for x in range(2):
                for z in range(n_z):
                    for y in range(2):
                        for c in range(2):
                            block = (z * 2 + y) * 2 + (at[0] + c) % 2
                            target = down_buf.at[x, pl.ds(pl.multiple_of(block * down_rows, 8), down_rows)]
                            pltpu.make_async_copy(downs[c].at[z, y, x], target, down_sems.at[x, block]).start()
            for k, z, x, block in piece_targets(pieces, at):
                pltpu.make_async_copy(refs[k].at[z], buf.at[x, block], sems.at[x, block]).start()
            out_ref[...] = jnp.zeros_like(out_ref)
            grad_ref[...] = jnp.zeros_like(grad_ref)

        for b in range(per):
            for x in range(2):
                block = step * per + b
                pltpu.make_async_copy(refs[0].at[0], buf.at[x, block], sems.at[x, block]).wait()
        @pl.when(step % 2 == 0)
        def _():
            for block in range(4 * n_z):
                target = down_buf.at[step // 2, pl.ds(block * down_rows, down_rows)]
                pltpu.make_async_copy(downs[0].at[0, 0, 0], target, down_sems.at[step // 2, block]).wait()

        low = buf[0, pl.ds(step * per, per)].reshape(units, width)
        high = buf[1, pl.ds(step * per, per)].reshape(units, width)
        gate = jnp.concatenate([low[:, :half], high[:, :half]], axis=1)
        up = jnp.concatenate([low[:, half:], high[:, half:]], axis=1)
        down = down_buf[step // 2, :, pl.ds(pl.multiple_of(step % 2 * units, 128), units)]
        nt, nn = ((1,), (1,)), ((1,), (0,))
        for part in range(2):
            at_rows = pl.ds(part * chunk, chunk)
            mid = mid_ref[at_rows, :]
            gate_pre = dot_f32(mid, gate, nt)
            up_pre = dot_f32(mid, up, nt)
            hidden_grad = dot_f32(mg_ref[at_rows, :], down, nn)
            sig = 1.0 / (1.0 + jnp.exp(-gate_pre))
            act = gate_pre * sig
            hidden = (act * up_pre).astype(BF16)
            gate_grad = (hidden_grad * up_pre * (sig * (1.0 + gate_pre * (1.0 - sig)))).astype(BF16)
            up_grad = (hidden_grad * act).astype(BF16)
            hid_ref[at_rows, :] = hidden
            gg_ref[:, at_rows] = gate_grad.T
            ug_ref[:, at_rows] = up_grad.T
            out_ref[at_rows, :] += dot_f32(hidden, down, nt)
            grad_ref[at_rows, :] += dot_f32(gate_grad, gate, nn) + dot_f32(up_grad, up, nn)

    whole = lambda i, at: (0, 0)
    once = pl.Buffered(1)
    return kernel_call(
        kernel,
        grid_spec=pltpu.PrefetchScalarGridSpec(
            num_scalar_prefetch=1,
            grid=(steps,),
            in_specs=[
                pl.BlockSpec((band, width), whole, pipeline_mode=once),
                pl.BlockSpec((band, width), whole, pipeline_mode=once),
            ]
            + [pl.BlockSpec(memory_space=pl.ANY)] * (len(pieces) + 2),
            out_specs=[
                pl.BlockSpec((band, units), lambda i, at: (0, i)),
                pl.BlockSpec((units, band), lambda i, at: (i, 0)),
                pl.BlockSpec((units, band), lambda i, at: (i, 0)),
                pl.BlockSpec((band, width), whole, pipeline_mode=once),
                pl.BlockSpec((band, width), whole, pipeline_mode=once),
            ],
            scratch_shapes=[
                pltpu.VMEM((2, blocks, rows, width), BF16),
                pltpu.VMEM((2, width, down_width), BF16),
                pltpu.SemaphoreType.DMA((2, blocks)),
                pltpu.SemaphoreType.DMA((2, 4 * n_z)),
            ],
        ),
        out_shape=[
            jax.ShapeDtypeStruct((band, blocks * rows), BF16),
            jax.ShapeDtypeStruct((blocks * rows, band), BF16),
            jax.ShapeDtypeStruct((blocks * rows, band), BF16),
            jax.ShapeDtypeStruct((band, width), F32),
            jax.ShapeDtypeStruct((band, width), F32),
        ],
        compiler_params=pltpu.CompilerParams(vmem_limit_bytes=56 << 20),
        name="mlp",
    )(place(), mid, mlp_grad, *[piece[0] for piece in pieces], down_own, down_other)


def after_attention(attended_t, proj_t, residual_low, modulation):
    width, band = attended_t.shape
    half = width // 2
    block = 128

    def kernel(att_ref, proj_ref, low_ref, mod_ref, branch_ref, middle_ref, normed_ref, mid_ref, att_out_ref):
        branch = dot_f32(att_ref[...], proj_ref[...], ((0,), (1,)))
        middle = low_ref[...].astype(F32) + mod_ref[2:3, :] * branch
        normed = modulate(middle, mod_ref[3:4, :], mod_ref[4:5, :]).astype(BF16)
        attended = att_ref[...].T
        branch_ref[...] = branch.astype(BF16)
        middle_ref[...] = middle
        normed_ref[...] = normed
        for x in range(2):
            mid_ref[x] = normed[:, x * half : (x + 1) * half]
            att_out_ref[x] = attended[:, x * half : (x + 1) * half]

    rows = pl.BlockSpec((block, width), lambda i: (i, 0))
    halves = pl.BlockSpec((2, block, half), lambda i: (0, i, 0))
    return kernel_call(
        kernel,
        grid=(band // block,),
        in_specs=[
            pl.BlockSpec((width, block), lambda i: (0, i)),
            pl.BlockSpec((width, width), lambda i: (0, 0)),
            rows,
            pl.BlockSpec((6, width), lambda i: (0, 0)),
        ],
        out_specs=[rows, rows, rows, halves, halves],
        out_shape=[
            pltpu.HBM((band, width), BF16),
            pltpu.HBM((band, width), F32),
            jax.ShapeDtypeStruct((band, width), BF16),
            jax.ShapeDtypeStruct((2, band, half), BF16),
            jax.ShapeDtypeStruct((2, band, half), BF16),
        ],
        compiler_params=pltpu.CompilerParams(vmem_limit_bytes=20 << 20),
        name="after_attention",
    )(*[pltpu.with_memory_space_constraint(v, pltpu.HBM) for v in (attended_t, proj_t, residual_low)], modulation)


def middle_back(normed_mid_grad, middle, out_grad, branch, mlp_out, proj_t, attended_t, modulation):
    band, width = middle.shape
    half = width // 2
    head_dim = width // HEADS
    block = 128

    def kernel(
        normed_grad_ref, mid_ref, out_ref, branch_ref, mlp_ref, proj_ref, att_ref, mod_ref,
        grad_ref, bg_ref, att_grad_ref, delta_ref, result_ref, sums_ref,
    ):
        @pl.when(pl.program_id(0) == 0)
        def _():
            sums_ref[...] = jnp.zeros_like(sums_ref)

        normed_grad = normed_grad_ref[...]
        middle, grad, mlp_out = mid_ref[...], out_ref[...].astype(F32), mlp_ref[...]
        fac = norm_factor(middle)
        hat = middle * fac
        hat_grad = normed_grad * (1.0 + mod_ref[4:5, :])
        along = jnp.mean(hat_grad * hat, axis=-1, keepdims=True)
        mid_grad = grad + fac * (hat_grad - hat * along)
        branch_grad = (mod_ref[2:3, :] * mid_grad).astype(BF16)
        attended_grad = dot_f32(branch_grad, proj_ref[...], ((1,), (0,))).astype(BF16).T
        grad_ref[...] = mid_grad
        bg_ref[...] = branch_grad.T
        att_grad_ref[...] = attended_grad
        both = attended_grad.astype(F32) * att_ref[...].astype(F32)
        delta_ref[...] = jnp.sum(both.reshape(HEADS, head_dim, block), axis=1, keepdims=True)
        result_ref[...] = (middle + mod_ref[5:6, :] * mlp_out).astype(BF16)
        sums_ref[0:1, :] += jnp.sum(normed_grad, axis=0, keepdims=True)
        sums_ref[1:2, :] += jnp.sum(normed_grad * hat, axis=0, keepdims=True)
        sums_ref[2:3, :] += jnp.sum(mid_grad * branch_ref[...].astype(F32), axis=0, keepdims=True)
        sums_ref[3:4, :] += jnp.sum(grad * mlp_out, axis=0, keepdims=True)

    rows = pl.BlockSpec((block, width), lambda i: (i, 0))
    columns = pl.BlockSpec((width, block), lambda i: (0, i))
    return kernel_call(
        kernel,
        grid=(band // block,),
        in_specs=[
            rows, rows, rows, rows, rows,
            pl.BlockSpec((width, width), lambda i: (0, 0)),
            columns,
            pl.BlockSpec((6, width), lambda i: (0, 0)),
        ],
        out_specs=[
            rows, columns, columns,
            pl.BlockSpec((HEADS, 1, block), lambda i: (0, 0, i)),
            rows,
            pl.BlockSpec((8, width), lambda i: (0, 0)),
        ],
        out_shape=[
            pltpu.HBM((band, width), F32),
            jax.ShapeDtypeStruct((width, band), BF16),
            jax.ShapeDtypeStruct((width, band), BF16),
            jax.ShapeDtypeStruct((HEADS, 1, band), F32),
            jax.ShapeDtypeStruct((band, width), BF16),
            jax.ShapeDtypeStruct((8, width), F32),
        ],
        compiler_params=pltpu.CompilerParams(vmem_limit_bytes=20 << 20),
        name="middle_back",
    )(normed_mid_grad, middle, out_grad, branch, mlp_out, proj_t, attended_t, modulation)


def input_back(projected_t, qkv_t, latents, mid_grad, modulation):
    inner, band = projected_t.shape
    width = qkv_t.shape[1]
    block = 128

    def kernel(left_ref, weight_ref, low_ref, grad_ref, mod_ref, out_ref, sums_ref):
        @pl.when(pl.program_id(0) == 0)
        def _():
            sums_ref[...] = jnp.zeros_like(sums_ref)

        normed_grad = dot_f32(left_ref[...], weight_ref[...], ((0,), (0,)))
        residual = low_ref[...].astype(F32)
        fac = norm_factor(residual)
        hat = residual * fac
        hat_grad = normed_grad * (1.0 + mod_ref[1:2, :])
        along = jnp.mean(hat_grad * hat, axis=-1, keepdims=True)
        out_ref[...] = grad_ref[...] + fac * (hat_grad - hat * along)
        sums_ref[0:1, :] += jnp.sum(normed_grad, axis=0, keepdims=True)
        sums_ref[1:2, :] += jnp.sum(normed_grad * hat, axis=0, keepdims=True)

    rows = pl.BlockSpec((block, width), lambda i: (i, 0))
    return kernel_call(
        kernel,
        grid=(band // block,),
        in_specs=[
            pl.BlockSpec((inner, block), lambda i: (0, i)),
            pl.BlockSpec((inner, width), lambda i: (0, 0), pipeline_mode=pl.Buffered(1)),
            rows,
            rows,
            pl.BlockSpec((6, width), lambda i: (0, 0)),
        ],
        out_specs=[rows, pl.BlockSpec((8, width), lambda i: (0, 0))],
        out_shape=[jax.ShapeDtypeStruct((band, width), F32), jax.ShapeDtypeStruct((8, width), F32)],
        compiler_params=pltpu.CompilerParams(vmem_limit_bytes=24 << 20),
        name="input_back",
    )(projected_t, *[pltpu.with_memory_space_constraint(v, pltpu.HBM) for v in (qkv_t, latents, mid_grad)], modulation)


def place():
    return jnp.stack([lax.axis_index(axis) for axis in ("c", "x", "y")]).astype(jnp.int32)


def terms(lefts, right, rows, side, received=None, z_first=0, n_z=4, y=(0, 1), order=(0, 1), stacked=True, split=0, kind=jax.ShapeDtypeStruct):
    patches = right.shape[0] if right.ndim == 2 else right.shape[1]
    wide = right.ndim == 2
    each = right.shape[-1] // 2 if wide else right.shape[-1]
    width = each * len(lefts)
    count = split or len(y) * n_z
    n = len(lefts)

    def left_map(i, at):
        if split:
            return (i, 0)
        z = z_first + i % n_z
        return ((z * 2 + (y[0] + i // n_z + at[2]) % 2) * 2 + (at[0] + side) % 2, 0)

    def right_spec(h):
        if wide:
            return pl.BlockSpec((patches, each), lambda i, at: (0, (at[1] + h) % 2))
        return pl.BlockSpec((1, patches, each), lambda i, at: ((at[1] + h) % 2, 0, 0))

    def kernel(at, *refs):
        rights, outs = refs[n : n + 2], refs[n + 2 :]
        if received is not None:
            got, outs = refs[n + 2 : n + 4], refs[n + 4 :]
        for k in range(2):
            half = rights[k][...] if wide else rights[k][0]
            values = [dot_f32(refs[m][...], half, ((1,), (0,))) for m in range(n)]
            value = values[0] if n == 1 else jnp.concatenate(values, axis=1)
            if received is not None:
                value = value + got[k][0, 0].astype(F32)
            if not stacked:
                outs[k][0] = value.astype(BF16)
            elif split:
                outs[0][0, k] = value.astype(BF16)
            else:
                outs[0][k, 0] = value.astype(BF16)

    received_specs = []
    if received is not None:
        skip = 0 if split else y[0] * n_z
        received_specs = [
            pl.BlockSpec((1, 1, rows, width), lambda i, at, k=k: (i, k, 0, 0) if split else (k, i + skip, 0, 0))
            for k in range(2)
        ]
    if stacked and split:
        out_shape = [kind((count, 2, rows, width), BF16)]
        out_specs = [pl.BlockSpec((1, 2, rows, width), lambda i, at: (i, 0, 0, 0))]
    elif stacked:
        out_shape = [kind((2, count, rows, width), BF16)]
        out_specs = [pl.BlockSpec((2, 1, rows, width), lambda i, at: (0, i, 0, 0))]
    else:
        out_shape = [jax.ShapeDtypeStruct((count, rows, width), BF16)] * 2
        out_specs = [pl.BlockSpec((1, rows, width), lambda i, at: (i, 0, 0))] * 2
    outs = kernel_call(
        kernel,
        grid_spec=pltpu.PrefetchScalarGridSpec(
            num_scalar_prefetch=1,
            grid=(count,),
            in_specs=[pl.BlockSpec((rows, patches), left_map)] * n
            + [right_spec(h) for h in order]
            + received_specs,
            out_specs=out_specs,
        ),
        out_shape=out_shape,
        compiler_params=pltpu.CompilerParams(vmem_limit_bytes=12 << 20),
        name="terms",
    )(place(), *lefts, right, right, *([received] * 2 if received is not None else []))
    return outs[0] if stacked else outs


def last_terms(left, right, rows, cut, received):
    patches, width = left.shape[-1], right.shape[-1]
    n_z = 4
    late = rows - cut

    def row_of(i):
        return 1 - i // n_z

    def kernel(at, left_ref, own_ref, other_ref, r0_ref, r1_ref, keep_ref, send_ref, up_send_ref, up_keep_ref):
        values = [
            (dot_f32(left_ref[...], ref[0], ((1,), (0,))) + got[0, 0].astype(F32)).astype(BF16)
            for ref, got in ((own_ref, r0_ref), (other_ref, r1_ref))
        ]
        keep_ref[0] = values[0][:cut]
        send_ref[0] = values[1][:cut]

        @pl.when(pl.program_id(0) < n_z)
        def _():
            for k in range(2):
                up_send_ref[1 - k, 0] = values[k][cut:]

        @pl.when(pl.program_id(0) >= n_z)
        def _():
            for k in range(2):
                up_keep_ref[1 - k, 0] = values[k][cut:]

    def got(h):
        return pl.BlockSpec((1, 1, rows, width), lambda i, at: (h, row_of(i) * n_z + i % n_z, 0, 0))

    early_spec = pl.BlockSpec((1, cut, width), lambda i, at: (row_of(i) * n_z + i % n_z, 0, 0))
    return kernel_call(
        kernel,
        grid_spec=pltpu.PrefetchScalarGridSpec(
            num_scalar_prefetch=1,
            grid=(2 * n_z,),
            in_specs=[
                pl.BlockSpec(
                    (rows, patches), lambda i, at: ((i % n_z * 2 + (row_of(i) + at[2]) % 2) * 2 + at[0], 0)
                ),
                pl.BlockSpec((1, patches, width), lambda i, at: (at[1], 0, 0)),
                pl.BlockSpec((1, patches, width), lambda i, at: ((at[1] + 1) % 2, 0, 0)),
                got(0),
                got(1),
            ],
            out_specs=[
                early_spec,
                early_spec,
                pl.BlockSpec((2, 1, late, width), lambda i, at: (0, jnp.minimum(i, n_z - 1), 0, 0)),
                pl.BlockSpec((2, 1, late, width), lambda i, at: (0, jnp.maximum(i - n_z, 0), 0, 0)),
            ],
        ),
        out_shape=[
            pltpu.HBM((2 * n_z, cut, width), BF16),
            jax.ShapeDtypeStruct((2 * n_z, cut, width), BF16),
            jax.ShapeDtypeStruct((2, n_z, late, width), BF16),
            pltpu.HBM((2, n_z, late, width), BF16),
        ],
        compiler_params=pltpu.CompilerParams(vmem_limit_bytes=12 << 20),
        name="last_terms",
    )(place(), left, right, right, received, received)


def split_rows(left_t, z_first):
    n_z, patches = lax.axis_size("z"), left_t.shape[-1]
    blocks = left_t.reshape(n_z, 2, 2, -1, patches)
    core, row = lax.axis_index("c"), lax.axis_index("y")

    def part(which):
        picked = lax.dynamic_index_in_dim(blocks, which, 2, keepdims=False)
        own = lax.dynamic_index_in_dim(picked, row, 1, keepdims=False)
        other = lax.dynamic_index_in_dim(picked, 1 - row, 1, keepdims=False)
        return jnp.stack([own, other], axis=1 if z_first else 0).reshape(-1, patches)

    return part(1 - core), part(core)


def summed_over(values, axes, size):
    low = values.astype(BF16)
    parts = [low] + [lax.ppermute(low, axes, [(i, i ^ hop) for i in range(size)]) for hop in range(1, size)]
    parts = [part.astype(F32) for part in parts]
    while len(parts) > 1:
        parts = [left + right for left, right in zip(parts[::2], parts[1::2])]
    return parts[0]


def spread_rows(hots, values):
    items, width = values.shape
    count = hots[0].shape[1]
    block = 384

    def kernel(values_ref, *refs):
        rest, parts = values_ref[...], []
        for _ in range(3):
            high = rest.astype(BF16)
            parts.append(high)
            rest = rest - high.astype(F32)
        for hot_ref, out_ref in zip(refs[: len(hots)], refs[len(hots) :]):
            hot = hot_ref[...]
            out_ref[...] = sum(dot_f32(hot, part, ((0,), (0,))) for part in parts)

    return kernel_call(
        kernel,
        grid=(width // block,),
        in_specs=[pl.BlockSpec((items, block), lambda i: (0, i))]
        + [pl.BlockSpec((items, count), lambda i: (0, 0))] * len(hots),
        out_specs=[pl.BlockSpec((count, block), lambda i: (0, i))] * len(hots),
        out_shape=[jax.ShapeDtypeStruct((count, width), F32)] * len(hots),
        compiler_params=pltpu.CompilerParams(vmem_limit_bytes=16 << 20),
        name="spread_rows",
    )(values, *hots)


def in_float32(values, rows, columns):
    sizes = [(r, c) for r in rows for c in columns]

    def kernel(in_ref, *out_refs):
        at_row = 0
        for m, r in enumerate(rows):
            at_column = 0
            for n, c in enumerate(columns):
                part = in_ref[at_row : at_row + r, at_column : at_column + c]
                out_refs[m * len(columns) + n][...] = part.astype(F32)
                at_column += c
            at_row += r

    return kernel_call(
        kernel,
        out_shape=[jax.ShapeDtypeStruct(size, F32) for size in sizes],
        compiler_params=pltpu.CompilerParams(vmem_limit_bytes=8 << 20),
        name="in_float32",
    )(values)


def outer_terms(left, right):
    def kernel(left_ref, right_ref, out_ref):
        out_ref[...] = dot_f32(left_ref[...], right_ref[...], ((0,), (0,)))

    return kernel_call(
        kernel,
        out_shape=[jax.ShapeDtypeStruct((left.shape[1], right.shape[1]), F32)],
        compiler_params=pltpu.CompilerParams(vmem_limit_bytes=8 << 20),
        name="outer_terms",
    )(left, right)[0]


def fast_shards(
    latents, out_grad, time_table, class_table, buckets, labels, row_start,
    ada_weight, qkv_weight, proj_weight, gate_weight, up_weight, down_weight, query_gain, key_gain,
):
    band, width = latents.shape[1:]
    head_dim = width // HEADS
    lat, out_g = latents[0], out_grad[0]
    half = width // 2
    n_z = lax.axis_size("z")

    qkv_s, proj_s = qkv_weight[0].T, proj_weight[0].T
    gate_s, up_s, down_s = gate_weight[0].T, up_weight[0].T, by_rows(down_weight[0].T)
    qkv_rows, proj_rows, gate_rows = qkv_s.shape[0], proj_s.shape[0], gate_s.shape[0]
    cut = (qkv_rows + proj_rows) // 2
    first = by_rows(jnp.concatenate([qkv_s[:cut], jnp.concatenate([qkv_s[cut:], proj_s])], axis=1))
    second = by_rows(jnp.concatenate([gate_s, up_s], axis=1))

    first_z = gather_z(first)
    second_z = gather_z(second)
    start_other = swap(row_start.astype(F32), "x")
    (down_r,) = together(swap(down_s, "x"))
    down_x = in_order(down_s, down_r, "x")
    down_x, lat_x = together(down_x, lat)
    lat_other = swap(lat_x, "x")
    down_r = swap(down_x, "y")

    bucket_hot = (buckets[:, None] == jnp.arange(BUCKETS, dtype=jnp.int32)[None, :]).astype(BF16)
    class_hot = (labels[:, None] == jnp.arange(CLASSES, dtype=jnp.int32)[None, :]).astype(BF16)
    cond = jnp.dot(bucket_hot, time_table, preferred_element_type=F32) + jnp.dot(
        class_hot, class_table, preferred_element_type=F32
    )
    cond_act = jax.nn.silu(cond).astype(BF16)
    mod_cols = jnp.dot(cond_act, ada_weight[0], preferred_element_type=F32)

    offsets = jnp.arange(band, dtype=jnp.int32)
    rows_in = (offsets // SIDE).astype(F32)
    row_pos = jnp.concatenate([row_start.astype(F32)[0, 0] + rows_in, start_other[0, 0] + rows_in])
    col_pos = jnp.tile((offsets % SIDE).astype(F32), 2)
    quarter = head_dim // 4
    frequency = THETA ** (-jnp.arange(quarter, dtype=F32) / quarter)
    angles = jnp.concatenate([frequency[:, None] * row_pos[None], frequency[:, None] * col_pos[None]])
    cos_h, sin_h = jnp.cos(angles), jnp.sin(angles)
    cos_t = jnp.concatenate([cos_h, cos_h])
    sin_t = jnp.concatenate([-sin_h, sin_h])
    gains_t = jnp.concatenate([query_gain, key_gain]).T
    first_z, lat_other, down_r, mod_cols, cos_t, sin_t = together(first_z, lat_other, down_r, mod_cols, cos_t, sin_t)

    a, b = by_rows(first_z[:2]), by_rows(first_z[2:])
    a_y, b_x, a_c, b_c = swap(a, "y"), swap(b, "x"), swap(a, "c"), swap(b, "c")
    down_z = gather_z(in_order(down_x, down_r, "y").reshape(-1, down_x.shape[-1]))
    modulation = lax.all_to_all(mod_cols, DP_AXES, split_axis=0, concat_axis=1, tiled=True)
    a_y, b_x, a_c, b_c, modulation = together(a_y, b_x, a_c, b_c, modulation)

    a_x, b_y, a_yc, b_xc = swap(a, "x"), swap(b, "y"), swap(a_y, "c"), swap(b_x, "c")
    mods = modulation.reshape(6, width)
    shift_attn, scale_attn, gate_attn, shift_mlp, scale_mlp, gate_mlp = jnp.split(modulation, 6, axis=-1)
    lat_full = jnp.concatenate([lat, lat_other]).astype(F32)
    normed_full = modulate(lat_full, shift_attn, scale_attn).astype(BF16)
    a_x, b_y, a_yc, b_xc, normed_full = together(a_x, b_y, a_yc, b_xc, normed_full)

    a_yx, b_xy, a_xc, b_yc = swap(a_y, "x"), swap(b_x, "y"), swap(a_x, "c"), swap(b_y, "c")
    mlp_grad = (gate_mlp * out_g.astype(F32)).astype(BF16)
    down_send, down_keep = split_rows(mlp_grad.T, True)
    normed = normed_full[:band]
    normed_2 = jnp.stack([normed[:, :half], normed[:, half:]])
    second_z, a_yx, b_xy, a_xc, b_yc, mlp_grad, down_send, down_keep, normed_2 = together(
        second_z, a_yx, b_xy, a_xc, b_yc, mlp_grad, down_send, down_keep, normed_2
    )

    a_yxc, b_xyc = swap(a_yx, "c"), swap(b_xy, "c")
    e, f = by_rows(second_z[:2]), by_rows(second_z[2:])
    e_y, f_x = swap(e, "y"), swap(f, "x")
    pieces_own = [
        (a, 0, 0, 0, 0), (a_y, 0, 0, 1, 0), (a_x, 0, 1, 0, 0), (a_yx, 0, 1, 1, 0),
        (b, 2, 0, 0, 0), (b_x, 2, 1, 0, 0), (b_y, 2, 0, 1, 0), (b_xy, 2, 1, 1, 0),
    ]
    tables = (cos_t, sin_t, gains_t, head_dim, band)
    parts = qkv_heads(normed_full, pieces_own, *tables)
    *parts, e_y, f_x, a_yxc, b_xyc = together(*parts, e_y, f_x, a_yxc, b_xyc)

    e_x, f_y, e_c, f_c, e_yc = swap(e, "x"), swap(f, "y"), swap(e, "c"), swap(f, "c"), swap(e_y, "c")
    pieces_other = [
        (a_c, 0, 0, 0, 1), (a_yc, 0, 0, 1, 1), (a_xc, 0, 1, 0, 1), (a_yxc, 0, 1, 1, 1),
        (b_c, 2, 0, 0, 1), (b_xc, 2, 1, 0, 1), (b_yc, 2, 0, 1, 1), (b_xyc, 2, 1, 1, 1),
    ]
    qkv, hat, fac, qkv_t = qkv_heads(normed_full, pieces_other, *tables, before=parts)
    e_x, f_y, e_c, f_c, e_yc, qkv = together(e_x, f_y, e_c, f_c, e_yc, qkv)

    e_yx, f_xy = swap(e_y, "x"), swap(f_x, "y")
    f_xc, e_xc, f_yc = swap(f_x, "c"), swap(e_x, "c"), swap(f_y, "c")
    attended_t, log_mass = attention_forward(qkv, HEADS, band)
    proj_t = join_rows(pieces_own + pieces_other, qkv_rows - cut, proj_rows).reshape(width, width)
    e_yx, f_xy, f_xc, e_xc, f_yc, attended_t, proj_t, down_z = together(
        e_yx, f_xy, f_xc, e_xc, f_yc, attended_t, proj_t, down_z
    )

    down_own = down_z.reshape(n_z, 2, 2, -1, down_z.shape[-1])
    down_other, e_yxc, f_xyc = swap(down_own, "c"), swap(e_yx, "c"), swap(f_xy, "c")
    attended_t = attended_t.reshape(width, band)
    branch, middle, normed_mid, mid_2, att_2 = after_attention(attended_t, proj_t, lat, mods)
    pieces = [
        (e, 0, 0, 0, 0), (e_y, 0, 0, 1, 0), (e_x, 0, 1, 0, 0), (e_yx, 0, 1, 1, 0),
        (e_c, 0, 0, 0, 1), (e_yc, 0, 0, 1, 1), (e_xc, 0, 1, 0, 1), (e_yxc, 0, 1, 1, 1),
        (f, 2, 0, 0, 0), (f_x, 2, 1, 0, 0), (f_y, 2, 0, 1, 0), (f_xy, 2, 1, 1, 0),
        (f_c, 2, 0, 0, 1), (f_xc, 2, 1, 0, 1), (f_yc, 2, 0, 1, 1), (f_xyc, 2, 1, 1, 1),
    ]
    hidden, gate_grad_t, up_grad_t, mlp_out, normed_mid_grad = mlp(
        normed_mid, mlp_grad, pieces, down_own, down_other
    )

    gates = (gate_grad_t, up_grad_t)
    a_g = terms([pltpu.with_memory_space_constraint(v, pltpu.HBM) for v in gates], mid_2, gate_rows, 1, n_z=2)
    a_g, hidden, *gates, mlp_out, normed_mid_grad = together(a_g, hidden, *gates, mlp_out, normed_mid_grad)

    a_gr = swap(a_g, "c")
    mid_grad, branch_grad_t, attended_grad, delta, result, sums = middle_back(
        normed_mid_grad, middle, out_g, branch, mlp_out, proj_t, attended_t, mods
    )
    b_g = terms(gates, mid_2, gate_rows, 1, z_first=2, n_z=2, order=(1, 0))
    by_head = attended_grad.reshape(HEADS, head_dim, band)
    a_gr, b_g, by_head, delta, branch_grad_t = together(a_gr, b_g, by_head, delta, branch_grad_t)

    b_gr = swap(b_g, "c")
    other_first = swap(by_head[:6], "x")
    a_k, a_s = terms(gates, mid_2, gate_rows, 0, received=a_gr, n_z=2, stacked=False)
    proj_send, proj_keep = split_rows(branch_grad_t, False)
    down_g = terms((down_send,), hidden, 2 * proj_rows, 1, split=n_z)
    b_gr, other_first, a_k, a_s, down_g, proj_send, proj_keep = together(
        b_gr, other_first, a_k, a_s, down_g, proj_send, proj_keep
    )

    down_gr = swap(down_g, "c")
    a_r1 = [swap(a_s[2:3], "x")]
    b_s = terms(gates, mid_2, gate_rows, 0, received=b_gr, z_first=2, n_z=2, y=(1,), order=(1, 0))
    b_k = terms(gates, mid_2, gate_rows, 0, received=b_gr, z_first=2, n_z=2, y=(0,), order=(1, 0), kind=pltpu.HBM)
    proj_g = terms((proj_send,), att_2, n_z * proj_rows, 1, order=(1, 0), split=2)
    down_gr, a_r1[0], b_s, b_k, proj_g = together(down_gr, a_r1[0], b_s, b_k, proj_g)

    proj_gr = swap(proj_g, "c")
    a_r1.append(swap(a_s[3:4], "x"))
    b_s = b_s.reshape(4, gate_rows, width)
    b_r1 = [swap(b_s[:1], "y")]
    down_sum = terms((down_keep,), hidden, 2 * proj_rows, 0, received=down_gr, split=n_z, kind=pltpu.HBM)
    proj_gr, a_r1[1], b_r1[0], down_sum = together(proj_gr, a_r1[1], b_r1[0], down_sum)

    down_sum = lax.psum_scatter(
        down_sum.reshape(-1, down_sum.shape[-1]), "z", scatter_dimension=0, tiled=True
    ).reshape(2, 2, proj_rows, -1)
    other_last = swap(by_head[6:], "x")
    other_rows = swap(jnp.stack([log_mass, delta]), "x")
    b_r1.append(swap(b_s[1:3], "y"))
    dq, dk, dv = attention_back_own(qkv, by_head, log_mass, delta, HEADS, band)
    b_r1[1], other_last, other_rows, dq = together(b_r1[1], other_last, other_rows, dq)

    a_r1.append(swap(a_s[:2], "x"))
    b_r1.append(swap(b_s[3:], "y"))
    a_s2 = add_low(a_k[2:], jnp.concatenate(a_r1[:2]))
    a_r2 = [swap(a_s2[:1], "y")]
    heads_grad, gain_q, gain_k = attention_back_other(
        qkv, hat, fac, cos_t, sin_t, gains_t, dq, dk, dv,
        (other_first, other_last), other_rows[0], other_rows[1], HEADS, band,
    )
    projected_t = heads_grad.reshape(3 * width, band)
    a_r1[2], b_r1[2], a_r2[0], projected_t = together(a_r1[2], b_r1[2], a_r2[0], projected_t)

    b_r1 = jnp.concatenate(b_r1).reshape(2, 2, gate_rows, width)
    b_s2 = add_low(b_k[0], b_r1[0])
    b_r2 = [swap(b_s2[:1], "x")]
    a_r2.append(swap(a_s2[1:], "y"))
    q_g = terms((projected_t,), normed_2, qkv_rows, 1)
    b_r2[0], a_r2[1], q_g, proj_gr = together(b_r2[0], a_r2[1], q_g, proj_gr)

    q_gr = swap(q_g, "c")
    b_r2.append(swap(b_s2[1:], "x"))
    proj_sum = terms((proj_keep,), att_2, n_z * proj_rows, 0, received=proj_gr, order=(1, 0), split=2)
    proj_r1 = [swap(proj_sum[1, 0], "y")]
    q_gr, b_r2[1], proj_r1[0], proj_sum = together(q_gr, b_r2[1], proj_r1[0], proj_sum)

    row_a = 112
    qa_keep, qa_send, qb_send, qb_keep = last_terms(projected_t, normed_2, qkv_rows, row_a, q_gr)
    proj_r1.append(swap(proj_sum[1, 1], "y"))
    proj_r2 = swap(add_low(proj_sum[0, 0], proj_r1[0]), "x")
    gu = jnp.concatenate(
        [add_low(a_k[:2], a_r1[2], jnp.concatenate(a_r2)), add_low(b_k[1], b_r1[1], jnp.concatenate(b_r2))]
    )
    qa_keep, qa_send, qb_send, qb_keep, proj_r1[1], proj_r2, projected_t, gu, gain_q, gain_k = together(
        qa_keep, qa_send, qb_send, qb_keep, proj_r1[1], proj_r2, projected_t, gu, gain_q, gain_k
    )

    gu = lax.psum_scatter(gu.reshape(-1, width), "z", scatter_dimension=0, tiled=True)
    qa_r1, qb_r1 = swap(qa_send, "x"), swap(qb_send, "y")
    input_grad, in_sums = input_back(projected_t, qkv_t, lat, mid_grad, mods)
    mod_grad = jnp.concatenate([in_sums[0:1], in_sums[1:2], sums[2:3], sums[0:1], sums[1:2], sums[3:4]], axis=-1)
    small = jnp.concatenate([mod_grad, gain_q.sum(0).T, gain_k.sum(0).T], axis=-1)
    small_r = swap(small, "x")
    qa_r1, qb_r1, down_sum, small_r = together(qa_r1, qb_r1, down_sum, small_r)

    qa_keep, qa_r1 = qa_keep.reshape(2, n_z, row_a, half), qa_r1.reshape(2, n_z, row_a, half)
    qa_s2, qb_s2, small = together(
        add_low(qa_keep[1], qa_r1[1]), add_low(qb_keep[0], qb_r1[0]), small + small_r
    )
    qa_r2, qb_r2 = swap(qa_s2, "y"), swap(qb_s2, "x")
    band_mod, band_gain = small[:, : 6 * width], small[:, 6 * width :]
    mod_cols_grad = lax.all_to_all(band_mod.astype(BF16), DP_AXES, split_axis=1, concat_axis=0, tiled=True)
    qa_r2, qb_r2, down_sum, mod_cols_grad = together(qa_r2, qb_r2, down_sum, mod_cols_grad)

    last = jnp.concatenate(
        [
            add_low(qa_keep[0], qa_r1[0], qa_r2),
            add_low(qb_keep[1], qb_r1[1], qb_r2),
            add_low(proj_sum[0, 1], proj_r1[1], proj_r2).reshape(n_z, proj_rows, half),
        ],
        axis=1,
    )
    last, gu, mod_cols_grad = together(last, gu, mod_cols_grad)
    last = lax.psum_scatter(last.reshape(-1, half), "z", scatter_dimension=0, tiled=True)
    cond_act_part = dot_f32(mod_cols_grad, ada_weight[0], ((1,), (1,)))
    tail = jnp.zeros((8, width), F32).at[0, : 2 * head_dim].set(band_gain[0])
    summed = summed_over(jnp.concatenate([cond_act_part, tail]), ("y", "c"), 4)
    summed, down_sum = together(summed, down_sum)
    down_r = swap(down_sum[:, 1], "y")
    down_sum = add_low(down_sum[:, 0], down_r)
    down_r2 = swap(down_sum[1], "x")
    summed = summed_over(summed, "z", n_z)
    ada_grad = outer_terms(mod_cols_grad, cond_act).T
    items = cond.shape[0]
    _, silu_back = jax.vjp(jax.nn.silu, cond)
    cond_grad = silu_back(summed[:items])[0]
    time_grad, class_grad = spread_rows((bucket_hot, class_hot), cond_grad)
    down_out = down_sum[0].astype(F32) + down_r2.astype(F32)

    qkv_grad, proj_grad = in_float32(last, [qkv_rows, proj_rows], [half])
    gate_grad, up_grad = in_float32(gu, [gate_rows], [half, half])

    def out(values):
        return values.T[None]

    return (
        result[None],
        input_grad[None],
        time_grad,
        class_grad,
        ada_grad[None],
        out(qkv_grad),
        out(proj_grad),
        out(gate_grad),
        out(up_grad),
        out(down_out),
        summed[items : items + 1, :head_dim],
        summed[items : items + 1, head_dim : 2 * head_dim],
    )


def fast_solution(mesh):
    dp = mesh.shape["dp"]
    fine = jax.sharding.Mesh(mesh.devices.reshape(dp // 4, 2, 2, 2), ("z", "y", "c", "x"))
    items, last = P(DP_AXES, "x", None), P(None, "x", DP_AXES)
    in_specs = (items, items, P(), P(), P(), P(), P(DP_AXES, "x"), P(None, None, DP_AXES)) + (last,) * 5 + (P(), P())
    out_specs = (items, items, P(), P(), P(None, None, DP_AXES)) + (last,) * 5 + (P(), P())
    return jax.shard_map(fast_shards, mesh=fine, in_specs=in_specs, out_specs=out_specs, check_vma=False)


def solution(mesh):
    if mesh.shape["dp"] == 16 and mesh.shape["seq"] == 2:
        return fast_solution(mesh)
    in_specs = (
        P("dp", "seq", None),
        P("dp", "seq", None),
        P(),
        P(),
        P(),
        P(),
        P("dp", "seq"),
        P(None, None, "dp"),
        P(None, "seq", "dp"),
        P(None, "seq", "dp"),
        P(None, "seq", "dp"),
        P(None, "seq", "dp"),
        P(None, "seq", "dp"),
        P(),
        P(),
    )
    out_specs = (
        P("dp", "seq", None),
        P("dp", "seq", None),
        P(),
        P(),
        P(None, None, "dp"),
        P(None, "seq", "dp"),
        P(None, "seq", "dp"),
        P(None, "seq", "dp"),
        P(None, "seq", "dp"),
        P(None, "seq", "dp"),
        P(),
        P(),
    )
    return jax.shard_map(shards, mesh=mesh, in_specs=in_specs, out_specs=out_specs, check_vma=False)
```
